32 devices in a mesh: seq: 16 (over z, y, x), batch: 2 (over core).
Axes of the slice: x: 2, y: 2, z: 4, core: 2. Of those that a mesh axis runs over, the one named last changes fastest.
Arguments:
- inputs: bfloat16 [2, 4096, 512], P('batch', 'seq'), may hold values from -6 to 6
- cotangent: bfloat16 [2, 4096, 512], P('batch', 'seq'), may hold values from -6 to 6
- lengths: int32 [2, 4], P('batch'), may hold values from 1 to 2048, as said below
- master: float32 [2759168], P(('seq', 'batch')), may hold values from -9.2 to 30, as said below
- first_moment: float32 [2759168], P(('seq', 'batch')), may hold values from -0.0014648438 to 0.0014648438
- second_moment: float32 [2759168], P(('seq', 'batch')), may hold values from 1e-10 to 1e-09
Outputs:
- output: bfloat16 [2, 4096, 512], P('batch', 'seq')
- input_grad: float32 [2, 4096, 512], P('batch', 'seq')
- grad: float32 [2759168], P(('seq', 'batch'))
- update: float32 [2759168], P(('seq', 'batch'))
- first_new: float32 [2759168], P(('seq', 'batch'))
- second_new: float32 [2759168], P(('seq', 'batch'))
- grad_norm: float32 [], replicated
The draws below stay inside these ranges and needn't reach their ends.
Inputs may be any that keep to these rules, and one draw needn't show every extreme that they name: `lengths`: each row sums to 4096; its last entry counts padding tokens at the stream's end, at most max(1, 128); the third entry is exactly 2048. `master`: step_log lies in -9.2 to -2.3, decay_log in -1.5 to 0.5, frequency in 0 to 30, norm_gain and second_gain in 0.7 to 1.3.
All inputs are finite; a program needn't handle non-finite values.
Results may differ from the reference program's by a relative error of at most 0.0064.
Values sent between devices are 32-bit elements; how exact they have to be, the bound alone decides.
No kernel may reach another device: no remote copies, remote signals or barrier semaphores. Data moves between devices by JAX's collectives and lax.ppermute only.
A program may use at most 512 MiB of HBM per device.

```python
import math
from functools import partial
import jax
import jax.numpy as jnp
from jax import lax

D = 512
NSTATE = 64
G = 1024
FF = 2048
DOCS = 4
TOK_DEV = 256
STREAM = 4096
STREAMS = 2
MOST = 2048
RAW = 2759168
PADDED = 2759168


def draw_lengths(key, part):
    pad_top = max(1, TOK_DEV // 2)
    key_pad = jax.random.fold_in(key, 11)
    key_split = jax.random.fold_in(key, 12)
    padding = jax.random.randint(key_pad, (STREAMS,), 1, pad_top + 1, dtype=jnp.int32)
    remaining = (STREAM - MOST - padding).astype(jnp.int32)
    first = jax.random.randint(key_split, (STREAMS,), 1, remaining, dtype=jnp.int32)
    second = remaining - first
    longest = jnp.full((STREAMS,), MOST, dtype=jnp.int32)
    return jnp.stack([first, second, longest, padding], axis=1).astype(jnp.int32)


def draw_master(key, part):
    keys = jax.random.split(key, 17)
    normal = lambda index, count: jax.random.truncated_normal(keys[index], -3.0, 3.0, (count,), jnp.float32)
    uniform = lambda index, count, lo, hi: jax.random.uniform(keys[index], (count,), jnp.float32, lo, hi)
    modes = D * NSTATE
    pieces = [uniform(0, D, 0.7, 1.3), 0.3 * normal(1, D), uniform(2, D, -9.2, -2.3), normal(3, D), uniform(4, modes, -1.5, 0.5), uniform(5, modes, 0.0, 30.0), 0.5 * normal(6, modes), 0.5 * normal(7, modes), normal(8, D * G) / jnp.sqrt(jnp.float32(D)), 0.3 * normal(9, G), uniform(10, D, 0.7, 1.3), 0.3 * normal(11, D), normal(12, D * FF) / jnp.sqrt(jnp.float32(D)), 0.3 * normal(13, FF), normal(14, FF * D) / jnp.sqrt(jnp.float32(FF)), 0.3 * normal(15, D)]
    joined = jnp.concatenate(pieces)
    spare = 0.02 * jax.random.truncated_normal(keys[16], -3.0, 3.0, (PADDED - RAW,), jnp.float32)
    return jnp.concatenate([joined, spare])


def shard_levels(key, shape, cuts, least, top_value):
    def one(dim, shards_of):
        heights = jax.random.uniform(jax.random.fold_in(jax.random.fold_in(key, 6), dim), (shards_of,), jnp.float32, least / len(cuts), top_value / len(cuts))
        return jnp.repeat(jnp.exp(heights), shape[dim] // shards_of).reshape((-1,) + (1,) * (len(shape) - dim - 1))

    factor_of = one(*cuts[0])
    for cut in cuts[1:]:
        factor_of = factor_of * one(*cut)
    return factor_of


def bell_draw(stream_key, shape, deviation, bound, cuts=(), kind=jnp.bfloat16):
    factor_of = shard_levels(stream_key, shape, cuts, -0.22, 0.18) if cuts else 1.0
    entries = jax.random.normal(stream_key, shape, jnp.float32) * deviation * factor_of
    return jnp.minimum(jnp.maximum(entries, -bound), bound).astype(kind)


def setup_inputs(seed: int = 0) -> dict:
    splits = jax.random.split(jax.random.key(seed), 7)
    return {
        "inputs": bell_draw(splits[0], (STREAMS, STREAM, D), 1.0, 6.0, ((0, 2), (1, 16))),
        "cotangent": bell_draw(splits[1], (STREAMS, STREAM, D), 1.0, 6.0, ((0, 2), (1, 16))),
        "lengths": draw_lengths(jax.random.fold_in(splits[6], 71), 0),
        "master": draw_master(jax.random.fold_in(splits[6], 71), 0),
        "first_moment": bell_draw(splits[4], (PADDED,), 0.0001, 0.0014648438, ((0, 32),), jnp.float32),
        "second_moment": jnp.clip(jnp.exp(math.log(9.999999717180685e-10) - 2.3025851 * jax.random.uniform(splits[5], (PADDED,), jnp.float32) ** shard_levels(splits[5], (PADDED,), ((0, 32),), -0.2, 0.2)), 1.000000013351432e-10, 9.999999717180685e-10),
    }


@jax.custom_vjp
def low(v):
    return lax.optimization_barrier(v.astype(jnp.bfloat16)).astype(jnp.float32)

@jax.custom_vjp
def low_back(v):
    return v

def low_keep(v):
    return (low(v), None)

def low_pass(kept, grad):
    return (grad,)

def back_keep(v):
    return (v, None)

def back_low(kept, grad):
    return (low(grad),)
low.defvjp(low_keep, low_pass)
low_back.defvjp(back_keep, back_low)
highest = lax.Precision.HIGHEST
norm_eps = 1e-05
root_half = 0.7071067811865476
inv_root_two_pi = 0.3989422804014327

def unpack(flat):
    layout = [('norm_gain', (D,)), ('norm_bias', (D,)), ('step_log', (D,)), ('skip_gain', (D,)), ('decay_log', (D, NSTATE)), ('frequency', (D, NSTATE)), ('out_real', (D, NSTATE)), ('out_imag', (D, NSTATE)), ('gate_weight', (D, G)), ('gate_bias', (G,)), ('second_gain', (D,)), ('second_bias', (D,)), ('expand_weight', (D, FF)), ('expand_bias', (FF,)), ('reduce_weight', (FF, D)), ('reduce_bias', (D,))]
    params = {}
    offset = 0
    for name, shape in layout:
        count = 1
        for extent in shape:
            count = count * extent
        params[name] = flat[offset:offset + count].reshape(shape)
        offset = offset + count
    return params

def gelu(values):
    return 0.5 * values * (1.0 + lax.erf(values * root_half))

def layer_norm(values, gain, bias):
    center = values - lax.optimization_barrier(jnp.mean(values, axis=-1, keepdims=True))
    scale = lax.rsqrt(lax.optimization_barrier(jnp.mean(center * center, axis=-1, keepdims=True)) + norm_eps)
    return center * scale * gain + bias

def pole_args(step_log, decay_log, frequency):
    delta = jnp.exp(step_log)[:, None]
    return (delta * -jnp.exp(decay_log), delta * frequency)

def powers(arg_re, arg_im, levels):
    magnitude = jnp.exp(arg_re[:, :, None] * levels)
    return (magnitude * jnp.cos(arg_im[:, :, None] * levels), magnitude * jnp.sin(arg_im[:, :, None] * levels))

def tables_of(step_log, decay_log, frequency, out_real, out_imag, width):
    arg_re, arg_im = pole_args(step_log, decay_log, frequency)
    rate_re = -jnp.exp(decay_log)
    magnitude = jnp.exp(arg_re)
    pole_re = magnitude * jnp.cos(arg_im) - 1.0
    pole_im = magnitude * jnp.sin(arg_im)
    denom = rate_re * rate_re + frequency * frequency
    ratio_re = (pole_re * rate_re + pole_im * frequency) / denom
    ratio_im = (pole_im * rate_re - pole_re * frequency) / denom
    mix_re = out_real * ratio_re - out_imag * ratio_im
    mix_im = out_real * ratio_im + out_imag * ratio_re
    levels = jnp.arange(width, dtype=jnp.float32)
    zero_re, zero_im = powers(arg_re, arg_im, levels)
    up_re, up_im = powers(arg_re, arg_im, levels + 1.0)
    kernel = lax.optimization_barrier(jnp.sum(mix_re[:, :, None] * zero_re - mix_im[:, :, None] * zero_im, axis=1))
    full_mag = jnp.exp(arg_re * width)
    full_re = full_mag * jnp.cos(arg_im * width)
    full_im = full_mag * jnp.sin(arg_im * width)
    return (kernel, up_re, up_im, zero_re[:, :, ::-1], zero_im[:, :, ::-1], full_re, full_im, mix_re, mix_im)

def block_apply(tables, carry, piece):
    kernel, up_re, up_im, down_re, down_im, full_re, full_im, mix_re, mix_im = tables
    state_re, state_im, prev = carry
    values, labels = piece
    width = labels.shape[0]
    mixed_re = mix_re * state_re - mix_im * state_im
    mixed_im = mix_re * state_im + mix_im * state_re
    carried = jnp.einsum('hnt,hn->th', up_re, mixed_re, precision=highest) - jnp.einsum('hnt,hn->th', up_im, mixed_im, precision=highest)
    joined = (labels == prev).astype(jnp.float32)
    result = carried * joined[:, None]
    last = labels[width - 1]
    keep = (last == prev).astype(jnp.float32)
    new_re = keep * (full_re * state_re - full_im * state_im)
    new_im = keep * (full_re * state_im + full_im * state_re)
    if values is not None:
        places = jnp.arange(width, dtype=jnp.int32)
        gap = places[:, None] - places[None, :]
        same = ((labels[:, None] == labels[None, :]) & (gap >= 0)).astype(jnp.float32)
        toeplitz = kernel[:, jnp.clip(gap, 0, width - 1)] * same[None]
        result = result + jnp.einsum('hts,sh->th', toeplitz, values, precision=highest)
        tail = values * (labels == last).astype(jnp.float32)[:, None]
        new_re = new_re + jnp.einsum('hns,sh->hn', down_re, tail, precision=highest)
        new_im = new_im + jnp.einsum('hns,sh->hn', down_im, tail, precision=highest)
    return ((new_re, new_im, last), result)

def group_response(tables, values, labels, prev, state_re, state_im, width):
    count = labels.shape[0] // width
    blocks = labels.reshape(count, width)
    pieces = (None if values is None else values.reshape(count, width, values.shape[-1]), blocks)
    stepper = jax.checkpoint(partial(block_apply, tables))
    finals, out = lax.scan(stepper, (state_re, state_im, prev), pieces)
    return (out.reshape(labels.shape[0], out.shape[-1]), finals[0], finals[1])

def reference(inputs, cotangent, lengths, master, first_moment, second_moment):
    width = min(128, TOK_DEV)
    rows = inputs.astype(jnp.float32)
    ends = jnp.cumsum(lengths, axis=1).astype(jnp.int32)
    where = jnp.arange(STREAM, dtype=jnp.int32)
    labels = lax.optimization_barrier(jnp.sum((where[None, :, None] >= ends[:, None, :]).astype(jnp.int32), axis=2)).astype(jnp.int32)
    valid = (labels < DOCS - 1).astype(jnp.float32)

    def forward(values, flat):
        params = unpack(flat)
        signal = layer_norm(values, params['norm_gain'], params['norm_bias'])
        tables = tables_of(params['step_log'], params['decay_log'], params['frequency'], params['out_real'], params['out_imag'], width)
        zero_state = jnp.zeros((D, NSTATE), jnp.float32)
        start = jnp.array(-1, dtype=jnp.int32)

        def stream(piece, marks):
            out, _, _ = group_response(tables, piece, marks, start, zero_state, zero_state, width)
            return out
        response = jax.vmap(stream)(signal, labels) + params['skip_gain'] * signal
        hidden = low(gelu(response))
        opened = low_back(jnp.einsum('btd,dg->btg', hidden, low(params['gate_weight']), precision=highest) + params['gate_bias'])
        mid = values + opened[..., :D] * jax.nn.sigmoid(opened[..., D:])
        normed = low(layer_norm(mid, params['second_gain'], params['second_bias']))
        lifted = low_back(jnp.einsum('btd,df->btf', normed, low(params['expand_weight']), precision=highest) + params['expand_bias'])
        active = low(gelu(lifted))
        return mid + jnp.einsum('btf,fd->btd', active, low(params['reduce_weight']), precision=highest) + params['reduce_bias']
    result, pull = jax.vjp(forward, rows, master)
    input_grad, grad = pull(cotangent.astype(jnp.float32) * valid[:, :, None])
    grad_norm = jnp.sqrt(jnp.sum(grad * grad))
    factor = jnp.minimum(1.0, 1.0 / (grad_norm + 1e-06))
    clipped = grad * factor
    first_new = 0.9 * first_moment + 0.1 * clipped
    second_new = 0.999 * second_moment + 0.001 * clipped * clipped
    first_hat = first_new / (1.0 - 0.9 ** 10)
    second_hat = second_new / (1.0 - 0.999 ** 10)
    update = -0.05 * (first_hat / (jnp.sqrt(second_hat) + 1e-08) + 0.1 * master)
    return (result.astype(jnp.bfloat16), input_grad, grad, update, first_new, second_new, grad_norm)
```

```python
from functools import partial
import jax, jax.numpy as jnp
from jax import lax
from jax.experimental import pallas as pl
from jax.experimental.pallas import tpu as pltpu
from jax.sharding import PartitionSpec as P

D = 512
NSTATE = 64
CH = 128
DOCS = 4
G = 1024
FF = 2048


norm_eps = 1e-05
root_half = 0.7071067811865476
inv_root_two_pi = 0.3989422804014327


f32 = jnp.float32
bf16 = jnp.bfloat16

def split(v):
    hi = v.astype(bf16)
    return hi, (v - hi.astype(f32)).astype(bf16)

def dot3(a, b, ca, cb):
    ah, al = a
    bh, bl = b
    lhs = jnp.concatenate([ah, ah, al], axis=ca)
    rhs = jnp.concatenate([bh, bl, bh], axis=cb)
    return lax.dot_general(lhs, rhs, (((ca,), (cb,)), ((), ())), preferred_element_type=f32)

def swap(v):
    return pltpu.roll(v, NSTATE, 1)

def twist(table, re, im):
    return re * table + im * swap(table)

def ladder(prm, order):
    sub = lax.broadcasted_iota(jnp.int32, (8, 2 * NSTATE), 0)
    lane = lax.broadcasted_iota(jnp.int32, (8, 2 * NSTATE), 1)
    power = sub if order == 1 else 7 - sub
    table = jnp.where(lane < NSTATE, 1.0, 0.0).astype(f32)
    for bit in range(3):
        table = jnp.where((power >> bit) & 1 == 1, twist(table, prm[2 * bit:2 * bit + 1], prm[2 * bit + 1:2 * bit + 2]), table)
    for bit in range(3, 7):
        more = twist(table, prm[2 * bit:2 * bit + 1], prm[2 * bit + 1:2 * bit + 2])
        table = jnp.concatenate([table, more] if order == 1 else [more, table], axis=0)
    return table

def toeplitz(prm, table):
    wrow = jnp.broadcast_to(prm[16:17], (8, 2 * NSTATE))
    taps = dot3(split(wrow), split(table), 1, 1)
    wide = jnp.broadcast_to(taps[0:1], (CH, CH))
    wide = pltpu.roll(wide, 0, 1, stride=1, stride_axis=0)
    row = lax.broadcasted_iota(jnp.int32, (CH, CH), 0)
    col = lax.broadcasted_iota(jnp.int32, (CH, CH), 1)
    return jnp.where(col >= row, wide, 0.0)

def label_at(ends, pos):
    total = jnp.zeros_like(pos)
    for k in range(DOCS):
        total = total + (pos >= ends[k]).astype(jnp.int32)
    return total

def make_masks(ends_ref, masks_ref, nck):
    ends = [ends_ref[k] for k in range(DOCS)]
    row = lax.broadcasted_iota(jnp.int32, (nck, CH), 0)
    lane = lax.broadcasted_iota(jnp.int32, (nck, CH), 1)
    base = row * CH
    label = label_at(ends, base + lane)
    prev = jnp.where(base == 0, -1, label_at(ends, base - 1))
    last = label_at(ends, base + CH - 1)
    for k in range(DOCS):
        masks_ref[k] = (label == k).astype(f32)
    masks_ref[DOCS] = (label == prev).astype(f32)
    masks_ref[DOCS + 1] = (label == last).astype(f32)

def keep_of(ends_ref, c):
    first = jnp.int32(0)
    second = jnp.int32(0)
    for k in range(DOCS):
        first = first + (c * CH - 1 >= ends_ref[k]).astype(jnp.int32)
        second = second + (c * CH + CH - 1 >= ends_ref[k]).astype(jnp.int32)
    return jnp.where((c > 0) & (first == second), 1.0, 0.0).astype(f32)

def masked_rows(v, masks_ref):
    return jnp.concatenate([v * masks_ref[k] for k in range(DOCS)], axis=0)

def fold_rows(v, masks_ref, nck):
    total = v[:nck] * masks_ref[0]
    for k in range(1, DOCS):
        total = total + v[k * nck:(k + 1) * nck] * masks_ref[k]
    return total

def fwd_body(nck, nch, ends_ref, prm_ref, x_ref, y_ref, prior_ref, masks_ref, end_ref, gt_ref):
    make_masks(ends_ref, masks_ref, nck)

    def one(h, _):
        prm = prm_ref[h]
        u = x_ref[pl.ds(h, nck, stride=nch), :] * prm[19:20] + prm[20:21]
        table = ladder(prm, 1)
        down = ladder(prm, -1)
        gt_ref[h] = twist(table, prm[17:18], prm[18:19])
        local = dot3(split(masked_rows(u, masks_ref)), split(toeplitz(prm, table)), 1, 0)
        y_ref[pl.ds(h, nck, stride=nch), :] = fold_rows(local, masks_ref, nck) + prm[21:22] * u
        end_ref[pl.ds(h, nck, stride=nch), :] = dot3(split(u * masks_ref[DOCS + 1]), split(down), 1, 0)
        return 0

    lax.fori_loop(0, nch, one, 0)
    full_re = prm_ref[:, 14, :]
    full_im = prm_ref[:, 15, :]

    def step(c, state):
        at = pl.ds(pl.multiple_of(c * nch, 8), nch)
        prior_ref[at, :] = state
        return keep_of(ends_ref, c) * twist(state, full_re, full_im) + end_ref[at, :]

    lax.fori_loop(0, nck, step, jnp.zeros((nch, 2 * NSTATE), f32))

    def two(h, _):
        prior = prior_ref[pl.ds(h, nck, stride=nch), :]
        carried = dot3(split(prior), split(gt_ref[h]), 1, 1) * masks_ref[DOCS]
        y_ref[pl.ds(h, nck, stride=nch), :] += carried
        return 0

    lax.fori_loop(0, nch, two, 0)

def ssm_forward(ends, prm, x, nck, nch):
    vm = pl.BlockSpec(memory_space=pltpu.VMEM)
    return pl.pallas_call(
        partial(fwd_body, nck, nch),
        out_shape=(jax.ShapeDtypeStruct((nck * nch, CH), f32), jax.ShapeDtypeStruct((nck * nch, 2 * NSTATE), f32)),
        in_specs=[pl.BlockSpec(memory_space=pltpu.SMEM), vm, vm],
        out_specs=(vm, vm),
        scratch_shapes=[
            pltpu.VMEM((DOCS + 2, nck, CH), f32),
            pltpu.VMEM((nck * nch, 2 * NSTATE), f32),
            pltpu.VMEM((nch, CH, 2 * NSTATE), f32),
        ],
        name="state_forward",
    )(ends, prm, x)

def bwd_body(nck, nch, ends_ref, prm_ref, x_ref, g_ref, prior_ref, dx_ref, rows_ref, masks_ref, lead_ref, adj_ref, table_ref):
    make_masks(ends_ref, masks_ref, nck)

    def one(h, _):
        prm = prm_ref[h]
        g = g_ref[pl.ds(h, nck, stride=nch), :]
        table = ladder(prm, 1)
        table_ref[h] = table
        gt = twist(table, prm[17:18], prm[18:19])
        lead_ref[pl.ds(h, nck, stride=nch), :] = dot3(split(g * masks_ref[DOCS]), split(gt), 1, 0)
        return 0

    lax.fori_loop(0, nch, one, 0)
    full_re = prm_ref[:, 14, :]
    full_im = prm_ref[:, 15, :]
    zero = jnp.zeros((nch, 2 * NSTATE), f32)

    def step(k, carry):
        adjoint, same, cross = carry
        c = nck - 1 - k
        at = pl.ds(pl.multiple_of(c * nch, 8), nch)
        adj_ref[at, :] = adjoint
        keep = keep_of(ends_ref, c)
        prior = prior_ref[at, :]
        same = same + keep * adjoint * prior
        cross = cross + keep * adjoint * swap(prior)
        adjoint = lead_ref[at, :] + keep * (full_re * adjoint - full_im * swap(adjoint))
        return adjoint, same, cross

    _, same, cross = lax.fori_loop(0, nck, step, (zero, zero, zero))
    rows_ref[8] = same
    rows_ref[9] = cross
    for k in range(13, 16):
        rows_ref[k] = zero
    row = lax.broadcasted_iota(jnp.int32, (CH, CH), 0)
    col = lax.broadcasted_iota(jnp.int32, (CH, CH), 1)
    flip = (row + col == CH - 1).astype(f32).astype(bf16)

    def two(h, _):
        prm = prm_ref[h]
        x = x_ref[pl.ds(h, nck, stride=nch), :]
        u = x * prm[19:20] + prm[20:21]
        g = g_ref[pl.ds(h, nck, stride=nch), :]
        table = table_ref[h]
        down = ladder(prm, -1)
        mat = split(toeplitz(prm, table))
        gm = split(masked_rows(g, masks_ref))
        um = split(masked_rows(u, masks_ref))
        adjoint = split(adj_ref[pl.ds(h, nck, stride=nch), :])
        prior = split(prior_ref[pl.ds(h, nck, stride=nch), :])
        du = fold_rows(dot3(gm, mat, 1, 1), masks_ref, nck)
        du = du + dot3(adjoint, split(down), 1, 1) * masks_ref[DOCS + 1]
        du = du + prm[21:22] * g
        dx_ref[pl.ds(h, nck, stride=nch), :] = du
        flipped = [jnp.dot(v, flip, preferred_element_type=f32).astype(bf16) for v in um]
        square = dot3(flipped, gm, 0, 0)
        square = jnp.where(row + col >= CH - 1, square, 0.0)
        square = pltpu.roll(square, 1, 1, stride=1, stride_axis=0)
        taps = jnp.sum(square, axis=0, keepdims=True)
        place = lax.broadcasted_iota(jnp.int32, (8, CH), 1).astype(f32)
        sub = lax.broadcasted_iota(jnp.int32, (8, CH), 0)
        both = jnp.where(sub == 0, 1.0, jnp.where(sub == 1, place, 0.0)) * taps
        both = dot3(split(both), split(table), 1, 0)
        rows_ref[0, pl.ds(h, 1), :] = both[0:1]
        rows_ref[1, pl.ds(h, 1), :] = both[1:2]
        late = row.astype(f32)
        dgt = dot3(split(g * masks_ref[DOCS]), prior, 0, 0)
        one = dgt * table
        two = dgt * swap(table)
        rows_ref[2, pl.ds(h, 1), :] = jnp.sum(one, axis=0, keepdims=True)
        rows_ref[3, pl.ds(h, 1), :] = jnp.sum(two, axis=0, keepdims=True)
        rows_ref[4, pl.ds(h, 1), :] = jnp.sum(one * late, axis=0, keepdims=True)
        rows_ref[5, pl.ds(h, 1), :] = jnp.sum(two * late, axis=0, keepdims=True)
        ddown = dot3(split(u * masks_ref[DOCS + 1]), adjoint, 0, 0) * ((CH - 1) - late)
        rows_ref[6, pl.ds(h, 1), :] = jnp.sum(ddown * down, axis=0, keepdims=True)
        rows_ref[7, pl.ds(h, 1), :] = jnp.sum(ddown * swap(down), axis=0, keepdims=True)
        rows_ref[10, pl.ds(h, 1), :] = jnp.sum(g * u, axis=0, keepdims=True)
        rows_ref[11, pl.ds(h, 1), :] = jnp.sum(du * x, axis=0, keepdims=True)
        rows_ref[12, pl.ds(h, 1), :] = jnp.sum(du, axis=0, keepdims=True)
        return 0

    lax.fori_loop(0, nch, two, 0)

def ssm_backward(ends, prm, x, g, prior, nck, nch):
    vm = pl.BlockSpec(memory_space=pltpu.VMEM)
    return pl.pallas_call(
        partial(bwd_body, nck, nch),
        out_shape=(jax.ShapeDtypeStruct((nck * nch, CH), f32), jax.ShapeDtypeStruct((16, nch, 2 * NSTATE), f32)),
        in_specs=[pl.BlockSpec(memory_space=pltpu.SMEM), vm, vm, vm, vm],
        out_specs=(vm, vm),
        scratch_shapes=[
            pltpu.VMEM((DOCS + 2, nck, CH), f32),
            pltpu.VMEM((nck * nch, 2 * NSTATE), f32),
            pltpu.VMEM((nck * nch, 2 * NSTATE), f32),
            pltpu.VMEM((nch, CH, 2 * NSTATE), f32),
        ],
        name="state_backward",
    )(ends, prm, x, g, prior)

def mixing(step_log, decay_log, frequency, out_real, out_imag):
    delta = jnp.exp(step_log)[:, None]
    rate_re = -jnp.exp(decay_log)
    arg_re, arg_im = delta * rate_re, delta * frequency
    magnitude = jnp.exp(arg_re)
    pole_re = magnitude * jnp.cos(arg_im) - 1.0
    pole_im = magnitude * jnp.sin(arg_im)
    denom = rate_re * rate_re + frequency * frequency
    ratio_re = (pole_re * rate_re + pole_im * frequency) / denom
    ratio_im = (pole_im * rate_re - pole_re * frequency) / denom
    mix_re = out_real * ratio_re - out_imag * ratio_im
    mix_im = out_real * ratio_im + out_imag * ratio_re
    return arg_re, arg_im, mix_re, mix_im

def pair(left, right):
    return jnp.concatenate([left, right], axis=-1)

def mode_rows(arg_re, arg_im, mix_re, mix_im, gain, bias, skip):
    nch = arg_re.shape[0]
    scale = jnp.asarray([2.0**b for b in range(8)], f32)[None, :, None]
    magnitude = jnp.exp(arg_re[:, None] * scale)
    p_re = magnitude * jnp.cos(arg_im[:, None] * scale)
    p_im = magnitude * jnp.sin(arg_im[:, None] * scale)
    powers = jnp.stack([pair(p_re, p_re), pair(-p_im, p_im)], axis=2).reshape(nch, 16, 2 * NSTATE)
    c_re = mix_re * p_re[:, 0] - mix_im * p_im[:, 0]
    c_im = mix_re * p_im[:, 0] + mix_im * p_re[:, 0]
    flat = lambda v: jnp.broadcast_to(v[:, None], (nch, 2 * NSTATE))
    rest = jnp.stack([pair(mix_re, -mix_im), pair(c_re, -c_re), pair(-c_im, -c_im), flat(gain), flat(bias), flat(skip), flat(0 * gain), flat(0 * gain)], axis=1)
    return jnp.concatenate([powers, rest], axis=1)

def mode_grads(rows, arg_re, arg_im, mix_re, mix_im):
    lo, hi = rows[:, :, :NSTATE], rows[:, :, NSTATE:]
    magnitude = jnp.exp(arg_re)
    p_re, p_im = magnitude * jnp.cos(arg_im), magnitude * jnp.sin(arg_im)
    magnitude = jnp.exp(arg_re * CH)
    f_re, f_im = magnitude * jnp.cos(arg_im * CH), magnitude * jnp.sin(arg_im * CH)
    a_re, a_im = lo[2] - hi[2], -(hi[3] + lo[3])
    b_re, b_im = lo[4] - hi[4], -(hi[5] + lo[5])
    b_re, b_im = b_re + a_re, b_im + a_im
    w_re = lo[0] + p_re * a_re + p_im * a_im
    w_im = -hi[0] + p_re * a_im - p_im * a_re
    v_re = lo[1] + p_re * b_re + p_im * b_im
    v_im = -hi[1] + p_re * b_im - p_im * b_re
    g_re = mix_re * v_re + mix_im * v_im
    g_im = mix_re * v_im - mix_im * v_re
    g_re = g_re + lo[6] + hi[6]
    g_im = g_im + hi[7] - lo[7]
    d_re, d_im = lo[8] + hi[8], hi[9] - lo[9]
    g_re = g_re + CH * (f_re * d_re + f_im * d_im)
    g_im = g_im + CH * (f_re * d_im - f_im * d_re)
    return g_re, g_im, w_re, w_im


def unpack(flat):
    layout = [
        ("norm_gain", (D,)),
        ("norm_bias", (D,)),
        ("step_log", (D,)),
        ("skip_gain", (D,)),
        ("decay_log", (D, NSTATE)),
        ("frequency", (D, NSTATE)),
        ("out_real", (D, NSTATE)),
        ("out_imag", (D, NSTATE)),
        ("gate_weight", (D, G)),
        ("gate_bias", (G,)),
        ("second_gain", (D,)),
        ("second_bias", (D,)),
        ("expand_weight", (D, FF)),
        ("expand_bias", (FF,)),
        ("reduce_weight", (FF, D)),
        ("reduce_bias", (D,)),
    ]
    params = {}
    offset = 0
    for name, shape in layout:
        count = 1
        for extent in shape:
            count = count * extent
        params[name] = flat[offset : offset + count].reshape(shape)
        offset = offset + count
    return params


def gelu(values):
    return 0.5 * values * (1.0 + lax.erf(values * root_half))


def gelu_slope(values):
    return (
        0.5 * (1.0 + lax.erf(values * root_half))
        + values * jnp.exp(-0.5 * values * values) * inv_root_two_pi
    )


def normalize(values):
    center = values - jnp.mean(values, axis=-1, keepdims=True)
    scale = lax.rsqrt(jnp.mean(center * center, axis=-1, keepdims=True) + norm_eps)
    return (center * scale, scale)


def norm_back(d_hat, hat, scale):
    return scale * (
        d_hat
        - jnp.mean(d_hat, axis=-1, keepdims=True)
        - hat * jnp.mean(d_hat * hat, axis=-1, keepdims=True)
    )


def to_channels(rows):
    seq = lax.axis_size("seq")
    parts = rows.shape[0] // CH
    turned = rows.reshape(parts, CH, seq, D // seq).transpose(2, 0, 3, 1)
    return lax.all_to_all(turned, "seq", 0, 0).reshape(-1, CH)


def to_tokens(rows, group):
    seq = lax.axis_size("seq")
    turned = lax.all_to_all(rows.reshape(seq, group // CH, D // seq, CH), "seq", 0, 0)
    return turned.transpose(1, 3, 0, 2).reshape(group, D)


def per_device(inputs, cotangent, lengths, master, first_moment, second_moment):
    seq, batch = lax.axis_size("seq"), lax.axis_size("batch")
    devices = seq * batch
    share = master.shape[0]
    padded = -(-share // 1024) * 1024
    full = lax.all_gather(jnp.pad(master, (0, padded - share)), ("seq", "batch"), axis=0, tiled=True)
    full = full.reshape(devices, padded)[:, :share].reshape(-1)
    params = unpack(full)
    group = inputs.shape[1]
    nch, nck = D // seq, seq * group // CH
    rows = inputs[0].astype(jnp.float32)
    ends = jnp.cumsum(lengths[0])
    offset = lax.axis_index("seq") * group
    where = offset + jnp.arange(group, dtype=jnp.int32)
    labels = jnp.sum((where[:, None] >= ends[None, :]).astype(jnp.int32), axis=1)
    valid = (labels < DOCS - 1).astype(jnp.float32)
    first_hat, first_scale = normalize(rows)
    mine = lambda v: lax.dynamic_slice_in_dim(v, lax.axis_index("seq") * nch, nch, 0)
    names = ("step_log", "decay_log", "frequency", "out_real", "out_imag")
    modes, modes_pull = jax.vjp(mixing, *(mine(params[name]) for name in names))
    prm = mode_rows(*modes, *(mine(params[name]) for name in ("norm_gain", "norm_bias", "skip_gain")))
    hats = to_channels(first_hat)
    outs, prior = ssm_forward(ends, prm, hats, nck, nch)
    response = to_tokens(outs, group)
    hidden_low = gelu(response).astype(jnp.bfloat16)
    gate_low = params["gate_weight"].astype(jnp.bfloat16)
    opened = jnp.dot(hidden_low, gate_low, preferred_element_type=jnp.float32) + params["gate_bias"]
    linear = opened[:, :D]
    gating = jax.nn.sigmoid(opened[:, D:])
    mid = rows + linear * gating
    second_hat, second_scale = normalize(mid)
    normed_low = (second_hat * params["second_gain"] + params["second_bias"]).astype(jnp.bfloat16)
    expand_low = params["expand_weight"].astype(jnp.bfloat16)
    lifted = (
        jnp.dot(normed_low, expand_low, preferred_element_type=jnp.float32) + params["expand_bias"]
    )
    active_low = gelu(lifted).astype(jnp.bfloat16)
    reduce_low = params["reduce_weight"].astype(jnp.bfloat16)
    result = (
        mid
        + jnp.dot(active_low, reduce_low, preferred_element_type=jnp.float32)
        + params["reduce_bias"]
    )
    output = result.astype(jnp.bfloat16)[None]
    back = cotangent[0].astype(jnp.float32) * valid[:, None]
    back_low = back.astype(jnp.bfloat16)
    g_reduce_w = jnp.einsum("tf,td->fd", active_low, back_low, preferred_element_type=jnp.float32)
    g_reduce_b = jnp.sum(back, axis=0)
    d_active = jnp.einsum("td,fd->tf", back_low, reduce_low, preferred_element_type=jnp.float32)
    d_lifted = (d_active * gelu_slope(lifted)).astype(jnp.bfloat16)
    g_expand_w = jnp.einsum("td,tf->df", normed_low, d_lifted, preferred_element_type=jnp.float32)
    g_expand_b = jnp.sum(d_lifted.astype(jnp.float32), axis=0)
    d_normed = jnp.einsum("tf,df->td", d_lifted, expand_low, preferred_element_type=jnp.float32)
    g_second_gain = jnp.sum(d_normed * second_hat, axis=0)
    g_second_bias = jnp.sum(d_normed, axis=0)
    d_mid = back + norm_back(d_normed * params["second_gain"], second_hat, second_scale)
    d_linear = d_mid * gating
    d_gating = d_mid * linear * gating * (1.0 - gating)
    d_opened = jnp.concatenate([d_linear, d_gating], axis=1).astype(jnp.bfloat16)
    g_gate_w = jnp.einsum("td,tg->dg", hidden_low, d_opened, preferred_element_type=jnp.float32)
    g_gate_b = jnp.sum(d_opened.astype(jnp.float32), axis=0)
    d_hidden = jnp.einsum("tg,dg->td", d_opened, gate_low, preferred_element_type=jnp.float32)
    d_response = d_hidden * gelu_slope(response)
    d_outs = to_channels(d_response)
    d_signals, sums = ssm_backward(ends, prm, hats, d_outs, prior, nck, nch)
    d_signal = to_tokens(d_signals, group)
    d_modes = modes_pull(mode_grads(sums, *modes))
    d_rows = d_mid + norm_back(d_signal * params["norm_gain"], first_hat, first_scale)
    lane_sums = jnp.sum(sums[10:13], axis=-1)

    def spread(v):
        whole = jnp.zeros((D,) + v.shape[1:], jnp.float32)
        return lax.dynamic_update_slice_in_dim(whole, v, lax.axis_index("seq") * nch, 0)

    parts = [
        spread(lane_sums[1]),
        spread(lane_sums[2]),
        spread(d_modes[0]),
        spread(lane_sums[0]),
        spread(d_modes[1]),
        spread(d_modes[2]),
        spread(d_modes[3]),
        spread(d_modes[4]),
        g_gate_w,
        g_gate_b,
        g_second_gain,
        g_second_bias,
        g_expand_w,
        g_expand_b,
        g_reduce_w,
        g_reduce_b,
    ]
    packed = jnp.concatenate([item.reshape(-1) for item in parts])
    packed = jnp.pad(packed, (0, full.shape[0] - packed.shape[0]))
    packed = jnp.pad(packed.reshape(devices, share), ((0, 0), (0, padded - share)))
    shard = lax.psum_scatter(packed.reshape(devices, padded // 128, 128), ("seq", "batch"), scatter_dimension=0)
    shard = shard.reshape(-1)[:share]
    total = lax.psum(jnp.sum(shard * shard), ("seq", "batch"))
    grad_norm = jnp.sqrt(total)
    factor = jnp.minimum(1.0, 1.0 / (grad_norm + 1e-06))
    clipped = shard * factor
    first_new = 0.9 * first_moment + 0.1 * clipped
    second_new = 0.999 * second_moment + 0.001 * clipped * clipped
    first_hat_new = first_new / (1.0 - 0.9**10)
    second_hat_new = second_new / (1.0 - 0.999**10)
    update = -0.05 * (first_hat_new / (jnp.sqrt(second_hat_new) + 1e-08) + 0.1 * master)
    return (output, d_rows[None], shard, update, first_new, second_new, grad_norm)


def solution(mesh):
    placed = (
        P("batch", "seq", None),
        P("batch", "seq", None),
        P("batch", None),
        P(("seq", "batch")),
        P(("seq", "batch")),
        P(("seq", "batch")),
    )
    return jax.shard_map(
        per_device,
        mesh=mesh,
        in_specs=placed,
        out_specs=(
            P("batch", "seq", None),
            P("batch", "seq", None),
            P(("seq", "batch")),
            P(("seq", "batch")),
            P(("seq", "batch")),
            P(("seq", "batch")),
            P(),
        ),
        check_vma=False,
    )
```

```python
from functools import partial
import jax, jax.numpy as jnp
from jax import lax
from jax.experimental import pallas as pl
from jax.experimental.pallas import tpu as pltpu
from jax.sharding import PartitionSpec as P

D = 512
NSTATE = 64
CH = 128
DOCS = 4
G = 1024
FF = 2048
GATHER_PART = 0.45
SCATTER_PART = 0.35


norm_eps = 1e-05
root_half = 0.7071067811865476
inv_root_two_pi = 0.3989422804014327


f32 = jnp.float32
bf16 = jnp.bfloat16

def split(v):
    hi = v.astype(bf16)
    return hi, (v - hi.astype(f32)).astype(bf16)

def dot3(a, b, ca, cb):
    ah, al = a
    bh, bl = b
    lhs = jnp.concatenate([ah, ah, al], axis=ca)
    rhs = jnp.concatenate([bh, bl, bh], axis=cb)
    return lax.dot_general(lhs, rhs, (((ca,), (cb,)), ((), ())), preferred_element_type=f32)

def swap(v):
    return pltpu.roll(v, NSTATE, 1)

def twist(table, re, im):
    return re * table + im * swap(table)

def ladder(prm, order):
    sub = lax.broadcasted_iota(jnp.int32, (8, 2 * NSTATE), 0)
    lane = lax.broadcasted_iota(jnp.int32, (8, 2 * NSTATE), 1)
    power = sub if order == 1 else 7 - sub
    table = jnp.where(lane < NSTATE, 1.0, 0.0).astype(f32)
    for bit in range(3):
        table = jnp.where((power >> bit) & 1 == 1, twist(table, prm[2 * bit:2 * bit + 1], prm[2 * bit + 1:2 * bit + 2]), table)
    for bit in range(3, 7):
        more = twist(table, prm[2 * bit:2 * bit + 1], prm[2 * bit + 1:2 * bit + 2])
        table = jnp.concatenate([table, more] if order == 1 else [more, table], axis=0)
    return table

def toeplitz(prm, table):
    wrow = jnp.broadcast_to(prm[16:17], (8, 2 * NSTATE))
    taps = dot3(split(wrow), split(table), 1, 1)
    wide = jnp.broadcast_to(taps[0:1], (CH, CH))
    wide = pltpu.roll(wide, 0, 1, stride=1, stride_axis=0)
    row = lax.broadcasted_iota(jnp.int32, (CH, CH), 0)
    col = lax.broadcasted_iota(jnp.int32, (CH, CH), 1)
    return jnp.where(col >= row, wide, 0.0)

def label_at(ends, pos):
    total = jnp.zeros_like(pos)
    for k in range(DOCS):
        total = total + (pos >= ends[k]).astype(jnp.int32)
    return total

def make_masks(ends_ref, masks_ref, nck):
    ends = [ends_ref[k] for k in range(DOCS)]
    row = lax.broadcasted_iota(jnp.int32, (nck, CH), 0)
    lane = lax.broadcasted_iota(jnp.int32, (nck, CH), 1)
    base = row * CH
    label = label_at(ends, base + lane)
    prev = jnp.where(base == 0, -1, label_at(ends, base - 1))
    last = label_at(ends, base + CH - 1)
    for k in range(DOCS):
        masks_ref[k] = (label == k).astype(f32)
    masks_ref[DOCS] = (label == prev).astype(f32)
    masks_ref[DOCS + 1] = (label == last).astype(f32)

def keep_of(ends_ref, c):
    first = jnp.int32(0)
    second = jnp.int32(0)
    for k in range(DOCS):
        first = first + (c * CH - 1 >= ends_ref[k]).astype(jnp.int32)
        second = second + (c * CH + CH - 1 >= ends_ref[k]).astype(jnp.int32)
    return jnp.where((c > 0) & (first == second), 1.0, 0.0).astype(f32)

def masked_rows(v, masks_ref):
    return jnp.concatenate([v * masks_ref[k] for k in range(DOCS)], axis=0)

def fold_rows(v, masks_ref, nck):
    total = v[:nck] * masks_ref[0]
    for k in range(1, DOCS):
        total = total + v[k * nck:(k + 1) * nck] * masks_ref[k]
    return total

def fwd_body(nck, nch, ends_ref, prm_ref, x_ref, y_ref, prior_ref, masks_ref, end_ref, gt_ref):
    make_masks(ends_ref, masks_ref, nck)

    def one(h, _):
        prm = prm_ref[h]
        u = x_ref[pl.ds(h, nck, stride=nch), :] * prm[19:20] + prm[20:21]
        table = ladder(prm, 1)
        down = ladder(prm, -1)
        gt_ref[h] = twist(table, prm[17:18], prm[18:19])
        local = dot3(split(masked_rows(u, masks_ref)), split(toeplitz(prm, table)), 1, 0)
        y_ref[pl.ds(h, nck, stride=nch), :] = fold_rows(local, masks_ref, nck) + prm[21:22] * u
        end_ref[pl.ds(h, nck, stride=nch), :] = dot3(split(u * masks_ref[DOCS + 1]), split(down), 1, 0)
        return 0

    lax.fori_loop(0, nch, one, 0)
    full_re = prm_ref[:, 14, :]
    full_im = prm_ref[:, 15, :]

    def step(c, state):
        at = pl.ds(pl.multiple_of(c * nch, 8), nch)
        prior_ref[at, :] = state
        return keep_of(ends_ref, c) * twist(state, full_re, full_im) + end_ref[at, :]

    lax.fori_loop(0, nck, step, jnp.zeros((nch, 2 * NSTATE), f32))

    def two(h, _):
        prior = prior_ref[pl.ds(h, nck, stride=nch), :]
        carried = dot3(split(prior), split(gt_ref[h]), 1, 1) * masks_ref[DOCS]
        y_ref[pl.ds(h, nck, stride=nch), :] += carried
        return 0

    lax.fori_loop(0, nch, two, 0)

def ssm_forward(ends, prm, x, nck, nch):
    vm = pl.BlockSpec(memory_space=pltpu.VMEM)
    return pl.pallas_call(
        partial(fwd_body, nck, nch),
        out_shape=(jax.ShapeDtypeStruct((nck * nch, CH), f32), jax.ShapeDtypeStruct((nck * nch, 2 * NSTATE), f32)),
        in_specs=[pl.BlockSpec(memory_space=pltpu.SMEM), vm, vm],
        out_specs=(vm, vm),
        scratch_shapes=[
            pltpu.VMEM((DOCS + 2, nck, CH), f32),
            pltpu.VMEM((nck * nch, 2 * NSTATE), f32),
            pltpu.VMEM((nch, CH, 2 * NSTATE), f32),
        ],
        name="state_forward",
    )(ends, prm, x)

def bwd_body(nck, nch, ends_ref, prm_ref, x_ref, g_ref, prior_ref, dx_ref, rows_ref, masks_ref, lead_ref, adj_ref, table_ref):
    make_masks(ends_ref, masks_ref, nck)

    def one(h, _):
        prm = prm_ref[h]
        g = g_ref[pl.ds(h, nck, stride=nch), :]
        table = ladder(prm, 1)
        table_ref[h] = table
        gt = twist(table, prm[17:18], prm[18:19])
        lead_ref[pl.ds(h, nck, stride=nch), :] = dot3(split(g * masks_ref[DOCS]), split(gt), 1, 0)
        return 0

    lax.fori_loop(0, nch, one, 0)
    full_re = prm_ref[:, 14, :]
    full_im = prm_ref[:, 15, :]
    zero = jnp.zeros((nch, 2 * NSTATE), f32)

    def step(k, carry):
        adjoint, same, cross = carry
        c = nck - 1 - k
        at = pl.ds(pl.multiple_of(c * nch, 8), nch)
        adj_ref[at, :] = adjoint
        keep = keep_of(ends_ref, c)
        prior = prior_ref[at, :]
        same = same + keep * adjoint * prior
        cross = cross + keep * adjoint * swap(prior)
        adjoint = lead_ref[at, :] + keep * (full_re * adjoint - full_im * swap(adjoint))
        return adjoint, same, cross

    _, same, cross = lax.fori_loop(0, nck, step, (zero, zero, zero))
    rows_ref[8] = same
    rows_ref[9] = cross
    for k in range(13, 16):
        rows_ref[k] = zero
    row = lax.broadcasted_iota(jnp.int32, (CH, CH), 0)
    col = lax.broadcasted_iota(jnp.int32, (CH, CH), 1)
    flip = (row + col == CH - 1).astype(f32).astype(bf16)

    def two(h, _):
        prm = prm_ref[h]
        x = x_ref[pl.ds(h, nck, stride=nch), :]
        u = x * prm[19:20] + prm[20:21]
        g = g_ref[pl.ds(h, nck, stride=nch), :]
        table = table_ref[h]
        down = ladder(prm, -1)
        mat = split(toeplitz(prm, table))
        gm = split(masked_rows(g, masks_ref))
        um = split(masked_rows(u, masks_ref))
        adjoint = split(adj_ref[pl.ds(h, nck, stride=nch), :])
        prior = split(prior_ref[pl.ds(h, nck, stride=nch), :])
        du = fold_rows(dot3(gm, mat, 1, 1), masks_ref, nck)
        du = du + dot3(adjoint, split(down), 1, 1) * masks_ref[DOCS + 1]
        du = du + prm[21:22] * g
        dx_ref[pl.ds(h, nck, stride=nch), :] = du
        flipped = [jnp.dot(v, flip, preferred_element_type=f32).astype(bf16) for v in um]
        square = dot3(flipped, gm, 0, 0)
        square = jnp.where(row + col >= CH - 1, square, 0.0)
        square = pltpu.roll(square, 1, 1, stride=1, stride_axis=0)
        taps = jnp.sum(square, axis=0, keepdims=True)
        place = lax.broadcasted_iota(jnp.int32, (8, CH), 1).astype(f32)
        sub = lax.broadcasted_iota(jnp.int32, (8, CH), 0)
        both = jnp.where(sub == 0, 1.0, jnp.where(sub == 1, place, 0.0)) * taps
        both = dot3(split(both), split(table), 1, 0)
        rows_ref[0, pl.ds(h, 1), :] = both[0:1]
        rows_ref[1, pl.ds(h, 1), :] = both[1:2]
        late = row.astype(f32)
        dgt = dot3(split(g * masks_ref[DOCS]), prior, 0, 0)
        one = dgt * table
        two = dgt * swap(table)
        rows_ref[2, pl.ds(h, 1), :] = jnp.sum(one, axis=0, keepdims=True)
        rows_ref[3, pl.ds(h, 1), :] = jnp.sum(two, axis=0, keepdims=True)
        rows_ref[4, pl.ds(h, 1), :] = jnp.sum(one * late, axis=0, keepdims=True)
        rows_ref[5, pl.ds(h, 1), :] = jnp.sum(two * late, axis=0, keepdims=True)
        ddown = dot3(split(u * masks_ref[DOCS + 1]), adjoint, 0, 0) * ((CH - 1) - late)
        rows_ref[6, pl.ds(h, 1), :] = jnp.sum(ddown * down, axis=0, keepdims=True)
        rows_ref[7, pl.ds(h, 1), :] = jnp.sum(ddown * swap(down), axis=0, keepdims=True)
        rows_ref[10, pl.ds(h, 1), :] = jnp.sum(g * u, axis=0, keepdims=True)
        rows_ref[11, pl.ds(h, 1), :] = jnp.sum(du * x, axis=0, keepdims=True)
        rows_ref[12, pl.ds(h, 1), :] = jnp.sum(du, axis=0, keepdims=True)
        return 0

    lax.fori_loop(0, nch, two, 0)

def ssm_backward(ends, prm, x, g, prior, nck, nch):
    vm = pl.BlockSpec(memory_space=pltpu.VMEM)
    return pl.pallas_call(
        partial(bwd_body, nck, nch),
        out_shape=(jax.ShapeDtypeStruct((nck * nch, CH), f32), jax.ShapeDtypeStruct((16, nch, 2 * NSTATE), f32)),
        in_specs=[pl.BlockSpec(memory_space=pltpu.SMEM), vm, vm, vm, vm],
        out_specs=(vm, vm),
        scratch_shapes=[
            pltpu.VMEM((DOCS + 2, nck, CH), f32),
            pltpu.VMEM((nck * nch, 2 * NSTATE), f32),
            pltpu.VMEM((nck * nch, 2 * NSTATE), f32),
            pltpu.VMEM((nch, CH, 2 * NSTATE), f32),
        ],
        name="state_backward",
    )(ends, prm, x, g, prior)

def mixing(step_log, decay_log, frequency, out_real, out_imag):
    delta = jnp.exp(step_log)[:, None]
    rate_re = -jnp.exp(decay_log)
    arg_re, arg_im = delta * rate_re, delta * frequency
    magnitude = jnp.exp(arg_re)
    pole_re = magnitude * jnp.cos(arg_im) - 1.0
    pole_im = magnitude * jnp.sin(arg_im)
    denom = rate_re * rate_re + frequency * frequency
    ratio_re = (pole_re * rate_re + pole_im * frequency) / denom
    ratio_im = (pole_im * rate_re - pole_re * frequency) / denom
    mix_re = out_real * ratio_re - out_imag * ratio_im
    mix_im = out_real * ratio_im + out_imag * ratio_re
    return arg_re, arg_im, mix_re, mix_im

def pair(left, right):
    return jnp.concatenate([left, right], axis=-1)

def mode_rows(arg_re, arg_im, mix_re, mix_im, gain, bias, skip):
    nch = arg_re.shape[0]
    scale = jnp.asarray([2.0**b for b in range(8)], f32)[None, :, None]
    magnitude = jnp.exp(arg_re[:, None] * scale)
    p_re = magnitude * jnp.cos(arg_im[:, None] * scale)
    p_im = magnitude * jnp.sin(arg_im[:, None] * scale)
    powers = jnp.stack([pair(p_re, p_re), pair(-p_im, p_im)], axis=2).reshape(nch, 16, 2 * NSTATE)
    c_re = mix_re * p_re[:, 0] - mix_im * p_im[:, 0]
    c_im = mix_re * p_im[:, 0] + mix_im * p_re[:, 0]
    flat = lambda v: jnp.broadcast_to(v[:, None], (nch, 2 * NSTATE))
    rest = jnp.stack([pair(mix_re, -mix_im), pair(c_re, -c_re), pair(-c_im, -c_im), flat(gain), flat(bias), flat(skip), flat(0 * gain), flat(0 * gain)], axis=1)
    return jnp.concatenate([powers, rest], axis=1)

def mode_grads(rows, arg_re, arg_im, mix_re, mix_im):
    lo, hi = rows[:, :, :NSTATE], rows[:, :, NSTATE:]
    magnitude = jnp.exp(arg_re)
    p_re, p_im = magnitude * jnp.cos(arg_im), magnitude * jnp.sin(arg_im)
    magnitude = jnp.exp(arg_re * CH)
    f_re, f_im = magnitude * jnp.cos(arg_im * CH), magnitude * jnp.sin(arg_im * CH)
    a_re, a_im = lo[2] - hi[2], -(hi[3] + lo[3])
    b_re, b_im = lo[4] - hi[4], -(hi[5] + lo[5])
    b_re, b_im = b_re + a_re, b_im + a_im
    w_re = lo[0] + p_re * a_re + p_im * a_im
    w_im = -hi[0] + p_re * a_im - p_im * a_re
    v_re = lo[1] + p_re * b_re + p_im * b_im
    v_im = -hi[1] + p_re * b_im - p_im * b_re
    g_re = mix_re * v_re + mix_im * v_im
    g_im = mix_re * v_im - mix_im * v_re
    g_re = g_re + lo[6] + hi[6]
    g_im = g_im + hi[7] - lo[7]
    d_re, d_im = lo[8] + hi[8], hi[9] - lo[9]
    g_re = g_re + CH * (f_re * d_re + f_im * d_im)
    g_im = g_im + CH * (f_re * d_im - f_im * d_re)
    return g_re, g_im, w_re, w_im


TILE = 1024
GATE_AT, EXPAND_AT, REDUCE_AT = 130, 644, 1670
SMALL_AT = (642, 643, 1668, 1669, 2694)
MODE_TILES = 130


def lay(share, devices):
    base = share // TILE
    return base, base + 2, (devices - 1) * share // TILE + base + 2


def strips():
    return ((GATE_AT, D, G // CH), (EXPAND_AT, D, FF // CH), (REDUCE_AT, FF, D // CH))


def unpack_body(streams, base, tiles, devices, *refs):
    n = len(streams)
    dest = refs[0]
    sources = refs[1:1 + n]
    gate_ref, expand_ref, reduce_ref, small_ref, modes_ref, flat, side, sem, side_sem = refs[1 + n:]

    def clear(j, _):
        at = pl.multiple_of(dest[j], 8)
        for tile in (0, base, base + 1):
            flat[pl.ds(at + tile * 8, 8), :] = jnp.zeros((8, CH), f32)
        return 0

    lax.fori_loop(0, devices, clear, 0)
    inside = 0
    for k, (first, last, order, slot, count) in enumerate(streams):
        lo, hi = max(first, 1), min(last, base)
        rows = (last - first) * 8

        def send(b, _, k=k, first=first, last=last, lo=lo, hi=hi, rows=rows, order=order, slot=slot):
            at = pl.multiple_of(dest[order + b], 8)
            begin = pl.multiple_of(b * rows, 8)
            pltpu.make_async_copy(sources[k].at[pl.ds(begin + (lo - first) * 8, (hi - lo) * 8), :], flat.at[pl.ds(at + lo * 8, (hi - lo) * 8), :], sem).start()
            for s, tile in enumerate((0, base, base + 1)):
                if first <= tile < last:
                    pltpu.make_async_copy(sources[k].at[pl.ds(begin + (tile - first) * 8, 8), :], side.at[s, pl.ds(pl.multiple_of((slot + b) * 8, 8), 8), :], side_sem).start()
            return 0

        lax.fori_loop(0, count, send, 0)
        inside += (hi - lo) * count
    pltpu.make_async_copy(flat.at[pl.ds(0, inside * 8), :], flat.at[pl.ds(0, inside * 8), :], sem).wait()
    pltpu.make_async_copy(side, side, side_sem).wait()
    for s, tile in enumerate((0, base, base + 1)):
        for first, last, order, slot, count in streams:
            if not first <= tile < last:
                continue

            def join(b, _, s=s, tile=tile, order=order, slot=slot):
                at = pl.multiple_of(dest[order + b], 8)
                flat[pl.ds(at + tile * 8, 8), :] += side[s, pl.ds(pl.multiple_of((slot + b) * 8, 8), 8), :]
                return 0

            lax.fori_loop(0, count, join, 0)
    for (first, rows, per), out in zip(strips(), (gate_ref, expand_ref, reduce_ref)):
        def narrow(i, _, first=first, per=per, out=out):
            for k in range(per):
                v = flat[pl.ds(first * 8 + i * 16 * per + k, 16, stride=per), :]
                out[pl.ds(pl.multiple_of(i * 16, 16), 16), k * CH:(k + 1) * CH] = v.astype(bf16)
            return 0

        lax.fori_loop(0, rows // 16, narrow, 0)
    for k, tile in enumerate(SMALL_AT):
        small_ref[k * 8:(k + 1) * 8, :] = flat[tile * 8:(tile + 1) * 8, :]
    modes_ref[...] = flat[:MODE_TILES * 8, :]


def unpack_kernel(streams, arrays, dest, share, devices):
    base, _, tiles = lay(share, devices)
    hbm = pl.BlockSpec(memory_space=pl.ANY)
    vm = pl.BlockSpec(memory_space=pltpu.VMEM)
    shapes = ((D, G), (D, FF), (FF, D))
    return pl.pallas_call(
        partial(unpack_body, streams, base, tiles, devices),
        out_shape=tuple(jax.ShapeDtypeStruct(s, bf16) for s in shapes)
        + (jax.ShapeDtypeStruct((len(SMALL_AT) * 8, CH), f32), jax.ShapeDtypeStruct((MODE_TILES * 8, CH), f32)),
        in_specs=[pl.BlockSpec(memory_space=pltpu.SMEM)] + [hbm] * len(arrays),
        out_specs=(vm,) * 5,
        scratch_shapes=[
            pltpu.VMEM((tiles * 8, CH), f32),
            pltpu.VMEM((3, devices * 8, CH), f32),
            pltpu.SemaphoreType.DMA,
            pltpu.SemaphoreType.DMA,
        ],
        name="unpack_weights",
    )(dest, *arrays)


def pack_body(streams, tiles, devices, has_modes, *refs):
    n = len(streams)
    dest, gate_ref, expand_ref, reduce_ref, small_ref = refs[:5]
    modes_ref = refs[5] if has_modes else None
    outs = refs[5 + has_modes:5 + has_modes + n]
    flat, sem = refs[5 + has_modes + n:]
    if has_modes:
        flat[:MODE_TILES * 8, :] = modes_ref[...]
    else:
        flat[:MODE_TILES * 8, :] = jnp.zeros((MODE_TILES * 8, CH), f32)
    for k, tile in enumerate(SMALL_AT):
        flat[tile * 8:(tile + 1) * 8, :] = small_ref[k * 8:(k + 1) * 8, :]
    flat[(SMALL_AT[-1] + 1) * 8:, :] = jnp.zeros(((tiles - SMALL_AT[-1] - 1) * 8, CH), f32)
    for (first, rows, per), src in zip(strips(), (gate_ref, expand_ref, reduce_ref)):
        def spread(i, _, first=first, per=per, src=src):
            for k in range(per):
                v = src[pl.ds(pl.multiple_of(i * 16, 16), 16), k * CH:(k + 1) * CH]
                flat[pl.ds(first * 8 + i * 16 * per + k, 16, stride=per), :] = v
            return 0

        lax.fori_loop(0, rows // 16, spread, 0)
    for k, (first, last, order) in enumerate(streams):
        rows = (last - first) * 8

        def send(b, _, k=k, first=first, rows=rows, order=order):
            at = pl.multiple_of(dest[order + b], 8)
            pltpu.make_async_copy(flat.at[pl.ds(at + first * 8, rows), :], outs[k].at[pl.ds(pl.multiple_of(b * rows, 8), rows), :], sem.at[k]).start()
            return 0

        lax.fori_loop(0, outs[k].shape[0] // rows, send, 0)
    for k, out in enumerate(outs):
        pltpu.make_async_copy(out, out, sem.at[k]).wait()


def pack_kernel(streams, dest, grads, small, modes, share, devices):
    _, _, tiles = lay(share, devices)
    hbm = pl.BlockSpec(memory_space=pl.ANY)
    vm = pl.BlockSpec(memory_space=pltpu.VMEM)
    has = int(modes is not None)
    return pl.pallas_call(
        partial(pack_body, tuple(s[:3] for s in streams), tiles, devices, has),
        out_shape=tuple(jax.ShapeDtypeStruct((blocks * (last - first) * 8, CH), f32) for first, last, _, blocks in streams),
        in_specs=[pl.BlockSpec(memory_space=pltpu.SMEM)] + [vm] * (4 + has),
        out_specs=(hbm,) * len(streams),
        scratch_shapes=[pltpu.VMEM((tiles * 8, CH), f32), pltpu.SemaphoreType.DMA((len(streams),))],
        name="pack_gradients",
    )(dest, *grads, small, *((modes,) if has else ()))


AXES = ("seq", "batch")
PAIR = [(0, 1), (1, 0)]


def columns(seq):
    return seq // 4, 4


def across(v, step):
    return lax.ppermute(v, "seq", [(i, i ^ step) for i in range(16)])


def along(v, step):
    return lax.ppermute(v, "seq", [(i, (i + 4 * step) % 16) for i in range(16)])


def swap_cores(v):
    return lax.ppermute(v, "batch", PAIR)


def direct():
    return lax.axis_size("seq") == 16 and lax.axis_size("batch") == 2


def first_rows(share, devices, ids):
    return ids * share // TILE * 8


def place_of(step_z, step_p, other):
    seq, batch = lax.axis_index("seq"), lax.axis_index("batch")
    z = (seq // 4 + 4 + step_z) % 4
    return 2 * (z * 4 + (seq % 4 ^ step_p)) + (batch ^ other)


def cuts_of(tiles, part):
    one = round(tiles * part)
    two = one + round((tiles - one) * 2 / 3)
    return one, two


def gather_weights(master, share, devices):
    base, tiles, _ = lay(share, devices)
    me = 2 * lax.axis_index("seq") + lax.axis_index("batch") if direct() else lax.axis_index("seq") * lax.axis_size("batch") + lax.axis_index("batch")
    box = lax.dynamic_update_slice(jnp.zeros((tiles * TILE,), f32), master, (me * share % TILE,)).reshape(tiles * 8, CH)
    natural = first_rows(share, devices, jnp.arange(devices, dtype=jnp.int32))
    if not direct():
        return (((0, tiles, 0, 0, devices),), [lax.all_gather(box, AXES, axis=0, tiled=True)], natural)
    one, two = cuts_of(tiles, GATHER_PART)
    lone, ltwo = box[one * 8:two * 8], box[two * 8:]
    streams, arrays, dest = [], [], []
    if one:
        arrays.append(lax.all_gather(box[:one * 8], AXES, axis=0, tiled=True))
        streams.append((0, one, 0, 0, devices))
        dest.append(natural)
    near_z = jnp.concatenate([lone] + [along(lone, k) for k in range(1, 4)])
    near_p = jnp.concatenate([ltwo] + [across(ltwo, p) for p in range(1, 4)])
    sets_z = [near_z] + [across(near_z, p) for p in range(1, 4)]
    sets_p = [near_p] + [along(near_p, k) for k in range(1, 4)]
    for lo, hi, sets, ids in (
        (one, two, sets_z, lambda s, b, o: place_of(-b, s, o)),
        (two, tiles, sets_p, lambda s, b, o: place_of(-s, b, o)),
    ):
        slot = 0
        for other in range(2):
            for s in range(4):
                arrays.append(swap_cores(sets[s]) if other else sets[s])
                streams.append((lo, hi, devices * bool(one) + 32 * (lo == two) + slot, slot, 4))
                dest.append(first_rows(share, devices, jnp.stack([ids(s, b, other) for b in range(4)])))
                slot += 4
    return tuple(streams), arrays, jnp.concatenate(dest).astype(jnp.int32)


def scatter_plan(share, devices):
    _, tiles, _ = lay(share, devices)
    natural = first_rows(share, devices, jnp.arange(devices, dtype=jnp.int32))
    if not direct():
        return ((0, tiles, 0, devices),), natural
    one, two = cuts_of(tiles, SCATTER_PART)
    streams, dest = [], []
    if one:
        streams.append((0, one, 0, devices))
        dest.append(natural)
    for lo, hi, ids in (
        (one, two, lambda s, b, o: place_of(b, s, o)),
        (two, tiles, lambda s, b, o: place_of(s, b, o)),
    ):
        for other in range(2):
            for s in range(4):
                streams.append((lo, hi, sum(d.shape[0] for d in dest), 4))
                dest.append(first_rows(share, devices, jnp.stack([ids(s, b, other) for b in range(4)])))
    return tuple(streams), jnp.concatenate(dest).astype(jnp.int32)


def scatter_gradients(arrays, share, devices):
    _, tiles, _ = lay(share, devices)
    if not direct():
        return lax.psum_scatter(arrays[0].reshape(devices, tiles * 8, CH), AXES, scatter_dimension=0)
    one, two = cuts_of(tiles, SCATTER_PART)
    pieces = []
    if one:
        pieces.append(lax.psum_scatter(arrays[0].reshape(devices, one * 8, CH), AXES, scatter_dimension=0))
        arrays = arrays[1:]
    both = [a + swap_cores(b) for a, b in zip(arrays[:4] + arrays[8:12], arrays[4:8] + arrays[12:16])]
    by_p, by_z = both[:4], both[4:]
    part_p = by_p[0] + across(by_p[1], 1) + across(by_p[2], 2) + across(by_p[3], 3)
    part_z = by_z[0] + along(by_z[1], 1) + along(by_z[2], 2) + along(by_z[3], 3)
    part_p, part_z = part_p.reshape(4, -1, CH), part_z.reshape(4, -1, CH)
    pieces.append(part_p[0] + along(part_p[1], 1) + along(part_p[2], 2) + along(part_p[3], 3))
    pieces.append(part_z[0] + across(part_z[1], 1) + across(part_z[2], 2) + across(part_z[3], 3))
    return jnp.concatenate(pieces)


MODE_ROWS = 65


def scatter_modes(master):
    other = swap_cores(master)
    even = lax.axis_index("batch") == 0
    lead = jnp.concatenate([jnp.where(even, master, other), jnp.where(even, other, master)])[:MODE_TILES * TILE]
    small = lead[:4 * D].reshape(4, 16, 32).transpose(1, 0, 2).reshape(16, 1, CH)
    rest = lead[4 * D:].reshape(4, 16, 16, CH).transpose(1, 0, 2, 3).reshape(16, 64, CH)
    blocks = jnp.concatenate([small, rest], axis=1)
    seq = lax.axis_index("seq")
    far = [lax.ppermute(blocks[4 * k:4 * k + 4], "seq", [(0, 4 * k)]) for k in range(1, 4)]
    plane = jnp.where(seq == 0, blocks[:4], far[0] + far[1] + far[2])
    near = [lax.ppermute(plane[p], "seq", [(4 * z, 4 * z + p) for z in range(4)]) for p in range(1, 4)]
    return jnp.where(seq % 4 == 0, plane[0], near[0] + near[1] + near[2])


def read_modes(block):
    nch = D // 16
    small = block[0].reshape(4, nch)
    rest = block[1:].reshape(4, nch, NSTATE)
    return small, rest


def gather_modes(small, rest):
    block = jnp.concatenate([small.reshape(1, CH), rest.reshape(64, CH)])
    near = [lax.ppermute(block, "seq", [(4 * z + p, 4 * z) for z in range(4)]) for p in range(1, 4)]
    plane = jnp.stack([block] + near)
    far = [lax.ppermute(plane, "seq", [(4 * k, 0)]) for k in range(1, 4)]
    blocks = jnp.concatenate([plane] + far)
    lead = blocks[:, 0].reshape(16, 4, 32).transpose(1, 0, 2).reshape(-1)
    tail = blocks[:, 1:].reshape(16, 4, 16, CH).transpose(1, 0, 2, 3).reshape(-1)
    return jnp.concatenate([lead, tail])


def total_of(v):
    if not direct():
        return lax.psum(v, AXES)
    v = jnp.broadcast_to(v, (8, CH))
    v = v + swap_cores(v)
    v = v + (across(v, 1) + across(v, 2) + across(v, 3))
    v = v + (along(v, 1) + along(v, 2) + along(v, 3))
    return v[0, 0]


def gelu(values):
    return 0.5 * values * (1.0 + lax.erf(values * root_half))


def gelu_slope(values):
    return (
        0.5 * (1.0 + lax.erf(values * root_half))
        + values * jnp.exp(-0.5 * values * values) * inv_root_two_pi
    )


def normalize(values):
    center = values - jnp.mean(values, axis=-1, keepdims=True)
    scale = lax.rsqrt(jnp.mean(center * center, axis=-1, keepdims=True) + norm_eps)
    return (center * scale, scale)


def norm_back(d_hat, hat, scale):
    return scale * (
        d_hat
        - jnp.mean(d_hat, axis=-1, keepdims=True)
        - hat * jnp.mean(d_hat * hat, axis=-1, keepdims=True)
    )


def to_channels(rows):
    seq = lax.axis_size("seq")
    parts = rows.shape[0] // CH
    turned = rows.reshape(parts, CH, seq, D // seq).transpose(2, 0, 3, 1)
    return lax.all_to_all(turned, "seq", 0, 0).reshape(-1, CH)


def to_tokens(rows, group):
    seq = lax.axis_size("seq")
    turned = lax.all_to_all(rows.reshape(seq, group // CH, D // seq, CH), "seq", 0, 0)
    return turned.transpose(1, 3, 0, 2).reshape(group, D)


def per_device(inputs, cotangent, lengths, master, first_moment, second_moment):
    seq, batch = lax.axis_size("seq"), lax.axis_size("batch")
    devices = seq * batch
    share = master.shape[0]
    streams, arrays, dest = gather_weights(master, share, devices)
    group = inputs.shape[1]
    nch, nck = D // seq, seq * group // CH
    rows = inputs[0].astype(jnp.float32)
    ends = jnp.cumsum(lengths[0])
    offset = lax.axis_index("seq") * group
    where = offset + jnp.arange(group, dtype=jnp.int32)
    labels = jnp.sum((where[:, None] >= ends[None, :]).astype(jnp.int32), axis=1)
    valid = (labels < DOCS - 1).astype(jnp.float32)
    first_hat, first_scale = normalize(rows)
    hats = to_channels(first_hat)
    mine = lambda v: lax.dynamic_slice_in_dim(v, lax.axis_index("seq") * nch, nch, 0)
    if direct():
        few, many = read_modes(scatter_modes(master))
        gate_low, expand_low, reduce_low, small, lead = unpack_kernel(streams, arrays, dest, share, devices)
        lead = lead.reshape(-1)
    else:
        gate_low, expand_low, reduce_low, small, lead = unpack_kernel(streams, arrays, dest, share, devices)
        lead = lead.reshape(-1)
        few = jnp.stack([mine(lead[k * D:(k + 1) * D]) for k in range(4)])
        many = jnp.stack([mine(v) for v in lead[4 * D:].reshape(4, D, NSTATE)])
    modes, modes_pull = jax.vjp(mixing, few[2], many[0], many[1], many[2], many[3])
    prm = mode_rows(*modes, few[0], few[1], few[3])
    outs, prior = ssm_forward(ends, prm, hats, nck, nch)
    small = small.reshape(-1)
    params = {
        "norm_gain": lead[:D],
        "gate_bias": small[:G],
        "second_gain": small[G:G + D],
        "second_bias": small[G + D:G + 2 * D],
        "expand_bias": small[2 * G:2 * G + FF],
        "reduce_bias": small[2 * G + FF:2 * G + FF + D],
    }
    response = to_tokens(outs, group)
    hidden_low = gelu(response).astype(jnp.bfloat16)
    opened = jnp.dot(hidden_low, gate_low, preferred_element_type=jnp.float32) + params["gate_bias"]
    linear = opened[:, :D]
    gating = jax.nn.sigmoid(opened[:, D:])
    mid = rows + linear * gating
    second_hat, second_scale = normalize(mid)
    normed_low = (second_hat * params["second_gain"] + params["second_bias"]).astype(jnp.bfloat16)
    lifted = (
        jnp.dot(normed_low, expand_low, preferred_element_type=jnp.float32) + params["expand_bias"]
    )
    active_low = gelu(lifted).astype(jnp.bfloat16)
    result = (
        mid
        + jnp.dot(active_low, reduce_low, preferred_element_type=jnp.float32)
        + params["reduce_bias"]
    )
    output = result.astype(jnp.bfloat16)[None]
    back = cotangent[0].astype(jnp.float32) * valid[:, None]
    back_low = back.astype(jnp.bfloat16)
    g_reduce_w = jnp.einsum("tf,td->fd", active_low, back_low, preferred_element_type=jnp.float32)
    g_reduce_b = jnp.sum(back, axis=0)
    d_active = jnp.einsum("td,fd->tf", back_low, reduce_low, preferred_element_type=jnp.float32)
    d_lifted = (d_active * gelu_slope(lifted)).astype(jnp.bfloat16)
    g_expand_w = jnp.einsum("td,tf->df", normed_low, d_lifted, preferred_element_type=jnp.float32)
    g_expand_b = jnp.sum(d_lifted.astype(jnp.float32), axis=0)
    d_normed = jnp.einsum("tf,df->td", d_lifted, expand_low, preferred_element_type=jnp.float32)
    g_second_gain = jnp.sum(d_normed * second_hat, axis=0)
    g_second_bias = jnp.sum(d_normed, axis=0)
    d_mid = back + norm_back(d_normed * params["second_gain"], second_hat, second_scale)
    d_linear = d_mid * gating
    d_gating = d_mid * linear * gating * (1.0 - gating)
    d_opened = jnp.concatenate([d_linear, d_gating], axis=1).astype(jnp.bfloat16)
    g_gate_w = jnp.einsum("td,tg->dg", hidden_low, d_opened, preferred_element_type=jnp.float32)
    g_gate_b = jnp.sum(d_opened.astype(jnp.float32), axis=0)
    d_hidden = jnp.einsum("tg,dg->td", d_opened, gate_low, preferred_element_type=jnp.float32)
    d_response = d_hidden * gelu_slope(response)
    d_outs = to_channels(d_response)
    flat_small = jnp.concatenate([g_gate_b, g_second_gain, g_second_bias, g_expand_b, g_reduce_b, jnp.zeros((D,), f32)]).reshape(-1, CH)
    plan, places = scatter_plan(share, devices)
    d_signals, sums = ssm_backward(ends, prm, hats, d_outs, prior, nck, nch)
    d_signal = to_tokens(d_signals, group)
    d_rows = d_mid + norm_back(d_signal * params["norm_gain"], first_hat, first_scale)
    lane_sums = jnp.sum(sums[10:13], axis=-1)
    d_modes = modes_pull(mode_grads(sums, *modes))
    few = jnp.stack([lane_sums[1], lane_sums[2], d_modes[0], lane_sums[0]])
    many = jnp.stack(d_modes[1:])
    if direct():
        packed = pack_kernel(plan, places, (g_gate_w, g_expand_w, g_reduce_w), flat_small, None, share, devices)
    else:

        def spread(v):
            whole = jnp.zeros((v.shape[0], D) + v.shape[2:], f32)
            return lax.dynamic_update_slice_in_dim(whole, v, lax.axis_index("seq") * nch, 1)

        lead = jnp.concatenate([spread(few).reshape(-1), spread(many).reshape(-1)]).reshape(-1, CH)
        packed = pack_kernel(plan, places, (g_gate_w, g_expand_w, g_reduce_w), flat_small, lead, share, devices)
    me = lax.axis_index("seq") * batch + lax.axis_index("batch")
    box = scatter_gradients(packed, share, devices)
    shard = lax.dynamic_slice(box.reshape(-1), (me * share % TILE,), (share,))
    if direct():
        few, many = few + swap_cores(few), many + swap_cores(many)
        lead = gather_modes(few, many)
        lead = jnp.pad(lead, (0, 2 * share - lead.shape[0]))
        mark = me * share + jnp.arange(share, dtype=jnp.int32) < MODE_TILES * TILE
        squares = jnp.sum(jnp.where(mark, 0.0, shard * shard))
        squares = squares + 0.5 * (jnp.sum(few * few) + jnp.sum(many * many))
        shard = jnp.where(mark, lax.dynamic_slice(lead, (jnp.minimum(me, 1) * share,), (share,)), shard)
    else:
        squares = jnp.sum(shard * shard)
    total = total_of(squares)
    grad_norm = jnp.sqrt(total)
    factor = jnp.minimum(1.0, 1.0 / (grad_norm + 1e-06))
    clipped = shard * factor
    first_new = 0.9 * first_moment + 0.1 * clipped
    second_new = 0.999 * second_moment + 0.001 * clipped * clipped
    first_hat_new = first_new / (1.0 - 0.9**10)
    second_hat_new = second_new / (1.0 - 0.999**10)
    update = -0.05 * (first_hat_new / (jnp.sqrt(second_hat_new) + 1e-08) + 0.1 * master)
    return (output, d_rows[None], shard, update, first_new, second_new, grad_norm)


def solution(mesh):
    placed = (
        P("batch", "seq", None),
        P("batch", "seq", None),
        P("batch", None),
        P(("seq", "batch")),
        P(("seq", "batch")),
        P(("seq", "batch")),
    )
    return jax.shard_map(
        per_device,
        mesh=mesh,
        in_specs=placed,
        out_specs=(
            P("batch", "seq", None),
            P("batch", "seq", None),
            P(("seq", "batch")),
            P(("seq", "batch")),
            P(("seq", "batch")),
            P(("seq", "batch")),
            P(),
        ),
        check_vma=False,
    )
```

```python
from functools import partial
import jax, jax.numpy as jnp
from jax import lax
from jax.experimental import pallas as pl
from jax.experimental.pallas import tpu as pltpu
from jax.sharding import PartitionSpec as P

D = 512
NSTATE = 64
CH = 128
DOCS = 4
G = 1024
FF = 2048
SCATTER_PART = 1


norm_eps = 1e-05
root_half = 0.7071067811865476
inv_root_two_pi = 0.3989422804014327


f32 = jnp.float32
bf16 = jnp.bfloat16

def split(v):
    hi = v.astype(bf16)
    return hi, (v - hi.astype(f32)).astype(bf16)

def dot3(a, b, ca, cb):
    ah, al = a
    bh, bl = b
    lhs = jnp.concatenate([ah, ah, al], axis=ca)
    rhs = jnp.concatenate([bh, bl, bh], axis=cb)
    return lax.dot_general(lhs, rhs, (((ca,), (cb,)), ((), ())), preferred_element_type=f32)

def swap(v):
    return pltpu.roll(v, NSTATE, 1)

def twist(table, re, im):
    return re * table + im * swap(table)

def ladder(prm, order):
    sub = lax.broadcasted_iota(jnp.int32, (8, 2 * NSTATE), 0)
    lane = lax.broadcasted_iota(jnp.int32, (8, 2 * NSTATE), 1)
    power = sub if order == 1 else 7 - sub
    table = jnp.where(lane < NSTATE, 1.0, 0.0).astype(f32)
    for bit in range(3):
        table = jnp.where((power >> bit) & 1 == 1, twist(table, prm[2 * bit:2 * bit + 1], prm[2 * bit + 1:2 * bit + 2]), table)
    for bit in range(3, 7):
        more = twist(table, prm[2 * bit:2 * bit + 1], prm[2 * bit + 1:2 * bit + 2])
        table = jnp.concatenate([table, more] if order == 1 else [more, table], axis=0)
    return table

def toeplitz(prm, table):
    wrow = jnp.broadcast_to(prm[16:17], (8, 2 * NSTATE))
    taps = dot3(split(wrow), split(table), 1, 1)
    wide = jnp.broadcast_to(taps[0:1], (CH, CH))
    wide = pltpu.roll(wide, 0, 1, stride=1, stride_axis=0)
    row = lax.broadcasted_iota(jnp.int32, (CH, CH), 0)
    col = lax.broadcasted_iota(jnp.int32, (CH, CH), 1)
    return jnp.where(col >= row, wide, 0.0)

def label_at(ends, pos):
    total = jnp.zeros_like(pos)
    for k in range(DOCS):
        total = total + (pos >= ends[k]).astype(jnp.int32)
    return total

def make_masks(ends_ref, masks_ref, nck):
    ends = [ends_ref[k] for k in range(DOCS)]
    row = lax.broadcasted_iota(jnp.int32, (nck, CH), 0)
    lane = lax.broadcasted_iota(jnp.int32, (nck, CH), 1)
    base = row * CH
    label = label_at(ends, base + lane)
    prev = jnp.where(base == 0, -1, label_at(ends, base - 1))
    last = label_at(ends, base + CH - 1)
    for k in range(DOCS):
        masks_ref[k] = (label == k).astype(f32)
    masks_ref[DOCS] = (label == prev).astype(f32)
    masks_ref[DOCS + 1] = (label == last).astype(f32)

def keep_of(ends_ref, c):
    first = jnp.int32(0)
    second = jnp.int32(0)
    for k in range(DOCS):
        first = first + (c * CH - 1 >= ends_ref[k]).astype(jnp.int32)
        second = second + (c * CH + CH - 1 >= ends_ref[k]).astype(jnp.int32)
    return jnp.where((c > 0) & (first == second), 1.0, 0.0).astype(f32)

def masked_rows(v, masks_ref):
    return jnp.concatenate([v * masks_ref[k] for k in range(DOCS)], axis=0)

def fold_rows(v, masks_ref, nck):
    total = v[:nck] * masks_ref[0]
    for k in range(1, DOCS):
        total = total + v[k * nck:(k + 1) * nck] * masks_ref[k]
    return total

def fwd_body(nck, nch, ends_ref, prm_ref, x_ref, y_ref, prior_ref, masks_ref, end_ref, gt_ref):
    make_masks(ends_ref, masks_ref, nck)

    def one(h, _):
        prm = prm_ref[h]
        u = x_ref[pl.ds(h, nck, stride=nch), :] * prm[19:20] + prm[20:21]
        table = ladder(prm, 1)
        down = ladder(prm, -1)
        gt_ref[h] = twist(table, prm[17:18], prm[18:19])
        local = dot3(split(masked_rows(u, masks_ref)), split(toeplitz(prm, table)), 1, 0)
        y_ref[pl.ds(h, nck, stride=nch), :] = fold_rows(local, masks_ref, nck) + prm[21:22] * u
        end_ref[pl.ds(h, nck, stride=nch), :] = dot3(split(u * masks_ref[DOCS + 1]), split(down), 1, 0)
        return 0

    lax.fori_loop(0, nch, one, 0, unroll=8)
    full_re = prm_ref[:, 14, :]
    full_im = prm_ref[:, 15, :]

    def step(c, state):
        at = pl.ds(pl.multiple_of(c * nch, 8), nch)
        prior_ref[at, :] = state
        return keep_of(ends_ref, c) * twist(state, full_re, full_im) + end_ref[at, :]

    lax.fori_loop(0, nck, step, jnp.zeros((nch, 2 * NSTATE), f32))

    def two(h, _):
        prior = prior_ref[pl.ds(h, nck, stride=nch), :]
        carried = dot3(split(prior), split(gt_ref[h]), 1, 1) * masks_ref[DOCS]
        y_ref[pl.ds(h, nck, stride=nch), :] += carried
        return 0

    lax.fori_loop(0, nch, two, 0, unroll=8)

def ssm_forward(ends, prm, x, nck, nch):
    vm = pl.BlockSpec(memory_space=pltpu.VMEM)
    return pl.pallas_call(
        partial(fwd_body, nck, nch),
        out_shape=(jax.ShapeDtypeStruct((nck * nch, CH), f32), jax.ShapeDtypeStruct((nck * nch, 2 * NSTATE), f32)),
        in_specs=[pl.BlockSpec(memory_space=pltpu.SMEM), vm, vm],
        out_specs=(vm, vm),
        scratch_shapes=[
            pltpu.VMEM((DOCS + 2, nck, CH), f32),
            pltpu.VMEM((nck * nch, 2 * NSTATE), f32),
            pltpu.VMEM((nch, CH, 2 * NSTATE), f32),
        ],
        name="state_forward",
    )(ends, prm, x)

def bwd_body(nck, nch, ends_ref, prm_ref, x_ref, g_ref, prior_ref, dx_ref, rows_ref, masks_ref, lead_ref, adj_ref, table_ref):
    make_masks(ends_ref, masks_ref, nck)

    def one(h, _):
        prm = prm_ref[h]
        g = g_ref[pl.ds(h, nck, stride=nch), :]
        table = ladder(prm, 1)
        table_ref[h] = table
        gt = twist(table, prm[17:18], prm[18:19])
        lead_ref[pl.ds(h, nck, stride=nch), :] = dot3(split(g * masks_ref[DOCS]), split(gt), 1, 0)
        return 0

    lax.fori_loop(0, nch, one, 0, unroll=8)
    full_re = prm_ref[:, 14, :]
    full_im = prm_ref[:, 15, :]
    zero = jnp.zeros((nch, 2 * NSTATE), f32)

    def step(k, carry):
        adjoint, same, cross = carry
        c = nck - 1 - k
        at = pl.ds(pl.multiple_of(c * nch, 8), nch)
        adj_ref[at, :] = adjoint
        keep = keep_of(ends_ref, c)
        prior = prior_ref[at, :]
        same = same + keep * adjoint * prior
        cross = cross + keep * adjoint * swap(prior)
        adjoint = lead_ref[at, :] + keep * (full_re * adjoint - full_im * swap(adjoint))
        return adjoint, same, cross

    _, same, cross = lax.fori_loop(0, nck, step, (zero, zero, zero))
    rows_ref[8] = same
    rows_ref[9] = cross
    for k in range(13, 16):
        rows_ref[k] = zero
    row = lax.broadcasted_iota(jnp.int32, (CH, CH), 0)
    col = lax.broadcasted_iota(jnp.int32, (CH, CH), 1)
    flip = (row + col == CH - 1).astype(f32).astype(bf16)

    def two(h, _):
        prm = prm_ref[h]
        x = x_ref[pl.ds(h, nck, stride=nch), :]
        u = x * prm[19:20] + prm[20:21]
        g = g_ref[pl.ds(h, nck, stride=nch), :]
        table = table_ref[h]
        down = ladder(prm, -1)
        mat = split(toeplitz(prm, table))
        gm = split(masked_rows(g, masks_ref))
        um = split(masked_rows(u, masks_ref))
        adjoint = split(adj_ref[pl.ds(h, nck, stride=nch), :])
        prior = split(prior_ref[pl.ds(h, nck, stride=nch), :])
        du = fold_rows(dot3(gm, mat, 1, 1), masks_ref, nck)
        du = du + dot3(adjoint, split(down), 1, 1) * masks_ref[DOCS + 1]
        du = du + prm[21:22] * g
        dx_ref[pl.ds(h, nck, stride=nch), :] = du
        flipped = [jnp.dot(v, flip, preferred_element_type=f32).astype(bf16) for v in um]
        square = dot3(flipped, gm, 0, 0)
        square = jnp.where(row + col >= CH - 1, square, 0.0)
        square = pltpu.roll(square, 1, 1, stride=1, stride_axis=0)
        taps = jnp.sum(square, axis=0, keepdims=True)
        place = lax.broadcasted_iota(jnp.int32, (8, CH), 1).astype(f32)
        sub = lax.broadcasted_iota(jnp.int32, (8, CH), 0)
        both = jnp.where(sub == 0, 1.0, jnp.where(sub == 1, place, 0.0)) * taps
        both = dot3(split(both), split(table), 1, 0)
        rows_ref[0, pl.ds(h, 1), :] = both[0:1]
        rows_ref[1, pl.ds(h, 1), :] = both[1:2]
        late = row.astype(f32)
        dgt = dot3(split(g * masks_ref[DOCS]), prior, 0, 0)
        one = dgt * table
        two = dgt * swap(table)
        rows_ref[2, pl.ds(h, 1), :] = jnp.sum(one, axis=0, keepdims=True)
        rows_ref[3, pl.ds(h, 1), :] = jnp.sum(two, axis=0, keepdims=True)
        rows_ref[4, pl.ds(h, 1), :] = jnp.sum(one * late, axis=0, keepdims=True)
        rows_ref[5, pl.ds(h, 1), :] = jnp.sum(two * late, axis=0, keepdims=True)
        ddown = dot3(split(u * masks_ref[DOCS + 1]), adjoint, 0, 0) * ((CH - 1) - late)
        rows_ref[6, pl.ds(h, 1), :] = jnp.sum(ddown * down, axis=0, keepdims=True)
        rows_ref[7, pl.ds(h, 1), :] = jnp.sum(ddown * swap(down), axis=0, keepdims=True)
        rows_ref[10, pl.ds(h, 1), :] = jnp.sum(g * u, axis=0, keepdims=True)
        rows_ref[11, pl.ds(h, 1), :] = jnp.sum(du * x, axis=0, keepdims=True)
        rows_ref[12, pl.ds(h, 1), :] = jnp.sum(du, axis=0, keepdims=True)
        return 0

    lax.fori_loop(0, nch, two, 0, unroll=8)

def ssm_backward(ends, prm, x, g, prior, nck, nch):
    vm = pl.BlockSpec(memory_space=pltpu.VMEM)
    return pl.pallas_call(
        partial(bwd_body, nck, nch),
        out_shape=(jax.ShapeDtypeStruct((nck * nch, CH), f32), jax.ShapeDtypeStruct((16, nch, 2 * NSTATE), f32)),
        in_specs=[pl.BlockSpec(memory_space=pltpu.SMEM), vm, vm, vm, vm],
        out_specs=(vm, vm),
        scratch_shapes=[
            pltpu.VMEM((DOCS + 2, nck, CH), f32),
            pltpu.VMEM((nck * nch, 2 * NSTATE), f32),
            pltpu.VMEM((nck * nch, 2 * NSTATE), f32),
            pltpu.VMEM((nch, CH, 2 * NSTATE), f32),
        ],
        name="state_backward",
    )(ends, prm, x, g, prior)

def mixing(step_log, decay_log, frequency, out_real, out_imag):
    delta = jnp.exp(step_log)[:, None]
    rate_re = -jnp.exp(decay_log)
    arg_re, arg_im = delta * rate_re, delta * frequency
    magnitude = jnp.exp(arg_re)
    pole_re = magnitude * jnp.cos(arg_im) - 1.0
    pole_im = magnitude * jnp.sin(arg_im)
    denom = rate_re * rate_re + frequency * frequency
    ratio_re = (pole_re * rate_re + pole_im * frequency) / denom
    ratio_im = (pole_im * rate_re - pole_re * frequency) / denom
    mix_re = out_real * ratio_re - out_imag * ratio_im
    mix_im = out_real * ratio_im + out_imag * ratio_re
    return arg_re, arg_im, mix_re, mix_im

def pair(left, right):
    return jnp.concatenate([left, right], axis=-1)

def mode_rows(arg_re, arg_im, mix_re, mix_im, gain, bias, skip):
    nch = arg_re.shape[0]
    scale = jnp.asarray([2.0**b for b in range(8)], f32)[None, :, None]
    magnitude = jnp.exp(arg_re[:, None] * scale)
    p_re = magnitude * jnp.cos(arg_im[:, None] * scale)
    p_im = magnitude * jnp.sin(arg_im[:, None] * scale)
    powers = jnp.stack([pair(p_re, p_re), pair(-p_im, p_im)], axis=2).reshape(nch, 16, 2 * NSTATE)
    c_re = mix_re * p_re[:, 0] - mix_im * p_im[:, 0]
    c_im = mix_re * p_im[:, 0] + mix_im * p_re[:, 0]
    flat = lambda v: jnp.broadcast_to(v[:, None], (nch, 2 * NSTATE))
    rest = jnp.stack([pair(mix_re, -mix_im), pair(c_re, -c_re), pair(-c_im, -c_im), flat(gain), flat(bias), flat(skip), flat(0 * gain), flat(0 * gain)], axis=1)
    return jnp.concatenate([powers, rest], axis=1)

def mode_grads(rows, arg_re, arg_im, mix_re, mix_im):
    lo, hi = rows[:, :, :NSTATE], rows[:, :, NSTATE:]
    magnitude = jnp.exp(arg_re)
    p_re, p_im = magnitude * jnp.cos(arg_im), magnitude * jnp.sin(arg_im)
    magnitude = jnp.exp(arg_re * CH)
    f_re, f_im = magnitude * jnp.cos(arg_im * CH), magnitude * jnp.sin(arg_im * CH)
    a_re, a_im = lo[2] - hi[2], -(hi[3] + lo[3])
    b_re, b_im = lo[4] - hi[4], -(hi[5] + lo[5])
    b_re, b_im = b_re + a_re, b_im + a_im
    w_re = lo[0] + p_re * a_re + p_im * a_im
    w_im = -hi[0] + p_re * a_im - p_im * a_re
    v_re = lo[1] + p_re * b_re + p_im * b_im
    v_im = -hi[1] + p_re * b_im - p_im * b_re
    g_re = mix_re * v_re + mix_im * v_im
    g_im = mix_re * v_im - mix_im * v_re
    g_re = g_re + lo[6] + hi[6]
    g_im = g_im + hi[7] - lo[7]
    d_re, d_im = lo[8] + hi[8], hi[9] - lo[9]
    g_re = g_re + CH * (f_re * d_re + f_im * d_im)
    g_im = g_im + CH * (f_re * d_im - f_im * d_re)
    return g_re, g_im, w_re, w_im


def gelu(values):
    return 0.5 * values * (1.0 + lax.erf(values * root_half))


def gelu_slope(values):
    return (
        0.5 * (1.0 + lax.erf(values * root_half))
        + values * jnp.exp(-0.5 * values * values) * inv_root_two_pi
    )


def normalize(values):
    center = values - jnp.mean(values, axis=-1, keepdims=True)
    scale = lax.rsqrt(jnp.mean(center * center, axis=-1, keepdims=True) + norm_eps)
    return (center * scale, scale)


def norm_back(d_hat, hat, scale):
    return scale * (
        d_hat
        - jnp.mean(d_hat, axis=-1, keepdims=True)
        - hat * jnp.mean(d_hat * hat, axis=-1, keepdims=True)
    )


TILE = 1024
GATE_AT, EXPAND_AT, REDUCE_AT = 130, 644, 1670
SMALL_AT = (642, 643, 1668, 1669, 2694)
MODE_TILES = 130
BLOCK = 512


def lay(share, devices):
    base = share // TILE
    return base, base + 2, (devices - 1) * share // TILE + base + 2


def product(a, b, ca, cb):
    return lax.dot_general(a, b, (((ca,), (cb,)), ((), ())), preferred_element_type=f32)


def narrow(flat, out, first, rows, per):
    def one(i, _):
        for k in range(per):
            v = flat[pl.ds(first * 8 + i * 16 * per + k, 16, stride=per), :]
            out[pl.ds(pl.multiple_of(i * 16, 16), 16), k * CH:(k + 1) * CH] = v.astype(bf16)
        return 0

    lax.fori_loop(0, rows // 16, one, 0, unroll=max(1, 16 // per))


def small_row(flat, tile, begin, count):
    return jnp.concatenate([flat[tile * 8 + (begin + k) // CH:tile * 8 + (begin + k) // CH + 1, :] for k in range(0, count, CH)], axis=1)


def put_small(small_ref, begin, row):
    for k in range(row.shape[1] // CH):
        small_ref[begin // CH + k:begin // CH + k + 1, :] = row[:, k * CH:(k + 1) * CH]


def column_sum(v):
    return jnp.sum(v, axis=0, keepdims=True)


def mlp_body(share, devices, nseq, place_ref, boxes, resp_ref, x_ref, cot_ref, out_ref, dmid_ref, dresp_ref, small_ref, lead_ref, hidden_ref, active_ref, normed_ref, back_ref, dopen_ref, dlift_ref, flat, side, gate, expand, reduce, acc, dnorm, sems):
    base, box, _ = lay(share, devices)
    nch = D // nseq
    group = x_ref.shape[0]
    start_of = lambda j: (j * share) // TILE
    edges = [0] + [min(devices, tile * TILE // share + 1) for tile in (EXPAND_AT, REDUCE_AT)] + [devices]

    def copy_side(j, _):
        for s, tile in enumerate((0, base, base + 1)):
            pltpu.make_async_copy(boxes.at[pl.ds(pl.multiple_of((j * box + tile) * 8, 8), 8), :], side.at[s, pl.ds(pl.multiple_of(j * 8, 8), 8), :], sems.at[3]).start()
        return 0

    lax.fori_loop(0, devices, copy_side, 0)
    for g in range(3):

        def copy_box(j, _, g=g):
            pltpu.make_async_copy(
                boxes.at[pl.ds(pl.multiple_of((j * box + 1) * 8, 8), (base - 1) * 8), :],
                flat.at[pl.ds(pl.multiple_of((start_of(j) + 1) * 8, 8), (base - 1) * 8), :],
                sems.at[g],
            ).start()
            return 0

        lax.fori_loop(edges[g], edges[g + 1], copy_box, 0)
    parts = group // CH
    turned = [
        jnp.concatenate([resp_ref[pl.ds((d * parts + k) * nch, nch), :] for d in range(nseq)], axis=0).T
        for k in range(parts)
    ]
    response = jnp.concatenate(turned, axis=0)
    hidden_ref[...] = gelu(response).astype(bf16)
    pos = place_ref[DOCS] + lax.broadcasted_iota(jnp.int32, (group, D), 0)
    total = jnp.zeros((group, D), jnp.int32)
    for k in range(DOCS):
        total = total + (pos >= place_ref[k]).astype(jnp.int32)
    back = jnp.where(total < DOCS - 1, cot_ref[...].astype(f32), 0.0)
    back_ref[...] = back.astype(bf16)
    acc[...] = back
    put_small(small_ref, 2 * G + FF, column_sum(back))
    small_ref[36:40, :] = jnp.zeros((4, CH), f32)
    inner = side.at[:, pl.ds(0, devices * 8), :]
    pltpu.make_async_copy(inner, inner, sems.at[3]).wait()
    side[0, devices * 8:, :] = jnp.zeros((8, CH), f32)
    flat[:8, :] = side[0, :8, :]

    def join(j, _):
        at = start_of(j)
        step = start_of(j + 1) - at
        far = jnp.broadcast_to(step, (8, CH)) > base
        here = pl.ds(pl.multiple_of(j * 8, 8), 8)
        one, two, then = side[1, here, :], side[2, here, :], side[0, pl.ds(pl.multiple_of(j * 8 + 8, 8), 8), :]
        flat[pl.ds(pl.multiple_of((at + base) * 8, 8), 8), :] = one + jnp.where(far, 0.0, then)
        flat[pl.ds(pl.multiple_of((at + step) * 8, 8), 8), :] = jnp.where(far, two, one) + then
        return 0

    lax.fori_loop(0, devices, join, 0)

    def arrived(g):
        rows = (edges[g + 1] - edges[g]) * (base - 1) * 8
        some = flat.at[pl.ds(0, rows), :]
        pltpu.make_async_copy(some, some, sems.at[g]).wait()

    arrived(0)
    lead_ref[...] = flat[:MODE_TILES * 8, :]
    narrow(flat, gate, GATE_AT, D, G // CH)
    gate_bias = small_row(flat, SMALL_AT[0], 0, G)
    second_gain = small_row(flat, SMALL_AT[1], 0, D)
    second_bias = small_row(flat, SMALL_AT[1], D, D)
    hidden = hidden_ref[...]
    linear = product(hidden, gate[:, :D], 1, 0) + gate_bias[:, :D]
    gating = jax.nn.sigmoid(product(hidden, gate[:, D:], 1, 0) + gate_bias[:, D:])
    mid = x_ref[...].astype(f32) + linear * gating
    hat, scale = normalize(mid)
    normed_ref[...] = (hat * second_gain + second_bias).astype(bf16)
    out_acc = mid
    arrived(1)
    narrow(flat, expand, EXPAND_AT, D, FF // CH)
    arrived(2)
    narrow(flat, reduce, REDUCE_AT, FF, D // CH)
    dnorm[...] = jnp.zeros((group, D), f32)
    acc[...] = mid + small_row(flat, SMALL_AT[4], 0, D)
    for b in range(FF // BLOCK):
        at = slice(b * BLOCK, (b + 1) * BLOCK)
        bias = small_row(flat, SMALL_AT[2] + b * BLOCK // TILE, b * BLOCK % TILE, BLOCK)
        lifted = product(normed_ref[...], expand[:, at], 1, 0) + bias
        half = 0.5 * (1.0 + lax.erf(lifted * root_half))
        active = (lifted * half).astype(bf16)
        active_ref[:, at] = active
        slope = half + lifted * jnp.exp(-0.5 * lifted * lifted) * inv_root_two_pi
        d_lifted = (product(back_ref[...], reduce[at, :], 1, 1) * slope).astype(bf16)
        dlift_ref[:, at] = d_lifted
        put_small(small_ref, 2 * G + b * BLOCK, column_sum(d_lifted.astype(f32)))
        acc[...] += product(active, reduce[at, :], 1, 0)
        dnorm[...] += product(d_lifted, expand[:, at], 1, 1)
    out_ref[...] = acc[...].astype(bf16)
    d_normed = dnorm[...]
    put_small(small_ref, G, column_sum(d_normed * hat))
    put_small(small_ref, G + D, column_sum(d_normed))
    d_mid = back_ref[...].astype(f32) + norm_back(d_normed * second_gain, hat, scale)
    dmid_ref[...] = d_mid
    d_linear = (d_mid * gating).astype(bf16)
    d_gating = (d_mid * linear * gating * (1.0 - gating)).astype(bf16)
    dopen_ref[:, :D] = d_linear
    dopen_ref[:, D:] = d_gating
    put_small(small_ref, 0, column_sum(d_linear.astype(f32)))
    put_small(small_ref, D, column_sum(d_gating.astype(f32)))
    d_hidden = product(d_linear, gate[:, :D], 1, 1) + product(d_gating, gate[:, D:], 1, 1)
    for k in range(parts):
        rows = resp_ref
        again = jnp.concatenate([resp_ref[pl.ds((d * parts + k) * nch, nch), :] for d in range(nseq)], axis=0)
        back_turned = d_hidden[k * CH:(k + 1) * CH].T * gelu_slope(again)
        for d in range(nseq):
            dresp_ref[pl.ds((d * parts + k) * nch, nch), :] = back_turned[d * nch:(d + 1) * nch]


def mlp_kernel(place, boxes, response, rows, cotangent, share, devices, nseq):
    base, box, tiles = lay(share, devices)
    group = rows.shape[0]
    vm = pl.BlockSpec(memory_space=pltpu.VMEM)
    shape = lambda r, c, t: jax.ShapeDtypeStruct((r, c), t)
    return pl.pallas_call(
        partial(mlp_body, share, devices, nseq),
        out_shape=(
            shape(group, D, bf16),
            shape(group, D, f32),
            jax.ShapeDtypeStruct(response.shape, f32),
            shape(len(SMALL_AT) * 8, CH, f32),
            shape(MODE_TILES * 8, CH, f32),
            shape(group, D, bf16),
            shape(group, FF, bf16),
            shape(group, D, bf16),
            shape(group, D, bf16),
            shape(group, G, bf16),
            shape(group, FF, bf16),
        ),
        in_specs=[pl.BlockSpec(memory_space=pltpu.SMEM), pl.BlockSpec(memory_space=pl.ANY)] + [vm] * 3,
        out_specs=(vm,) * 11,
        scratch_shapes=[
            pltpu.VMEM((tiles * 8, CH), f32),
            pltpu.VMEM((3, devices * 8 + 8, CH), f32),
            pltpu.VMEM((D, G), bf16),
            pltpu.VMEM((D, FF), bf16),
            pltpu.VMEM((FF, D), bf16),
            pltpu.VMEM((group, D), f32),
            pltpu.VMEM((group, D), f32),
            pltpu.SemaphoreType.DMA((4,)),
        ],
        name="feed_forward",
    )(place, boxes, response, rows, cotangent)


def pack_body(streams, tiles, has_lead, *refs):
    n = len(streams)
    dest, hidden, active, normed, back, dopen, dlift, small_ref = refs[:8]
    outs = refs[8 + has_lead:8 + has_lead + n]
    flat, sem = refs[8 + has_lead + n:]
    if has_lead:
        flat[:MODE_TILES * 8, :] = refs[8][...]
    else:
        flat[:MODE_TILES * 8, :] = jnp.zeros((MODE_TILES * 8, CH), f32)
    for k, tile in enumerate(SMALL_AT):
        flat[tile * 8:(tile + 1) * 8, :] = small_ref[k * 8:(k + 1) * 8, :]
    flat[(SMALL_AT[-1] + 1) * 8:, :] = jnp.zeros(((tiles - SMALL_AT[-1] - 1) * 8, CH), f32)
    for first, left, right, per in ((GATE_AT, hidden, dopen, G // CH), (EXPAND_AT, normed, dlift, FF // CH), (REDUCE_AT, active, back, D // CH)):
        wide = 128
        flip = left[...].T

        for k in range(left.shape[1] // wide):
            v = product(flip[k * wide:(k + 1) * wide], right[...], 1, 0)
            for c in range(per):
                flat[pl.ds(first * 8 + k * wide * per + c, wide, stride=per), :] = v[:, c * CH:(c + 1) * CH]
    for k, (first, last, order) in enumerate(streams):
        rows = (last - first) * 8

        def send(b, _, k=k, first=first, rows=rows, order=order):
            at = pl.multiple_of(dest[order + b], 8)
            pltpu.make_async_copy(flat.at[pl.ds(at + first * 8, rows), :], outs[k].at[pl.ds(pl.multiple_of(b * rows, 8), rows), :], sem.at[k]).start()
            return 0

        lax.fori_loop(0, outs[k].shape[0] // rows, send, 0)
    for k, out in enumerate(outs):
        pltpu.make_async_copy(out, out, sem.at[k]).wait()


def pack_kernel(streams, dest, values, small, lead, share, devices):
    _, _, tiles = lay(share, devices)
    hbm = pl.BlockSpec(memory_space=pl.ANY)
    vm = pl.BlockSpec(memory_space=pltpu.VMEM)
    has = int(lead is not None)
    return pl.pallas_call(
        partial(pack_body, tuple(s[:3] for s in streams), tiles, has),
        out_shape=tuple(jax.ShapeDtypeStruct((blocks * (last - first) * 8, CH), f32) for first, last, _, blocks in streams),
        in_specs=[pl.BlockSpec(memory_space=pltpu.SMEM)] + [vm] * (7 + has),
        out_specs=(hbm,) * len(streams),
        scratch_shapes=[pltpu.VMEM((tiles * 8, CH), f32), pltpu.SemaphoreType.DMA((len(streams),))],
        name="weight_gradients",
    )(dest, *values, small, *((lead,) if has else ()))


AXES = ("seq", "batch")
PAIR = [(0, 1), (1, 0)]


def columns(seq):
    return seq // 4, 4


def across(v, step):
    return lax.ppermute(v, "seq", [(i, i ^ step) for i in range(16)])


def along(v, step):
    return lax.ppermute(v, "seq", [(i, (i + 4 * step) % 16) for i in range(16)])


def swap_cores(v):
    return lax.ppermute(v, "batch", PAIR)


def direct():
    return lax.axis_size("seq") == 16 and lax.axis_size("batch") == 2


def first_rows(share, devices, ids):
    return ids * share // TILE * 8


def place_of(step_z, step_p, other):
    seq, batch = lax.axis_index("seq"), lax.axis_index("batch")
    z = (seq // 4 + 4 + step_z) % 4
    return 2 * (z * 4 + (seq % 4 ^ step_p)) + (batch ^ other)


def cuts_of(tiles, part):
    one = round(tiles * part)
    two = one + round((tiles - one) * 2 / 3)
    return one, two


def device_index():
    return lax.axis_index("seq") * lax.axis_size("batch") + lax.axis_index("batch")


def gather_weights(master, share, devices):
    _, tiles, _ = lay(share, devices)
    box = lax.dynamic_update_slice(jnp.zeros((tiles * TILE,), f32), master, (device_index() * share % TILE,))
    return lax.all_gather(box.reshape(tiles * 8, CH), AXES, axis=0, tiled=True)


def scatter_plan(share, devices):
    _, tiles, _ = lay(share, devices)
    natural = first_rows(share, devices, jnp.arange(devices, dtype=jnp.int32))
    if not direct() or SCATTER_PART == 1:
        return ((0, tiles, 0, devices),), natural
    one, two = cuts_of(tiles, SCATTER_PART)
    streams, dest = [], []
    if one:
        streams.append((0, one, 0, devices))
        dest.append(natural)
    for lo, hi, ids in (
        (one, two, lambda s, b, o: place_of(b, s, o)),
        (two, tiles, lambda s, b, o: place_of(s, b, o)),
    ):
        for other in range(2):
            for s in range(4):
                streams.append((lo, hi, sum(d.shape[0] for d in dest), 4))
                dest.append(first_rows(share, devices, jnp.stack([ids(s, b, other) for b in range(4)])))
    return tuple(streams), jnp.concatenate(dest).astype(jnp.int32)


def scatter_gradients(arrays, share, devices):
    _, tiles, _ = lay(share, devices)
    if not direct() or SCATTER_PART == 1:
        return lax.psum_scatter(arrays[0].reshape(devices, tiles * 8, CH), AXES, scatter_dimension=0)
    one, two = cuts_of(tiles, SCATTER_PART)
    pieces = []
    if one:
        pieces.append(lax.psum_scatter(arrays[0].reshape(devices, one * 8, CH), AXES, scatter_dimension=0))
        arrays = arrays[1:]
    both = [a + swap_cores(b) for a, b in zip(arrays[:4] + arrays[8:12], arrays[4:8] + arrays[12:16])]
    by_p, by_z = both[:4], both[4:]
    part_p = by_p[0] + across(by_p[1], 1) + across(by_p[2], 2) + across(by_p[3], 3)
    part_z = by_z[0] + along(by_z[1], 1) + along(by_z[2], 2) + along(by_z[3], 3)
    part_p, part_z = part_p.reshape(4, -1, CH), part_z.reshape(4, -1, CH)
    pieces.append(part_p[0] + along(part_p[1], 1) + along(part_p[2], 2) + along(part_p[3], 3))
    pieces.append(part_z[0] + across(part_z[1], 1) + across(part_z[2], 2) + across(part_z[3], 3))
    return jnp.concatenate(pieces)


MODE_ROWS = 65


def scatter_modes(master):
    other = swap_cores(master)
    even = lax.axis_index("batch") == 0
    lead = jnp.concatenate([jnp.where(even, master, other), jnp.where(even, other, master)])[:MODE_TILES * TILE]
    small = lead[:4 * D].reshape(4, 16, 32).transpose(1, 0, 2).reshape(16, 1, CH)
    rest = lead[4 * D:].reshape(4, 16, 16, CH).transpose(1, 0, 2, 3).reshape(16, 64, CH)
    blocks = jnp.concatenate([small, rest], axis=1)
    seq = lax.axis_index("seq")
    far = [lax.ppermute(blocks[4 * k:4 * k + 4], "seq", [(0, 4 * k)]) for k in range(1, 4)]
    plane = jnp.where(seq == 0, blocks[:4], far[0] + far[1] + far[2])
    near = [lax.ppermute(plane[p], "seq", [(4 * z, 4 * z + p) for z in range(4)]) for p in range(1, 4)]
    return jnp.where(seq % 4 == 0, plane[0], near[0] + near[1] + near[2])


def read_modes(block):
    nch = D // 16
    small = block[0].reshape(4, nch)
    rest = block[1:].reshape(4, nch, NSTATE)
    return small, rest


def gather_modes(small, rest):
    block = jnp.concatenate([small.reshape(1, CH), rest.reshape(64, CH)])
    near = [lax.ppermute(block, "seq", [(4 * z + p, 4 * z) for z in range(4)]) for p in range(1, 4)]
    plane = jnp.stack([block] + near)
    far = [lax.ppermute(plane, "seq", [(4 * k, 0)]) for k in range(1, 4)]
    blocks = jnp.concatenate([plane] + far)
    lead = blocks[:, 0].reshape(16, 4, 32).transpose(1, 0, 2).reshape(-1)
    tail = blocks[:, 1:].reshape(16, 4, 16, CH).transpose(1, 0, 2, 3).reshape(-1)
    return jnp.concatenate([lead, tail])


def total_of(v):
    if not direct():
        return lax.psum(v, AXES)
    v = jnp.broadcast_to(v, (8, CH))
    v = v + swap_cores(v)
    v = v + (across(v, 1) + across(v, 2) + across(v, 3))
    v = v + (along(v, 1) + along(v, 2) + along(v, 3))
    return v[0, 0]


def to_channels(rows):
    seq = lax.axis_size("seq")
    parts = rows.shape[0] // CH
    turned = rows.reshape(parts, CH, seq, D // seq).transpose(2, 0, 3, 1)
    return lax.all_to_all(turned, "seq", 0, 0).reshape(-1, CH)


def to_tokens(rows, group):
    seq = lax.axis_size("seq")
    turned = lax.all_to_all(rows.reshape(seq, group // CH, D // seq, CH), "seq", 0, 0)
    return turned.transpose(1, 3, 0, 2).reshape(group, D)


def per_device(inputs, cotangent, lengths, master, first_moment, second_moment):
    seq, batch = lax.axis_size("seq"), lax.axis_size("batch")
    devices = seq * batch
    share = master.shape[0]
    boxes = gather_weights(master, share, devices)
    group = inputs.shape[1]
    nch, nck = D // seq, seq * group // CH
    rows = inputs[0].astype(jnp.float32)
    ends = jnp.cumsum(lengths[0]).astype(jnp.int32)
    place = jnp.concatenate([ends, lax.axis_index("seq")[None] * group]).astype(jnp.int32)
    first_hat, first_scale = normalize(rows)
    hats = to_channels(first_hat)

    def feed_forward(outs):
        response = lax.all_to_all(outs.reshape(seq, -1, nch, CH), "seq", 0, 0).reshape(-1, CH)
        return mlp_kernel(place, boxes, response, inputs[0], cotangent[0], share, devices, seq)

    if direct():
        few, many = read_modes(scatter_modes(master))
    else:
        lead = jnp.concatenate([lax.dynamic_slice(boxes[j * (boxes.shape[0] // devices):(j + 1) * (boxes.shape[0] // devices)].reshape(-1), (j * share % TILE,), (share,)) for j in range(MODE_TILES * TILE // share + 1)])
        mine = lambda v: lax.dynamic_slice_in_dim(v, lax.axis_index("seq") * nch, nch, 1)
        few = mine(lead[:4 * D].reshape(4, D))
        many = mine(lead[4 * D:MODE_TILES * TILE].reshape(4, D, NSTATE))
    modes, modes_pull = jax.vjp(mixing, few[2], many[0], many[1], many[2], many[3])
    prm = mode_rows(*modes, few[0], few[1], few[3])
    outs, prior = ssm_forward(ends, prm, hats, nck, nch)
    output, d_mid, d_response, small, lead, *values = feed_forward(outs)
    d_outs = lax.all_to_all(d_response.reshape(seq, -1, nch, CH), "seq", 0, 0).reshape(-1, CH)
    plan, places = scatter_plan(share, devices)
    d_signals, sums = ssm_backward(ends, prm, hats, d_outs, prior, nck, nch)
    d_signal = to_tokens(d_signals, group)
    norm_gain = lead[:D // CH].reshape(D)
    d_rows = d_mid + norm_back(d_signal * norm_gain, first_hat, first_scale)
    lane_sums = jnp.sum(sums[10:13], axis=-1)
    d_modes = modes_pull(mode_grads(sums, *modes))
    few = jnp.stack([lane_sums[1], lane_sums[2], d_modes[0], lane_sums[0]])
    many = jnp.stack(d_modes[1:])
    if direct():
        packed = pack_kernel(plan, places, values, small, None, share, devices)
    else:

        def spread(v):
            whole = jnp.zeros((v.shape[0], D) + v.shape[2:], f32)
            return lax.dynamic_update_slice_in_dim(whole, v, lax.axis_index("seq") * nch, 1)

        lead = jnp.concatenate([spread(few).reshape(-1), spread(many).reshape(-1)]).reshape(-1, CH)
        packed = pack_kernel(plan, places, values, small, lead, share, devices)
    me = device_index()
    box = scatter_gradients(packed, share, devices)
    shard = lax.dynamic_slice(box.reshape(-1), (me * share % TILE,), (share,))
    if direct():
        few, many = few + swap_cores(few), many + swap_cores(many)
        lead = gather_modes(few, many)
        lead = jnp.pad(lead, (0, 2 * share - lead.shape[0]))
        mark = me * share + jnp.arange(share, dtype=jnp.int32) < MODE_TILES * TILE
        squares = jnp.sum(jnp.where(mark, 0.0, shard * shard))
        squares = squares + 0.5 * (jnp.sum(few * few) + jnp.sum(many * many))
        shard = jnp.where(mark, lax.dynamic_slice(lead, (jnp.minimum(me, 1) * share,), (share,)), shard)
    else:
        squares = jnp.sum(shard * shard)
    total = total_of(squares)
    grad_norm = jnp.sqrt(total)
    factor = jnp.minimum(1.0, 1.0 / (grad_norm + 1e-06))
    clipped = shard * factor
    first_new = 0.9 * first_moment + 0.1 * clipped
    second_new = 0.999 * second_moment + 0.001 * clipped * clipped
    first_hat_new = first_new / (1.0 - 0.9**10)
    second_hat_new = second_new / (1.0 - 0.999**10)
    update = -0.05 * (first_hat_new / (jnp.sqrt(second_hat_new) + 1e-08) + 0.1 * master)
    return (output[None], d_rows[None], shard, update, first_new, second_new, grad_norm)


def solution(mesh):
    placed = (
        P("batch", "seq", None),
        P("batch", "seq", None),
        P("batch", None),
        P(("seq", "batch")),
        P(("seq", "batch")),
        P(("seq", "batch")),
    )
    return jax.shard_map(
        per_device,
        mesh=mesh,
        in_specs=placed,
        out_specs=(
            P("batch", "seq", None),
            P("batch", "seq", None),
            P(("seq", "batch")),
            P(("seq", "batch")),
            P(("seq", "batch")),
            P(("seq", "batch")),
            P(),
        ),
        check_vma=False,
    )
```

```python
from functools import partial
import jax
import jax.numpy as jnp
import numpy as np
from jax import lax
from jax.experimental import pallas as pl
from jax.experimental.pallas import tpu as pltpu
from jax.sharding import PartitionSpec as P

D = 512
NSTATE = 64
CH = 128
DOCS = 4
G = 1024
FF = 2048
ALONG_PART = 0.75


norm_eps = 1e-05
root_half = 0.7071067811865476
inv_root_two_pi = 0.3989422804014327


f32 = jnp.float32
bf16 = jnp.bfloat16

def split(v):
    hi = v.astype(bf16)
    return hi, (v - hi.astype(f32)).astype(bf16)

def dot3(a, b, ca, cb):
    ah, al = a
    bh, bl = b
    lhs = jnp.concatenate([ah, ah, al], axis=ca)
    rhs = jnp.concatenate([bh, bl, bh], axis=cb)
    return lax.dot_general(lhs, rhs, (((ca,), (cb,)), ((), ())), preferred_element_type=f32)

def swap(v):
    return pltpu.roll(v, NSTATE, 1)

def twist(table, re, im):
    return re * table + im * swap(table)

def ladder(prm, order):
    sub = lax.broadcasted_iota(jnp.int32, (8, 2 * NSTATE), 0)
    lane = lax.broadcasted_iota(jnp.int32, (8, 2 * NSTATE), 1)
    power = sub if order == 1 else 7 - sub
    table = jnp.where(lane < NSTATE, 1.0, 0.0).astype(f32)
    for bit in range(3):
        table = jnp.where((power >> bit) & 1 == 1, twist(table, prm[2 * bit:2 * bit + 1], prm[2 * bit + 1:2 * bit + 2]), table)
    for bit in range(3, 7):
        more = twist(table, prm[2 * bit:2 * bit + 1], prm[2 * bit + 1:2 * bit + 2])
        table = jnp.concatenate([table, more] if order == 1 else [more, table], axis=0)
    return table

def toeplitz(prm, table):
    wrow = jnp.broadcast_to(prm[16:17], (8, 2 * NSTATE))
    taps = dot3(split(wrow), split(table), 1, 1)
    wide = jnp.broadcast_to(taps[0:1], (CH, CH))
    wide = pltpu.roll(wide, 0, 1, stride=1, stride_axis=0)
    row = lax.broadcasted_iota(jnp.int32, (CH, CH), 0)
    col = lax.broadcasted_iota(jnp.int32, (CH, CH), 1)
    return jnp.where(col >= row, wide, 0.0)

def label_at(ends, pos):
    total = jnp.zeros_like(pos)
    for k in range(DOCS):
        total = total + (pos >= ends[k]).astype(jnp.int32)
    return total

def make_masks(ends_ref, masks_ref, nck):
    ends = [ends_ref[k] for k in range(DOCS)]
    row = lax.broadcasted_iota(jnp.int32, (nck, CH), 0)
    lane = lax.broadcasted_iota(jnp.int32, (nck, CH), 1)
    base = row * CH
    label = label_at(ends, base + lane)
    prev = jnp.where(base == 0, -1, label_at(ends, base - 1))
    last = label_at(ends, base + CH - 1)
    for k in range(DOCS):
        masks_ref[k] = (label == k).astype(f32)
    masks_ref[DOCS] = (label == prev).astype(f32)
    masks_ref[DOCS + 1] = (label == last).astype(f32)

def keep_of(ends_ref, c):
    first = jnp.int32(0)
    second = jnp.int32(0)
    for k in range(DOCS):
        first = first + (c * CH - 1 >= ends_ref[k]).astype(jnp.int32)
        second = second + (c * CH + CH - 1 >= ends_ref[k]).astype(jnp.int32)
    return jnp.where((c > 0) & (first == second), 1.0, 0.0).astype(f32)

def masked_rows(v, masks_ref):
    return jnp.concatenate([v * masks_ref[k] for k in range(DOCS)], axis=0)

def fold_rows(v, masks_ref, nck):
    total = v[:nck] * masks_ref[0]
    for k in range(1, DOCS):
        total = total + v[k * nck:(k + 1) * nck] * masks_ref[k]
    return total

def fwd_body(nck, nch, apart, ends_ref, prm_ref, x_ref, y_ref, prior_ref, masks_ref, end_ref, gt_ref):
    make_masks(ends_ref, masks_ref, nck)

    def one(h, _):
        prm = prm_ref[h]
        u = x_ref[pl.ds(h, nck, stride=apart), :] * prm[19:20] + prm[20:21]
        table = ladder(prm, 1)
        down = ladder(prm, -1)
        gt_ref[h] = twist(table, prm[17:18], prm[18:19])
        local = dot3(split(masked_rows(u, masks_ref)), split(toeplitz(prm, table)), 1, 0)
        y_ref[pl.ds(h, nck, stride=nch), :] = fold_rows(local, masks_ref, nck) + prm[21:22] * u
        end_ref[pl.ds(h, nck, stride=nch), :] = dot3(split(u * masks_ref[DOCS + 1]), split(down), 1, 0)
        return 0

    lax.fori_loop(0, nch, one, 0, unroll=8)
    full_re = prm_ref[:, 14, :]
    full_im = prm_ref[:, 15, :]

    def step(c, state):
        at = pl.ds(pl.multiple_of(c * nch, 8), nch)
        prior_ref[at, :] = state
        return keep_of(ends_ref, c) * twist(state, full_re, full_im) + end_ref[at, :]

    lax.fori_loop(0, nck, step, jnp.zeros((nch, 2 * NSTATE), f32))

    def two(h, _):
        prior = prior_ref[pl.ds(h, nck, stride=nch), :]
        carried = dot3(split(prior), split(gt_ref[h]), 1, 1) * masks_ref[DOCS]
        y_ref[pl.ds(h, nck, stride=nch), :] += carried
        return 0

    lax.fori_loop(0, nch, two, 0, unroll=8)

def ssm_forward(ends, prm, x, nck, nch):
    vm = pl.BlockSpec(memory_space=pltpu.VMEM)
    return pl.pallas_call(
        partial(fwd_body, nck, nch, x.shape[0] // nck),
        out_shape=(jax.ShapeDtypeStruct((nck * nch, CH), f32), jax.ShapeDtypeStruct((nck * nch, 2 * NSTATE), f32)),
        in_specs=[pl.BlockSpec(memory_space=pltpu.SMEM), vm, vm],
        out_specs=(vm, vm),
        scratch_shapes=[
            pltpu.VMEM((DOCS + 2, nck, CH), f32),
            pltpu.VMEM((nck * nch, 2 * NSTATE), f32),
            pltpu.VMEM((nch, CH, 2 * NSTATE), f32),
        ],
        cost_estimate=pl.CostEstimate(flops=int(2.0e10), bytes_accessed=3 * 2**20, transcendentals=0),
        name="state_forward",
    )(ends, prm, x)

def bwd_body(nck, nch, apart, ends_ref, prm_ref, x_ref, g_ref, prior_ref, dx_ref, rows_ref, masks_ref, lead_ref, adj_ref, table_ref):
    make_masks(ends_ref, masks_ref, nck)

    def one(h, _):
        prm = prm_ref[h]
        g = g_ref[pl.ds(h, nck, stride=nch), :]
        table = ladder(prm, 1)
        table_ref[h] = table
        gt = twist(table, prm[17:18], prm[18:19])
        lead_ref[pl.ds(h, nck, stride=nch), :] = dot3(split(g * masks_ref[DOCS]), split(gt), 1, 0)
        return 0

    lax.fori_loop(0, nch, one, 0, unroll=8)
    full_re = prm_ref[:, 14, :]
    full_im = prm_ref[:, 15, :]
    zero = jnp.zeros((nch, 2 * NSTATE), f32)

    def step(k, carry):
        adjoint, same, cross = carry
        c = nck - 1 - k
        at = pl.ds(pl.multiple_of(c * nch, 8), nch)
        adj_ref[at, :] = adjoint
        keep = keep_of(ends_ref, c)
        prior = prior_ref[at, :]
        same = same + keep * adjoint * prior
        cross = cross + keep * adjoint * swap(prior)
        adjoint = lead_ref[at, :] + keep * (full_re * adjoint - full_im * swap(adjoint))
        return adjoint, same, cross

    _, same, cross = lax.fori_loop(0, nck, step, (zero, zero, zero))
    rows_ref[8] = same
    rows_ref[9] = cross
    for k in range(13, 16):
        rows_ref[k] = zero
    row = lax.broadcasted_iota(jnp.int32, (CH, CH), 0)
    col = lax.broadcasted_iota(jnp.int32, (CH, CH), 1)
    flip = (row + col == CH - 1).astype(f32).astype(bf16)

    def two(h, _):
        prm = prm_ref[h]
        x = x_ref[pl.ds(h, nck, stride=apart), :]
        u = x * prm[19:20] + prm[20:21]
        g = g_ref[pl.ds(h, nck, stride=nch), :]
        table = table_ref[h]
        down = ladder(prm, -1)
        mat = split(toeplitz(prm, table))
        gm = split(masked_rows(g, masks_ref))
        um = split(masked_rows(u, masks_ref))
        adjoint = split(adj_ref[pl.ds(h, nck, stride=nch), :])
        prior = split(prior_ref[pl.ds(h, nck, stride=nch), :])
        du = fold_rows(dot3(gm, mat, 1, 1), masks_ref, nck)
        du = du + dot3(adjoint, split(down), 1, 1) * masks_ref[DOCS + 1]
        du = du + prm[21:22] * g
        dx_ref[pl.ds(h, nck, stride=apart), :] = du
        flipped = [jnp.dot(v, flip, preferred_element_type=f32).astype(bf16) for v in um]
        square = dot3(flipped, gm, 0, 0)
        square = jnp.where(row + col >= CH - 1, square, 0.0)
        square = pltpu.roll(square, 1, 1, stride=1, stride_axis=0)
        taps = jnp.sum(square, axis=0, keepdims=True)
        place = lax.broadcasted_iota(jnp.int32, (8, CH), 1).astype(f32)
        sub = lax.broadcasted_iota(jnp.int32, (8, CH), 0)
        both = jnp.where(sub == 0, 1.0, jnp.where(sub == 1, place, 0.0)) * taps
        both = dot3(split(both), split(table), 1, 0)
        rows_ref[0, pl.ds(h, 1), :] = both[0:1]
        rows_ref[1, pl.ds(h, 1), :] = both[1:2]
        late = row.astype(f32)
        dgt = dot3(split(g * masks_ref[DOCS]), prior, 0, 0)
        one = dgt * table
        two = dgt * swap(table)
        rows_ref[2, pl.ds(h, 1), :] = jnp.sum(one, axis=0, keepdims=True)
        rows_ref[3, pl.ds(h, 1), :] = jnp.sum(two, axis=0, keepdims=True)
        rows_ref[4, pl.ds(h, 1), :] = jnp.sum(one * late, axis=0, keepdims=True)
        rows_ref[5, pl.ds(h, 1), :] = jnp.sum(two * late, axis=0, keepdims=True)
        ddown = dot3(split(u * masks_ref[DOCS + 1]), adjoint, 0, 0) * ((CH - 1) - late)
        rows_ref[6, pl.ds(h, 1), :] = jnp.sum(ddown * down, axis=0, keepdims=True)
        rows_ref[7, pl.ds(h, 1), :] = jnp.sum(ddown * swap(down), axis=0, keepdims=True)
        rows_ref[10, pl.ds(h, 1), :] = jnp.sum(g * u, axis=0, keepdims=True)
        rows_ref[11, pl.ds(h, 1), :] = jnp.sum(du * x, axis=0, keepdims=True)
        rows_ref[12, pl.ds(h, 1), :] = jnp.sum(du, axis=0, keepdims=True)
        return 0

    lax.fori_loop(0, nch, two, 0, unroll=8)

def ssm_backward(ends, prm, x, g, prior, nck, nch):
    vm = pl.BlockSpec(memory_space=pltpu.VMEM)
    return pl.pallas_call(
        partial(bwd_body, nck, nch, x.shape[0] // nck),
        out_shape=(jax.ShapeDtypeStruct((nck * nch, CH), f32), jax.ShapeDtypeStruct((16, nch, 2 * NSTATE), f32)),
        in_specs=[pl.BlockSpec(memory_space=pltpu.SMEM), vm, vm, vm, vm],
        out_specs=(vm, vm),
        scratch_shapes=[
            pltpu.VMEM((DOCS + 2, nck, CH), f32),
            pltpu.VMEM((nck * nch, 2 * NSTATE), f32),
            pltpu.VMEM((nck * nch, 2 * NSTATE), f32),
            pltpu.VMEM((nch, CH, 2 * NSTATE), f32),
        ],
        cost_estimate=pl.CostEstimate(flops=int(3.5e10), bytes_accessed=4 * 2**20, transcendentals=0),
        name="state_backward",
    )(ends, prm, x, g, prior)

def mixing(step_log, decay_log, frequency, out_real, out_imag):
    delta = jnp.exp(step_log)[:, None]
    rate_re = -jnp.exp(decay_log)
    arg_re, arg_im = delta * rate_re, delta * frequency
    magnitude = jnp.exp(arg_re)
    pole_re = magnitude * jnp.cos(arg_im) - 1.0
    pole_im = magnitude * jnp.sin(arg_im)
    denom = rate_re * rate_re + frequency * frequency
    ratio_re = (pole_re * rate_re + pole_im * frequency) / denom
    ratio_im = (pole_im * rate_re - pole_re * frequency) / denom
    mix_re = out_real * ratio_re - out_imag * ratio_im
    mix_im = out_real * ratio_im + out_imag * ratio_re
    return arg_re, arg_im, mix_re, mix_im

def pair(left, right):
    return jnp.concatenate([left, right], axis=-1)

def mode_rows(arg_re, arg_im, mix_re, mix_im, gain, bias, skip):
    nch = arg_re.shape[0]
    scale = jnp.asarray([2.0**b for b in range(8)], f32)[None, :, None]
    magnitude = jnp.exp(arg_re[:, None] * scale)
    p_re = magnitude * jnp.cos(arg_im[:, None] * scale)
    p_im = magnitude * jnp.sin(arg_im[:, None] * scale)
    powers = jnp.stack([pair(p_re, p_re), pair(-p_im, p_im)], axis=2).reshape(nch, 16, 2 * NSTATE)
    c_re = mix_re * p_re[:, 0] - mix_im * p_im[:, 0]
    c_im = mix_re * p_im[:, 0] + mix_im * p_re[:, 0]
    flat = lambda v: jnp.broadcast_to(v[:, None], (nch, 2 * NSTATE))
    rest = jnp.stack([pair(mix_re, -mix_im), pair(c_re, -c_re), pair(-c_im, -c_im), flat(gain), flat(bias), flat(skip), flat(0 * gain), flat(0 * gain)], axis=1)
    return jnp.concatenate([powers, rest], axis=1)

def mode_grads(rows, arg_re, arg_im, mix_re, mix_im):
    lo, hi = rows[:, :, :NSTATE], rows[:, :, NSTATE:]
    magnitude = jnp.exp(arg_re)
    p_re, p_im = magnitude * jnp.cos(arg_im), magnitude * jnp.sin(arg_im)
    magnitude = jnp.exp(arg_re * CH)
    f_re, f_im = magnitude * jnp.cos(arg_im * CH), magnitude * jnp.sin(arg_im * CH)
    a_re, a_im = lo[2] - hi[2], -(hi[3] + lo[3])
    b_re, b_im = lo[4] - hi[4], -(hi[5] + lo[5])
    b_re, b_im = b_re + a_re, b_im + a_im
    w_re = lo[0] + p_re * a_re + p_im * a_im
    w_im = -hi[0] + p_re * a_im - p_im * a_re
    v_re = lo[1] + p_re * b_re + p_im * b_im
    v_im = -hi[1] + p_re * b_im - p_im * b_re
    g_re = mix_re * v_re + mix_im * v_im
    g_im = mix_re * v_im - mix_im * v_re
    g_re = g_re + lo[6] + hi[6]
    g_im = g_im + hi[7] - lo[7]
    d_re, d_im = lo[8] + hi[8], hi[9] - lo[9]
    g_re = g_re + CH * (f_re * d_re + f_im * d_im)
    g_im = g_im + CH * (f_re * d_im - f_im * d_re)
    return g_re, g_im, w_re, w_im


def gelu(values):
    return 0.5 * values * (1.0 + lax.erf(values * root_half))


def gelu_slope(values):
    return (
        0.5 * (1.0 + lax.erf(values * root_half))
        + values * jnp.exp(-0.5 * values * values) * inv_root_two_pi
    )


def normalize(values):
    center = values - jnp.mean(values, axis=-1, keepdims=True)
    scale = lax.rsqrt(jnp.mean(center * center, axis=-1, keepdims=True) + norm_eps)
    return (center * scale, scale)


def norm_back(d_hat, hat, scale):
    return scale * (
        d_hat
        - jnp.mean(d_hat, axis=-1, keepdims=True)
        - hat * jnp.mean(d_hat * hat, axis=-1, keepdims=True)
    )


TILE = 1024
GATE_AT, EXPAND_AT, REDUCE_AT = 130, 644, 1670
SMALL_AT = (642, 643, 1668, 1669, 2694)
MODE_TILES = 130
BLOCK = 512


def lay(share, devices):
    base = share // TILE
    return base, base + 2, (devices - 1) * share // TILE + base + 2


def product(a, b, ca, cb):
    return lax.dot_general(a, b, (((ca,), (cb,)), ((), ())), preferred_element_type=f32)


def narrow(flat, out, first, rows, per):
    def one(i, _):
        for k in range(per):
            v = flat[pl.ds(first * 8 + i * 16 * per + k, 16, stride=per), :]
            out[pl.ds(pl.multiple_of(i * 16, 16), 16), k * CH:(k + 1) * CH] = v.astype(bf16)
        return 0

    lax.fori_loop(0, rows // 16, one, 0, unroll=max(1, 16 // per))


def small_row(flat, tile, begin, count):
    return jnp.concatenate([flat[tile * 8 + (begin + k) // CH:tile * 8 + (begin + k) // CH + 1, :] for k in range(0, count, CH)], axis=1)


def put_small(small_ref, begin, row):
    for k in range(row.shape[1] // CH):
        small_ref[begin // CH + k:begin // CH + k + 1, :] = row[:, k * CH:(k + 1) * CH]


def column_sum(v):
    return jnp.sum(v, axis=0, keepdims=True)


def mlp_body(share, devices, nseq, streams, place_ref, ids, *refs):
    boxes = refs[:len(streams)]
    resp_ref, x_ref, cot_ref, out_ref, dmid_ref, dresp_ref, small_ref, lead_ref, hidden_ref, active_ref, normed_ref, back_ref, dopen_ref, dlift_ref, flat, side, gate, expand, reduce, acc, dnorm, sems = refs[len(streams):]
    base, box, _ = lay(share, devices)
    nch = D // nseq
    group = x_ref.shape[0]
    start_of = lambda j: (j * share) // TILE
    inside = 0
    for k, (first, last, off, count) in enumerate(streams):
        lo, hi = max(first, 1), min(last, base)

        def copy_box(i, _, k=k, first=first, last=last, lo=lo, hi=hi, off=off):
            j = ids[off + i]
            begin = (i * (last - first) - first) * 8
            for s, tile in enumerate((0, base, base + 1)):
                if first <= tile < last:
                    pltpu.make_async_copy(boxes[k].at[pl.ds(pl.multiple_of(begin + tile * 8, 8), 8), :], side.at[s, pl.ds(pl.multiple_of(j * 8, 8), 8), :], sems.at[1]).start()
            pltpu.make_async_copy(
                boxes[k].at[pl.ds(pl.multiple_of(begin + lo * 8, 8), (hi - lo) * 8), :],
                flat.at[pl.ds(pl.multiple_of((start_of(j) + lo) * 8, 8), (hi - lo) * 8), :],
                sems.at[0],
            ).start()
            return 0

        lax.fori_loop(0, count, copy_box, 0)
        inside += (hi - lo) * count
    parts = group // CH
    turned = [
        jnp.concatenate([resp_ref[pl.ds((d * parts + k) * nch, nch), :] for d in range(nseq)], axis=0).T
        for k in range(parts)
    ]
    response = jnp.concatenate(turned, axis=0)
    hidden_ref[...] = gelu(response).astype(bf16)
    pos = place_ref[DOCS] + lax.broadcasted_iota(jnp.int32, (group, D), 0)
    total = jnp.zeros((group, D), jnp.int32)
    for k in range(DOCS):
        total = total + (pos >= place_ref[k]).astype(jnp.int32)
    back = jnp.where(total < DOCS - 1, cot_ref[...].astype(f32), 0.0)
    back_ref[...] = back.astype(bf16)
    put_small(small_ref, 2 * G + FF, column_sum(back))
    small_ref[36:40, :] = jnp.zeros((4, CH), f32)
    inner = side.at[:, pl.ds(0, devices * 8), :]
    pltpu.make_async_copy(inner, inner, sems.at[1]).wait()
    side[0, devices * 8:, :] = jnp.zeros((8, CH), f32)
    flat[:8, :] = side[0, :8, :]

    def join(j, _):
        at = start_of(j)
        step = start_of(j + 1) - at
        far = jnp.broadcast_to(step, (8, CH)) > base
        here = pl.ds(pl.multiple_of(j * 8, 8), 8)
        one, two, then = side[1, here, :], side[2, here, :], side[0, pl.ds(pl.multiple_of(j * 8 + 8, 8), 8), :]
        flat[pl.ds(pl.multiple_of((at + base) * 8, 8), 8), :] = one + jnp.where(far, 0.0, then)
        flat[pl.ds(pl.multiple_of((at + step) * 8, 8), 8), :] = jnp.where(far, two, one) + then
        return 0

    lax.fori_loop(0, devices, join, 0)

    some = flat.at[pl.ds(0, inside * 8), :]
    pltpu.make_async_copy(some, some, sems.at[0]).wait()
    lead_ref[...] = flat[:MODE_TILES * 8, :]
    narrow(flat, gate, GATE_AT, D, G // CH)
    gate_bias = small_row(flat, SMALL_AT[0], 0, G)
    second_gain = small_row(flat, SMALL_AT[1], 0, D)
    second_bias = small_row(flat, SMALL_AT[1], D, D)
    hidden = hidden_ref[...]
    linear = product(hidden, gate[:, :D], 1, 0) + gate_bias[:, :D]
    gating = jax.nn.sigmoid(product(hidden, gate[:, D:], 1, 0) + gate_bias[:, D:])
    mid = x_ref[...].astype(f32) + linear * gating
    hat, scale = normalize(mid)
    normed_ref[...] = (hat * second_gain + second_bias).astype(bf16)
    narrow(flat, expand, EXPAND_AT, D, FF // CH)
    narrow(flat, reduce, REDUCE_AT, FF, D // CH)
    dnorm[...] = jnp.zeros((group, D), f32)
    acc[...] = mid + small_row(flat, SMALL_AT[4], 0, D)
    for b in range(FF // BLOCK):
        at = slice(b * BLOCK, (b + 1) * BLOCK)
        bias = small_row(flat, SMALL_AT[2] + b * BLOCK // TILE, b * BLOCK % TILE, BLOCK)
        lifted = product(normed_ref[...], expand[:, at], 1, 0) + bias
        half = 0.5 * (1.0 + lax.erf(lifted * root_half))
        active = (lifted * half).astype(bf16)
        active_ref[:, at] = active
        slope = half + lifted * jnp.exp(-0.5 * lifted * lifted) * inv_root_two_pi
        d_lifted = (product(back_ref[...], reduce[at, :], 1, 1) * slope).astype(bf16)
        dlift_ref[:, at] = d_lifted
        put_small(small_ref, 2 * G + b * BLOCK, column_sum(d_lifted.astype(f32)))
        acc[...] += product(active, reduce[at, :], 1, 0)
        dnorm[...] += product(d_lifted, expand[:, at], 1, 1)
    out_ref[...] = acc[...].astype(bf16)
    d_normed = dnorm[...]
    put_small(small_ref, G, column_sum(d_normed * hat))
    put_small(small_ref, G + D, column_sum(d_normed))
    d_mid = back_ref[...].astype(f32) + norm_back(d_normed * second_gain, hat, scale)
    dmid_ref[...] = d_mid
    d_linear = (d_mid * gating).astype(bf16)
    d_gating = (d_mid * linear * gating * (1.0 - gating)).astype(bf16)
    dopen_ref[:, :D] = d_linear
    dopen_ref[:, D:] = d_gating
    put_small(small_ref, 0, column_sum(d_linear.astype(f32)))
    put_small(small_ref, D, column_sum(d_gating.astype(f32)))
    d_hidden = product(d_linear, gate[:, :D], 1, 1) + product(d_gating, gate[:, D:], 1, 1)
    for k in range(parts):
        again = jnp.concatenate([resp_ref[pl.ds((d * parts + k) * nch, nch), :] for d in range(nseq)], axis=0)
        back_turned = d_hidden[k * CH:(k + 1) * CH].T * gelu_slope(again)
        for d in range(nseq):
            dresp_ref[pl.ds((d * parts + k) * nch, nch), :] = back_turned[d * nch:(d + 1) * nch]


def mlp_kernel(place, streams, ids, boxes, response, rows, cotangent, share, devices, nseq):
    base, box, tiles = lay(share, devices)
    group = rows.shape[0]
    vm = pl.BlockSpec(memory_space=pltpu.VMEM)
    shape = lambda r, c, t: jax.ShapeDtypeStruct((r, c), t)
    return pl.pallas_call(
        partial(mlp_body, share, devices, nseq, streams),
        out_shape=(
            shape(group, D, bf16),
            shape(group, D, f32),
            jax.ShapeDtypeStruct(response.shape, f32),
            shape(len(SMALL_AT) * 8, CH, f32),
            shape(MODE_TILES * 8, CH, f32),
            shape(group, D, bf16),
            shape(group, FF, bf16),
            shape(group, D, bf16),
            shape(group, D, bf16),
            shape(group, G, bf16),
            shape(group, FF, bf16),
        ),
        in_specs=[pl.BlockSpec(memory_space=pltpu.SMEM)] * 2 + [pl.BlockSpec(memory_space=pl.ANY)] * len(boxes) + [vm] * 3,
        out_specs=(vm,) * 11,
        scratch_shapes=[
            pltpu.VMEM((tiles * 8, CH), f32),
            pltpu.VMEM((3, devices * 8 + 8, CH), f32),
            pltpu.VMEM((D, G), bf16),
            pltpu.VMEM((D, FF), bf16),
            pltpu.VMEM((FF, D), bf16),
            pltpu.VMEM((group, D), f32),
            pltpu.VMEM((group, D), f32),
            pltpu.SemaphoreType.DMA((2,)),
        ],
        cost_estimate=pl.CostEstimate(flops=int(1.0e10), bytes_accessed=20 * 2**20, transcendentals=0),
        name="feed_forward",
    )(place, ids, *boxes, response, rows, cotangent)


def pack_body(streams, tiles, has_lead, *refs):
    n = len(streams)
    dest, hidden, active, normed, back, dopen, dlift, small_ref = refs[:8]
    outs = refs[8 + has_lead:8 + has_lead + n]
    flat, sem = refs[8 + has_lead + n:]
    if has_lead:
        flat[:MODE_TILES * 8, :] = refs[8][...]
    else:
        flat[:MODE_TILES * 8, :] = jnp.zeros((MODE_TILES * 8, CH), f32)
    for k, tile in enumerate(SMALL_AT):
        flat[tile * 8:(tile + 1) * 8, :] = small_ref[k * 8:(k + 1) * 8, :]
    flat[(SMALL_AT[-1] + 1) * 8:, :] = jnp.zeros(((tiles - SMALL_AT[-1] - 1) * 8, CH), f32)
    for first, left, right, per in ((GATE_AT, hidden, dopen, G // CH), (EXPAND_AT, normed, dlift, FF // CH), (REDUCE_AT, active, back, D // CH)):
        wide = 128
        flip = left[...].T

        for k in range(left.shape[1] // wide):
            v = product(flip[k * wide:(k + 1) * wide], right[...], 1, 0)
            for c in range(per):
                flat[pl.ds(first * 8 + k * wide * per + c, wide, stride=per), :] = v[:, c * CH:(c + 1) * CH]
    for k, (first, last, order) in enumerate(streams):
        rows = (last - first) * 8

        def send(b, _, k=k, first=first, rows=rows, order=order):
            at = pl.multiple_of(dest[order + b], 8)
            pltpu.make_async_copy(flat.at[pl.ds(at + first * 8, rows), :], outs[k].at[pl.ds(pl.multiple_of(b * rows, 8), rows), :], sem.at[k]).start()
            return 0

        lax.fori_loop(0, outs[k].shape[0] // rows, send, 0)
    for k, out in enumerate(outs):
        pltpu.make_async_copy(out, out, sem.at[k]).wait()


def pack_kernel(streams, dest, values, small, lead, share, devices):
    _, _, tiles = lay(share, devices)
    hbm = pl.BlockSpec(memory_space=pl.ANY)
    vm = pl.BlockSpec(memory_space=pltpu.VMEM)
    has = int(lead is not None)
    return pl.pallas_call(
        partial(pack_body, tuple(s[:3] for s in streams), tiles, has),
        out_shape=tuple(jax.ShapeDtypeStruct((blocks * (last - first) * 8, CH), f32) for first, last, _, blocks in streams),
        in_specs=[pl.BlockSpec(memory_space=pltpu.SMEM)] + [vm] * (7 + has),
        out_specs=(hbm,) * len(streams),
        scratch_shapes=[pltpu.VMEM((tiles * 8, CH), f32), pltpu.SemaphoreType.DMA((len(streams),))],
        cost_estimate=pl.CostEstimate(flops=int(0.8e10), bytes_accessed=16 * 2**20, transcendentals=0),
        name="weight_gradients",
    )(dest, *values, small, *((lead,) if has else ()))


AXES = ("seq", "batch")
PAIR = [(0, 1), (1, 0)]


def hop(v, step):
    return lax.ppermute(v, "seq", [(i, i ^ step) for i in range(16)])


def swap_cores(v):
    return lax.ppermute(v, "batch", PAIR)


def direct():
    return lax.axis_size("seq") == 16 and lax.axis_size("batch") == 2


def device_index():
    return lax.axis_index("seq") * lax.axis_size("batch") + lax.axis_index("batch")


def places_of(steps, other):
    seq, batch = lax.axis_index("seq"), lax.axis_index("batch")
    return 2 * (seq ^ np.asarray(steps, np.int32)) + (batch ^ other)


def cut_of(tiles):
    return round(tiles * ALONG_PART)


def container(master, share, devices):
    _, tiles, _ = lay(share, devices)
    box = lax.dynamic_update_slice(jnp.zeros((tiles * TILE,), f32), master, (device_index() * share % TILE,))
    return box.reshape(tiles * 8, CH)


def gather_weights(box, share, devices):
    _, tiles, _ = lay(share, devices)
    ids = jnp.arange(devices, dtype=jnp.int32)
    return ((0, tiles, 0, devices),), ids, [lax.all_gather(box, AXES, axis=0, tiled=True)]


def scatter_plan(share, devices):
    _, tiles, _ = lay(share, devices)
    if not direct():
        return ((0, tiles, 0, devices),), jnp.arange(devices, dtype=jnp.int32) * share // TILE * 8
    cut = cut_of(tiles)
    by_p = [4 * z + p for p in range(4) for z in range(4)]
    by_z = [4 * z + p for z in range(4) for p in range(4)]
    ids = jnp.concatenate([places_of(steps, other) for steps in (by_p, by_z) for other in range(2)])
    streams = ((0, cut, 0, 16), (0, cut, 16, 16), (cut, tiles, 32, 16), (cut, tiles, 48, 16))
    return streams, (ids * share // TILE * 8).astype(jnp.int32)


def pieces(v, count):
    return v.reshape(count, -1, CH)


def join_cores(arrays):
    own_p, far_p, own_z, far_z = arrays
    far_p, far_z = pieces(swap_cores(far_p), 4), pieces(swap_cores(far_z), 2)
    own_p, own_z = pieces(own_p, 4), pieces(own_z, 2)
    return [own_p[k] + far_p[k] for k in range(4)], [own_z[k] + far_z[k] for k in range(2)]


def join_first(by_p, by_z):
    part_p = by_p[0] + hop(by_p[1], 1) + hop(by_p[2], 2) + hop(by_p[3], 3)
    part_z = by_z[0] + hop(by_z[1], 8)
    return pieces(part_p, 4), pieces(part_z, 2)


def join_last(part_p, part_z):
    one = part_p[0] + hop(part_p[1], 4) + hop(part_p[2], 8) + hop(part_p[3], 12)
    part_z = pieces(part_z[0] + hop(part_z[1], 4), 4)
    two = part_z[0] + hop(part_z[1], 1) + hop(part_z[2], 2) + hop(part_z[3], 3)
    return jnp.concatenate([one, two])


MODE_ROWS = 65


def scatter_modes(master):
    other = swap_cores(master)
    even = lax.axis_index("batch") == 0
    lead = jnp.concatenate([jnp.where(even, master, other), jnp.where(even, other, master)])[:MODE_TILES * TILE]
    small = lead[:4 * D].reshape(4, 16, 32).transpose(1, 0, 2).reshape(16, 1, CH)
    rest = lead[4 * D:].reshape(4, 16, 16, CH).transpose(1, 0, 2, 3).reshape(16, 64, CH)
    blocks = jnp.concatenate([small, rest], axis=1)
    seq = lax.axis_index("seq")
    far = [lax.ppermute(blocks[4 * k:4 * k + 4], "seq", [(0, 4 * k)]) for k in range(1, 4)]
    plane = jnp.where(seq == 0, blocks[:4], far[0] + far[1] + far[2])
    near = [lax.ppermute(plane[p], "seq", [(4 * z, 4 * z + p) for z in range(4)]) for p in range(1, 4)]
    return jnp.where(seq % 4 == 0, plane[0], near[0] + near[1] + near[2])


def read_modes(block):
    nch = D // 16
    small = block[0].reshape(4, nch)
    rest = block[1:].reshape(4, nch, NSTATE)
    return small, rest


def gather_modes(block):
    for step in (1, 2, 4, 8):
        pairs = [(i, i - step) for i in range(16) if i % (2 * step) == step]
        block = jnp.concatenate([block, lax.ppermute(block, "seq", pairs)])
    blocks = block.reshape(16, MODE_ROWS, CH)
    lead = blocks[:, 0].reshape(16, 4, 32).transpose(1, 0, 2).reshape(-1)
    tail = blocks[:, 1:].reshape(16, 4, 16, CH).transpose(1, 0, 2, 3).reshape(-1)
    return jnp.concatenate([lead, tail])


def total_of(v):
    if not direct():
        return lax.psum(v, AXES)
    v = jnp.broadcast_to(v, (8, CH))
    v = v + swap_cores(v)
    v = v + (hop(v, 1) + hop(v, 2) + hop(v, 3))
    v = v + (hop(v, 4) + hop(v, 8) + hop(v, 12))
    return v[0, 0]


def to_channels(rows):
    seq = lax.axis_size("seq")
    parts = rows.shape[0] // CH
    turned = rows.reshape(parts, CH, seq, D // seq).transpose(2, 0, 3, 1)
    return lax.all_to_all(turned, "seq", 0, 0).reshape(-1, CH)


def to_tokens(rows, group):
    seq = lax.axis_size("seq")
    turned = lax.all_to_all(rows.reshape(seq, group // CH, D // seq, CH), "seq", 0, 0)
    return turned.transpose(1, 3, 0, 2).reshape(group, D)


def per_device(inputs, cotangent, lengths, master, first_moment, second_moment):
    seq, batch = lax.axis_size("seq"), lax.axis_size("batch")
    devices = seq * batch
    share = master.shape[0]
    box = container(master, share, devices)
    streams, ids, boxes = gather_weights(box, share, devices)
    group = inputs.shape[1]
    nch, nck = D // seq, seq * group // CH
    rows = inputs[0].astype(jnp.float32)
    ends = jnp.cumsum(lengths[0]).astype(jnp.int32)
    place = jnp.concatenate([ends, lax.axis_index("seq")[None] * group]).astype(jnp.int32)
    first_hat, first_scale = normalize(rows)
    hats = to_channels(first_hat)

    def feed_forward(outs):
        response = lax.all_to_all(outs.reshape(seq, -1, nch, CH), "seq", 0, 0).reshape(-1, CH)
        return mlp_kernel(place, streams, ids, boxes, response, inputs[0], cotangent[0], share, devices, seq)

    if direct():
        few, many = read_modes(scatter_modes(master))
    else:
        lead = jnp.concatenate([lax.dynamic_slice(boxes[0][j * box.shape[0]:(j + 1) * box.shape[0]].reshape(-1), (j * share % TILE,), (share,)) for j in range(MODE_TILES * TILE // share + 1)])
        mine = lambda v: lax.dynamic_slice_in_dim(v, lax.axis_index("seq") * nch, nch, 1)
        few = mine(lead[:4 * D].reshape(4, D))
        many = mine(lead[4 * D:MODE_TILES * TILE].reshape(4, D, NSTATE))
    modes, modes_pull = jax.vjp(mixing, few[2], many[0], many[1], many[2], many[3])
    prm = mode_rows(*modes, few[0], few[1], few[3])
    outs, prior = ssm_forward(ends, prm, hats, nck, nch)
    output, d_mid, d_response, small, lead, *values = feed_forward(outs)
    d_outs = lax.all_to_all(d_response.reshape(seq, -1, nch, CH), "seq", 0, 0).reshape(-1, CH)
    plan, places = scatter_plan(share, devices)
    if direct():
        packed = join_cores(pack_kernel(plan, places, values, small, None, share, devices))
        d_outs, packed = lax.optimization_barrier((d_outs, packed))
    d_signals, sums = ssm_backward(ends, prm, hats, d_outs, prior, nck, nch)
    if direct():
        d_signals, sums, packed = lax.optimization_barrier((d_signals, sums, join_first(*packed)))
    d_signal = to_tokens(d_signals, group)
    norm_gain = lead[:D // CH].reshape(D)
    lane_sums = jnp.sum(sums[10:13], axis=-1)
    d_modes = modes_pull(mode_grads(sums, *modes))
    few = jnp.stack([lane_sums[1], lane_sums[2], d_modes[0], lane_sums[0]])
    many = jnp.stack(d_modes[1:])
    if not direct():

        def spread(v):
            whole = jnp.zeros((v.shape[0], D) + v.shape[2:], f32)
            return lax.dynamic_update_slice_in_dim(whole, v, lax.axis_index("seq") * nch, 1)

        lead = jnp.concatenate([spread(few).reshape(-1), spread(many).reshape(-1)]).reshape(-1, CH)
        packed = pack_kernel(plan, places, values, small, lead, share, devices)
    me = device_index()
    if direct():
        box, d_signal = lax.optimization_barrier((join_last(*packed), d_signal))
    else:
        box = lax.psum_scatter(packed[0].reshape(devices, -1, CH), AXES, scatter_dimension=0)
    d_rows = d_mid + norm_back(d_signal * norm_gain, first_hat, first_scale)
    shard = lax.dynamic_slice(box.reshape(-1), (me * share % TILE,), (share,))
    if direct():
        block = jnp.concatenate([few.reshape(1, CH), many.reshape(64, CH)])
        block = block + swap_cores(block)
        lead = gather_modes(block)
        lead = jnp.pad(lead, (0, 2 * share - lead.shape[0]))
        mark = me * share + jnp.arange(share, dtype=jnp.int32) < MODE_TILES * TILE
        squares = jnp.sum(jnp.where(mark, 0.0, shard * shard))
        squares = squares + 0.5 * jnp.sum(block * block)
        shard = jnp.where(mark, lax.dynamic_slice(lead, (jnp.minimum(me, 1) * share,), (share,)), shard)
    else:
        squares = jnp.sum(shard * shard)
    total = total_of(squares)
    grad_norm = jnp.sqrt(total)
    factor = jnp.minimum(1.0, 1.0 / (grad_norm + 1e-06))
    clipped = shard * factor
    first_new = 0.9 * first_moment + 0.1 * clipped
    second_new = 0.999 * second_moment + 0.001 * clipped * clipped
    first_hat_new = first_new / (1.0 - 0.9**10)
    second_hat_new = second_new / (1.0 - 0.999**10)
    update = -0.05 * (first_hat_new / (jnp.sqrt(second_hat_new) + 1e-08) + 0.1 * master)
    return (output[None], d_rows[None], shard, update, first_new, second_new, grad_norm)


def solution(mesh):
    placed = (
        P("batch", "seq", None),
        P("batch", "seq", None),
        P("batch", None),
        P(("seq", "batch")),
        P(("seq", "batch")),
        P(("seq", "batch")),
    )
    return jax.shard_map(
        per_device,
        mesh=mesh,
        in_specs=placed,
        out_specs=(
            P("batch", "seq", None),
            P("batch", "seq", None),
            P(("seq", "batch")),
            P(("seq", "batch")),
            P(("seq", "batch")),
            P(("seq", "batch")),
            P(),
        ),
        check_vma=False,
    )
```

```python
from functools import partial
import jax
import jax.numpy as jnp
import numpy as np
from jax import lax
from jax.experimental import pallas as pl
from jax.experimental.pallas import tpu as pltpu
from jax.sharding import PartitionSpec as P

D = 512
NSTATE = 64
CH = 128
DOCS = 4
G = 1024
FF = 2048
Z_FIRST = 0.2


norm_eps = 1e-05
root_half = 0.7071067811865476
inv_root_two_pi = 0.3989422804014327


f32 = jnp.float32
bf16 = jnp.bfloat16

def split(v):
    hi = v.astype(bf16)
    return hi, (v - hi.astype(f32)).astype(bf16)

def dot3(a, b, ca, cb):
    ah, al = a
    bh, bl = b
    lhs = jnp.concatenate([ah, ah, al], axis=ca)
    rhs = jnp.concatenate([bh, bl, bh], axis=cb)
    return lax.dot_general(lhs, rhs, (((ca,), (cb,)), ((), ())), preferred_element_type=f32)

def dot2(data, table, ct):
    hi, lo = data
    both = jnp.concatenate([hi, lo], axis=0)
    out = lax.dot_general(both, table, (((1,), (ct,)), ((), ())), preferred_element_type=f32)
    return out[:hi.shape[0]] + out[hi.shape[0]:]

def swap(v):
    return pltpu.roll(v, NSTATE, 1)

def twist(table, re, im):
    return re * table + im * swap(table)

def ladder(prm, order):
    sub = lax.broadcasted_iota(jnp.int32, (8, 2 * NSTATE), 0)
    lane = lax.broadcasted_iota(jnp.int32, (8, 2 * NSTATE), 1)
    power = sub if order == 1 else 7 - sub
    table = jnp.where(lane < NSTATE, 1.0, 0.0).astype(f32)
    for bit in range(3):
        table = jnp.where((power >> bit) & 1 == 1, twist(table, prm[2 * bit:2 * bit + 1], prm[2 * bit + 1:2 * bit + 2]), table)
    for bit in range(3, 7):
        more = twist(table, prm[2 * bit:2 * bit + 1], prm[2 * bit + 1:2 * bit + 2])
        table = jnp.concatenate([table, more] if order == 1 else [more, table], axis=0)
    return table

def toeplitz(taps):
    wide = pltpu.roll(jnp.broadcast_to(taps, (CH, CH)), 0, 1, stride=1, stride_axis=0)
    row = lax.broadcasted_iota(jnp.int32, (CH, CH), 0)
    col = lax.broadcasted_iota(jnp.int32, (CH, CH), 1)
    return jnp.where(col >= row, wide, 0.0).astype(bf16)

def label_at(ends, pos):
    total = jnp.zeros_like(pos)
    for k in range(DOCS):
        total = total + (pos >= ends[k]).astype(jnp.int32)
    return total

def make_masks(ends_ref, masks_ref, low_ref, nck):
    ends = [ends_ref[k] for k in range(DOCS)]
    row = lax.broadcasted_iota(jnp.int32, (nck, CH), 0)
    lane = lax.broadcasted_iota(jnp.int32, (nck, CH), 1)
    base = row * CH
    label = label_at(ends, base + lane)
    prev = jnp.where(base == 0, -1, label_at(ends, base - 1))
    last = label_at(ends, base + CH - 1)
    for k in range(DOCS):
        masks_ref[k] = (label == k).astype(f32)
    masks_ref[DOCS] = (label == prev).astype(f32)
    masks_ref[DOCS + 1] = (label == last).astype(f32)
    low_ref[:DOCS + 2] = masks_ref[...].astype(bf16)
    if low_ref.shape[0] > DOCS + 2:
        label = label_at(ends, base + (CH - 1 - lane))
        for k in range(DOCS):
            low_ref[DOCS + 2 + k] = (label == k).astype(f32).astype(bf16)

def keep_of(ends_ref, c):
    first = jnp.int32(0)
    second = jnp.int32(0)
    for k in range(DOCS):
        first = first + (c * CH - 1 >= ends_ref[k]).astype(jnp.int32)
        second = second + (c * CH + CH - 1 >= ends_ref[k]).astype(jnp.int32)
    return jnp.where((c > 0) & (first == second), 1.0, 0.0).astype(f32)

def masked_rows(v, low_ref):
    return [jnp.concatenate([part * low_ref[k] for k in range(DOCS)], axis=0) for part in v]

def masked(v, low_ref, k):
    return [part * low_ref[k] for part in v]

def fold_rows(v, masks_ref, nck):
    total = v[:nck] * masks_ref[0]
    for k in range(1, DOCS):
        total = total + v[k * nck:(k + 1) * nck] * masks_ref[k]
    return total

def for_channels(nch, body):
    lax.fori_loop(0, nch, lambda h, _: body(h) or 0, 0, unroll=min(nch, 16))

def fwd_body(nck, nch, apart, ends_ref, prm_ref, x_ref, y_ref, prior_ref, table_ref, down_ref, out_ref, mat_ref, masks_ref, low_ref, end_ref):
    make_masks(ends_ref, masks_ref, low_ref, nck)

    def tables(h):
        prm = prm_ref[h]
        table = ladder(prm, 1)
        table_ref[h] = table.astype(bf16)
        out_ref[h] = twist(table, prm[17:18], prm[18:19]).astype(bf16)

    def falling(h):
        down_ref[h] = ladder(prm_ref[h], -1).astype(bf16)

    def taps(h):
        wrow = jnp.broadcast_to(prm_ref[h, 16:17, :], (16, 2 * NSTATE))
        mat_ref[h] = toeplitz(dot2(split(wrow), table_ref[h], 1)[0:1])

    def local(h):
        prm = prm_ref[h, 16:24, :]
        u = x_ref[pl.ds(h, nck, stride=apart), :] * prm[3:4] + prm[4:5]
        parts = split(u)
        local = dot2(masked_rows(parts, low_ref), mat_ref[h], 0)
        y_ref[pl.ds(h, nck, stride=nch), :] = fold_rows(local, masks_ref, nck) + prm[5:6] * u
        end_ref[pl.ds(h, nck, stride=nch), :] = dot2(masked(parts, low_ref, DOCS + 1), down_ref[h], 0)

    for body in (tables, falling, taps, local):
        for_channels(nch, body)
    full_re = prm_ref[:, 14, :]
    full_im = prm_ref[:, 15, :]

    def step(c, state):
        at = pl.ds(pl.multiple_of(c * nch, 8), nch)
        prior_ref[at, :] = state
        return keep_of(ends_ref, c) * twist(state, full_re, full_im) + end_ref[at, :]

    lax.fori_loop(0, nck, step, jnp.zeros((nch, 2 * NSTATE), f32))

    def carried(h):
        prior = split(prior_ref[pl.ds(h, nck, stride=nch), :])
        y_ref[pl.ds(h, nck, stride=nch), :] += dot2(prior, out_ref[h], 1) * masks_ref[DOCS]

    for_channels(nch, carried)

def ssm_forward(ends, prm, x, nck, nch):
    vm = pl.BlockSpec(memory_space=pltpu.VMEM)
    table = jax.ShapeDtypeStruct((nch, CH, 2 * NSTATE), bf16)
    return pl.pallas_call(
        partial(fwd_body, nck, nch, x.shape[0] // nck),
        out_shape=(jax.ShapeDtypeStruct((nck * nch, CH), f32), jax.ShapeDtypeStruct((nck * nch, 2 * NSTATE), f32)) + (table,) * 4,
        in_specs=[pl.BlockSpec(memory_space=pltpu.SMEM), vm, vm],
        out_specs=(vm,) * 6,
        scratch_shapes=[
            pltpu.VMEM((DOCS + 2, nck, CH), f32),
            pltpu.VMEM((DOCS + 2, nck, CH), bf16),
            pltpu.VMEM((nck * nch, 2 * NSTATE), f32),
        ],
        cost_estimate=pl.CostEstimate(flops=int(2.0e10), bytes_accessed=3 * 2**20, transcendentals=0),
        name="state_forward",
    )(ends, prm, x)

def bwd_body(nck, nch, apart, ends_ref, prm_ref, x_ref, g_ref, prior_ref, table_ref, down_ref, out_ref, mat_ref, dx_ref, rows_ref, masks_ref, low_ref, lead_ref, adj_ref, taps_ref):
    make_masks(ends_ref, masks_ref, low_ref, nck)
    at_channel = lambda h: pl.ds(h, nck, stride=nch)

    def lead(h):
        lead_ref[at_channel(h), :] = dot2(masked(split(g_ref[at_channel(h), :]), low_ref, DOCS), out_ref[h], 0)

    for_channels(nch, lead)
    full_re = prm_ref[:, 14, :]
    full_im = prm_ref[:, 15, :]
    zero = jnp.zeros((nch, 2 * NSTATE), f32)

    def step(k, carry):
        adjoint, same, cross = carry
        c = nck - 1 - k
        at = pl.ds(pl.multiple_of(c * nch, 8), nch)
        adj_ref[at, :] = adjoint
        keep = keep_of(ends_ref, c)
        prior = prior_ref[at, :]
        same = same + keep * adjoint * prior
        cross = cross + keep * adjoint * swap(prior)
        adjoint = lead_ref[at, :] + keep * (full_re * adjoint - full_im * swap(adjoint))
        return adjoint, same, cross

    _, same, cross = lax.fori_loop(0, nck, step, (zero, zero, zero))
    rows_ref[8] = same
    rows_ref[9] = cross
    for k in range(13, 16):
        rows_ref[k] = zero
    row = lax.broadcasted_iota(jnp.int32, (CH, CH), 0)
    col = lax.broadcasted_iota(jnp.int32, (CH, CH), 1)
    flip = (row + col == CH - 1).astype(f32).astype(bf16)
    put = lambda k, h, v: rows_ref.__setitem__((k, pl.ds(h, 1), slice(None)), jnp.sum(v, axis=0, keepdims=True))

    def signal(h):
        prm = prm_ref[h, 16:24, :]
        x = x_ref[pl.ds(h, nck, stride=apart), :]
        g = g_ref[at_channel(h), :]
        du = fold_rows(dot2(masked_rows(split(g), low_ref), mat_ref[h], 1), masks_ref, nck)
        du = du + dot2(split(adj_ref[at_channel(h), :]), down_ref[h], 1) * masks_ref[DOCS + 1]
        du = du + prm[5:6] * g
        dx_ref[at_channel(h), :] = du
        put(10, h, g * (x * prm[3:4] + prm[4:5]))
        put(11, h, du * x)
        put(12, h, du)

    def taps(h):
        prm = prm_ref[h, 16:24, :]
        u = split(x_ref[pl.ds(h, nck, stride=apart), :] * prm[3:4] + prm[4:5])
        both = jnp.dot(jnp.concatenate(u, axis=0), flip, preferred_element_type=f32).astype(bf16)
        um = []
        for part in (both[:nck], both[nck:]):
            um.append(jnp.concatenate([part * low_ref[DOCS + 2 + k] for k in range(DOCS)], axis=0))
        square = dot3(um, masked_rows(split(g_ref[at_channel(h), :]), low_ref), 0, 0)
        square = jnp.where(row + col >= CH - 1, square, 0.0)
        square = pltpu.roll(square, 1, 1, stride=1, stride_axis=0)
        taps_ref[pl.ds(h, 1), :] = jnp.sum(square, axis=0, keepdims=True)

    def kernel(h):
        place = lax.broadcasted_iota(jnp.int32, (16, CH), 1).astype(f32)
        sub = lax.broadcasted_iota(jnp.int32, (16, CH), 0)
        both = jnp.where(sub == 0, 1.0, jnp.where(sub == 1, place, 0.0)) * taps_ref[pl.ds(h, 1), :]
        both = dot2(split(both), table_ref[h], 0)
        rows_ref[0, pl.ds(h, 1), :] = both[0:1]
        rows_ref[1, pl.ds(h, 1), :] = both[1:2]

    late = row.astype(f32)

    def carried(h):
        dgt = dot3(masked(split(g_ref[at_channel(h), :]), low_ref, DOCS), split(prior_ref[at_channel(h), :]), 0, 0)
        table = table_ref[h].astype(f32)
        same, cross = dgt * table, dgt * swap(table)
        put(2, h, same)
        put(3, h, cross)
        put(4, h, same * late)
        put(5, h, cross * late)

    def ending(h):
        prm = prm_ref[h, 16:24, :]
        u = split(x_ref[pl.ds(h, nck, stride=apart), :] * prm[3:4] + prm[4:5])
        ddown = dot3(masked(u, low_ref, DOCS + 1), split(adj_ref[at_channel(h), :]), 0, 0) * ((CH - 1) - late)
        down = down_ref[h].astype(f32)
        put(6, h, ddown * down)
        put(7, h, ddown * swap(down))

    for body in (signal, taps, kernel, carried, ending):
        for_channels(nch, body)

def ssm_backward(ends, prm, x, g, prior, tables, nck, nch):
    vm = pl.BlockSpec(memory_space=pltpu.VMEM)
    return pl.pallas_call(
        partial(bwd_body, nck, nch, x.shape[0] // nck),
        out_shape=(jax.ShapeDtypeStruct((nck * nch, CH), f32), jax.ShapeDtypeStruct((16, nch, 2 * NSTATE), f32)),
        in_specs=[pl.BlockSpec(memory_space=pltpu.SMEM)] + [vm] * 8,
        out_specs=(vm, vm),
        scratch_shapes=[
            pltpu.VMEM((DOCS + 2, nck, CH), f32),
            pltpu.VMEM((2 * DOCS + 2, nck, CH), bf16),
            pltpu.VMEM((nck * nch, 2 * NSTATE), f32),
            pltpu.VMEM((nck * nch, 2 * NSTATE), f32),
            pltpu.VMEM((nch, CH), f32),
        ],
        cost_estimate=pl.CostEstimate(flops=int(3.5e10), bytes_accessed=4 * 2**20, transcendentals=0),
        name="state_backward",
    )(ends, prm, x, g, prior, *tables)

def mixing(step_log, decay_log, frequency, out_real, out_imag):
    delta = jnp.exp(step_log)[:, None]
    rate_re = -jnp.exp(decay_log)
    arg_re, arg_im = delta * rate_re, delta * frequency
    magnitude = jnp.exp(arg_re)
    pole_re = magnitude * jnp.cos(arg_im) - 1.0
    pole_im = magnitude * jnp.sin(arg_im)
    denom = rate_re * rate_re + frequency * frequency
    ratio_re = (pole_re * rate_re + pole_im * frequency) / denom
    ratio_im = (pole_im * rate_re - pole_re * frequency) / denom
    mix_re = out_real * ratio_re - out_imag * ratio_im
    mix_im = out_real * ratio_im + out_imag * ratio_re
    return arg_re, arg_im, mix_re, mix_im

def pair(left, right):
    return jnp.concatenate([left, right], axis=-1)

def mode_rows(arg_re, arg_im, mix_re, mix_im, gain, bias, skip):
    nch = arg_re.shape[0]
    scale = jnp.asarray([2.0**b for b in range(8)], f32)[None, :, None]
    magnitude = jnp.exp(arg_re[:, None] * scale)
    p_re = magnitude * jnp.cos(arg_im[:, None] * scale)
    p_im = magnitude * jnp.sin(arg_im[:, None] * scale)
    powers = jnp.stack([pair(p_re, p_re), pair(-p_im, p_im)], axis=2).reshape(nch, 16, 2 * NSTATE)
    c_re = mix_re * p_re[:, 0] - mix_im * p_im[:, 0]
    c_im = mix_re * p_im[:, 0] + mix_im * p_re[:, 0]
    flat = lambda v: jnp.broadcast_to(v[:, None], (nch, 2 * NSTATE))
    rest = jnp.stack([pair(mix_re, -mix_im), pair(c_re, -c_re), pair(-c_im, -c_im), flat(gain), flat(bias), flat(skip), flat(0 * gain), flat(0 * gain)], axis=1)
    return jnp.concatenate([powers, rest], axis=1)

def mode_grads(rows, arg_re, arg_im, mix_re, mix_im):
    lo, hi = rows[:, :, :NSTATE], rows[:, :, NSTATE:]
    magnitude = jnp.exp(arg_re)
    p_re, p_im = magnitude * jnp.cos(arg_im), magnitude * jnp.sin(arg_im)
    magnitude = jnp.exp(arg_re * CH)
    f_re, f_im = magnitude * jnp.cos(arg_im * CH), magnitude * jnp.sin(arg_im * CH)
    a_re, a_im = lo[2] - hi[2], -(hi[3] + lo[3])
    b_re, b_im = lo[4] - hi[4], -(hi[5] + lo[5])
    b_re, b_im = b_re + a_re, b_im + a_im
    w_re = lo[0] + p_re * a_re + p_im * a_im
    w_im = -hi[0] + p_re * a_im - p_im * a_re
    v_re = lo[1] + p_re * b_re + p_im * b_im
    v_im = -hi[1] + p_re * b_im - p_im * b_re
    g_re = mix_re * v_re + mix_im * v_im
    g_im = mix_re * v_im - mix_im * v_re
    g_re = g_re + lo[6] + hi[6]
    g_im = g_im + hi[7] - lo[7]
    d_re, d_im = lo[8] + hi[8], hi[9] - lo[9]
    g_re = g_re + CH * (f_re * d_re + f_im * d_im)
    g_im = g_im + CH * (f_re * d_im - f_im * d_re)
    return g_re, g_im, w_re, w_im


def gelu(values):
    return 0.5 * values * (1.0 + lax.erf(values * root_half))


def gelu_slope(values):
    return (
        0.5 * (1.0 + lax.erf(values * root_half))
        + values * jnp.exp(-0.5 * values * values) * inv_root_two_pi
    )


def normalize(values):
    center = values - jnp.mean(values, axis=-1, keepdims=True)
    scale = lax.rsqrt(jnp.mean(center * center, axis=-1, keepdims=True) + norm_eps)
    return (center * scale, scale)


def norm_back(d_hat, hat, scale):
    return scale * (
        d_hat
        - jnp.mean(d_hat, axis=-1, keepdims=True)
        - hat * jnp.mean(d_hat * hat, axis=-1, keepdims=True)
    )


TILE = 1024
GATE_AT, EXPAND_AT, REDUCE_AT = 130, 644, 1670
SMALL_AT = (642, 643, 1668, 1669, 2694)
MODE_TILES = 130
BLOCK = 512


def lay(share, devices):
    base = share // TILE
    return base, base + 2, (devices - 1) * share // TILE + base + 2


def product(a, b, ca, cb):
    return lax.dot_general(a, b, (((ca,), (cb,)), ((), ())), preferred_element_type=f32)


def narrow(flat, out, first, rows, per):
    def one(i, _):
        for k in range(per):
            v = flat[pl.ds(first * 8 + i * 16 * per + k, 16, stride=per), :]
            out[pl.ds(pl.multiple_of(i * 16, 16), 16), k * CH:(k + 1) * CH] = v.astype(bf16)
        return 0

    lax.fori_loop(0, rows // 16, one, 0, unroll=max(1, 16 // per))


def small_row(flat, tile, begin, count):
    return jnp.concatenate([flat[tile * 8 + (begin + k) // CH:tile * 8 + (begin + k) // CH + 1, :] for k in range(0, count, CH)], axis=1)


def put_small(small_ref, begin, row):
    for k in range(row.shape[1] // CH):
        small_ref[begin // CH + k:begin // CH + k + 1, :] = row[:, k * CH:(k + 1) * CH]


def column_sum(v):
    return jnp.sum(v, axis=0, keepdims=True)


def mlp_body(share, devices, nseq, streams, place_ref, ids, *refs):
    boxes = refs[:len(streams)]
    resp_ref, x_ref, cot_ref, out_ref, dmid_ref, dresp_ref, small_ref, lead_ref, hidden_ref, active_ref, normed_ref, back_ref, dopen_ref, dlift_ref, flat, side, gate, expand, reduce, acc, dnorm, sems = refs[len(streams):]
    base, box, _ = lay(share, devices)
    nch = D // nseq
    group = x_ref.shape[0]
    start_of = lambda j: (j * share) // TILE
    inside = 0
    for k, (first, last, off, count) in enumerate(streams):
        lo, hi = max(first, 1), min(last, base)

        def copy_box(i, _, k=k, first=first, last=last, lo=lo, hi=hi, off=off):
            j = ids[off + i]
            begin = (i * (last - first) - first) * 8
            for s, tile in enumerate((0, base, base + 1)):
                if first <= tile < last:
                    pltpu.make_async_copy(boxes[k].at[pl.ds(pl.multiple_of(begin + tile * 8, 8), 8), :], side.at[s, pl.ds(pl.multiple_of(j * 8, 8), 8), :], sems.at[1]).start()
            pltpu.make_async_copy(
                boxes[k].at[pl.ds(pl.multiple_of(begin + lo * 8, 8), (hi - lo) * 8), :],
                flat.at[pl.ds(pl.multiple_of((start_of(j) + lo) * 8, 8), (hi - lo) * 8), :],
                sems.at[0],
            ).start()
            return 0

        lax.fori_loop(0, count, copy_box, 0)
        inside += (hi - lo) * count
    parts = group // CH
    turned = [
        jnp.concatenate([resp_ref[pl.ds((d * parts + k) * nch, nch), :] for d in range(nseq)], axis=0).T
        for k in range(parts)
    ]
    response = jnp.concatenate(turned, axis=0)
    hidden_ref[...] = gelu(response).astype(bf16)
    pos = place_ref[DOCS] + lax.broadcasted_iota(jnp.int32, (group, D), 0)
    total = jnp.zeros((group, D), jnp.int32)
    for k in range(DOCS):
        total = total + (pos >= place_ref[k]).astype(jnp.int32)
    back = jnp.where(total < DOCS - 1, cot_ref[...].astype(f32), 0.0)
    back_ref[...] = back.astype(bf16)
    put_small(small_ref, 2 * G + FF, column_sum(back))
    small_ref[36:40, :] = jnp.zeros((4, CH), f32)
    inner = side.at[:, pl.ds(0, devices * 8), :]
    pltpu.make_async_copy(inner, inner, sems.at[1]).wait()
    side[0, devices * 8:, :] = jnp.zeros((8, CH), f32)
    flat[:8, :] = side[0, :8, :]

    def join(j, _):
        at = start_of(j)
        step = start_of(j + 1) - at
        far = jnp.broadcast_to(step, (8, CH)) > base
        here = pl.ds(pl.multiple_of(j * 8, 8), 8)
        one, two, then = side[1, here, :], side[2, here, :], side[0, pl.ds(pl.multiple_of(j * 8 + 8, 8), 8), :]
        flat[pl.ds(pl.multiple_of((at + base) * 8, 8), 8), :] = one + jnp.where(far, 0.0, then)
        flat[pl.ds(pl.multiple_of((at + step) * 8, 8), 8), :] = jnp.where(far, two, one) + then
        return 0

    lax.fori_loop(0, devices, join, 0)

    some = flat.at[pl.ds(0, inside * 8), :]
    pltpu.make_async_copy(some, some, sems.at[0]).wait()
    lead_ref[...] = flat[:MODE_TILES * 8, :]
    narrow(flat, gate, GATE_AT, D, G // CH)
    gate_bias = small_row(flat, SMALL_AT[0], 0, G)
    second_gain = small_row(flat, SMALL_AT[1], 0, D)
    second_bias = small_row(flat, SMALL_AT[1], D, D)
    hidden = hidden_ref[...]
    linear = product(hidden, gate[:, :D], 1, 0) + gate_bias[:, :D]
    gating = jax.nn.sigmoid(product(hidden, gate[:, D:], 1, 0) + gate_bias[:, D:])
    mid = x_ref[...].astype(f32) + linear * gating
    hat, scale = normalize(mid)
    normed_ref[...] = (hat * second_gain + second_bias).astype(bf16)
    narrow(flat, expand, EXPAND_AT, D, FF // CH)
    narrow(flat, reduce, REDUCE_AT, FF, D // CH)
    dnorm[...] = jnp.zeros((group, D), f32)
    acc[...] = mid + small_row(flat, SMALL_AT[4], 0, D)
    for b in range(FF // BLOCK):
        at = slice(b * BLOCK, (b + 1) * BLOCK)
        bias = small_row(flat, SMALL_AT[2] + b * BLOCK // TILE, b * BLOCK % TILE, BLOCK)
        lifted = product(normed_ref[...], expand[:, at], 1, 0) + bias
        half = 0.5 * (1.0 + lax.erf(lifted * root_half))
        active = (lifted * half).astype(bf16)
        active_ref[:, at] = active
        slope = half + lifted * jnp.exp(-0.5 * lifted * lifted) * inv_root_two_pi
        d_lifted = (product(back_ref[...], reduce[at, :], 1, 1) * slope).astype(bf16)
        dlift_ref[:, at] = d_lifted
        put_small(small_ref, 2 * G + b * BLOCK, column_sum(d_lifted.astype(f32)))
        acc[...] += product(active, reduce[at, :], 1, 0)
        dnorm[...] += product(d_lifted, expand[:, at], 1, 1)
    out_ref[...] = acc[...].astype(bf16)
    d_normed = dnorm[...]
    put_small(small_ref, G, column_sum(d_normed * hat))
    put_small(small_ref, G + D, column_sum(d_normed))
    d_mid = back_ref[...].astype(f32) + norm_back(d_normed * second_gain, hat, scale)
    dmid_ref[...] = d_mid
    d_linear = (d_mid * gating).astype(bf16)
    d_gating = (d_mid * linear * gating * (1.0 - gating)).astype(bf16)
    dopen_ref[:, :D] = d_linear
    dopen_ref[:, D:] = d_gating
    put_small(small_ref, 0, column_sum(d_linear.astype(f32)))
    put_small(small_ref, D, column_sum(d_gating.astype(f32)))
    d_hidden = product(d_linear, gate[:, :D], 1, 1) + product(d_gating, gate[:, D:], 1, 1)
    for k in range(parts):
        again = jnp.concatenate([resp_ref[pl.ds((d * parts + k) * nch, nch), :] for d in range(nseq)], axis=0)
        back_turned = d_hidden[k * CH:(k + 1) * CH].T * gelu_slope(again)
        for d in range(nseq):
            dresp_ref[pl.ds((d * parts + k) * nch, nch), :] = back_turned[d * nch:(d + 1) * nch]


def mlp_kernel(place, streams, ids, boxes, response, rows, cotangent, share, devices, nseq):
    base, box, tiles = lay(share, devices)
    group = rows.shape[0]
    vm = pl.BlockSpec(memory_space=pltpu.VMEM)
    shape = lambda r, c, t: jax.ShapeDtypeStruct((r, c), t)
    return pl.pallas_call(
        partial(mlp_body, share, devices, nseq, streams),
        out_shape=(
            shape(group, D, bf16),
            shape(group, D, f32),
            jax.ShapeDtypeStruct(response.shape, f32),
            shape(len(SMALL_AT) * 8, CH, f32),
            shape(MODE_TILES * 8, CH, f32),
            shape(group, D, bf16),
            shape(group, FF, bf16),
            shape(group, D, bf16),
            shape(group, D, bf16),
            shape(group, G, bf16),
            shape(group, FF, bf16),
        ),
        in_specs=[pl.BlockSpec(memory_space=pltpu.SMEM)] * 2 + [pl.BlockSpec(memory_space=pl.ANY)] * len(boxes) + [vm] * 3,
        out_specs=(vm,) * 11,
        scratch_shapes=[
            pltpu.VMEM((tiles * 8, CH), f32),
            pltpu.VMEM((3, devices * 8 + 8, CH), f32),
            pltpu.VMEM((D, G), bf16),
            pltpu.VMEM((D, FF), bf16),
            pltpu.VMEM((FF, D), bf16),
            pltpu.VMEM((group, D), f32),
            pltpu.VMEM((group, D), f32),
            pltpu.SemaphoreType.DMA((2,)),
        ],
        cost_estimate=pl.CostEstimate(flops=int(1.0e10), bytes_accessed=20 * 2**20, transcendentals=0),
        name="feed_forward",
    )(place, ids, *boxes, response, rows, cotangent)


def pack_body(streams, tiles, has_lead, *refs):
    n = len(streams)
    dest, hidden, active, normed, back, dopen, dlift, small_ref = refs[:8]
    outs = refs[8 + has_lead:8 + has_lead + n]
    flat, sem = refs[8 + has_lead + n:]
    if has_lead:
        flat[:MODE_TILES * 8, :] = refs[8][...]
    else:
        flat[:MODE_TILES * 8, :] = jnp.zeros((MODE_TILES * 8, CH), f32)
    for k, tile in enumerate(SMALL_AT):
        flat[tile * 8:(tile + 1) * 8, :] = small_ref[k * 8:(k + 1) * 8, :]
    flat[(SMALL_AT[-1] + 1) * 8:, :] = jnp.zeros(((tiles - SMALL_AT[-1] - 1) * 8, CH), f32)
    for first, left, right, per in ((GATE_AT, hidden, dopen, G // CH), (EXPAND_AT, normed, dlift, FF // CH), (REDUCE_AT, active, back, D // CH)):
        wide = 128
        flip = left[...].T

        for k in range(left.shape[1] // wide):
            v = product(flip[k * wide:(k + 1) * wide], right[...], 1, 0)
            for c in range(per):
                flat[pl.ds(first * 8 + k * wide * per + c, wide, stride=per), :] = v[:, c * CH:(c + 1) * CH]
    for k, (first, last, order) in enumerate(streams):
        rows = (last - first) * 8

        def send(b, _, k=k, first=first, rows=rows, order=order):
            at = pl.multiple_of(dest[order + b], 8)
            pltpu.make_async_copy(flat.at[pl.ds(at + first * 8, rows), :], outs[k].at[pl.ds(pl.multiple_of(b * rows, 8), rows), :], sem.at[k]).start()
            return 0

        lax.fori_loop(0, outs[k].shape[0] // rows, send, 0)
    for k, out in enumerate(outs):
        pltpu.make_async_copy(out, out, sem.at[k]).wait()


def pack_kernel(streams, dest, values, small, lead, share, devices):
    _, _, tiles = lay(share, devices)
    hbm = pl.BlockSpec(memory_space=pl.ANY)
    vm = pl.BlockSpec(memory_space=pltpu.VMEM)
    has = int(lead is not None)
    return pl.pallas_call(
        partial(pack_body, tuple(s[:3] for s in streams), tiles, has),
        out_shape=tuple(jax.ShapeDtypeStruct((blocks * (last - first) * 8, CH), f32) for first, last, _, blocks in streams),
        in_specs=[pl.BlockSpec(memory_space=pltpu.SMEM)] + [vm] * (7 + has),
        out_specs=(hbm,) * len(streams),
        scratch_shapes=[pltpu.VMEM((tiles * 8, CH), f32), pltpu.SemaphoreType.DMA((len(streams),))],
        cost_estimate=pl.CostEstimate(flops=int(0.8e10), bytes_accessed=16 * 2**20, transcendentals=0),
        name="weight_gradients",
    )(dest, *values, small, *((lead,) if has else ()))


AXES = ("seq", "batch")
PAIR = [(0, 1), (1, 0)]


def hop(v, step):
    return lax.ppermute(v, "seq", [(i, i ^ step) for i in range(16)])


def swap_cores(v):
    return lax.ppermute(v, "batch", PAIR)


def direct():
    return lax.axis_size("seq") == 16 and lax.axis_size("batch") == 2


def device_index():
    return lax.axis_index("seq") * lax.axis_size("batch") + lax.axis_index("batch")


def places_of(steps, other):
    seq, batch = lax.axis_index("seq"), lax.axis_index("batch")
    return 2 * (seq ^ np.asarray(steps, np.int32)) + (batch ^ other)


def cuts_of(tiles):
    one = round(tiles * (1.0 - Z_FIRST) / 2)
    return one, 2 * one


def container(master, share, devices):
    _, tiles, _ = lay(share, devices)
    box = lax.dynamic_update_slice(jnp.zeros((tiles * TILE,), f32), master, (device_index() * share % TILE,))
    return box.reshape(tiles * 8, CH)


def gather_near(box):
    half = box.shape[0] // 16 * 8
    sets = [box] + [hop(box, step) for step in (4, 8, 12)]
    return [jnp.concatenate([v[at] for v in sets]) for at in (slice(0, half), slice(half, None))]


def gather_plane(near):
    return [jnp.concatenate([near[0], hop(near[0], 1)]), jnp.concatenate([near[1], hop(near[1], 2)])]


def gather_cores(plane, far, tiles):
    half = tiles // 2
    arrays, streams, ids = [], [], []
    for v, first, second in ((plane[0], 0, 1), (plane[1], 0, 2), (far[0], 2, 3), (far[1], 1, 3)):
        for other in range(2):
            arrays.append(swap_cores(v) if other else v)
            streams.append(((0, half) if len(arrays) % 4 in (1, 2) else (half, tiles)) + (8 * len(ids), 8))
            ids.append(places_of([4 * z + p for p in (first, second) for z in range(4)], other))
    return tuple(streams), jnp.concatenate(ids).astype(jnp.int32), arrays


def scatter_plan(share, devices):
    _, tiles, _ = lay(share, devices)
    if not direct():
        return ((0, tiles, 0, devices),), jnp.arange(devices, dtype=jnp.int32) * share // TILE * 8
    one, two = cuts_of(tiles)
    streams, ids = [], []
    for first, last, bits in ((0, one, (1, 2, 8, 4)), (one, two, (2, 1, 8, 4)), (two, tiles, (8, 4, 2, 1))):
        steps = [0]
        for bit in bits[::-1]:
            steps = steps + [bit + step for step in steps]
        for other in range(2):
            streams.append((first, last, 16 * len(ids), 16))
            ids.append(places_of(steps, other))
    return tuple(streams), (jnp.concatenate(ids) * share // TILE * 8).astype(jnp.int32)


def pieces(v, count):
    return v.reshape(count, -1, CH)


def halve(two, step):
    return pieces(two[0] + hop(two[1], step), 2)


def join_cores(arrays):
    sums = []
    for own, far in zip(arrays[::2], arrays[1::2]):
        own, far = pieces(own, 2), pieces(swap_cores(far), 2)
        sums.append([own[k] + far[k] for k in range(2)])
    return sums


def join_first(sums):
    return [halve(v, step) for v, step in zip(sums, (1, 2, 8))]


def join_second(sums):
    return [halve(v, step) for v, step in zip(sums, (2, 1, 4))]


def join_last(sums):
    rows = [pieces(v.reshape(-1, CH), 4) for v in sums[:2]]
    four = [jnp.concatenate([v[k] for v in rows]) for k in range(4)]
    near = halve(sums[2], 2)
    one = four[0] + hop(four[1], 4) + hop(four[2], 8) + hop(four[3], 12)
    return jnp.concatenate([one, near[0] + hop(near[1], 1)])


MODE_ROWS = 65


def scatter_modes(master):
    other = swap_cores(master)
    even = lax.axis_index("batch") == 0
    lead = jnp.concatenate([jnp.where(even, master, other), jnp.where(even, other, master)])[:MODE_TILES * TILE]
    small = lead[:4 * D].reshape(4, 16, 32).transpose(1, 0, 2).reshape(16, 1, CH)
    rest = lead[4 * D:].reshape(4, 16, 16, CH).transpose(1, 0, 2, 3).reshape(16, 64, CH)
    blocks = jnp.concatenate([small, rest], axis=1)
    seq = lax.axis_index("seq")
    blocks = blocks.reshape(2, 2, 2, 2, MODE_ROWS, CH).transpose(3, 2, 1, 0, 4, 5)
    for step in (1, 2, 4, 8):
        come = lax.ppermute(blocks[1], "seq", [(i, i + step) for i in range(step)])
        blocks = jnp.where(seq & step == 0, blocks[0], come)
    return blocks


def read_modes(block):
    nch = D // 16
    small = block[0].reshape(4, nch)
    rest = block[1:].reshape(4, nch, NSTATE)
    return small, rest


def gather_modes(block, steps):
    for step in steps:
        pairs = [(i, i - step) for i in range(2 * step) if i >= step]
        block = jnp.concatenate([block, lax.ppermute(block, "seq", pairs)])
    return block


def mode_vector(block):
    blocks = block.reshape(2, 2, 2, 2, MODE_ROWS, CH).transpose(3, 2, 1, 0, 4, 5).reshape(16, MODE_ROWS, CH)
    lead = blocks[:, 0].reshape(16, 4, 32).transpose(1, 0, 2).reshape(-1)
    tail = blocks[:, 1:].reshape(16, 4, 16, CH).transpose(1, 0, 2, 3).reshape(-1)
    return jnp.concatenate([lead, tail])


def total_of(v):
    if not direct():
        return lax.psum(v, AXES)
    v = jnp.broadcast_to(v, (8, CH))
    v = v + swap_cores(v)
    v = v + (hop(v, 1) + hop(v, 2) + hop(v, 3))
    v = v + (hop(v, 4) + hop(v, 8) + hop(v, 12))
    return v[0, 0]


def to_channels(rows):
    seq = lax.axis_size("seq")
    parts = rows.shape[0] // CH
    turned = rows.reshape(parts, CH, seq, D // seq).transpose(2, 0, 3, 1)
    return lax.all_to_all(turned, "seq", 0, 0).reshape(-1, CH)


def to_tokens(rows, group):
    seq = lax.axis_size("seq")
    turned = lax.all_to_all(rows.reshape(seq, group // CH, D // seq, CH), "seq", 0, 0)
    return turned.transpose(1, 3, 0, 2).reshape(group, D)


def per_device(inputs, cotangent, lengths, master, first_moment, second_moment):
    seq, batch = lax.axis_size("seq"), lax.axis_size("batch")
    devices = seq * batch
    share = master.shape[0]
    box = container(master, share, devices)
    if direct():
        near = gather_near(box)
    else:
        streams, ids = ((0, box.shape[0] // 8, 0, devices),), jnp.arange(devices, dtype=jnp.int32)
        boxes = [lax.all_gather(box, AXES, axis=0, tiled=True)]
    group = inputs.shape[1]
    nch, nck = D // seq, seq * group // CH
    rows = inputs[0].astype(jnp.float32)
    ends = jnp.cumsum(lengths[0]).astype(jnp.int32)
    place = jnp.concatenate([ends, lax.axis_index("seq")[None] * group]).astype(jnp.int32)
    first_hat, first_scale = normalize(rows)
    hats = to_channels(first_hat)

    def feed_forward(response):
        return mlp_kernel(place, streams, ids, boxes, response, inputs[0], cotangent[0], share, devices, seq)

    if direct():
        few, many = read_modes(scatter_modes(master))
    else:
        lead = jnp.concatenate([lax.dynamic_slice(boxes[0][j * box.shape[0]:(j + 1) * box.shape[0]].reshape(-1), (j * share % TILE,), (share,)) for j in range(MODE_TILES * TILE // share + 1)])
        mine = lambda v: lax.dynamic_slice_in_dim(v, lax.axis_index("seq") * nch, nch, 1)
        few = mine(lead[:4 * D].reshape(4, D))
        many = mine(lead[4 * D:MODE_TILES * TILE].reshape(4, D, NSTATE))
    if direct():
        plane = gather_plane(near)
    modes, modes_pull = jax.vjp(mixing, few[2], many[0], many[1], many[2], many[3])
    prm = mode_rows(*modes, few[0], few[1], few[3])
    outs, prior, *tables = ssm_forward(ends, prm, hats, nck, nch)
    if direct():
        outs, plane = lax.optimization_barrier((outs, plane))
    response = lax.all_to_all(outs.reshape(seq, -1, nch, CH), "seq", 0, 0).reshape(-1, CH)
    if direct():
        far = [hop(plane[0], 2), hop(plane[1], 1)]
        response, far = lax.optimization_barrier((response, far))
        streams, ids, boxes = gather_cores(plane, far, box.shape[0] // 8)
    output, d_mid, d_response, small, lead, *values = feed_forward(response)
    d_outs = lax.all_to_all(d_response.reshape(seq, -1, nch, CH), "seq", 0, 0).reshape(-1, CH)
    plan, places = scatter_plan(share, devices)
    if direct():
        packed = join_cores(pack_kernel(plan, places, values, small, None, share, devices))
        d_outs, packed = lax.optimization_barrier((d_outs, packed))
    d_signals, sums = ssm_backward(ends, prm, hats, d_outs, prior, tables, nck, nch)
    if direct():
        d_signals, sums, packed = lax.optimization_barrier((d_signals, sums, join_first(packed)))
    d_signal = to_tokens(d_signals, group)
    norm_gain = lead[:D // CH].reshape(D)
    lane_sums = jnp.sum(sums[10:13], axis=-1)
    d_modes = modes_pull(mode_grads(sums, *modes))
    few = jnp.stack([lane_sums[1], lane_sums[2], d_modes[0], lane_sums[0]])
    many = jnp.stack(d_modes[1:])
    if not direct():

        def spread(v):
            whole = jnp.zeros((v.shape[0], D) + v.shape[2:], f32)
            return lax.dynamic_update_slice_in_dim(whole, v, lax.axis_index("seq") * nch, 1)

        lead = jnp.concatenate([spread(few).reshape(-1), spread(many).reshape(-1)]).reshape(-1, CH)
        packed = pack_kernel(plan, places, values, small, lead, share, devices)
    me = device_index()
    if direct():
        own = jnp.concatenate([few.reshape(1, CH), many.reshape(64, CH)])
        own, packed = lax.optimization_barrier((own + swap_cores(own), join_second(packed)))
        box, block, d_signal = lax.optimization_barrier((join_last(packed), gather_modes(own, (8, 4)), d_signal))
    else:
        box = lax.psum_scatter(packed[0].reshape(devices, -1, CH), AXES, scatter_dimension=0)
    d_rows = d_mid + norm_back(d_signal * norm_gain, first_hat, first_scale)
    shard = lax.dynamic_slice(box.reshape(-1), (me * share % TILE,), (share,))
    if direct():
        lead = mode_vector(gather_modes(block, (2, 1)))
        lead = jnp.pad(lead, (0, 2 * share - lead.shape[0]))
        mark = me * share + jnp.arange(share, dtype=jnp.int32) < MODE_TILES * TILE
        squares = jnp.sum(jnp.where(mark, 0.0, shard * shard))
        squares = squares + 0.5 * jnp.sum(own * own)
        shard = jnp.where(mark, lax.dynamic_slice(lead, (jnp.minimum(me, 1) * share,), (share,)), shard)
    else:
        squares = jnp.sum(shard * shard)
    total = total_of(squares)
    grad_norm = jnp.sqrt(total)
    factor = jnp.minimum(1.0, 1.0 / (grad_norm + 1e-06))
    clipped = shard * factor
    first_new = 0.9 * first_moment + 0.1 * clipped
    second_new = 0.999 * second_moment + 0.001 * clipped * clipped
    first_hat_new = first_new / (1.0 - 0.9**10)
    second_hat_new = second_new / (1.0 - 0.999**10)
    update = -0.05 * (first_hat_new / (jnp.sqrt(second_hat_new) + 1e-08) + 0.1 * master)
    return (output[None], d_rows[None], shard, update, first_new, second_new, grad_norm)


def solution(mesh):
    placed = (
        P("batch", "seq", None),
        P("batch", "seq", None),
        P("batch", None),
        P(("seq", "batch")),
        P(("seq", "batch")),
        P(("seq", "batch")),
    )
    return jax.shard_map(
        per_device,
        mesh=mesh,
        in_specs=placed,
        out_specs=(
            P("batch", "seq", None),
            P("batch", "seq", None),
            P(("seq", "batch")),
            P(("seq", "batch")),
            P(("seq", "batch")),
            P(("seq", "batch")),
            P(),
        ),
        check_vma=False,
    )
```

```python
from functools import partial
import jax
import jax.numpy as jnp
import numpy as np
from jax import lax
from jax.experimental import pallas as pl
from jax.experimental.pallas import tpu as pltpu
from jax.sharding import PartitionSpec as P

D = 512
NSTATE = 64
CH = 128
DOCS = 4
G = 1024
FF = 2048
Z_FIRST = 0.2


norm_eps = 1e-05
root_half = 0.7071067811865476
inv_root_two_pi = 0.3989422804014327


f32 = jnp.float32
bf16 = jnp.bfloat16

def split(v):
    hi = v.astype(bf16)
    return hi, (v - hi.astype(f32)).astype(bf16)

def dot3(a, b, ca, cb):
    ah, al = a
    bh, bl = b
    lhs = jnp.concatenate([ah, ah, al], axis=ca)
    rhs = jnp.concatenate([bh, bl, bh], axis=cb)
    return lax.dot_general(lhs, rhs, (((ca,), (cb,)), ((), ())), preferred_element_type=f32)

def dot2(data, table, ct):
    return dot3(data, (table[0], table[1]), 1, ct)

def swap(v):
    return pltpu.roll(v, NSTATE, 1)

def twist(table, re, im):
    return re * table + im * swap(table)

def ladder(prm, order):
    sub = lax.broadcasted_iota(jnp.int32, (8, 2 * NSTATE), 0)
    lane = lax.broadcasted_iota(jnp.int32, (8, 2 * NSTATE), 1)
    power = sub if order == 1 else 7 - sub
    table = jnp.where(lane < NSTATE, 1.0, 0.0).astype(f32)
    for bit in range(3):
        table = jnp.where((power >> bit) & 1 == 1, twist(table, prm[2 * bit:2 * bit + 1], prm[2 * bit + 1:2 * bit + 2]), table)
    for bit in range(3, 7):
        more = twist(table, prm[2 * bit:2 * bit + 1], prm[2 * bit + 1:2 * bit + 2])
        table = jnp.concatenate([table, more] if order == 1 else [more, table], axis=0)
    return table

def toeplitz(taps):
    wide = pltpu.roll(jnp.broadcast_to(taps, (CH, CH)), 0, 1, stride=1, stride_axis=0)
    row = lax.broadcasted_iota(jnp.int32, (CH, CH), 0)
    col = lax.broadcasted_iota(jnp.int32, (CH, CH), 1)
    return jnp.where(col >= row, wide, 0.0)

def label_at(ends, pos):
    total = jnp.zeros_like(pos)
    for k in range(DOCS):
        total = total + (pos >= ends[k]).astype(jnp.int32)
    return total

def make_masks(ends_ref, masks_ref, low_ref, nck):
    ends = [ends_ref[k] for k in range(DOCS)]
    row = lax.broadcasted_iota(jnp.int32, (nck, CH), 0)
    lane = lax.broadcasted_iota(jnp.int32, (nck, CH), 1)
    base = row * CH
    label = label_at(ends, base + lane)
    prev = jnp.where(base == 0, -1, label_at(ends, base - 1))
    last = label_at(ends, base + CH - 1)
    for k in range(DOCS):
        masks_ref[k] = (label == k).astype(f32)
    masks_ref[DOCS] = (label == prev).astype(f32)
    masks_ref[DOCS + 1] = (label == last).astype(f32)
    low_ref[:DOCS + 2] = masks_ref[...].astype(bf16)
    if low_ref.shape[0] > DOCS + 2:
        label = label_at(ends, base + (CH - 1 - lane))
        for k in range(DOCS):
            low_ref[DOCS + 2 + k] = (label == k).astype(f32).astype(bf16)

def keep_of(ends_ref, c):
    first = jnp.int32(0)
    second = jnp.int32(0)
    for k in range(DOCS):
        first = first + (c * CH - 1 >= ends_ref[k]).astype(jnp.int32)
        second = second + (c * CH + CH - 1 >= ends_ref[k]).astype(jnp.int32)
    return jnp.where((c > 0) & (first == second), 1.0, 0.0).astype(f32)

def masked_rows(v, low_ref):
    return [jnp.concatenate([part * low_ref[k] for k in range(DOCS)], axis=0) for part in v]

def masked(v, low_ref, k):
    return [part * low_ref[k] for part in v]

def fold_rows(v, masks_ref, nck):
    total = v[:nck] * masks_ref[0]
    for k in range(1, DOCS):
        total = total + v[k * nck:(k + 1) * nck] * masks_ref[k]
    return total

def keep(ref, h, v):
    ref[h, 0], ref[h, 1] = split(v)

def for_channels(nch, body):
    lax.fori_loop(0, nch, lambda h, _: body(h) or 0, 0, unroll=min(nch, 16))

def fwd_body(nck, nch, apart, ends_ref, prm_ref, x_ref, y_ref, prior_ref, table_ref, down_ref, out_ref, mat_ref, masks_ref, low_ref, end_ref):
    make_masks(ends_ref, masks_ref, low_ref, nck)

    def tables(h):
        prm = prm_ref[h]
        table = ladder(prm, 1)
        keep(table_ref, h, table)
        keep(out_ref, h, twist(table, prm[17:18], prm[18:19]))

    def falling(h):
        keep(down_ref, h, ladder(prm_ref[h], -1))

    def taps(h):
        wrow = jnp.broadcast_to(prm_ref[h, 16:17, :], (16, 2 * NSTATE))
        keep(mat_ref, h, toeplitz(dot2(split(wrow), table_ref[h], 1)[0:1]))

    def local(h):
        prm = prm_ref[h, 16:24, :]
        u = x_ref[pl.ds(h, nck, stride=apart), :] * prm[3:4] + prm[4:5]
        parts = split(u)
        local = dot2(masked_rows(parts, low_ref), mat_ref[h], 0)
        y_ref[pl.ds(h, nck, stride=nch), :] = fold_rows(local, masks_ref, nck) + prm[5:6] * u
        end_ref[pl.ds(h, nck, stride=nch), :] = dot2(masked(parts, low_ref, DOCS + 1), down_ref[h], 0)

    for body in (tables, falling, taps, local):
        for_channels(nch, body)
    full_re = prm_ref[:, 14, :]
    full_im = prm_ref[:, 15, :]

    def step(c, state):
        at = pl.ds(pl.multiple_of(c * nch, 8), nch)
        prior_ref[at, :] = state
        return keep_of(ends_ref, c) * twist(state, full_re, full_im) + end_ref[at, :]

    lax.fori_loop(0, nck, step, jnp.zeros((nch, 2 * NSTATE), f32))

    def carried(h):
        prior = split(prior_ref[pl.ds(h, nck, stride=nch), :])
        y_ref[pl.ds(h, nck, stride=nch), :] += dot2(prior, out_ref[h], 1) * masks_ref[DOCS]

    for_channels(nch, carried)

def ssm_forward(ends, prm, x, nck, nch):
    vm = pl.BlockSpec(memory_space=pltpu.VMEM)
    table = jax.ShapeDtypeStruct((nch, 2, CH, 2 * NSTATE), bf16)
    return pl.pallas_call(
        partial(fwd_body, nck, nch, x.shape[0] // nck),
        out_shape=(jax.ShapeDtypeStruct((nck * nch, CH), f32), jax.ShapeDtypeStruct((nck * nch, 2 * NSTATE), f32)) + (table,) * 4,
        in_specs=[pl.BlockSpec(memory_space=pltpu.SMEM), vm, vm],
        out_specs=(vm,) * 6,
        scratch_shapes=[
            pltpu.VMEM((DOCS + 2, nck, CH), f32),
            pltpu.VMEM((DOCS + 2, nck, CH), bf16),
            pltpu.VMEM((nck * nch, 2 * NSTATE), f32),
        ],
        cost_estimate=pl.CostEstimate(flops=int(2.0e10), bytes_accessed=3 * 2**20, transcendentals=0),
        name="state_forward",
    )(ends, prm, x)

def bwd_body(nck, nch, apart, ends_ref, prm_ref, x_ref, g_ref, prior_ref, table_ref, down_ref, out_ref, mat_ref, dx_ref, rows_ref, masks_ref, low_ref, lead_ref, adj_ref, taps_ref):
    make_masks(ends_ref, masks_ref, low_ref, nck)
    at_channel = lambda h: pl.ds(h, nck, stride=nch)

    def lead(h):
        lead_ref[at_channel(h), :] = dot2(masked(split(g_ref[at_channel(h), :]), low_ref, DOCS), out_ref[h], 0)

    for_channels(nch, lead)
    full_re = prm_ref[:, 14, :]
    full_im = prm_ref[:, 15, :]
    zero = jnp.zeros((nch, 2 * NSTATE), f32)

    def step(k, carry):
        adjoint, same, cross = carry
        c = nck - 1 - k
        at = pl.ds(pl.multiple_of(c * nch, 8), nch)
        adj_ref[at, :] = adjoint
        keep = keep_of(ends_ref, c)
        prior = prior_ref[at, :]
        same = same + keep * adjoint * prior
        cross = cross + keep * adjoint * swap(prior)
        adjoint = lead_ref[at, :] + keep * (full_re * adjoint - full_im * swap(adjoint))
        return adjoint, same, cross

    _, same, cross = lax.fori_loop(0, nck, step, (zero, zero, zero))
    rows_ref[8] = same
    rows_ref[9] = cross
    for k in range(13, 16):
        rows_ref[k] = zero
    row = lax.broadcasted_iota(jnp.int32, (CH, CH), 0)
    col = lax.broadcasted_iota(jnp.int32, (CH, CH), 1)
    flip = (row + col == CH - 1).astype(f32).astype(bf16)
    put = lambda k, h, v: rows_ref.__setitem__((k, pl.ds(h, 1), slice(None)), jnp.sum(v, axis=0, keepdims=True))

    def signal(h):
        prm = prm_ref[h, 16:24, :]
        x = x_ref[pl.ds(h, nck, stride=apart), :]
        g = g_ref[at_channel(h), :]
        du = fold_rows(dot2(masked_rows(split(g), low_ref), mat_ref[h], 1), masks_ref, nck)
        du = du + dot2(split(adj_ref[at_channel(h), :]), down_ref[h], 1) * masks_ref[DOCS + 1]
        du = du + prm[5:6] * g
        dx_ref[at_channel(h), :] = du
        put(10, h, g * (x * prm[3:4] + prm[4:5]))
        put(11, h, du * x)
        put(12, h, du)

    def taps(h):
        prm = prm_ref[h, 16:24, :]
        u = split(x_ref[pl.ds(h, nck, stride=apart), :] * prm[3:4] + prm[4:5])
        both = jnp.dot(jnp.concatenate(u, axis=0), flip, preferred_element_type=f32).astype(bf16)
        um = []
        for part in (both[:nck], both[nck:]):
            um.append(jnp.concatenate([part * low_ref[DOCS + 2 + k] for k in range(DOCS)], axis=0))
        square = dot3(um, masked_rows(split(g_ref[at_channel(h), :]), low_ref), 0, 0)
        square = jnp.where(row + col >= CH - 1, square, 0.0)
        square = pltpu.roll(square, 1, 1, stride=1, stride_axis=0)
        taps_ref[pl.ds(h, 1), :] = jnp.sum(square, axis=0, keepdims=True)

    def kernel(h):
        place = lax.broadcasted_iota(jnp.int32, (16, CH), 1).astype(f32)
        sub = lax.broadcasted_iota(jnp.int32, (16, CH), 0)
        both = jnp.where(sub == 0, 1.0, jnp.where(sub == 1, place, 0.0)) * taps_ref[pl.ds(h, 1), :]
        both = dot2(split(both), table_ref[h], 0)
        rows_ref[0, pl.ds(h, 1), :] = both[0:1]
        rows_ref[1, pl.ds(h, 1), :] = both[1:2]

    late = row.astype(f32)

    def carried(h):
        dgt = dot3(masked(split(g_ref[at_channel(h), :]), low_ref, DOCS), split(prior_ref[at_channel(h), :]), 0, 0)
        table = table_ref[h, 0].astype(f32) + table_ref[h, 1].astype(f32)
        same, cross = dgt * table, dgt * swap(table)
        put(2, h, same)
        put(3, h, cross)
        put(4, h, same * late)
        put(5, h, cross * late)

    def ending(h):
        prm = prm_ref[h, 16:24, :]
        u = split(x_ref[pl.ds(h, nck, stride=apart), :] * prm[3:4] + prm[4:5])
        ddown = dot3(masked(u, low_ref, DOCS + 1), split(adj_ref[at_channel(h), :]), 0, 0) * ((CH - 1) - late)
        down = down_ref[h, 0].astype(f32) + down_ref[h, 1].astype(f32)
        put(6, h, ddown * down)
        put(7, h, ddown * swap(down))

    for body in (signal, taps, kernel, carried, ending):
        for_channels(nch, body)

def ssm_backward(ends, prm, x, g, prior, tables, nck, nch):
    vm = pl.BlockSpec(memory_space=pltpu.VMEM)
    return pl.pallas_call(
        partial(bwd_body, nck, nch, x.shape[0] // nck),
        out_shape=(jax.ShapeDtypeStruct((nck * nch, CH), f32), jax.ShapeDtypeStruct((16, nch, 2 * NSTATE), f32)),
        in_specs=[pl.BlockSpec(memory_space=pltpu.SMEM)] + [vm] * 8,
        out_specs=(vm, vm),
        scratch_shapes=[
            pltpu.VMEM((DOCS + 2, nck, CH), f32),
            pltpu.VMEM((2 * DOCS + 2, nck, CH), bf16),
            pltpu.VMEM((nck * nch, 2 * NSTATE), f32),
            pltpu.VMEM((nck * nch, 2 * NSTATE), f32),
            pltpu.VMEM((nch, CH), f32),
        ],
        cost_estimate=pl.CostEstimate(flops=int(3.5e10), bytes_accessed=4 * 2**20, transcendentals=0),
        name="state_backward",
    )(ends, prm, x, g, prior, *tables)

def mixing(step_log, decay_log, frequency, out_real, out_imag):
    delta = jnp.exp(step_log)[:, None]
    rate_re = -jnp.exp(decay_log)
    arg_re, arg_im = delta * rate_re, delta * frequency
    magnitude = jnp.exp(arg_re)
    pole_re = magnitude * jnp.cos(arg_im) - 1.0
    pole_im = magnitude * jnp.sin(arg_im)
    denom = rate_re * rate_re + frequency * frequency
    ratio_re = (pole_re * rate_re + pole_im * frequency) / denom
    ratio_im = (pole_im * rate_re - pole_re * frequency) / denom
    mix_re = out_real * ratio_re - out_imag * ratio_im
    mix_im = out_real * ratio_im + out_imag * ratio_re
    return arg_re, arg_im, mix_re, mix_im

def pair(left, right):
    return jnp.concatenate([left, right], axis=-1)

def mode_rows(arg_re, arg_im, mix_re, mix_im, gain, bias, skip):
    nch = arg_re.shape[0]
    scale = jnp.asarray([2.0**b for b in range(8)], f32)[None, :, None]
    magnitude = jnp.exp(arg_re[:, None] * scale)
    p_re = magnitude * jnp.cos(arg_im[:, None] * scale)
    p_im = magnitude * jnp.sin(arg_im[:, None] * scale)
    powers = jnp.stack([pair(p_re, p_re), pair(-p_im, p_im)], axis=2).reshape(nch, 16, 2 * NSTATE)
    c_re = mix_re * p_re[:, 0] - mix_im * p_im[:, 0]
    c_im = mix_re * p_im[:, 0] + mix_im * p_re[:, 0]
    flat = lambda v: jnp.broadcast_to(v[:, None], (nch, 2 * NSTATE))
    rest = jnp.stack([pair(mix_re, -mix_im), pair(c_re, -c_re), pair(-c_im, -c_im), flat(gain), flat(bias), flat(skip), flat(0 * gain), flat(0 * gain)], axis=1)
    return jnp.concatenate([powers, rest], axis=1)

def mode_grads(rows, arg_re, arg_im, mix_re, mix_im):
    lo, hi = rows[:, :, :NSTATE], rows[:, :, NSTATE:]
    magnitude = jnp.exp(arg_re)
    p_re, p_im = magnitude * jnp.cos(arg_im), magnitude * jnp.sin(arg_im)
    magnitude = jnp.exp(arg_re * CH)
    f_re, f_im = magnitude * jnp.cos(arg_im * CH), magnitude * jnp.sin(arg_im * CH)
    a_re, a_im = lo[2] - hi[2], -(hi[3] + lo[3])
    b_re, b_im = lo[4] - hi[4], -(hi[5] + lo[5])
    b_re, b_im = b_re + a_re, b_im + a_im
    w_re = lo[0] + p_re * a_re + p_im * a_im
    w_im = -hi[0] + p_re * a_im - p_im * a_re
    v_re = lo[1] + p_re * b_re + p_im * b_im
    v_im = -hi[1] + p_re * b_im - p_im * b_re
    g_re = mix_re * v_re + mix_im * v_im
    g_im = mix_re * v_im - mix_im * v_re
    g_re = g_re + lo[6] + hi[6]
    g_im = g_im + hi[7] - lo[7]
    d_re, d_im = lo[8] + hi[8], hi[9] - lo[9]
    g_re = g_re + CH * (f_re * d_re + f_im * d_im)
    g_im = g_im + CH * (f_re * d_im - f_im * d_re)
    return g_re, g_im, w_re, w_im


def gelu(values):
    return 0.5 * values * (1.0 + lax.erf(values * root_half))


def gelu_slope(values):
    return (
        0.5 * (1.0 + lax.erf(values * root_half))
        + values * jnp.exp(-0.5 * values * values) * inv_root_two_pi
    )


def normalize(values):
    center = values - jnp.mean(values, axis=-1, keepdims=True)
    scale = lax.rsqrt(jnp.mean(center * center, axis=-1, keepdims=True) + norm_eps)
    return (center * scale, scale)


def norm_back(d_hat, hat, scale):
    return scale * (
        d_hat
        - jnp.mean(d_hat, axis=-1, keepdims=True)
        - hat * jnp.mean(d_hat * hat, axis=-1, keepdims=True)
    )


TILE = 1024
GATE_AT, EXPAND_AT, REDUCE_AT = 130, 644, 1670
SMALL_AT = (642, 643, 1668, 1669, 2694)
MODE_TILES = 130
BLOCK = 512


def lay(share, devices):
    base = share // TILE
    return base, base + 2, (devices - 1) * share // TILE + base + 2


def product(a, b, ca, cb):
    return lax.dot_general(a, b, (((ca,), (cb,)), ((), ())), preferred_element_type=f32)


def narrow(flat, out, first, rows, per):
    def one(i, _):
        for k in range(per):
            v = flat[pl.ds(first * 8 + i * 16 * per + k, 16, stride=per), :]
            out[pl.ds(pl.multiple_of(i * 16, 16), 16), k * CH:(k + 1) * CH] = v.astype(bf16)
        return 0

    lax.fori_loop(0, rows // 16, one, 0, unroll=max(1, 16 // per))


def small_row(flat, tile, begin, count):
    return jnp.concatenate([flat[tile * 8 + (begin + k) // CH:tile * 8 + (begin + k) // CH + 1, :] for k in range(0, count, CH)], axis=1)


def put_small(small_ref, begin, row):
    for k in range(row.shape[1] // CH):
        small_ref[begin // CH + k:begin // CH + k + 1, :] = row[:, k * CH:(k + 1) * CH]


def column_sum(v):
    return jnp.sum(v, axis=0, keepdims=True)


def mlp_body(share, devices, nseq, streams, place_ref, ids, *refs):
    boxes = refs[:len(streams)]
    resp_ref, x_ref, cot_ref, out_ref, dmid_ref, dresp_ref, small_ref, lead_ref, hidden_ref, active_ref, normed_ref, back_ref, dopen_ref, dlift_ref, flat, side, gate, expand, reduce, acc, dnorm, sems = refs[len(streams):]
    base, box, _ = lay(share, devices)
    nch = D // nseq
    group = x_ref.shape[0]
    start_of = lambda j: (j * share) // TILE
    inside = 0
    for k, (first, last, off, count) in enumerate(streams):
        lo, hi = max(first, 1), min(last, base)

        def copy_box(i, _, k=k, first=first, last=last, lo=lo, hi=hi, off=off):
            j = ids[off + i]
            begin = (i * (last - first) - first) * 8
            for s, tile in enumerate((0, base, base + 1)):
                if first <= tile < last:
                    pltpu.make_async_copy(boxes[k].at[pl.ds(pl.multiple_of(begin + tile * 8, 8), 8), :], side.at[s, pl.ds(pl.multiple_of(j * 8, 8), 8), :], sems.at[1]).start()
            pltpu.make_async_copy(
                boxes[k].at[pl.ds(pl.multiple_of(begin + lo * 8, 8), (hi - lo) * 8), :],
                flat.at[pl.ds(pl.multiple_of((start_of(j) + lo) * 8, 8), (hi - lo) * 8), :],
                sems.at[0],
            ).start()
            return 0

        lax.fori_loop(0, count, copy_box, 0)
        inside += (hi - lo) * count
    parts = group // CH
    turned = [
        jnp.concatenate([resp_ref[pl.ds((d * parts + k) * nch, nch), :] for d in range(nseq)], axis=0).T
        for k in range(parts)
    ]
    response = jnp.concatenate(turned, axis=0)
    hidden_ref[...] = gelu(response).astype(bf16)
    pos = place_ref[DOCS] + lax.broadcasted_iota(jnp.int32, (group, D), 0)
    total = jnp.zeros((group, D), jnp.int32)
    for k in range(DOCS):
        total = total + (pos >= place_ref[k]).astype(jnp.int32)
    back = jnp.where(total < DOCS - 1, cot_ref[...].astype(f32), 0.0)
    back_ref[...] = back.astype(bf16)
    put_small(small_ref, 2 * G + FF, column_sum(back))
    small_ref[36:40, :] = jnp.zeros((4, CH), f32)
    inner = side.at[:, pl.ds(0, devices * 8), :]
    pltpu.make_async_copy(inner, inner, sems.at[1]).wait()
    side[0, devices * 8:, :] = jnp.zeros((8, CH), f32)
    flat[:8, :] = side[0, :8, :]

    def join(j, _):
        at = start_of(j)
        step = start_of(j + 1) - at
        far = jnp.broadcast_to(step, (8, CH)) > base
        here = pl.ds(pl.multiple_of(j * 8, 8), 8)
        one, two, then = side[1, here, :], side[2, here, :], side[0, pl.ds(pl.multiple_of(j * 8 + 8, 8), 8), :]
        flat[pl.ds(pl.multiple_of((at + base) * 8, 8), 8), :] = one + jnp.where(far, 0.0, then)
        flat[pl.ds(pl.multiple_of((at + step) * 8, 8), 8), :] = jnp.where(far, two, one) + then
        return 0

    lax.fori_loop(0, devices, join, 0)

    some = flat.at[pl.ds(0, inside * 8), :]
    pltpu.make_async_copy(some, some, sems.at[0]).wait()
    lead_ref[...] = flat[:MODE_TILES * 8, :]
    narrow(flat, gate, GATE_AT, D, G // CH)
    gate_bias = small_row(flat, SMALL_AT[0], 0, G)
    second_gain = small_row(flat, SMALL_AT[1], 0, D)
    second_bias = small_row(flat, SMALL_AT[1], D, D)
    hidden = hidden_ref[...]
    linear = product(hidden, gate[:, :D], 1, 0) + gate_bias[:, :D]
    gating = jax.nn.sigmoid(product(hidden, gate[:, D:], 1, 0) + gate_bias[:, D:])
    mid = x_ref[...].astype(f32) + linear * gating
    hat, scale = normalize(mid)
    normed_ref[...] = (hat * second_gain + second_bias).astype(bf16)
    narrow(flat, expand, EXPAND_AT, D, FF // CH)
    narrow(flat, reduce, REDUCE_AT, FF, D // CH)
    dnorm[...] = jnp.zeros((group, D), f32)
    acc[...] = mid + small_row(flat, SMALL_AT[4], 0, D)
    for b in range(FF // BLOCK):
        at = slice(b * BLOCK, (b + 1) * BLOCK)
        bias = small_row(flat, SMALL_AT[2] + b * BLOCK // TILE, b * BLOCK % TILE, BLOCK)
        lifted = product(normed_ref[...], expand[:, at], 1, 0) + bias
        half = 0.5 * (1.0 + lax.erf(lifted * root_half))
        active = (lifted * half).astype(bf16)
        active_ref[:, at] = active
        slope = half + lifted * jnp.exp(-0.5 * lifted * lifted) * inv_root_two_pi
        d_lifted = (product(back_ref[...], reduce[at, :], 1, 1) * slope).astype(bf16)
        dlift_ref[:, at] = d_lifted
        put_small(small_ref, 2 * G + b * BLOCK, column_sum(d_lifted.astype(f32)))
        acc[...] += product(active, reduce[at, :], 1, 0)
        dnorm[...] += product(d_lifted, expand[:, at], 1, 1)
    out_ref[...] = acc[...].astype(bf16)
    d_normed = dnorm[...]
    put_small(small_ref, G, column_sum(d_normed * hat))
    put_small(small_ref, G + D, column_sum(d_normed))
    d_mid = back_ref[...].astype(f32) + norm_back(d_normed * second_gain, hat, scale)
    dmid_ref[...] = d_mid
    d_linear = (d_mid * gating).astype(bf16)
    d_gating = (d_mid * linear * gating * (1.0 - gating)).astype(bf16)
    dopen_ref[:, :D] = d_linear
    dopen_ref[:, D:] = d_gating
    put_small(small_ref, 0, column_sum(d_linear.astype(f32)))
    put_small(small_ref, D, column_sum(d_gating.astype(f32)))
    d_hidden = product(d_linear, gate[:, :D], 1, 1) + product(d_gating, gate[:, D:], 1, 1)
    for k in range(parts):
        again = jnp.concatenate([resp_ref[pl.ds((d * parts + k) * nch, nch), :] for d in range(nseq)], axis=0)
        back_turned = d_hidden[k * CH:(k + 1) * CH].T * gelu_slope(again)
        for d in range(nseq):
            dresp_ref[pl.ds((d * parts + k) * nch, nch), :] = back_turned[d * nch:(d + 1) * nch]


def mlp_kernel(place, streams, ids, boxes, response, rows, cotangent, share, devices, nseq):
    base, box, tiles = lay(share, devices)
    group = rows.shape[0]
    vm = pl.BlockSpec(memory_space=pltpu.VMEM)
    shape = lambda r, c, t: jax.ShapeDtypeStruct((r, c), t)
    return pl.pallas_call(
        partial(mlp_body, share, devices, nseq, streams),
        out_shape=(
            shape(group, D, bf16),
            shape(group, D, f32),
            jax.ShapeDtypeStruct(response.shape, f32),
            shape(len(SMALL_AT) * 8, CH, f32),
            shape(MODE_TILES * 8, CH, f32),
            shape(group, D, bf16),
            shape(group, FF, bf16),
            shape(group, D, bf16),
            shape(group, D, bf16),
            shape(group, G, bf16),
            shape(group, FF, bf16),
        ),
        in_specs=[pl.BlockSpec(memory_space=pltpu.SMEM)] * 2 + [pl.BlockSpec(memory_space=pl.ANY)] * len(boxes) + [vm] * 3,
        out_specs=(vm,) * 11,
        scratch_shapes=[
            pltpu.VMEM((tiles * 8, CH), f32),
            pltpu.VMEM((3, devices * 8 + 8, CH), f32),
            pltpu.VMEM((D, G), bf16),
            pltpu.VMEM((D, FF), bf16),
            pltpu.VMEM((FF, D), bf16),
            pltpu.VMEM((group, D), f32),
            pltpu.VMEM((group, D), f32),
            pltpu.SemaphoreType.DMA((2,)),
        ],
        cost_estimate=pl.CostEstimate(flops=int(1.0e10), bytes_accessed=20 * 2**20, transcendentals=0),
        name="feed_forward",
    )(place, ids, *boxes, response, rows, cotangent)


def pack_body(streams, tiles, has_lead, *refs):
    n = len(streams)
    dest, hidden, active, normed, back, dopen, dlift, small_ref = refs[:8]
    outs = refs[8 + has_lead:8 + has_lead + n]
    flat, sem = refs[8 + has_lead + n:]
    if has_lead:
        flat[:MODE_TILES * 8, :] = refs[8][...]
    else:
        flat[:MODE_TILES * 8, :] = jnp.zeros((MODE_TILES * 8, CH), f32)
    for k, tile in enumerate(SMALL_AT):
        flat[tile * 8:(tile + 1) * 8, :] = small_ref[k * 8:(k + 1) * 8, :]
    flat[(SMALL_AT[-1] + 1) * 8:, :] = jnp.zeros(((tiles - SMALL_AT[-1] - 1) * 8, CH), f32)
    for first, left, right, per in ((GATE_AT, hidden, dopen, G // CH), (EXPAND_AT, normed, dlift, FF // CH), (REDUCE_AT, active, back, D // CH)):
        wide = 128
        flip = left[...].T

        for k in range(left.shape[1] // wide):
            v = product(flip[k * wide:(k + 1) * wide], right[...], 1, 0)
            for c in range(per):
                flat[pl.ds(first * 8 + k * wide * per + c, wide, stride=per), :] = v[:, c * CH:(c + 1) * CH]
    for k, (first, last, order) in enumerate(streams):
        rows = (last - first) * 8

        def send(b, _, k=k, first=first, rows=rows, order=order):
            at = pl.multiple_of(dest[order + b], 8)
            pltpu.make_async_copy(flat.at[pl.ds(at + first * 8, rows), :], outs[k].at[pl.ds(pl.multiple_of(b * rows, 8), rows), :], sem.at[k]).start()
            return 0

        lax.fori_loop(0, outs[k].shape[0] // rows, send, 0)
    for k, out in enumerate(outs):
        pltpu.make_async_copy(out, out, sem.at[k]).wait()


def pack_kernel(streams, dest, values, small, lead, share, devices):
    _, _, tiles = lay(share, devices)
    hbm = pl.BlockSpec(memory_space=pl.ANY)
    vm = pl.BlockSpec(memory_space=pltpu.VMEM)
    has = int(lead is not None)
    return pl.pallas_call(
        partial(pack_body, tuple(s[:3] for s in streams), tiles, has),
        out_shape=tuple(jax.ShapeDtypeStruct((blocks * (last - first) * 8, CH), f32) for first, last, _, blocks in streams),
        in_specs=[pl.BlockSpec(memory_space=pltpu.SMEM)] + [vm] * (7 + has),
        out_specs=(hbm,) * len(streams),
        scratch_shapes=[pltpu.VMEM((tiles * 8, CH), f32), pltpu.SemaphoreType.DMA((len(streams),))],
        cost_estimate=pl.CostEstimate(flops=int(0.8e10), bytes_accessed=16 * 2**20, transcendentals=0),
        name="weight_gradients",
    )(dest, *values, small, *((lead,) if has else ()))


AXES = ("seq", "batch")
PAIR = [(0, 1), (1, 0)]


def hop(v, step):
    return lax.ppermute(v, "seq", [(i, i ^ step) for i in range(16)])


def swap_cores(v):
    return lax.ppermute(v, "batch", PAIR)


def direct():
    return lax.axis_size("seq") == 16 and lax.axis_size("batch") == 2


def device_index():
    return lax.axis_index("seq") * lax.axis_size("batch") + lax.axis_index("batch")


def places_of(steps, other):
    seq, batch = lax.axis_index("seq"), lax.axis_index("batch")
    return 2 * (seq ^ np.asarray(steps, np.int32)) + (batch ^ other)


def cuts_of(tiles):
    one = round(tiles * (1.0 - Z_FIRST) / 2)
    return one, 2 * one


def container(master, share, devices):
    _, tiles, _ = lay(share, devices)
    box = lax.dynamic_update_slice(jnp.zeros((tiles * TILE,), f32), master, (device_index() * share % TILE,))
    return box.reshape(tiles * 8, CH)


def gather_near(box):
    half = box.shape[0] // 16 * 8
    sets = [box] + [hop(box, step) for step in (4, 8, 12)]
    return [jnp.concatenate([v[at] for v in sets]) for at in (slice(0, half), slice(half, None))]


def gather_plane(near):
    return [jnp.concatenate([near[0], hop(near[0], 1)]), jnp.concatenate([near[1], hop(near[1], 2)])]


def gather_cores(plane, far, tiles):
    half = tiles // 2
    arrays, streams, ids = [], [], []
    for v, first, second in ((plane[0], 0, 1), (plane[1], 0, 2), (far[0], 2, 3), (far[1], 1, 3)):
        for other in range(2):
            arrays.append(swap_cores(v) if other else v)
            streams.append(((0, half) if len(arrays) % 4 in (1, 2) else (half, tiles)) + (8 * len(ids), 8))
            ids.append(places_of([4 * z + p for p in (first, second) for z in range(4)], other))
    return tuple(streams), jnp.concatenate(ids).astype(jnp.int32), arrays


def scatter_plan(share, devices):
    _, tiles, _ = lay(share, devices)
    if not direct():
        return ((0, tiles, 0, devices),), jnp.arange(devices, dtype=jnp.int32) * share // TILE * 8
    one, two = cuts_of(tiles)
    streams, ids = [], []
    for first, last, bits in ((0, one, (1, 2, 8, 4)), (one, two, (2, 1, 8, 4)), (two, tiles, (8, 4, 2, 1))):
        steps = [0]
        for bit in bits[::-1]:
            steps = steps + [bit + step for step in steps]
        for other in range(2):
            streams.append((first, last, 16 * len(ids), 16))
            ids.append(places_of(steps, other))
    return tuple(streams), (jnp.concatenate(ids) * share // TILE * 8).astype(jnp.int32)


def pieces(v, count):
    return v.reshape(count, -1, CH)


def halve(two, step):
    return pieces(two[0] + hop(two[1], step), 2)


def join_cores(arrays):
    sums = []
    for own, far in zip(arrays[::2], arrays[1::2]):
        own, far = pieces(own, 2), pieces(swap_cores(far), 2)
        sums.append([own[k] + far[k] for k in range(2)])
    return sums


def join_first(sums):
    return [halve(v, step) for v, step in zip(sums, (1, 2, 8))]


def join_second(sums):
    return [halve(v, step) for v, step in zip(sums, (2, 1, 4))]


def join_last(sums):
    rows = [pieces(v.reshape(-1, CH), 4) for v in sums[:2]]
    four = [jnp.concatenate([v[k] for v in rows]) for k in range(4)]
    near = halve(sums[2], 2)
    one = four[0] + hop(four[1], 4) + hop(four[2], 8) + hop(four[3], 12)
    return jnp.concatenate([one, near[0] + hop(near[1], 1)])


MODE_ROWS = 65


def scatter_modes(master):
    other = swap_cores(master)
    even = lax.axis_index("batch") == 0
    lead = jnp.concatenate([jnp.where(even, master, other), jnp.where(even, other, master)])[:MODE_TILES * TILE]
    small = lead[:4 * D].reshape(4, 16, 32).transpose(1, 0, 2).reshape(16, 1, CH)
    rest = lead[4 * D:].reshape(4, 16, 16, CH).transpose(1, 0, 2, 3).reshape(16, 64, CH)
    blocks = jnp.concatenate([small, rest], axis=1)
    seq = lax.axis_index("seq")
    blocks = blocks.reshape(2, 2, 2, 2, MODE_ROWS, CH).transpose(3, 2, 1, 0, 4, 5)
    for step in (1, 2, 4, 8):
        come = lax.ppermute(blocks[1], "seq", [(i, i + step) for i in range(step)])
        blocks = jnp.where(seq & step == 0, blocks[0], come)
    return blocks


def read_modes(block):
    nch = D // 16
    small = block[0].reshape(4, nch)
    rest = block[1:].reshape(4, nch, NSTATE)
    return small, rest


def gather_modes(block, steps):
    for step in steps:
        pairs = [(i, i - step) for i in range(2 * step) if i >= step]
        block = jnp.concatenate([block, lax.ppermute(block, "seq", pairs)])
    return block


def mode_vector(block):
    blocks = block.reshape(2, 2, 2, 2, MODE_ROWS, CH).transpose(3, 2, 1, 0, 4, 5).reshape(16, MODE_ROWS, CH)
    lead = blocks[:, 0].reshape(16, 4, 32).transpose(1, 0, 2).reshape(-1)
    tail = blocks[:, 1:].reshape(16, 4, 16, CH).transpose(1, 0, 2, 3).reshape(-1)
    return jnp.concatenate([lead, tail])


def total_of(v):
    if not direct():
        return lax.psum(v, AXES)
    v = jnp.broadcast_to(v, (8, CH))
    v = v + swap_cores(v)
    v = v + (hop(v, 1) + hop(v, 2) + hop(v, 3))
    v = v + (hop(v, 4) + hop(v, 8) + hop(v, 12))
    return v[0, 0]


def to_channels(rows):
    seq = lax.axis_size("seq")
    parts = rows.shape[0] // CH
    turned = rows.reshape(parts, CH, seq, D // seq).transpose(2, 0, 3, 1)
    return lax.all_to_all(turned, "seq", 0, 0).reshape(-1, CH)


def to_tokens(rows, group):
    seq = lax.axis_size("seq")
    turned = lax.all_to_all(rows.reshape(seq, group // CH, D // seq, CH), "seq", 0, 0)
    return turned.transpose(1, 3, 0, 2).reshape(group, D)


def per_device(inputs, cotangent, lengths, master, first_moment, second_moment):
    seq, batch = lax.axis_size("seq"), lax.axis_size("batch")
    devices = seq * batch
    share = master.shape[0]
    box = container(master, share, devices)
    if direct():
        near = gather_near(box)
    else:
        streams, ids = ((0, box.shape[0] // 8, 0, devices),), jnp.arange(devices, dtype=jnp.int32)
        boxes = [lax.all_gather(box, AXES, axis=0, tiled=True)]
    group = inputs.shape[1]
    nch, nck = D // seq, seq * group // CH
    rows = inputs[0].astype(jnp.float32)
    ends = jnp.cumsum(lengths[0]).astype(jnp.int32)
    place = jnp.concatenate([ends, lax.axis_index("seq")[None] * group]).astype(jnp.int32)
    first_hat, first_scale = normalize(rows)
    hats = to_channels(first_hat)

    def feed_forward(response):
        return mlp_kernel(place, streams, ids, boxes, response, inputs[0], cotangent[0], share, devices, seq)

    if direct():
        few, many = read_modes(scatter_modes(master))
    else:
        lead = jnp.concatenate([lax.dynamic_slice(boxes[0][j * box.shape[0]:(j + 1) * box.shape[0]].reshape(-1), (j * share % TILE,), (share,)) for j in range(MODE_TILES * TILE // share + 1)])
        mine = lambda v: lax.dynamic_slice_in_dim(v, lax.axis_index("seq") * nch, nch, 1)
        few = mine(lead[:4 * D].reshape(4, D))
        many = mine(lead[4 * D:MODE_TILES * TILE].reshape(4, D, NSTATE))
    if direct():
        plane = gather_plane(near)
    modes, modes_pull = jax.vjp(mixing, few[2], many[0], many[1], many[2], many[3])
    prm = mode_rows(*modes, few[0], few[1], few[3])
    outs, prior, *tables = ssm_forward(ends, prm, hats, nck, nch)
    response = lax.all_to_all(outs.reshape(seq, -1, nch, CH), "seq", 0, 0).reshape(-1, CH)
    if direct():
        far = [hop(plane[0], 2), hop(plane[1], 1)]
        response, far = lax.optimization_barrier((response, far))
        streams, ids, boxes = gather_cores(plane, far, box.shape[0] // 8)
    output, d_mid, d_response, small, lead, *values = feed_forward(response)
    d_outs = lax.all_to_all(d_response.reshape(seq, -1, nch, CH), "seq", 0, 0).reshape(-1, CH)
    plan, places = scatter_plan(share, devices)
    if direct():
        packed = join_cores(pack_kernel(plan, places, values, small, None, share, devices))
        d_outs, packed = lax.optimization_barrier((d_outs, packed))
    d_signals, sums = ssm_backward(ends, prm, hats, d_outs, prior, tables, nck, nch)
    if direct():
        d_signals, sums, packed = lax.optimization_barrier((d_signals, sums, join_first(packed)))
    d_signal = to_tokens(d_signals, group)
    norm_gain = lead[:D // CH].reshape(D)
    lane_sums = jnp.sum(sums[10:13], axis=-1)
    d_modes = modes_pull(mode_grads(sums, *modes))
    few = jnp.stack([lane_sums[1], lane_sums[2], d_modes[0], lane_sums[0]])
    many = jnp.stack(d_modes[1:])
    if not direct():

        def spread(v):
            whole = jnp.zeros((v.shape[0], D) + v.shape[2:], f32)
            return lax.dynamic_update_slice_in_dim(whole, v, lax.axis_index("seq") * nch, 1)

        lead = jnp.concatenate([spread(few).reshape(-1), spread(many).reshape(-1)]).reshape(-1, CH)
        packed = pack_kernel(plan, places, values, small, lead, share, devices)
    me = device_index()
    if direct():
        own = jnp.concatenate([few.reshape(1, CH), many.reshape(64, CH)])
        own, packed = lax.optimization_barrier((own + swap_cores(own), join_second(packed)))
        box, block, d_signal = lax.optimization_barrier((join_last(packed), gather_modes(own, (8, 4)), d_signal))
    else:
        box = lax.psum_scatter(packed[0].reshape(devices, -1, CH), AXES, scatter_dimension=0)
    d_rows = d_mid + norm_back(d_signal * norm_gain, first_hat, first_scale)
    shard = lax.dynamic_slice(box.reshape(-1), (me * share % TILE,), (share,))
    if direct():
        lead = mode_vector(gather_modes(block, (2, 1)))
        lead = jnp.pad(lead, (0, 2 * share - lead.shape[0]))
        mark = me * share + jnp.arange(share, dtype=jnp.int32) < MODE_TILES * TILE
        squares = jnp.sum(jnp.where(mark, 0.0, shard * shard))
        squares = squares + 0.5 * jnp.sum(own * own)
        shard = jnp.where(mark, lax.dynamic_slice(lead, (jnp.minimum(me, 1) * share,), (share,)), shard)
    else:
        squares = jnp.sum(shard * shard)
    total = total_of(squares)
    grad_norm = jnp.sqrt(total)
    factor = jnp.minimum(1.0, 1.0 / (grad_norm + 1e-06))
    clipped = shard * factor
    first_new = 0.9 * first_moment + 0.1 * clipped
    second_new = 0.999 * second_moment + 0.001 * clipped * clipped
    first_hat_new = first_new / (1.0 - 0.9**10)
    second_hat_new = second_new / (1.0 - 0.999**10)
    update = -0.05 * (first_hat_new / (jnp.sqrt(second_hat_new) + 1e-08) + 0.1 * master)
    return (output[None], d_rows[None], shard, update, first_new, second_new, grad_norm)


def solution(mesh):
    placed = (
        P("batch", "seq", None),
        P("batch", "seq", None),
        P("batch", None),
        P(("seq", "batch")),
        P(("seq", "batch")),
        P(("seq", "batch")),
    )
    return jax.shard_map(
        per_device,
        mesh=mesh,
        in_specs=placed,
        out_specs=(
            P("batch", "seq", None),
            P("batch", "seq", None),
            P(("seq", "batch")),
            P(("seq", "batch")),
            P(("seq", "batch")),
            P(("seq", "batch")),
            P(),
        ),
        check_vma=False,
    )
```

```python
from functools import partial
import jax
import jax.numpy as jnp
import numpy as np
from jax import lax
from jax.experimental import pallas as pl
from jax.experimental.pallas import tpu as pltpu
from jax.sharding import PartitionSpec as P

D = 512
NSTATE = 64
CH = 128
DOCS = 4
G = 1024
FF = 2048
Z_FIRST = 0.2


norm_eps = 1e-05
root_half = 0.7071067811865476
inv_root_two_pi = 0.3989422804014327


f32 = jnp.float32
bf16 = jnp.bfloat16

def split(v):
    hi = v.astype(bf16)
    return hi, (v - hi.astype(f32)).astype(bf16)

def dot3(a, b, ca, cb):
    ah, al = a
    bh, bl = b
    lhs = jnp.concatenate([ah, ah, al], axis=ca)
    rhs = jnp.concatenate([bh, bl, bh], axis=cb)
    return lax.dot_general(lhs, rhs, (((ca,), (cb,)), ((), ())), preferred_element_type=f32)

def dot2(data, table, ct):
    return dot3(data, (table[0], table[1]), 1, ct)

def swap(v):
    return pltpu.roll(v, NSTATE, 1)

def twist(table, re, im):
    return re * table + im * swap(table)

def ladder(prm, order):
    sub = lax.broadcasted_iota(jnp.int32, (8, 2 * NSTATE), 0)
    lane = lax.broadcasted_iota(jnp.int32, (8, 2 * NSTATE), 1)
    power = sub if order == 1 else 7 - sub
    table = jnp.where(lane < NSTATE, 1.0, 0.0).astype(f32)
    for bit in range(3):
        table = jnp.where((power >> bit) & 1 == 1, twist(table, prm[2 * bit:2 * bit + 1], prm[2 * bit + 1:2 * bit + 2]), table)
    for bit in range(3, 7):
        more = twist(table, prm[2 * bit:2 * bit + 1], prm[2 * bit + 1:2 * bit + 2])
        table = jnp.concatenate([table, more] if order == 1 else [more, table], axis=0)
    return table

def toeplitz(taps):
    wide = pltpu.roll(jnp.broadcast_to(taps, (CH, CH)), 0, 1, stride=1, stride_axis=0)
    row = lax.broadcasted_iota(jnp.int32, (CH, CH), 0)
    col = lax.broadcasted_iota(jnp.int32, (CH, CH), 1)
    return jnp.where(col >= row, wide, 0.0)

def label_at(ends, pos):
    total = jnp.zeros_like(pos)
    for k in range(DOCS):
        total = total + (pos >= ends[k]).astype(jnp.int32)
    return total

def make_masks(ends_ref, masks_ref, low_ref, nck):
    ends = [ends_ref[k] for k in range(DOCS)]
    row = lax.broadcasted_iota(jnp.int32, (nck, CH), 0)
    lane = lax.broadcasted_iota(jnp.int32, (nck, CH), 1)
    base = row * CH
    label = label_at(ends, base + lane)
    prev = jnp.where(base == 0, -1, label_at(ends, base - 1))
    last = label_at(ends, base + CH - 1)
    for k in range(DOCS):
        masks_ref[k] = (label == k).astype(f32)
    masks_ref[DOCS] = (label == prev).astype(f32)
    masks_ref[DOCS + 1] = (label == last).astype(f32)
    low_ref[:DOCS + 2] = masks_ref[...].astype(bf16)
    if low_ref.shape[0] > DOCS + 2:
        label = label_at(ends, base + (CH - 1 - lane))
        for k in range(DOCS):
            low_ref[DOCS + 2 + k] = (label == k).astype(f32).astype(bf16)

def keep_of(ends_ref, c):
    first = jnp.int32(0)
    second = jnp.int32(0)
    for k in range(DOCS):
        first = first + (c * CH - 1 >= ends_ref[k]).astype(jnp.int32)
        second = second + (c * CH + CH - 1 >= ends_ref[k]).astype(jnp.int32)
    return jnp.where((c > 0) & (first == second), 1.0, 0.0).astype(f32)

def masked_rows(v, low_ref):
    return [jnp.concatenate([part * low_ref[k] for k in range(DOCS)], axis=0) for part in v]

def masked(v, low_ref, k):
    return [part * low_ref[k] for part in v]

def fold_rows(v, masks_ref, nck):
    total = v[:nck] * masks_ref[0]
    for k in range(1, DOCS):
        total = total + v[k * nck:(k + 1) * nck] * masks_ref[k]
    return total

def keep(ref, h, v):
    ref[h, 0], ref[h, 1] = split(v)

def for_channels(nch, body):
    lax.fori_loop(0, nch, lambda h, _: body(h) or 0, 0, unroll=min(nch, 16))

def fwd_body(nck, nch, apart, ends_ref, prm_ref, x_ref, y_ref, prior_ref, table_ref, down_ref, out_ref, mat_ref, masks_ref, low_ref, end_ref):
    make_masks(ends_ref, masks_ref, low_ref, nck)

    def tables(h):
        prm = prm_ref[h]
        table = ladder(prm, 1)
        keep(table_ref, h, table)
        keep(out_ref, h, twist(table, prm[17:18], prm[18:19]))

    def falling(h):
        keep(down_ref, h, ladder(prm_ref[h], -1))

    def taps(h):
        wrow = jnp.broadcast_to(prm_ref[h, 16:17, :], (16, 2 * NSTATE))
        keep(mat_ref, h, toeplitz(dot2(split(wrow), table_ref[h], 1)[0:1]))

    def local(h):
        prm = prm_ref[h, 16:24, :]
        u = x_ref[pl.ds(h, nck, stride=apart), :] * prm[3:4] + prm[4:5]
        parts = split(u)
        local = dot2(masked_rows(parts, low_ref), mat_ref[h], 0)
        y_ref[pl.ds(h, nck, stride=nch), :] = fold_rows(local, masks_ref, nck) + prm[5:6] * u
        end_ref[pl.ds(h, nck, stride=nch), :] = dot2(masked(parts, low_ref, DOCS + 1), down_ref[h], 0)

    for body in (tables, falling, taps, local):
        for_channels(nch, body)
    full_re = prm_ref[:, 14, :]
    full_im = prm_ref[:, 15, :]

    def step(c, state):
        at = pl.ds(pl.multiple_of(c * nch, 8), nch)
        prior_ref[at, :] = state
        return keep_of(ends_ref, c) * twist(state, full_re, full_im) + end_ref[at, :]

    lax.fori_loop(0, nck, step, jnp.zeros((nch, 2 * NSTATE), f32))

    def carried(h):
        prior = split(prior_ref[pl.ds(h, nck, stride=nch), :])
        y_ref[pl.ds(h, nck, stride=nch), :] += dot2(prior, out_ref[h], 1) * masks_ref[DOCS]

    for_channels(nch, carried)

def ssm_forward(ends, prm, x, nck, nch):
    vm = pl.BlockSpec(memory_space=pltpu.VMEM)
    table = jax.ShapeDtypeStruct((nch, 2, CH, 2 * NSTATE), bf16)
    return pl.pallas_call(
        partial(fwd_body, nck, nch, x.shape[0] // nck),
        out_shape=(jax.ShapeDtypeStruct((nck * nch, CH), f32), jax.ShapeDtypeStruct((nck * nch, 2 * NSTATE), f32)) + (table,) * 4,
        in_specs=[pl.BlockSpec(memory_space=pltpu.SMEM), vm, vm],
        out_specs=(vm,) * 6,
        scratch_shapes=[
            pltpu.VMEM((DOCS + 2, nck, CH), f32),
            pltpu.VMEM((DOCS + 2, nck, CH), bf16),
            pltpu.VMEM((nck * nch, 2 * NSTATE), f32),
        ],
        cost_estimate=pl.CostEstimate(flops=int(2.0e10), bytes_accessed=3 * 2**20, transcendentals=0),
        name="state_forward",
    )(ends, prm, x)

def bwd_body(nck, nch, apart, ends_ref, prm_ref, x_ref, g_ref, prior_ref, table_ref, down_ref, out_ref, mat_ref, dx_ref, rows_ref, masks_ref, low_ref, lead_ref, adj_ref, taps_ref):
    make_masks(ends_ref, masks_ref, low_ref, nck)
    at_channel = lambda h: pl.ds(h, nck, stride=nch)

    def lead(h):
        lead_ref[at_channel(h), :] = dot2(masked(split(g_ref[at_channel(h), :]), low_ref, DOCS), out_ref[h], 0)

    for_channels(nch, lead)
    full_re = prm_ref[:, 14, :]
    full_im = prm_ref[:, 15, :]
    zero = jnp.zeros((nch, 2 * NSTATE), f32)

    def step(k, carry):
        adjoint, same, cross = carry
        c = nck - 1 - k
        at = pl.ds(pl.multiple_of(c * nch, 8), nch)
        adj_ref[at, :] = adjoint
        keep = keep_of(ends_ref, c)
        prior = prior_ref[at, :]
        same = same + keep * adjoint * prior
        cross = cross + keep * adjoint * swap(prior)
        adjoint = lead_ref[at, :] + keep * (full_re * adjoint - full_im * swap(adjoint))
        return adjoint, same, cross

    _, same, cross = lax.fori_loop(0, nck, step, (zero, zero, zero))
    rows_ref[8] = same
    rows_ref[9] = cross
    for k in range(13, 16):
        rows_ref[k] = zero
    row = lax.broadcasted_iota(jnp.int32, (CH, CH), 0)
    col = lax.broadcasted_iota(jnp.int32, (CH, CH), 1)
    flip = (row + col == CH - 1).astype(f32).astype(bf16)
    put = lambda k, h, v: rows_ref.__setitem__((k, pl.ds(h, 1), slice(None)), jnp.sum(v, axis=0, keepdims=True))

    def signal(h):
        prm = prm_ref[h, 16:24, :]
        x = x_ref[pl.ds(h, nck, stride=apart), :]
        g = g_ref[at_channel(h), :]
        du = fold_rows(dot2(masked_rows(split(g), low_ref), mat_ref[h], 1), masks_ref, nck)
        du = du + dot2(split(adj_ref[at_channel(h), :]), down_ref[h], 1) * masks_ref[DOCS + 1]
        du = du + prm[5:6] * g
        dx_ref[at_channel(h), :] = du
        put(10, h, g * (x * prm[3:4] + prm[4:5]))
        put(11, h, du * x)
        put(12, h, du)

    def taps(h):
        prm = prm_ref[h, 16:24, :]
        u = split(x_ref[pl.ds(h, nck, stride=apart), :] * prm[3:4] + prm[4:5])
        both = jnp.dot(jnp.concatenate(u, axis=0), flip, preferred_element_type=f32).astype(bf16)
        um = []
        for part in (both[:nck], both[nck:]):
            um.append(jnp.concatenate([part * low_ref[DOCS + 2 + k] for k in range(DOCS)], axis=0))
        square = dot3(um, masked_rows(split(g_ref[at_channel(h), :]), low_ref), 0, 0)
        square = jnp.where(row + col >= CH - 1, square, 0.0)
        square = pltpu.roll(square, 1, 1, stride=1, stride_axis=0)
        taps_ref[pl.ds(h, 1), :] = jnp.sum(square, axis=0, keepdims=True)

    def kernel(h):
        place = lax.broadcasted_iota(jnp.int32, (16, CH), 1).astype(f32)
        sub = lax.broadcasted_iota(jnp.int32, (16, CH), 0)
        both = jnp.where(sub == 0, 1.0, jnp.where(sub == 1, place, 0.0)) * taps_ref[pl.ds(h, 1), :]
        both = dot2(split(both), table_ref[h], 0)
        rows_ref[0, pl.ds(h, 1), :] = both[0:1]
        rows_ref[1, pl.ds(h, 1), :] = both[1:2]

    late = row.astype(f32)

    def carried(h):
        dgt = dot3(masked(split(g_ref[at_channel(h), :]), low_ref, DOCS), split(prior_ref[at_channel(h), :]), 0, 0)
        table = table_ref[h, 0].astype(f32) + table_ref[h, 1].astype(f32)
        same, cross = dgt * table, dgt * swap(table)
        put(2, h, same)
        put(3, h, cross)
        put(4, h, same * late)
        put(5, h, cross * late)

    def ending(h):
        prm = prm_ref[h, 16:24, :]
        u = split(x_ref[pl.ds(h, nck, stride=apart), :] * prm[3:4] + prm[4:5])
        ddown = dot3(masked(u, low_ref, DOCS + 1), split(adj_ref[at_channel(h), :]), 0, 0) * ((CH - 1) - late)
        down = down_ref[h, 0].astype(f32) + down_ref[h, 1].astype(f32)
        put(6, h, ddown * down)
        put(7, h, ddown * swap(down))

    for body in (signal, taps, kernel, carried, ending):
        for_channels(nch, body)

def ssm_backward(ends, prm, x, g, prior, tables, nck, nch):
    vm = pl.BlockSpec(memory_space=pltpu.VMEM)
    return pl.pallas_call(
        partial(bwd_body, nck, nch, x.shape[0] // nck),
        out_shape=(jax.ShapeDtypeStruct((nck * nch, CH), f32), jax.ShapeDtypeStruct((16, nch, 2 * NSTATE), f32)),
        in_specs=[pl.BlockSpec(memory_space=pltpu.SMEM)] + [vm] * 8,
        out_specs=(vm, vm),
        scratch_shapes=[
            pltpu.VMEM((DOCS + 2, nck, CH), f32),
            pltpu.VMEM((2 * DOCS + 2, nck, CH), bf16),
            pltpu.VMEM((nck * nch, 2 * NSTATE), f32),
            pltpu.VMEM((nck * nch, 2 * NSTATE), f32),
            pltpu.VMEM((nch, CH), f32),
        ],
        cost_estimate=pl.CostEstimate(flops=int(3.5e10), bytes_accessed=4 * 2**20, transcendentals=0),
        name="state_backward",
    )(ends, prm, x, g, prior, *tables)

def mixing(step_log, decay_log, frequency, out_real, out_imag):
    delta = jnp.exp(step_log)[:, None]
    rate_re = -jnp.exp(decay_log)
    arg_re, arg_im = delta * rate_re, delta * frequency
    magnitude = jnp.exp(arg_re)
    pole_re = magnitude * jnp.cos(arg_im) - 1.0
    pole_im = magnitude * jnp.sin(arg_im)
    denom = rate_re * rate_re + frequency * frequency
    ratio_re = (pole_re * rate_re + pole_im * frequency) / denom
    ratio_im = (pole_im * rate_re - pole_re * frequency) / denom
    mix_re = out_real * ratio_re - out_imag * ratio_im
    mix_im = out_real * ratio_im + out_imag * ratio_re
    return arg_re, arg_im, mix_re, mix_im

def pair(left, right):
    return jnp.concatenate([left, right], axis=-1)

def mode_rows(arg_re, arg_im, mix_re, mix_im, gain, bias, skip):
    nch = arg_re.shape[0]
    scale = jnp.asarray([2.0**b for b in range(8)], f32)[None, :, None]
    magnitude = jnp.exp(arg_re[:, None] * scale)
    p_re = magnitude * jnp.cos(arg_im[:, None] * scale)
    p_im = magnitude * jnp.sin(arg_im[:, None] * scale)
    powers = jnp.stack([pair(p_re, p_re), pair(-p_im, p_im)], axis=2).reshape(nch, 16, 2 * NSTATE)
    c_re = mix_re * p_re[:, 0] - mix_im * p_im[:, 0]
    c_im = mix_re * p_im[:, 0] + mix_im * p_re[:, 0]
    flat = lambda v: jnp.broadcast_to(v[:, None], (nch, 2 * NSTATE))
    rest = jnp.stack([pair(mix_re, -mix_im), pair(c_re, -c_re), pair(-c_im, -c_im), flat(gain), flat(bias), flat(skip), flat(0 * gain), flat(0 * gain)], axis=1)
    return jnp.concatenate([powers, rest], axis=1)

def mode_grads(rows, arg_re, arg_im, mix_re, mix_im):
    lo, hi = rows[:, :, :NSTATE], rows[:, :, NSTATE:]
    magnitude = jnp.exp(arg_re)
    p_re, p_im = magnitude * jnp.cos(arg_im), magnitude * jnp.sin(arg_im)
    magnitude = jnp.exp(arg_re * CH)
    f_re, f_im = magnitude * jnp.cos(arg_im * CH), magnitude * jnp.sin(arg_im * CH)
    a_re, a_im = lo[2] - hi[2], -(hi[3] + lo[3])
    b_re, b_im = lo[4] - hi[4], -(hi[5] + lo[5])
    b_re, b_im = b_re + a_re, b_im + a_im
    w_re = lo[0] + p_re * a_re + p_im * a_im
    w_im = -hi[0] + p_re * a_im - p_im * a_re
    v_re = lo[1] + p_re * b_re + p_im * b_im
    v_im = -hi[1] + p_re * b_im - p_im * b_re
    g_re = mix_re * v_re + mix_im * v_im
    g_im = mix_re * v_im - mix_im * v_re
    g_re = g_re + lo[6] + hi[6]
    g_im = g_im + hi[7] - lo[7]
    d_re, d_im = lo[8] + hi[8], hi[9] - lo[9]
    g_re = g_re + CH * (f_re * d_re + f_im * d_im)
    g_im = g_im + CH * (f_re * d_im - f_im * d_re)
    return g_re, g_im, w_re, w_im


def gelu(values):
    return 0.5 * values * (1.0 + lax.erf(values * root_half))


def gelu_slope(values):
    return (
        0.5 * (1.0 + lax.erf(values * root_half))
        + values * jnp.exp(-0.5 * values * values) * inv_root_two_pi
    )


def normalize(values):
    center = values - jnp.mean(values, axis=-1, keepdims=True)
    scale = lax.rsqrt(jnp.mean(center * center, axis=-1, keepdims=True) + norm_eps)
    return (center * scale, scale)


def norm_back(d_hat, hat, scale):
    return scale * (
        d_hat
        - jnp.mean(d_hat, axis=-1, keepdims=True)
        - hat * jnp.mean(d_hat * hat, axis=-1, keepdims=True)
    )


TILE = 1024
GATE_AT, EXPAND_AT, REDUCE_AT = 130, 644, 1670
SMALL_AT = (642, 643, 1668, 1669, 2694)
MODE_TILES = 130
BLOCK = 512


def lay(share, devices):
    base = share // TILE
    return base, base + 2, (devices - 1) * share // TILE + base + 2


def product(a, b, ca, cb):
    return lax.dot_general(a, b, (((ca,), (cb,)), ((), ())), preferred_element_type=f32)


def narrow(flat, out, first, rows, per):
    def one(i, _):
        for k in range(per):
            v = flat[pl.ds(first * 8 + i * 16 * per + k, 16, stride=per), :]
            out[pl.ds(pl.multiple_of(i * 16, 16), 16), k * CH:(k + 1) * CH] = v.astype(bf16)
        return 0

    lax.fori_loop(0, rows // 16, one, 0, unroll=max(1, 16 // per))


def small_row(flat, tile, begin, count):
    return jnp.concatenate([flat[tile * 8 + (begin + k) // CH:tile * 8 + (begin + k) // CH + 1, :] for k in range(0, count, CH)], axis=1)


def put_small(small_ref, begin, row):
    for k in range(row.shape[1] // CH):
        small_ref[begin // CH + k:begin // CH + k + 1, :] = row[:, k * CH:(k + 1) * CH]


def column_sum(v):
    return jnp.sum(v, axis=0, keepdims=True)


def mlp_body(share, devices, nseq, streams, plan, place_ref, ids, slots, *refs):
    boxes = refs[:len(streams)]
    resp_ref, x_ref, cot_ref, out_ref, dmid_ref, dresp_ref, lead_ref = refs[len(streams):len(streams) + 7]
    ways = 2 if len(plan) > 1 else 1
    outs = refs[len(streams) + 7:len(streams) + 7 + ways * len(plan)]
    small_ref, hidden_ref, active_ref, normed_ref, back_ref, dopen_ref, dlift_ref, flat, side, gate, expand, reduce, acc, dnorm, sems, out_sems = refs[len(streams) + 7 + len(outs):]
    base, box, _ = lay(share, devices)
    nch = D // nseq
    group = x_ref.shape[0]
    start_of = lambda j: (j * share) // TILE
    inside = 0
    for k, (first, last, off, count) in enumerate(streams):
        lo, hi = max(first, 1), min(last, base)

        def copy_box(i, _, k=k, first=first, last=last, lo=lo, hi=hi, off=off):
            j = ids[off + i]
            begin = (i * (last - first) - first) * 8
            for s, tile in enumerate((0, base, base + 1)):
                if first <= tile < last:
                    pltpu.make_async_copy(boxes[k].at[pl.ds(pl.multiple_of(begin + tile * 8, 8), 8), :], side.at[s, pl.ds(pl.multiple_of(j * 8, 8), 8), :], sems.at[1]).start()
            pltpu.make_async_copy(
                boxes[k].at[pl.ds(pl.multiple_of(begin + lo * 8, 8), (hi - lo) * 8), :],
                flat.at[pl.ds(pl.multiple_of((start_of(j) + lo) * 8, 8), (hi - lo) * 8), :],
                sems.at[0],
            ).start()
            return 0

        lax.fori_loop(0, count, copy_box, 0)
        inside += (hi - lo) * count
    parts = group // CH
    turned = [
        jnp.concatenate([resp_ref[pl.ds((d * parts + k) * nch, nch), :] for d in range(nseq)], axis=0).T
        for k in range(parts)
    ]
    response = jnp.concatenate(turned, axis=0)
    hidden_ref[...] = gelu(response).astype(bf16)
    pos = place_ref[DOCS] + lax.broadcasted_iota(jnp.int32, (group, D), 0)
    total = jnp.zeros((group, D), jnp.int32)
    for k in range(DOCS):
        total = total + (pos >= place_ref[k]).astype(jnp.int32)
    back = jnp.where(total < DOCS - 1, cot_ref[...].astype(f32), 0.0)
    back_ref[...] = back.astype(bf16)
    put_small(small_ref, 2 * G + FF, column_sum(back))
    small_ref[36:40, :] = jnp.zeros((4, CH), f32)
    inner = side.at[:, pl.ds(0, devices * 8), :]
    pltpu.make_async_copy(inner, inner, sems.at[1]).wait()
    side[0, devices * 8:, :] = jnp.zeros((8, CH), f32)
    flat[:8, :] = side[0, :8, :]

    def join(j, _):
        at = start_of(j)
        step = start_of(j + 1) - at
        far = jnp.broadcast_to(step, (8, CH)) > base
        here = pl.ds(pl.multiple_of(j * 8, 8), 8)
        one, two, then = side[1, here, :], side[2, here, :], side[0, pl.ds(pl.multiple_of(j * 8 + 8, 8), 8), :]
        flat[pl.ds(pl.multiple_of((at + base) * 8, 8), 8), :] = one + jnp.where(far, 0.0, then)
        flat[pl.ds(pl.multiple_of((at + step) * 8, 8), 8), :] = jnp.where(far, two, one) + then
        return 0

    lax.fori_loop(0, devices, join, 0)

    some = flat.at[pl.ds(0, inside * 8), :]
    pltpu.make_async_copy(some, some, sems.at[0]).wait()
    lead_ref[...] = flat[:MODE_TILES * 8, :]
    narrow(flat, gate, GATE_AT, D, G // CH)
    gate_bias = small_row(flat, SMALL_AT[0], 0, G)
    second_gain = small_row(flat, SMALL_AT[1], 0, D)
    second_bias = small_row(flat, SMALL_AT[1], D, D)
    hidden = hidden_ref[...]
    linear = product(hidden, gate[:, :D], 1, 0) + gate_bias[:, :D]
    gating = jax.nn.sigmoid(product(hidden, gate[:, D:], 1, 0) + gate_bias[:, D:])
    mid = x_ref[...].astype(f32) + linear * gating
    hat, scale = normalize(mid)
    normed_ref[...] = (hat * second_gain + second_bias).astype(bf16)
    narrow(flat, expand, EXPAND_AT, D, FF // CH)
    narrow(flat, reduce, REDUCE_AT, FF, D // CH)
    dnorm[...] = jnp.zeros((group, D), f32)
    acc[...] = mid + small_row(flat, SMALL_AT[4], 0, D)
    for b in range(FF // BLOCK):
        at = slice(b * BLOCK, (b + 1) * BLOCK)
        bias = small_row(flat, SMALL_AT[2] + b * BLOCK // TILE, b * BLOCK % TILE, BLOCK)
        lifted = product(normed_ref[...], expand[:, at], 1, 0) + bias
        half = 0.5 * (1.0 + lax.erf(lifted * root_half))
        active = (lifted * half).astype(bf16)
        active_ref[:, at] = active
        slope = half + lifted * jnp.exp(-0.5 * lifted * lifted) * inv_root_two_pi
        d_lifted = (product(back_ref[...], reduce[at, :], 1, 1) * slope).astype(bf16)
        dlift_ref[:, at] = d_lifted
        put_small(small_ref, 2 * G + b * BLOCK, column_sum(d_lifted.astype(f32)))
        acc[...] += product(active, reduce[at, :], 1, 0)
        dnorm[...] += product(d_lifted, expand[:, at], 1, 1)
    out_ref[...] = acc[...].astype(bf16)
    d_normed = dnorm[...]
    put_small(small_ref, G, column_sum(d_normed * hat))
    put_small(small_ref, G + D, column_sum(d_normed))
    d_mid = back_ref[...].astype(f32) + norm_back(d_normed * second_gain, hat, scale)
    dmid_ref[...] = d_mid
    d_linear = (d_mid * gating).astype(bf16)
    d_gating = (d_mid * linear * gating * (1.0 - gating)).astype(bf16)
    dopen_ref[:, :D] = d_linear
    dopen_ref[:, D:] = d_gating
    put_small(small_ref, 0, column_sum(d_linear.astype(f32)))
    put_small(small_ref, D, column_sum(d_gating.astype(f32)))
    d_hidden = product(d_linear, gate[:, :D], 1, 1) + product(d_gating, gate[:, D:], 1, 1)
    for k in range(parts):
        again = jnp.concatenate([resp_ref[pl.ds((d * parts + k) * nch, nch), :] for d in range(nseq)], axis=0)
        back_turned = d_hidden[k * CH:(k + 1) * CH].T * gelu_slope(again)
        for d in range(nseq):
            dresp_ref[pl.ds((d * parts + k) * nch, nch), :] = back_turned[d * nch:(d + 1) * nch]

    flat[:MODE_TILES * 8, :] = jnp.zeros((MODE_TILES * 8, CH), f32)
    for k, tile in enumerate(SMALL_AT):
        flat[tile * 8:(tile + 1) * 8, :] = small_ref[k * 8:(k + 1) * 8, :]
    flat[(SMALL_AT[-1] + 1) * 8:, :] = jnp.zeros((flat.shape[0] - (SMALL_AT[-1] + 1) * 8, CH), f32)
    sent = 0
    for first, left, right, per, until in (
        (GATE_AT, hidden_ref, dopen_ref, G // CH, EXPAND_AT),
        (EXPAND_AT, normed_ref, dlift_ref, FF // CH, REDUCE_AT),
        (REDUCE_AT, active_ref, back_ref, D // CH, flat.shape[0]),
    ):
        flip = left[...].T
        for k in range(left.shape[1] // CH):
            v = product(flip[k * CH:(k + 1) * CH], right[...], 1, 0)
            for c in range(per):
                flat[pl.ds(first * 8 + k * CH * per + c, CH, stride=per), :] = v[:, c * CH:(c + 1) * CH]
        ready = sum((j * share) // TILE + box <= until for j in range(devices))
        for k, (low, high) in enumerate(plan):
            rows = (high - low) * 8

            def send(j, _, k=k, low=low, rows=rows):
                slot = slots[k * devices + j]
                block = flat.at[pl.ds(pl.multiple_of((start_of(j) + low) * 8, 8), rows), :]
                for o in range(ways):
                    at = slot - o * (devices // ways)

                    @pl.when((at >= 0) & (at < devices // ways))
                    def _():
                        target = outs[k * ways + o].at[pl.ds(pl.multiple_of(at * rows, 8), rows), :]
                        pltpu.make_async_copy(block, target, out_sems.at[k * ways + o]).start()

                return 0

            lax.fori_loop(sent, ready, send, 0)
        sent = ready
    for k, out in enumerate(outs):
        pltpu.make_async_copy(out, out, out_sems.at[k]).wait()


def mlp_kernel(place, streams, ids, boxes, plan, slots, response, rows, cotangent, share, devices, nseq):
    base, box, tiles = lay(share, devices)
    group = rows.shape[0]
    vm = pl.BlockSpec(memory_space=pltpu.VMEM)
    hbm = pl.BlockSpec(memory_space=pl.ANY)
    smem = pl.BlockSpec(memory_space=pltpu.SMEM)
    shape = lambda r, c, t: jax.ShapeDtypeStruct((r, c), t)
    count = 2 if len(plan) > 1 else 1
    packed = [shape(devices // count * (high - low) * 8, CH, f32) for low, high in plan for _ in range(count)]
    return pl.pallas_call(
        partial(mlp_body, share, devices, nseq, streams, plan),
        out_shape=(
            shape(group, D, bf16),
            shape(group, D, f32),
            jax.ShapeDtypeStruct(response.shape, f32),
            shape(MODE_TILES * 8, CH, f32),
            *packed,
        ),
        in_specs=[smem] * 3 + [hbm] * len(boxes) + [vm] * 3,
        out_specs=(vm,) * 4 + (hbm,) * len(packed),
        scratch_shapes=[
            pltpu.VMEM((len(SMALL_AT) * 8, CH), f32),
            pltpu.VMEM((group, D), bf16),
            pltpu.VMEM((group, FF), bf16),
            pltpu.VMEM((group, D), bf16),
            pltpu.VMEM((group, D), bf16),
            pltpu.VMEM((group, G), bf16),
            pltpu.VMEM((group, FF), bf16),
            pltpu.VMEM((tiles * 8, CH), f32),
            pltpu.VMEM((3, devices * 8 + 8, CH), f32),
            pltpu.VMEM((D, G), bf16),
            pltpu.VMEM((D, FF), bf16),
            pltpu.VMEM((FF, D), bf16),
            pltpu.VMEM((group, D), f32),
            pltpu.VMEM((group, D), f32),
            pltpu.SemaphoreType.DMA((2,)),
            pltpu.SemaphoreType.DMA((len(packed),)),
        ],
        cost_estimate=pl.CostEstimate(flops=int(2.0e10), bytes_accessed=30 * 2**20, transcendentals=0),
        name="feed_forward",
    )(place, ids, slots, *boxes, response, rows, cotangent)


AXES = ("seq", "batch")
PAIR = [(0, 1), (1, 0)]


def hop(v, step):
    return lax.ppermute(v, "seq", [(i, i ^ step) for i in range(16)])


def swap_cores(v):
    return lax.ppermute(v, "batch", PAIR)


def direct():
    return lax.axis_size("seq") == 16 and lax.axis_size("batch") == 2


def device_index():
    return lax.axis_index("seq") * lax.axis_size("batch") + lax.axis_index("batch")


def places_of(steps, other):
    seq, batch = lax.axis_index("seq"), lax.axis_index("batch")
    return 2 * (seq ^ np.asarray(steps, np.int32)) + (batch ^ other)


def cuts_of(tiles):
    one = round(tiles * (1.0 - Z_FIRST) / 2)
    return one, 2 * one


def container(master, share, devices):
    _, tiles, _ = lay(share, devices)
    box = lax.dynamic_update_slice(jnp.zeros((tiles * TILE,), f32), master, (device_index() * share % TILE,))
    return box.reshape(tiles * 8, CH)


def gather_near(box):
    half = box.shape[0] // 16 * 8
    sets = [box] + [hop(box, step) for step in (4, 8, 12)]
    return [jnp.concatenate([v[at] for v in sets]) for at in (slice(0, half), slice(half, None))]


def gather_plane(near):
    return [jnp.concatenate([near[0], hop(near[0], 1)]), jnp.concatenate([near[1], hop(near[1], 2)])]


def gather_cores(plane, far, tiles):
    half = tiles // 2
    arrays, streams, ids = [], [], []
    for v, first, second in ((plane[0], 0, 1), (plane[1], 0, 2), (far[0], 2, 3), (far[1], 1, 3)):
        for other in range(2):
            arrays.append(swap_cores(v) if other else v)
            streams.append(((0, half) if len(arrays) % 4 in (1, 2) else (half, tiles)) + (8 * len(ids), 8))
            ids.append(places_of([4 * z + p for p in (first, second) for z in range(4)], other))
    return tuple(streams), jnp.concatenate(ids).astype(jnp.int32), arrays


def scatter_plan(share, devices):
    _, tiles, _ = lay(share, devices)
    if not direct():
        return ((0, tiles),), jnp.arange(devices, dtype=jnp.int32)
    one, two = cuts_of(tiles)
    index = np.arange(devices, dtype=np.int32)
    step, other = index // 2 ^ lax.axis_index("seq"), index % 2 ^ lax.axis_index("batch")
    slots = []
    for bits in ((1, 2, 8, 4), (2, 1, 8, 4), (8, 4, 2, 1)):
        at = 16 * other
        for k, bit in enumerate(bits[::-1]):
            at = at + jnp.where(step & bit != 0, 1 << k, 0)
        slots.append(at)
    return ((0, one), (one, two), (two, tiles)), jnp.concatenate(slots).astype(jnp.int32)


def pieces(v, count):
    return v.reshape(count, -1, CH)


def halve(two, step):
    return pieces(two[0] + hop(two[1], step), 2)


def join_cores(arrays):
    sums = []
    for own, far in zip(arrays[::2], arrays[1::2]):
        own, far = pieces(own, 2), pieces(swap_cores(far), 2)
        sums.append([own[k] + far[k] for k in range(2)])
    return sums


def join_first(sums):
    return [halve(v, step) for v, step in zip(sums, (1, 2, 8))]


def join_second(sums):
    return [halve(v, step) for v, step in zip(sums, (2, 1, 4))]


def join_last(sums):
    rows = [pieces(v.reshape(-1, CH), 4) for v in sums[:2]]
    four = [jnp.concatenate([v[k] for v in rows]) for k in range(4)]
    near = halve(sums[2], 2)
    one = four[0] + hop(four[1], 4) + hop(four[2], 8) + hop(four[3], 12)
    return jnp.concatenate([one, near[0] + hop(near[1], 1)])


MODE_ROWS = 65


def scatter_modes(master):
    other = swap_cores(master)
    even = lax.axis_index("batch") == 0
    lead = jnp.concatenate([jnp.where(even, master, other), jnp.where(even, other, master)])[:MODE_TILES * TILE]
    small = lead[:4 * D].reshape(4, 16, 32).transpose(1, 0, 2).reshape(16, 1, CH)
    rest = lead[4 * D:].reshape(4, 16, 16, CH).transpose(1, 0, 2, 3).reshape(16, 64, CH)
    blocks = jnp.concatenate([small, rest], axis=1)
    seq = lax.axis_index("seq")
    blocks = blocks.reshape(2, 2, 2, 2, MODE_ROWS, CH).transpose(3, 2, 1, 0, 4, 5)
    for step in (1, 2, 4, 8):
        come = lax.ppermute(blocks[1], "seq", [(i, i + step) for i in range(step)])
        blocks = jnp.where(seq & step == 0, blocks[0], come)
    return blocks


def read_modes(block):
    nch = D // 16
    small = block[0].reshape(4, nch)
    rest = block[1:].reshape(4, nch, NSTATE)
    return small, rest


def gather_modes(block, steps):
    for step in steps:
        pairs = [(i, i - step) for i in range(2 * step) if i >= step]
        block = jnp.concatenate([block, lax.ppermute(block, "seq", pairs)])
    return block


def mode_vector(block):
    blocks = block.reshape(2, 2, 2, 2, MODE_ROWS, CH).transpose(3, 2, 1, 0, 4, 5).reshape(16, MODE_ROWS, CH)
    lead = blocks[:, 0].reshape(16, 4, 32).transpose(1, 0, 2).reshape(-1)
    tail = blocks[:, 1:].reshape(16, 4, 16, CH).transpose(1, 0, 2, 3).reshape(-1)
    return jnp.concatenate([lead, tail])


def total_of(v):
    if not direct():
        return lax.psum(v, AXES)
    terms = lax.all_to_all(jnp.broadcast_to(v, (32, 8, CH)), AXES, 0, 0)
    return jnp.sum(terms[:, 0, 0])


def to_channels(rows):
    seq = lax.axis_size("seq")
    parts = rows.shape[0] // CH
    turned = rows.reshape(parts, CH, seq, D // seq).transpose(2, 0, 3, 1)
    return lax.all_to_all(turned, "seq", 0, 0).reshape(-1, CH)


def to_tokens(rows, group):
    seq = lax.axis_size("seq")
    turned = lax.all_to_all(rows.reshape(seq, group // CH, D // seq, CH), "seq", 0, 0)
    return turned.transpose(1, 3, 0, 2).reshape(group, D)


def per_device(inputs, cotangent, lengths, master, first_moment, second_moment):
    seq, batch = lax.axis_size("seq"), lax.axis_size("batch")
    devices = seq * batch
    share = master.shape[0]
    box = container(master, share, devices)
    if direct():
        near = gather_near(box)
    else:
        streams, ids = ((0, box.shape[0] // 8, 0, devices),), jnp.arange(devices, dtype=jnp.int32)
        boxes = [lax.all_gather(box, AXES, axis=0, tiled=True)]
    group = inputs.shape[1]
    nch, nck = D // seq, seq * group // CH
    rows = inputs[0].astype(jnp.float32)
    ends = jnp.cumsum(lengths[0]).astype(jnp.int32)
    place = jnp.concatenate([ends, lax.axis_index("seq")[None] * group]).astype(jnp.int32)
    first_hat, first_scale = normalize(rows)
    hats = to_channels(first_hat)

    plan, slots = scatter_plan(share, devices)

    def feed_forward(response):
        return mlp_kernel(place, streams, ids, boxes, plan, slots, response, inputs[0], cotangent[0], share, devices, seq)

    if direct():
        few, many = read_modes(scatter_modes(master))
    else:
        lead = jnp.concatenate([lax.dynamic_slice(boxes[0][j * box.shape[0]:(j + 1) * box.shape[0]].reshape(-1), (j * share % TILE,), (share,)) for j in range(MODE_TILES * TILE // share + 1)])
        mine = lambda v: lax.dynamic_slice_in_dim(v, lax.axis_index("seq") * nch, nch, 1)
        few = mine(lead[:4 * D].reshape(4, D))
        many = mine(lead[4 * D:MODE_TILES * TILE].reshape(4, D, NSTATE))
    if direct():
        plane = gather_plane(near)
    modes, modes_pull = jax.vjp(mixing, few[2], many[0], many[1], many[2], many[3])
    prm = mode_rows(*modes, few[0], few[1], few[3])
    outs, prior, *tables = ssm_forward(ends, prm, hats, nck, nch)
    response = lax.all_to_all(outs.reshape(seq, -1, nch, CH), "seq", 0, 0).reshape(-1, CH)
    if direct():
        far = [hop(plane[0], 2), hop(plane[1], 1)]
        response, far = lax.optimization_barrier((response, far))
        streams, ids, boxes = gather_cores(plane, far, box.shape[0] // 8)
    output, d_mid, d_response, lead, *packed = feed_forward(response)
    d_outs = lax.all_to_all(d_response.reshape(seq, -1, nch, CH), "seq", 0, 0).reshape(-1, CH)
    if direct():
        packed = join_cores(packed)
        d_outs, packed = lax.optimization_barrier((d_outs, packed))
    d_signals, sums = ssm_backward(ends, prm, hats, d_outs, prior, tables, nck, nch)
    if direct():
        d_signals, sums, packed = lax.optimization_barrier((d_signals, sums, join_first(packed)))
    d_signal = to_tokens(d_signals, group)
    norm_gain = lead[:D // CH].reshape(D)
    lane_sums = jnp.sum(sums[10:13], axis=-1)
    d_modes = modes_pull(mode_grads(sums, *modes))
    few = jnp.stack([lane_sums[1], lane_sums[2], d_modes[0], lane_sums[0]])
    many = jnp.stack(d_modes[1:])
    me = device_index()
    if direct():
        own = jnp.concatenate([few.reshape(1, CH), many.reshape(64, CH)])
        own, packed = lax.optimization_barrier((own + swap_cores(own), join_second(packed)))
        box, block, d_signal = lax.optimization_barrier((join_last(packed), gather_modes(own, (8, 4, 2)), d_signal))
    else:
        box = lax.psum_scatter(packed[0].reshape(devices, -1, CH), AXES, scatter_dimension=0)
    d_rows = d_mid + norm_back(d_signal * norm_gain, first_hat, first_scale)
    shard = lax.dynamic_slice(box.reshape(-1), (me * share % TILE,), (share,))
    mark = me * share + jnp.arange(share, dtype=jnp.int32) < MODE_TILES * TILE
    squares = jnp.sum(jnp.where(mark, 0.0, shard * shard))
    if direct():
        squares = squares + 0.5 * jnp.sum(own * own)
        lead = mode_vector(gather_modes(block, (1,)))
    else:

        def spread(v):
            whole = jnp.zeros((v.shape[0], D) + v.shape[2:], f32)
            return lax.dynamic_update_slice_in_dim(whole, v, lax.axis_index("seq") * nch, 1)

        lead = lax.psum(jnp.concatenate([spread(few).reshape(-1), spread(many).reshape(-1)]), AXES)
        squares = squares + jnp.sum(lead * lead) / devices
    lead = lax.dynamic_slice(jnp.pad(lead, (0, share)), (jnp.minimum(me * share, MODE_TILES * TILE),), (share,))
    shard = jnp.where(mark, lead, shard)
    total = total_of(squares)
    grad_norm = jnp.sqrt(total)
    factor = jnp.minimum(1.0, 1.0 / (grad_norm + 1e-06))
    clipped = shard * factor
    first_new = 0.9 * first_moment + 0.1 * clipped
    second_new = 0.999 * second_moment + 0.001 * clipped * clipped
    first_hat_new = first_new / (1.0 - 0.9**10)
    second_hat_new = second_new / (1.0 - 0.999**10)
    update = -0.05 * (first_hat_new / (jnp.sqrt(second_hat_new) + 1e-08) + 0.1 * master)
    return (output[None], d_rows[None], shard, update, first_new, second_new, grad_norm)


def solution(mesh):
    placed = (
        P("batch", "seq", None),
        P("batch", "seq", None),
        P("batch", None),
        P(("seq", "batch")),
        P(("seq", "batch")),
        P(("seq", "batch")),
    )
    return jax.shard_map(
        per_device,
        mesh=mesh,
        in_specs=placed,
        out_specs=(
            P("batch", "seq", None),
            P("batch", "seq", None),
            P(("seq", "batch")),
            P(("seq", "batch")),
            P(("seq", "batch")),
            P(("seq", "batch")),
            P(),
        ),
        check_vma=False,
    )
```

```python
from functools import partial
import jax
import jax.numpy as jnp
import numpy as np
from jax import lax
from jax.experimental import pallas as pl
from jax.experimental.pallas import tpu as pltpu
from jax.sharding import PartitionSpec as P

D = 512
NSTATE = 64
CH = 128
DOCS = 4
G = 1024
FF = 2048
Z_FIRST = 0.2


norm_eps = 1e-05
root_half = 0.7071067811865476
inv_root_two_pi = 0.3989422804014327


f32 = jnp.float32
bf16 = jnp.bfloat16

def split(v):
    hi = v.astype(bf16)
    return hi, (v - hi.astype(f32)).astype(bf16)

def dot3(a, b, ca, cb):
    ah, al = a
    bh, bl = b
    lhs = jnp.concatenate([ah, ah, al], axis=ca)
    rhs = jnp.concatenate([bh, bl, bh], axis=cb)
    return lax.dot_general(lhs, rhs, (((ca,), (cb,)), ((), ())), preferred_element_type=f32)

def dot2(data, table, ct):
    return dot3(data, (table[0], table[1]), 1, ct)

def swap(v):
    return pltpu.roll(v, NSTATE, 1)

def twist(table, re, im):
    return re * table + im * swap(table)

def ladder(prm, order):
    sub = lax.broadcasted_iota(jnp.int32, (8, 2 * NSTATE), 0)
    lane = lax.broadcasted_iota(jnp.int32, (8, 2 * NSTATE), 1)
    power = sub if order == 1 else 7 - sub
    table = jnp.where(lane < NSTATE, 1.0, 0.0).astype(f32)
    for bit in range(3):
        table = jnp.where((power >> bit) & 1 == 1, twist(table, prm[2 * bit:2 * bit + 1], prm[2 * bit + 1:2 * bit + 2]), table)
    for bit in range(3, 7):
        more = twist(table, prm[2 * bit:2 * bit + 1], prm[2 * bit + 1:2 * bit + 2])
        table = jnp.concatenate([table, more] if order == 1 else [more, table], axis=0)
    return table

def toeplitz(taps):
    wide = pltpu.roll(jnp.broadcast_to(taps, (CH, CH)), 0, 1, stride=1, stride_axis=0)
    row = lax.broadcasted_iota(jnp.int32, (CH, CH), 0)
    col = lax.broadcasted_iota(jnp.int32, (CH, CH), 1)
    return jnp.where(col >= row, wide, 0.0)

def label_at(ends, pos):
    total = jnp.zeros_like(pos)
    for k in range(DOCS):
        total = total + (pos >= ends[k]).astype(jnp.int32)
    return total

def make_masks(ends_ref, masks_ref, low_ref, nck):
    ends = [ends_ref[k] for k in range(DOCS)]
    row = lax.broadcasted_iota(jnp.int32, (nck, CH), 0)
    lane = lax.broadcasted_iota(jnp.int32, (nck, CH), 1)
    base = row * CH
    label = label_at(ends, base + lane)
    prev = jnp.where(base == 0, -1, label_at(ends, base - 1))
    last = label_at(ends, base + CH - 1)
    for k in range(DOCS):
        masks_ref[k] = (label == k).astype(f32)
    masks_ref[DOCS] = (label == prev).astype(f32)
    masks_ref[DOCS + 1] = (label == last).astype(f32)
    low_ref[:DOCS + 2] = masks_ref[...].astype(bf16)
    if low_ref.shape[0] > DOCS + 2:
        label = label_at(ends, base + (CH - 1 - lane))
        for k in range(DOCS):
            low_ref[DOCS + 2 + k] = (label == k).astype(f32).astype(bf16)

def keep_of(ends_ref, c):
    first = jnp.int32(0)
    second = jnp.int32(0)
    for k in range(DOCS):
        first = first + (c * CH - 1 >= ends_ref[k]).astype(jnp.int32)
        second = second + (c * CH + CH - 1 >= ends_ref[k]).astype(jnp.int32)
    return jnp.where((c > 0) & (first == second), 1.0, 0.0).astype(f32)

def masked_rows(v, low_ref):
    return [jnp.concatenate([part * low_ref[k] for k in range(DOCS)], axis=0) for part in v]

def masked(v, low_ref, k):
    return [part * low_ref[k] for part in v]

def fold_rows(v, masks_ref, nck):
    total = v[:nck] * masks_ref[0]
    for k in range(1, DOCS):
        total = total + v[k * nck:(k + 1) * nck] * masks_ref[k]
    return total

def keep(ref, h, v):
    ref[h, 0], ref[h, 1] = split(v)

def for_channels(nch, body):
    lax.fori_loop(0, nch, lambda h, _: body(h) or 0, 0, unroll=min(nch, 16))

def fwd_body(nck, nch, apart, ends_ref, prm_ref, x_ref, y_ref, prior_ref, table_ref, down_ref, out_ref, mat_ref, masks_ref, low_ref, end_ref):
    make_masks(ends_ref, masks_ref, low_ref, nck)

    def tables(h):
        prm = prm_ref[h]
        table = ladder(prm, 1)
        keep(table_ref, h, table)
        keep(out_ref, h, twist(table, prm[17:18], prm[18:19]))

    def falling(h):
        keep(down_ref, h, ladder(prm_ref[h], -1))

    def taps(h):
        wrow = jnp.broadcast_to(prm_ref[h, 16:17, :], (16, 2 * NSTATE))
        keep(mat_ref, h, toeplitz(dot2(split(wrow), table_ref[h], 1)[0:1]))

    def local(h):
        prm = prm_ref[h, 16:24, :]
        u = x_ref[pl.ds(h, nck, stride=apart), :] * prm[3:4] + prm[4:5]
        parts = split(u)
        local = dot2(masked_rows(parts, low_ref), mat_ref[h], 0)
        y_ref[pl.ds(h, nck, stride=nch), :] = fold_rows(local, masks_ref, nck) + prm[5:6] * u
        end_ref[pl.ds(h, nck, stride=nch), :] = dot2(masked(parts, low_ref, DOCS + 1), down_ref[h], 0)

    for body in (tables, falling, taps, local):
        for_channels(nch, body)
    full_re = prm_ref[:, 14, :]
    full_im = prm_ref[:, 15, :]

    def step(c, state):
        at = pl.ds(pl.multiple_of(c * nch, 8), nch)
        prior_ref[at, :] = state
        return keep_of(ends_ref, c) * twist(state, full_re, full_im) + end_ref[at, :]

    lax.fori_loop(0, nck, step, jnp.zeros((nch, 2 * NSTATE), f32))

    def carried(h):
        prior = split(prior_ref[pl.ds(h, nck, stride=nch), :])
        y_ref[pl.ds(h, nck, stride=nch), :] += dot2(prior, out_ref[h], 1) * masks_ref[DOCS]

    for_channels(nch, carried)

def ssm_forward(ends, prm, x, nck, nch):
    vm = pl.BlockSpec(memory_space=pltpu.VMEM)
    table = jax.ShapeDtypeStruct((nch, 2, CH, 2 * NSTATE), bf16)
    return pl.pallas_call(
        partial(fwd_body, nck, nch, x.shape[0] // nck),
        out_shape=(jax.ShapeDtypeStruct((nck * nch, CH), f32), jax.ShapeDtypeStruct((nck * nch, 2 * NSTATE), f32)) + (table,) * 4,
        in_specs=[pl.BlockSpec(memory_space=pltpu.SMEM), vm, vm],
        out_specs=(vm,) * 6,
        scratch_shapes=[
            pltpu.VMEM((DOCS + 2, nck, CH), f32),
            pltpu.VMEM((DOCS + 2, nck, CH), bf16),
            pltpu.VMEM((nck * nch, 2 * NSTATE), f32),
        ],
        cost_estimate=pl.CostEstimate(flops=int(2.0e10), bytes_accessed=3 * 2**20, transcendentals=0),
        name="state_forward",
    )(ends, prm, x)

def bwd_body(nck, nch, apart, ends_ref, prm_ref, x_ref, g_ref, prior_ref, table_ref, down_ref, out_ref, mat_ref, coef_ref, dx_ref, grad_ref, rows_ref, masks_ref, low_ref, lead_ref, adj_ref, taps_ref):
    make_masks(ends_ref, masks_ref, low_ref, nck)
    at_channel = lambda h: pl.ds(h, nck, stride=nch)

    def lead(h):
        lead_ref[at_channel(h), :] = dot2(masked(split(g_ref[at_channel(h), :]), low_ref, DOCS), out_ref[h], 0)

    for_channels(nch, lead)
    full_re = prm_ref[:, 14, :]
    full_im = prm_ref[:, 15, :]
    zero = jnp.zeros((nch, 2 * NSTATE), f32)

    def step(k, carry):
        adjoint, same, cross = carry
        c = nck - 1 - k
        at = pl.ds(pl.multiple_of(c * nch, 8), nch)
        adj_ref[at, :] = adjoint
        keep = keep_of(ends_ref, c)
        prior = prior_ref[at, :]
        same = same + keep * adjoint * prior
        cross = cross + keep * adjoint * swap(prior)
        adjoint = lead_ref[at, :] + keep * (full_re * adjoint - full_im * swap(adjoint))
        return adjoint, same, cross

    _, same, cross = lax.fori_loop(0, nck, step, (zero, zero, zero))
    rows_ref[8] = same
    rows_ref[9] = cross
    row = lax.broadcasted_iota(jnp.int32, (CH, CH), 0)
    col = lax.broadcasted_iota(jnp.int32, (CH, CH), 1)
    flip = (row + col == CH - 1).astype(f32).astype(bf16)
    put = lambda k, h, v: rows_ref.__setitem__((k, pl.ds(h, 1), slice(None)), jnp.sum(v, axis=0, keepdims=True))

    def signal(h):
        prm = prm_ref[h, 16:24, :]
        x = x_ref[pl.ds(h, nck, stride=apart), :]
        g = g_ref[at_channel(h), :]
        du = fold_rows(dot2(masked_rows(split(g), low_ref), mat_ref[h], 1), masks_ref, nck)
        du = du + dot2(split(adj_ref[at_channel(h), :]), down_ref[h], 1) * masks_ref[DOCS + 1]
        du = du + prm[5:6] * g
        dx_ref[at_channel(h), :] = du
        put(10, h, g * (x * prm[3:4] + prm[4:5]))
        put(11, h, du * x)
        put(12, h, du)

    def taps(h):
        prm = prm_ref[h, 16:24, :]
        u = split(x_ref[pl.ds(h, nck, stride=apart), :] * prm[3:4] + prm[4:5])
        both = jnp.dot(jnp.concatenate(u, axis=0), flip, preferred_element_type=f32).astype(bf16)
        um = []
        for part in (both[:nck], both[nck:]):
            um.append(jnp.concatenate([part * low_ref[DOCS + 2 + k] for k in range(DOCS)], axis=0))
        square = dot3(um, masked_rows(split(g_ref[at_channel(h), :]), low_ref), 0, 0)
        square = jnp.where(row + col >= CH - 1, square, 0.0)
        square = pltpu.roll(square, 1, 1, stride=1, stride_axis=0)
        taps_ref[pl.ds(h, 1), :] = jnp.sum(square, axis=0, keepdims=True)

    def kernel(h):
        place = lax.broadcasted_iota(jnp.int32, (16, CH), 1).astype(f32)
        sub = lax.broadcasted_iota(jnp.int32, (16, CH), 0)
        both = jnp.where(sub == 0, 1.0, jnp.where(sub == 1, place, 0.0)) * taps_ref[pl.ds(h, 1), :]
        both = dot2(split(both), table_ref[h], 0)
        rows_ref[0, pl.ds(h, 1), :] = both[0:1]
        rows_ref[1, pl.ds(h, 1), :] = both[1:2]

    late = row.astype(f32)

    def carried(h):
        dgt = dot3(masked(split(g_ref[at_channel(h), :]), low_ref, DOCS), split(prior_ref[at_channel(h), :]), 0, 0)
        table = table_ref[h, 0].astype(f32) + table_ref[h, 1].astype(f32)
        same, cross = dgt * table, dgt * swap(table)
        put(2, h, same)
        put(3, h, cross)
        put(4, h, same * late)
        put(5, h, cross * late)

    def ending(h):
        prm = prm_ref[h, 16:24, :]
        u = split(x_ref[pl.ds(h, nck, stride=apart), :] * prm[3:4] + prm[4:5])
        ddown = dot3(masked(u, low_ref, DOCS + 1), split(adj_ref[at_channel(h), :]), 0, 0) * ((CH - 1) - late)
        down = down_ref[h, 0].astype(f32) + down_ref[h, 1].astype(f32)
        put(6, h, ddown * down)
        put(7, h, ddown * swap(down))

    for body in (signal, taps, kernel, carried, ending):
        for_channels(nch, body)
    rows = [rows_ref[k] for k in range(13)]
    total = lambda v: jnp.sum(v, axis=1, keepdims=True)
    d_step, d_decay, d_frequency, d_real, d_imag = mode_grads(rows, [coef_ref[k] for k in range(14)])
    grad_ref[0] = jnp.concatenate([d_decay, d_frequency], axis=1)
    grad_ref[1] = jnp.concatenate([d_real, d_imag], axis=1)
    lane = lax.broadcasted_iota(jnp.int32, (nch, CH), 1)
    few = jnp.zeros((nch, CH), f32)
    for k, v in enumerate((total(rows[11]), total(rows[12]), total(d_step), total(rows[10]))):
        few = jnp.where(lane == k, v, few)
    grad_ref[2] = few

def ssm_backward(ends, prm, x, g, prior, tables, coefs, nck, nch):
    vm = pl.BlockSpec(memory_space=pltpu.VMEM)
    return pl.pallas_call(
        partial(bwd_body, nck, nch, x.shape[0] // nck),
        out_shape=(jax.ShapeDtypeStruct((nck * nch, CH), f32), jax.ShapeDtypeStruct((3, nch, 2 * NSTATE), f32)),
        in_specs=[pl.BlockSpec(memory_space=pltpu.SMEM)] + [vm] * 9,
        out_specs=(vm, vm),
        scratch_shapes=[
            pltpu.VMEM((13, nch, 2 * NSTATE), f32),
            pltpu.VMEM((DOCS + 2, nck, CH), f32),
            pltpu.VMEM((2 * DOCS + 2, nck, CH), bf16),
            pltpu.VMEM((nck * nch, 2 * NSTATE), f32),
            pltpu.VMEM((nck * nch, 2 * NSTATE), f32),
            pltpu.VMEM((nch, CH), f32),
        ],
        cost_estimate=pl.CostEstimate(flops=int(3.5e10), bytes_accessed=4 * 2**20, transcendentals=0),
        name="state_backward",
    )(ends, prm, x, g, prior, *tables, coefs)

def mixing(step_log, decay_log, frequency, out_real, out_imag):
    delta = jnp.exp(step_log)[:, None]
    rate_re = -jnp.exp(decay_log)
    arg_re, arg_im = delta * rate_re, delta * frequency
    magnitude = jnp.exp(arg_re)
    p_re, p_im = magnitude * jnp.cos(arg_im), magnitude * jnp.sin(arg_im)
    inverse = 1.0 / (rate_re * rate_re + frequency * frequency)
    ratio_re = ((p_re - 1.0) * rate_re + p_im * frequency) * inverse
    ratio_im = (p_im * rate_re - (p_re - 1.0) * frequency) * inverse
    mix_re = out_real * ratio_re - out_imag * ratio_im
    mix_im = out_real * ratio_im + out_imag * ratio_re
    magnitude = jnp.exp(arg_re * CH)
    f_re, f_im = magnitude * jnp.cos(arg_im * CH), magnitude * jnp.sin(arg_im * CH)
    wide = jnp.broadcast_to(delta, arg_re.shape)
    coefs = jnp.stack([p_re, p_im, f_re, f_im, mix_re, mix_im, out_real, out_imag, ratio_re, ratio_im, rate_re, frequency, inverse, wide])
    return (arg_re, arg_im, mix_re, mix_im), coefs

def pair(left, right):
    return jnp.concatenate([left, right], axis=-1)

def mode_rows(arg_re, arg_im, mix_re, mix_im, gain, bias, skip):
    nch = arg_re.shape[0]
    scale = jnp.asarray([2.0**b for b in range(8)], f32)[None, :, None]
    magnitude = jnp.exp(arg_re[:, None] * scale)
    p_re = magnitude * jnp.cos(arg_im[:, None] * scale)
    p_im = magnitude * jnp.sin(arg_im[:, None] * scale)
    powers = jnp.stack([pair(p_re, p_re), pair(-p_im, p_im)], axis=2).reshape(nch, 16, 2 * NSTATE)
    c_re = mix_re * p_re[:, 0] - mix_im * p_im[:, 0]
    c_im = mix_re * p_im[:, 0] + mix_im * p_re[:, 0]
    flat = lambda v: jnp.broadcast_to(v[:, None], (nch, 2 * NSTATE))
    rest = jnp.stack([pair(mix_re, -mix_im), pair(c_re, -c_re), pair(-c_im, -c_im), flat(gain), flat(bias), flat(skip), flat(0 * gain), flat(0 * gain)], axis=1)
    return jnp.concatenate([powers, rest], axis=1)

def mode_grads(rows, coefs):
    p_re, p_im, f_re, f_im, mix_re, mix_im, out_real, out_imag, ratio_re, ratio_im, rate, freq, inverse, delta = coefs
    lo = [v[:, :NSTATE] for v in rows]
    hi = [v[:, NSTATE:] for v in rows]
    a_re, a_im = lo[2] - hi[2], -(hi[3] + lo[3])
    b_re, b_im = lo[4] - hi[4] + a_re, a_im - (hi[5] + lo[5])
    w_re = lo[0] + p_re * a_re + p_im * a_im
    w_im = -hi[0] + p_re * a_im - p_im * a_re
    v_re = lo[1] + p_re * b_re + p_im * b_im
    v_im = -hi[1] + p_re * b_im - p_im * b_re
    d_re, d_im = lo[8] + hi[8], hi[9] - lo[9]
    g_re = mix_re * v_re + mix_im * v_im + lo[6] + hi[6] + CH * (f_re * d_re + f_im * d_im)
    g_im = mix_re * v_im - mix_im * v_re + hi[7] - lo[7] + CH * (f_re * d_im - f_im * d_re)
    d_real, d_imag = w_re * ratio_re + w_im * ratio_im, w_im * ratio_re - w_re * ratio_im
    r_re = (w_re * out_real + w_im * out_imag) * inverse
    r_im = (w_im * out_real - w_re * out_imag) * inverse
    fall = 2.0 * (r_re * ratio_re + r_im * ratio_im)
    pole_re = r_re * rate - r_im * freq
    pole_im = r_re * freq + r_im * rate
    d_rate = r_re * (p_re - 1.0) + r_im * p_im - fall * rate
    d_freq = r_re * p_im - r_im * (p_re - 1.0) - fall * freq
    g_re = g_re + pole_re * p_re + pole_im * p_im
    g_im = g_im + pole_im * p_re - pole_re * p_im
    d_step = delta * (rate * g_re + freq * g_im)
    return d_step, (d_rate + delta * g_re) * rate, d_freq + delta * g_im, d_real, d_imag


def gelu(values):
    return 0.5 * values * (1.0 + lax.erf(values * root_half))


def gelu_slope(values):
    return (
        0.5 * (1.0 + lax.erf(values * root_half))
        + values * jnp.exp(-0.5 * values * values) * inv_root_two_pi
    )


def normalize(values):
    center = values - jnp.mean(values, axis=-1, keepdims=True)
    scale = lax.rsqrt(jnp.mean(center * center, axis=-1, keepdims=True) + norm_eps)
    return (center * scale, scale)


def norm_back(d_hat, hat, scale):
    return scale * (
        d_hat
        - jnp.mean(d_hat, axis=-1, keepdims=True)
        - hat * jnp.mean(d_hat * hat, axis=-1, keepdims=True)
    )


TILE = 1024
GATE_AT, EXPAND_AT, REDUCE_AT = 130, 644, 1670
SMALL_AT = (642, 643, 1668, 1669, 2694)
MODE_TILES = 130
BLOCK = 512


def lay(share, devices):
    base = share // TILE
    return base, base + 2, (devices - 1) * share // TILE + base + 2


def product(a, b, ca, cb):
    return lax.dot_general(a, b, (((ca,), (cb,)), ((), ())), preferred_element_type=f32)


def narrow(flat, out, first, rows, per):
    def one(i, _):
        for k in range(per):
            v = flat[pl.ds(first * 8 + i * 16 * per + k, 16, stride=per), :]
            out[pl.ds(pl.multiple_of(i * 16, 16), 16), k * CH:(k + 1) * CH] = v.astype(bf16)
        return 0

    lax.fori_loop(0, rows // 16, one, 0, unroll=max(1, 16 // per))


def small_row(flat, tile, begin, count):
    return jnp.concatenate([flat[tile * 8 + (begin + k) // CH:tile * 8 + (begin + k) // CH + 1, :] for k in range(0, count, CH)], axis=1)


def put_small(small_ref, begin, row):
    for k in range(row.shape[1] // CH):
        small_ref[begin // CH + k:begin // CH + k + 1, :] = row[:, k * CH:(k + 1) * CH]


def column_sum(v):
    return jnp.sum(v, axis=0, keepdims=True)


def mlp_body(share, devices, nseq, streams, plan, place_ref, ids, slots, *refs):
    boxes = refs[:len(streams)]
    resp_ref, x_ref, cot_ref, out_ref, dmid_ref, dresp_ref, lead_ref = refs[len(streams):len(streams) + 7]
    ways = 2 if len(plan) > 1 else 1
    outs = refs[len(streams) + 7:len(streams) + 7 + ways * len(plan)]
    small_ref, hidden_ref, active_ref, normed_ref, back_ref, dopen_ref, dlift_ref, flat, side, gate, expand, reduce, acc, dnorm, sems, out_sems = refs[len(streams) + 7 + len(outs):]
    base, box, _ = lay(share, devices)
    nch = D // nseq
    group = x_ref.shape[0]
    start_of = lambda j: (j * share) // TILE
    inside = 0
    for k, (first, last, off, count) in enumerate(streams):
        lo, hi = max(first, 1), min(last, base)

        def copy_box(i, _, k=k, first=first, last=last, lo=lo, hi=hi, off=off):
            j = ids[off + i]
            begin = (i * (last - first) - first) * 8
            for s, tile in enumerate((0, base, base + 1)):
                if first <= tile < last:
                    pltpu.make_async_copy(boxes[k].at[pl.ds(pl.multiple_of(begin + tile * 8, 8), 8), :], side.at[s, pl.ds(pl.multiple_of(j * 8, 8), 8), :], sems.at[1]).start()
            pltpu.make_async_copy(
                boxes[k].at[pl.ds(pl.multiple_of(begin + lo * 8, 8), (hi - lo) * 8), :],
                flat.at[pl.ds(pl.multiple_of((start_of(j) + lo) * 8, 8), (hi - lo) * 8), :],
                sems.at[0],
            ).start()
            return 0

        lax.fori_loop(0, count, copy_box, 0)
        inside += (hi - lo) * count
    parts = group // CH
    turned = [
        jnp.concatenate([resp_ref[pl.ds((d * parts + k) * nch, nch), :] for d in range(nseq)], axis=0).T
        for k in range(parts)
    ]
    response = jnp.concatenate(turned, axis=0)
    hidden_ref[...] = gelu(response).astype(bf16)
    pos = place_ref[DOCS] + lax.broadcasted_iota(jnp.int32, (group, D), 0)
    total = jnp.zeros((group, D), jnp.int32)
    for k in range(DOCS):
        total = total + (pos >= place_ref[k]).astype(jnp.int32)
    back = jnp.where(total < DOCS - 1, cot_ref[...].astype(f32), 0.0)
    back_ref[...] = back.astype(bf16)
    put_small(small_ref, 2 * G + FF, column_sum(back))
    small_ref[36:40, :] = jnp.zeros((4, CH), f32)
    inner = side.at[:, pl.ds(0, devices * 8), :]
    pltpu.make_async_copy(inner, inner, sems.at[1]).wait()
    side[0, devices * 8:, :] = jnp.zeros((8, CH), f32)
    flat[:8, :] = side[0, :8, :]

    def join(j, _):
        at = start_of(j)
        step = start_of(j + 1) - at
        far = jnp.broadcast_to(step, (8, CH)) > base
        here = pl.ds(pl.multiple_of(j * 8, 8), 8)
        one, two, then = side[1, here, :], side[2, here, :], side[0, pl.ds(pl.multiple_of(j * 8 + 8, 8), 8), :]
        flat[pl.ds(pl.multiple_of((at + base) * 8, 8), 8), :] = one + jnp.where(far, 0.0, then)
        flat[pl.ds(pl.multiple_of((at + step) * 8, 8), 8), :] = jnp.where(far, two, one) + then
        return 0

    lax.fori_loop(0, devices, join, 0)

    some = flat.at[pl.ds(0, inside * 8), :]
    pltpu.make_async_copy(some, some, sems.at[0]).wait()
    lead_ref[...] = flat[:MODE_TILES * 8, :]
    narrow(flat, gate, GATE_AT, D, G // CH)
    gate_bias = small_row(flat, SMALL_AT[0], 0, G)
    second_gain = small_row(flat, SMALL_AT[1], 0, D)
    second_bias = small_row(flat, SMALL_AT[1], D, D)
    hidden = hidden_ref[...]
    linear = product(hidden, gate[:, :D], 1, 0) + gate_bias[:, :D]
    gating = jax.nn.sigmoid(product(hidden, gate[:, D:], 1, 0) + gate_bias[:, D:])
    mid = x_ref[...].astype(f32) + linear * gating
    hat, scale = normalize(mid)
    normed_ref[...] = (hat * second_gain + second_bias).astype(bf16)
    narrow(flat, expand, EXPAND_AT, D, FF // CH)
    narrow(flat, reduce, REDUCE_AT, FF, D // CH)
    dnorm[...] = jnp.zeros((group, D), f32)
    acc[...] = mid + small_row(flat, SMALL_AT[4], 0, D)
    for b in range(FF // BLOCK):
        at = slice(b * BLOCK, (b + 1) * BLOCK)
        bias = small_row(flat, SMALL_AT[2] + b * BLOCK // TILE, b * BLOCK % TILE, BLOCK)
        lifted = product(normed_ref[...], expand[:, at], 1, 0) + bias
        half = 0.5 * (1.0 + lax.erf(lifted * root_half))
        active = (lifted * half).astype(bf16)
        active_ref[:, at] = active
        slope = half + lifted * jnp.exp(-0.5 * lifted * lifted) * inv_root_two_pi
        d_lifted = (product(back_ref[...], reduce[at, :], 1, 1) * slope).astype(bf16)
        dlift_ref[:, at] = d_lifted
        put_small(small_ref, 2 * G + b * BLOCK, column_sum(d_lifted.astype(f32)))
        acc[...] += product(active, reduce[at, :], 1, 0)
        dnorm[...] += product(d_lifted, expand[:, at], 1, 1)
    out_ref[...] = acc[...].astype(bf16)
    d_normed = dnorm[...]
    put_small(small_ref, G, column_sum(d_normed * hat))
    put_small(small_ref, G + D, column_sum(d_normed))
    d_mid = back_ref[...].astype(f32) + norm_back(d_normed * second_gain, hat, scale)
    dmid_ref[...] = d_mid
    d_linear = (d_mid * gating).astype(bf16)
    d_gating = (d_mid * linear * gating * (1.0 - gating)).astype(bf16)
    dopen_ref[:, :D] = d_linear
    dopen_ref[:, D:] = d_gating
    put_small(small_ref, 0, column_sum(d_linear.astype(f32)))
    put_small(small_ref, D, column_sum(d_gating.astype(f32)))
    d_hidden = product(d_linear, gate[:, :D], 1, 1) + product(d_gating, gate[:, D:], 1, 1)
    for k in range(parts):
        again = jnp.concatenate([resp_ref[pl.ds((d * parts + k) * nch, nch), :] for d in range(nseq)], axis=0)
        back_turned = d_hidden[k * CH:(k + 1) * CH].T * gelu_slope(again)
        for d in range(nseq):
            dresp_ref[pl.ds((d * parts + k) * nch, nch), :] = back_turned[d * nch:(d + 1) * nch]

    flat[:MODE_TILES * 8, :] = jnp.zeros((MODE_TILES * 8, CH), f32)
    for k, tile in enumerate(SMALL_AT):
        flat[tile * 8:(tile + 1) * 8, :] = small_ref[k * 8:(k + 1) * 8, :]
    flat[(SMALL_AT[-1] + 1) * 8:, :] = jnp.zeros((flat.shape[0] - (SMALL_AT[-1] + 1) * 8, CH), f32)
    sent = 0
    for first, left, right, per, until in (
        (GATE_AT, hidden_ref, dopen_ref, G // CH, EXPAND_AT),
        (EXPAND_AT, normed_ref, dlift_ref, FF // CH, REDUCE_AT),
        (REDUCE_AT, active_ref, back_ref, D // CH, flat.shape[0]),
    ):
        flip = left[...].T
        for k in range(left.shape[1] // CH):
            v = product(flip[k * CH:(k + 1) * CH], right[...], 1, 0)
            for c in range(per):
                flat[pl.ds(first * 8 + k * CH * per + c, CH, stride=per), :] = v[:, c * CH:(c + 1) * CH]
        ready = sum((j * share) // TILE + box <= until for j in range(devices))
        for k, (low, high) in enumerate(plan):
            rows = (high - low) * 8

            def send(j, _, k=k, low=low, rows=rows):
                slot = slots[k * devices + j]
                block = flat.at[pl.ds(pl.multiple_of((start_of(j) + low) * 8, 8), rows), :]
                for o in range(ways):
                    at = slot - o * (devices // ways)

                    @pl.when((at >= 0) & (at < devices // ways))
                    def _():
                        target = outs[k * ways + o].at[pl.ds(pl.multiple_of(at * rows, 8), rows), :]
                        pltpu.make_async_copy(block, target, out_sems.at[k * ways + o]).start()

                return 0

            lax.fori_loop(sent, ready, send, 0)
        sent = ready
    for k, out in enumerate(outs):
        pltpu.make_async_copy(out, out, out_sems.at[k]).wait()


def mlp_kernel(place, streams, ids, boxes, plan, slots, response, rows, cotangent, share, devices, nseq):
    base, box, tiles = lay(share, devices)
    group = rows.shape[0]
    vm = pl.BlockSpec(memory_space=pltpu.VMEM)
    hbm = pl.BlockSpec(memory_space=pl.ANY)
    smem = pl.BlockSpec(memory_space=pltpu.SMEM)
    shape = lambda r, c, t: jax.ShapeDtypeStruct((r, c), t)
    count = 2 if len(plan) > 1 else 1
    packed = [shape(devices // count * (high - low) * 8, CH, f32) for low, high in plan for _ in range(count)]
    return pl.pallas_call(
        partial(mlp_body, share, devices, nseq, streams, plan),
        out_shape=(
            shape(group, D, bf16),
            shape(group, D, f32),
            jax.ShapeDtypeStruct(response.shape, f32),
            shape(MODE_TILES * 8, CH, f32),
            *packed,
        ),
        in_specs=[smem] * 3 + [hbm] * len(boxes) + [vm] * 3,
        out_specs=(vm,) * 4 + (hbm,) * len(packed),
        scratch_shapes=[
            pltpu.VMEM((len(SMALL_AT) * 8, CH), f32),
            pltpu.VMEM((group, D), bf16),
            pltpu.VMEM((group, FF), bf16),
            pltpu.VMEM((group, D), bf16),
            pltpu.VMEM((group, D), bf16),
            pltpu.VMEM((group, G), bf16),
            pltpu.VMEM((group, FF), bf16),
            pltpu.VMEM((tiles * 8, CH), f32),
            pltpu.VMEM((3, devices * 8 + 8, CH), f32),
            pltpu.VMEM((D, G), bf16),
            pltpu.VMEM((D, FF), bf16),
            pltpu.VMEM((FF, D), bf16),
            pltpu.VMEM((group, D), f32),
            pltpu.VMEM((group, D), f32),
            pltpu.SemaphoreType.DMA((2,)),
            pltpu.SemaphoreType.DMA((len(packed),)),
        ],
        cost_estimate=pl.CostEstimate(flops=int(2.0e10), bytes_accessed=30 * 2**20, transcendentals=0),
        name="feed_forward",
    )(place, ids, slots, *boxes, response, rows, cotangent)


AXES = ("seq", "batch")
PAIR = [(0, 1), (1, 0)]


def hop(v, step):
    return lax.ppermute(v, "seq", [(i, i ^ step) for i in range(16)])


def swap_cores(v):
    return lax.ppermute(v, "batch", PAIR)


def direct():
    return lax.axis_size("seq") == 16 and lax.axis_size("batch") == 2


def device_index():
    return lax.axis_index("seq") * lax.axis_size("batch") + lax.axis_index("batch")


def places_of(steps, other):
    seq, batch = lax.axis_index("seq"), lax.axis_index("batch")
    return 2 * (seq ^ np.asarray(steps, np.int32)) + (batch ^ other)


def cuts_of(tiles):
    one = round(tiles * (1.0 - Z_FIRST) / 2)
    return one, 2 * one


def container(master, share, devices):
    _, tiles, _ = lay(share, devices)
    box = lax.dynamic_update_slice(jnp.zeros((tiles * TILE,), f32), master, (device_index() * share % TILE,))
    return box.reshape(tiles * 8, CH)


def gather_near(box):
    half = box.shape[0] // 16 * 8
    sets = [box] + [hop(box, step) for step in (4, 8, 12)]
    return [jnp.concatenate([v[at] for v in sets]) for at in (slice(0, half), slice(half, None))]


def gather_plane(near):
    return [jnp.concatenate([near[0], hop(near[0], 1)]), jnp.concatenate([near[1], hop(near[1], 2)])]


def gather_cores(plane, far, tiles):
    half = tiles // 2
    arrays, streams, ids = [], [], []
    for v, first, second in ((plane[0], 0, 1), (plane[1], 0, 2), (far[0], 2, 3), (far[1], 1, 3)):
        for other in range(2):
            arrays.append(swap_cores(v) if other else v)
            streams.append(((0, half) if len(arrays) % 4 in (1, 2) else (half, tiles)) + (8 * len(ids), 8))
            ids.append(places_of([4 * z + p for p in (first, second) for z in range(4)], other))
    return tuple(streams), jnp.concatenate(ids).astype(jnp.int32), arrays


def scatter_plan(share, devices):
    _, tiles, _ = lay(share, devices)
    if not direct():
        return ((0, tiles),), jnp.arange(devices, dtype=jnp.int32)
    one, two = cuts_of(tiles)
    index = np.arange(devices, dtype=np.int32)
    step, other = index // 2 ^ lax.axis_index("seq"), index % 2 ^ lax.axis_index("batch")
    slots = []
    for bits in ((1, 2, 8, 4), (2, 1, 8, 4), (8, 4, 2, 1)):
        at = 16 * other
        for k, bit in enumerate(bits[::-1]):
            at = at + jnp.where(step & bit != 0, 1 << k, 0)
        slots.append(at)
    return ((0, one), (one, two), (two, tiles)), jnp.concatenate(slots).astype(jnp.int32)


def pieces(v, count):
    return v.reshape(count, -1, CH)


def halve(two, step):
    return pieces(two[0] + hop(two[1], step), 2)


def join_cores(arrays):
    sums = []
    for own, far in zip(arrays[::2], arrays[1::2]):
        own, far = pieces(own, 2), pieces(swap_cores(far), 2)
        sums.append([own[k] + far[k] for k in range(2)])
    return sums


def join_first(sums):
    return [halve(v, step) for v, step in zip(sums, (1, 2, 8))]


def join_second(sums):
    return [halve(v, step) for v, step in zip(sums, (2, 1, 4))]


def join_last(sums):
    rows = [pieces(v.reshape(-1, CH), 4) for v in sums[:2]]
    four = [jnp.concatenate([v[k] for v in rows]) for k in range(4)]
    near = halve(sums[2], 2)
    one = four[0] + hop(four[1], 4) + hop(four[2], 8) + hop(four[3], 12)
    return jnp.concatenate([one, near[0] + hop(near[1], 1)])


MODE_ROWS = 65


def scatter_modes(master):
    other = swap_cores(master)
    even = lax.axis_index("batch") == 0
    lead = jnp.concatenate([jnp.where(even, master, other), jnp.where(even, other, master)])[:MODE_TILES * TILE]
    small = lead[:4 * D].reshape(4, 16, 32).transpose(1, 0, 2).reshape(16, 1, CH)
    rest = lead[4 * D:].reshape(4, 16, 16, CH).transpose(1, 0, 2, 3).reshape(16, 64, CH)
    blocks = jnp.concatenate([small, rest], axis=1)
    seq = lax.axis_index("seq")
    blocks = blocks.reshape(2, 2, 2, 2, MODE_ROWS, CH).transpose(3, 2, 1, 0, 4, 5)
    for step in (1, 2, 4, 8):
        come = lax.ppermute(blocks[1], "seq", [(i, i + step) for i in range(step)])
        blocks = jnp.where(seq & step == 0, blocks[0], come)
    return blocks


def read_modes(block):
    nch = D // 16
    small = block[0].reshape(4, nch)
    rest = block[1:].reshape(4, nch, NSTATE)
    return small, rest


def gather_modes(block, steps):
    for step in steps:
        pairs = [(i, i - step) for i in range(2 * step) if i >= step]
        block = jnp.concatenate([block, lax.ppermute(block, "seq", pairs)])
    return block


def mode_vector(block):
    blocks = block.reshape(2, 2, 2, 2, 3, -1, CH).transpose(4, 3, 2, 1, 0, 5, 6).reshape(3, D, CH)
    few = blocks[2, :, :4].T
    return jnp.concatenate([v.reshape(-1) for v in (few, blocks[0, :, :NSTATE], blocks[0, :, NSTATE:], blocks[1, :, :NSTATE], blocks[1, :, NSTATE:])])


def total_of(v):
    if not direct():
        return lax.psum(v, AXES)
    terms = lax.all_to_all(jnp.broadcast_to(v, (32, 8, CH)), AXES, 0, 0)
    return jnp.sum(terms[:, 0, 0])


def to_channels(rows):
    seq = lax.axis_size("seq")
    parts = rows.shape[0] // CH
    turned = rows.reshape(parts, CH, seq, D // seq).transpose(2, 0, 3, 1)
    return lax.all_to_all(turned, "seq", 0, 0).reshape(-1, CH)


def to_tokens(rows, group):
    seq = lax.axis_size("seq")
    turned = lax.all_to_all(rows.reshape(seq, group // CH, D // seq, CH), "seq", 0, 0)
    return turned.transpose(1, 3, 0, 2).reshape(group, D)


def per_device(inputs, cotangent, lengths, master, first_moment, second_moment):
    seq, batch = lax.axis_size("seq"), lax.axis_size("batch")
    devices = seq * batch
    share = master.shape[0]
    box = container(master, share, devices)
    if direct():
        near = gather_near(box)
    else:
        streams, ids = ((0, box.shape[0] // 8, 0, devices),), jnp.arange(devices, dtype=jnp.int32)
        boxes = [lax.all_gather(box, AXES, axis=0, tiled=True)]
    group = inputs.shape[1]
    nch, nck = D // seq, seq * group // CH
    rows = inputs[0].astype(jnp.float32)
    ends = jnp.cumsum(lengths[0]).astype(jnp.int32)
    place = jnp.concatenate([ends, lax.axis_index("seq")[None] * group]).astype(jnp.int32)
    first_hat, first_scale = normalize(rows)
    hats = to_channels(first_hat)

    plan, slots = scatter_plan(share, devices)

    def feed_forward(response):
        return mlp_kernel(place, streams, ids, boxes, plan, slots, response, inputs[0], cotangent[0], share, devices, seq)

    if direct():
        few, many = read_modes(scatter_modes(master))
    else:
        lead = jnp.concatenate([lax.dynamic_slice(boxes[0][j * box.shape[0]:(j + 1) * box.shape[0]].reshape(-1), (j * share % TILE,), (share,)) for j in range(MODE_TILES * TILE // share + 1)])
        mine = lambda v: lax.dynamic_slice_in_dim(v, lax.axis_index("seq") * nch, nch, 1)
        few = mine(lead[:4 * D].reshape(4, D))
        many = mine(lead[4 * D:MODE_TILES * TILE].reshape(4, D, NSTATE))
    if direct():
        plane = gather_plane(near)
    modes, coefs = mixing(few[2], many[0], many[1], many[2], many[3])
    prm = mode_rows(*modes, few[0], few[1], few[3])
    outs, prior, *tables = ssm_forward(ends, prm, hats, nck, nch)
    response = lax.all_to_all(outs.reshape(seq, -1, nch, CH), "seq", 0, 0).reshape(-1, CH)
    if direct():
        far = [hop(plane[0], 2), hop(plane[1], 1)]
        response, far = lax.optimization_barrier((response, far))
        streams, ids, boxes = gather_cores(plane, far, box.shape[0] // 8)
    output, d_mid, d_response, lead, *packed = feed_forward(response)
    d_outs = lax.all_to_all(d_response.reshape(seq, -1, nch, CH), "seq", 0, 0).reshape(-1, CH)
    if direct():
        packed = join_cores(packed)
        d_outs, packed = lax.optimization_barrier((d_outs, packed))
    d_signals, sums = ssm_backward(ends, prm, hats, d_outs, prior, tables, coefs, nck, nch)
    if direct():
        d_signals, sums, packed = lax.optimization_barrier((d_signals, sums, join_first(packed)))
    d_signal = to_tokens(d_signals, group)
    norm_gain = lead[:D // CH].reshape(D)
    me = device_index()
    if direct():
        own = sums.reshape(-1, CH)
        own, packed = lax.optimization_barrier((own + swap_cores(own), join_second(packed)))
        box, block, d_signal = lax.optimization_barrier((join_last(packed), gather_modes(own, (8, 4, 2)), d_signal))
    else:
        box = lax.psum_scatter(packed[0].reshape(devices, -1, CH), AXES, scatter_dimension=0)
    d_rows = d_mid + norm_back(d_signal * norm_gain, first_hat, first_scale)
    shard = lax.dynamic_slice(box.reshape(-1), (me * share % TILE,), (share,))
    mark = me * share + jnp.arange(share, dtype=jnp.int32) < MODE_TILES * TILE
    squares = jnp.sum(jnp.where(mark, 0.0, shard * shard))
    if direct():
        squares = squares + 0.5 * jnp.sum(own * own)
        lead = mode_vector(gather_modes(block, (1,)))
    else:

        def spread(v):
            whole = jnp.zeros((v.shape[0], D) + v.shape[2:], f32)
            return lax.dynamic_update_slice_in_dim(whole, v, lax.axis_index("seq") * nch, 1)

        few = sums[2, :, :4].T
        many = jnp.stack([sums[0, :, :NSTATE], sums[0, :, NSTATE:], sums[1, :, :NSTATE], sums[1, :, NSTATE:]])
        lead = lax.psum(jnp.concatenate([spread(few).reshape(-1), spread(many).reshape(-1)]), AXES)
        squares = squares + jnp.sum(lead * lead) / devices
    lead = lax.dynamic_slice(jnp.pad(lead, (0, share)), (jnp.minimum(me * share, MODE_TILES * TILE),), (share,))
    shard = jnp.where(mark, lead, shard)
    total = total_of(squares)
    grad_norm = jnp.sqrt(total)
    factor = jnp.minimum(1.0, 1.0 / (grad_norm + 1e-06))
    clipped = shard * factor
    first_new = 0.9 * first_moment + 0.1 * clipped
    second_new = 0.999 * second_moment + 0.001 * clipped * clipped
    first_hat_new = first_new / (1.0 - 0.9**10)
    second_hat_new = second_new / (1.0 - 0.999**10)
    update = -0.05 * (first_hat_new / (jnp.sqrt(second_hat_new) + 1e-08) + 0.1 * master)
    return (output[None], d_rows[None], shard, update, first_new, second_new, grad_norm)


def solution(mesh):
    placed = (
        P("batch", "seq", None),
        P("batch", "seq", None),
        P("batch", None),
        P(("seq", "batch")),
        P(("seq", "batch")),
        P(("seq", "batch")),
    )
    return jax.shard_map(
        per_device,
        mesh=mesh,
        in_specs=placed,
        out_specs=(
            P("batch", "seq", None),
            P("batch", "seq", None),
            P(("seq", "batch")),
            P(("seq", "batch")),
            P(("seq", "batch")),
            P(("seq", "batch")),
            P(),
        ),
        check_vma=False,
    )
```

```python
from functools import partial
import jax
import jax.numpy as jnp
import numpy as np
from jax import lax
from jax.experimental import pallas as pl
from jax.experimental.pallas import tpu as pltpu
from jax.sharding import PartitionSpec as P

D = 512
NSTATE = 64
CH = 128
DOCS = 4
G = 1024
FF = 2048
Z_FIRST = 0.2


norm_eps = 1e-05
root_half = 0.7071067811865476
inv_root_two_pi = 0.3989422804014327


f32 = jnp.float32
bf16 = jnp.bfloat16

def split(v):
    hi = v.astype(bf16)
    return hi, (v - hi.astype(f32)).astype(bf16)

def dot3(a, b, ca, cb):
    ah, al = a
    bh, bl = b
    lhs = jnp.concatenate([ah, ah, al], axis=ca)
    rhs = jnp.concatenate([bh, bl, bh], axis=cb)
    return lax.dot_general(lhs, rhs, (((ca,), (cb,)), ((), ())), preferred_element_type=f32)

def dot2(data, table, ct):
    return dot3(data, (table[0], table[1]), 1, ct)

def swap(v):
    return pltpu.roll(v, NSTATE, 1)

def twist(table, re, im):
    return re * table + im * swap(table)

def ladder(prm, order):
    sub = lax.broadcasted_iota(jnp.int32, (8, 2 * NSTATE), 0)
    lane = lax.broadcasted_iota(jnp.int32, (8, 2 * NSTATE), 1)
    power = sub if order == 1 else 7 - sub
    table = jnp.where(lane < NSTATE, 1.0, 0.0).astype(f32)
    for bit in range(3):
        table = jnp.where((power >> bit) & 1 == 1, twist(table, prm[2 * bit:2 * bit + 1], prm[2 * bit + 1:2 * bit + 2]), table)
    for bit in range(3, 7):
        more = twist(table, prm[2 * bit:2 * bit + 1], prm[2 * bit + 1:2 * bit + 2])
        table = jnp.concatenate([table, more] if order == 1 else [more, table], axis=0)
    return table

def toeplitz(taps):
    wide = pltpu.roll(jnp.broadcast_to(taps, (CH, CH)), 0, 1, stride=1, stride_axis=0)
    row = lax.broadcasted_iota(jnp.int32, (CH, CH), 0)
    col = lax.broadcasted_iota(jnp.int32, (CH, CH), 1)
    return jnp.where(col >= row, wide, 0.0)

def label_at(ends, pos):
    total = jnp.zeros_like(pos)
    for k in range(DOCS):
        total = total + (pos >= ends[k]).astype(jnp.int32)
    return total

def make_masks(ends_ref, masks_ref, low_ref, nck):
    ends = [ends_ref[k] for k in range(DOCS)]
    row = lax.broadcasted_iota(jnp.int32, (nck, CH), 0)
    lane = lax.broadcasted_iota(jnp.int32, (nck, CH), 1)
    base = row * CH
    label = label_at(ends, base + lane)
    prev = jnp.where(base == 0, -1, label_at(ends, base - 1))
    last = label_at(ends, base + CH - 1)
    for k in range(DOCS):
        masks_ref[k] = (label == k).astype(f32)
    masks_ref[DOCS] = (label == prev).astype(f32)
    masks_ref[DOCS + 1] = (label == last).astype(f32)
    low_ref[:DOCS + 2] = masks_ref[...].astype(bf16)
    if low_ref.shape[0] > DOCS + 2:
        label = label_at(ends, base + (CH - 1 - lane))
        for k in range(DOCS):
            low_ref[DOCS + 2 + k] = (label == k).astype(f32).astype(bf16)

def keep_of(ends_ref, c):
    first = jnp.int32(0)
    second = jnp.int32(0)
    for k in range(DOCS):
        first = first + (c * CH - 1 >= ends_ref[k]).astype(jnp.int32)
        second = second + (c * CH + CH - 1 >= ends_ref[k]).astype(jnp.int32)
    return jnp.where((c > 0) & (first == second), 1.0, 0.0).astype(f32)

def masked_rows(v, low_ref):
    return [jnp.concatenate([part * low_ref[k] for k in range(DOCS)], axis=0) for part in v]

def masked(v, low_ref, k):
    return [part * low_ref[k] for part in v]

def fold_rows(v, masks_ref, nck):
    total = v[:nck] * masks_ref[0]
    for k in range(1, DOCS):
        total = total + v[k * nck:(k + 1) * nck] * masks_ref[k]
    return total

def keep(ref, h, v):
    ref[h, 0], ref[h, 1] = split(v)

def for_channels(nch, body):
    lax.fori_loop(0, nch, lambda h, _: body(h) or 0, 0, unroll=min(nch, 16))

def fwd_body(nck, nch, apart, ends_ref, prm_ref, x_ref, y_ref, prior_ref, table_ref, down_ref, out_ref, mat_ref, masks_ref, low_ref, end_ref):
    make_masks(ends_ref, masks_ref, low_ref, nck)

    def tables(h):
        prm = prm_ref[h]
        table = ladder(prm, 1)
        keep(table_ref, h, table)
        keep(out_ref, h, twist(table, prm[17:18], prm[18:19]))

    def falling(h):
        keep(down_ref, h, ladder(prm_ref[h], -1))

    def taps(h):
        wrow = jnp.broadcast_to(prm_ref[h, 16:17, :], (16, 2 * NSTATE))
        keep(mat_ref, h, toeplitz(dot2(split(wrow), table_ref[h], 1)[0:1]))

    def local(h):
        prm = prm_ref[h, 16:24, :]
        u = x_ref[pl.ds(h, nck, stride=apart), :] * prm[3:4] + prm[4:5]
        parts = split(u)
        local = dot2(masked_rows(parts, low_ref), mat_ref[h], 0)
        y_ref[pl.ds(h, nck, stride=nch), :] = fold_rows(local, masks_ref, nck) + prm[5:6] * u
        end_ref[pl.ds(h, nck, stride=nch), :] = dot2(masked(parts, low_ref, DOCS + 1), down_ref[h], 0)

    for body in (tables, falling, taps, local):
        for_channels(nch, body)
    full_re = prm_ref[:, 14, :]
    full_im = prm_ref[:, 15, :]

    def step(c, state):
        at = pl.ds(pl.multiple_of(c * nch, 8), nch)
        prior_ref[at, :] = state
        return keep_of(ends_ref, c) * twist(state, full_re, full_im) + end_ref[at, :]

    lax.fori_loop(0, nck, step, jnp.zeros((nch, 2 * NSTATE), f32))

    def carried(h):
        prior = split(prior_ref[pl.ds(h, nck, stride=nch), :])
        y_ref[pl.ds(h, nck, stride=nch), :] += dot2(prior, out_ref[h], 1) * masks_ref[DOCS]

    for_channels(nch, carried)

def ssm_forward(ends, prm, x, nck, nch):
    vm = pl.BlockSpec(memory_space=pltpu.VMEM)
    table = jax.ShapeDtypeStruct((nch, 2, CH, 2 * NSTATE), bf16)
    return pl.pallas_call(
        partial(fwd_body, nck, nch, x.shape[0] // nck),
        out_shape=(jax.ShapeDtypeStruct((nck * nch, CH), f32), jax.ShapeDtypeStruct((nck * nch, 2 * NSTATE), f32)) + (table,) * 4,
        in_specs=[pl.BlockSpec(memory_space=pltpu.SMEM), vm, vm],
        out_specs=(vm,) * 6,
        scratch_shapes=[
            pltpu.VMEM((DOCS + 2, nck, CH), f32),
            pltpu.VMEM((DOCS + 2, nck, CH), bf16),
            pltpu.VMEM((nck * nch, 2 * NSTATE), f32),
        ],
        cost_estimate=pl.CostEstimate(flops=int(2.0e10), bytes_accessed=3 * 2**20, transcendentals=0),
        name="state_forward",
    )(ends, prm, x)

def bwd_body(nck, nch, apart, ends_ref, prm_ref, x_ref, g_ref, prior_ref, table_ref, down_ref, out_ref, mat_ref, coef_ref, dx_ref, grad_ref, rows_ref, masks_ref, low_ref, lead_ref, adj_ref, taps_ref):
    make_masks(ends_ref, masks_ref, low_ref, nck)
    at_channel = lambda h: pl.ds(h, nck, stride=nch)

    def lead(h):
        lead_ref[at_channel(h), :] = dot2(masked(split(g_ref[at_channel(h), :]), low_ref, DOCS), out_ref[h], 0)

    for_channels(nch, lead)
    full_re = prm_ref[:, 14, :]
    full_im = prm_ref[:, 15, :]
    zero = jnp.zeros((nch, 2 * NSTATE), f32)

    def step(k, carry):
        adjoint, same, cross = carry
        c = nck - 1 - k
        at = pl.ds(pl.multiple_of(c * nch, 8), nch)
        adj_ref[at, :] = adjoint
        keep = keep_of(ends_ref, c)
        prior = prior_ref[at, :]
        same = same + keep * adjoint * prior
        cross = cross + keep * adjoint * swap(prior)
        adjoint = lead_ref[at, :] + keep * (full_re * adjoint - full_im * swap(adjoint))
        return adjoint, same, cross

    _, same, cross = lax.fori_loop(0, nck, step, (zero, zero, zero))
    rows_ref[8] = same
    rows_ref[9] = cross
    row = lax.broadcasted_iota(jnp.int32, (CH, CH), 0)
    col = lax.broadcasted_iota(jnp.int32, (CH, CH), 1)
    flip = (row + col == CH - 1).astype(f32).astype(bf16)
    put = lambda k, h, v: rows_ref.__setitem__((k, pl.ds(h, 1), slice(None)), jnp.sum(v, axis=0, keepdims=True))

    def signal(h):
        prm = prm_ref[h, 16:24, :]
        x = x_ref[pl.ds(h, nck, stride=apart), :]
        g = g_ref[at_channel(h), :]
        du = fold_rows(dot2(masked_rows(split(g), low_ref), mat_ref[h], 1), masks_ref, nck)
        du = du + dot2(split(adj_ref[at_channel(h), :]), down_ref[h], 1) * masks_ref[DOCS + 1]
        du = du + prm[5:6] * g
        dx_ref[at_channel(h), :] = du
        put(10, h, g * (x * prm[3:4] + prm[4:5]))
        put(11, h, du * x)
        put(12, h, du)

    def taps(h):
        prm = prm_ref[h, 16:24, :]
        u = split(x_ref[pl.ds(h, nck, stride=apart), :] * prm[3:4] + prm[4:5])
        both = jnp.dot(jnp.concatenate(u, axis=0), flip, preferred_element_type=f32).astype(bf16)
        um = []
        for part in (both[:nck], both[nck:]):
            um.append(jnp.concatenate([part * low_ref[DOCS + 2 + k] for k in range(DOCS)], axis=0))
        square = dot3(um, masked_rows(split(g_ref[at_channel(h), :]), low_ref), 0, 0)
        square = jnp.where(row + col >= CH - 1, square, 0.0)
        square = pltpu.roll(square, 1, 1, stride=1, stride_axis=0)
        taps_ref[pl.ds(h, 1), :] = jnp.sum(square, axis=0, keepdims=True)

    def kernel(h):
        place = lax.broadcasted_iota(jnp.int32, (16, CH), 1).astype(f32)
        sub = lax.broadcasted_iota(jnp.int32, (16, CH), 0)
        both = jnp.where(sub == 0, 1.0, jnp.where(sub == 1, place, 0.0)) * taps_ref[pl.ds(h, 1), :]
        both = dot2(split(both), table_ref[h], 0)
        rows_ref[0, pl.ds(h, 1), :] = both[0:1]
        rows_ref[1, pl.ds(h, 1), :] = both[1:2]

    late = row.astype(f32)

    def carried(h):
        dgt = dot3(masked(split(g_ref[at_channel(h), :]), low_ref, DOCS), split(prior_ref[at_channel(h), :]), 0, 0)
        table = table_ref[h, 0].astype(f32) + table_ref[h, 1].astype(f32)
        same, cross = dgt * table, dgt * swap(table)
        put(2, h, same)
        put(3, h, cross)
        put(4, h, same * late)
        put(5, h, cross * late)

    def ending(h):
        prm = prm_ref[h, 16:24, :]
        u = split(x_ref[pl.ds(h, nck, stride=apart), :] * prm[3:4] + prm[4:5])
        ddown = dot3(masked(u, low_ref, DOCS + 1), split(adj_ref[at_channel(h), :]), 0, 0) * ((CH - 1) - late)
        down = down_ref[h, 0].astype(f32) + down_ref[h, 1].astype(f32)
        put(6, h, ddown * down)
        put(7, h, ddown * swap(down))

    for body in (signal, taps, kernel, carried, ending):
        for_channels(nch, body)
    rows = [rows_ref[k] for k in range(13)]
    total = lambda v: jnp.sum(v, axis=1, keepdims=True)
    d_step, d_decay, d_frequency, d_real, d_imag = mode_grads(rows, [coef_ref[k] for k in range(14)])
    grad_ref[0] = jnp.concatenate([d_decay, d_frequency], axis=1)
    grad_ref[1] = jnp.concatenate([d_real, d_imag], axis=1)
    lane = lax.broadcasted_iota(jnp.int32, (nch, CH), 1)
    few = jnp.zeros((nch, CH), f32)
    for k, v in enumerate((total(rows[11]), total(rows[12]), total(d_step), total(rows[10]))):
        few = jnp.where(lane == k, v, few)
    grad_ref[2] = few

def ssm_backward(ends, prm, x, g, prior, tables, coefs, nck, nch):
    vm = pl.BlockSpec(memory_space=pltpu.VMEM)
    return pl.pallas_call(
        partial(bwd_body, nck, nch, x.shape[0] // nck),
        out_shape=(jax.ShapeDtypeStruct((nck * nch, CH), f32), jax.ShapeDtypeStruct((3, nch, 2 * NSTATE), f32)),
        in_specs=[pl.BlockSpec(memory_space=pltpu.SMEM)] + [vm] * 9,
        out_specs=(vm, vm),
        scratch_shapes=[
            pltpu.VMEM((13, nch, 2 * NSTATE), f32),
            pltpu.VMEM((DOCS + 2, nck, CH), f32),
            pltpu.VMEM((2 * DOCS + 2, nck, CH), bf16),
            pltpu.VMEM((nck * nch, 2 * NSTATE), f32),
            pltpu.VMEM((nck * nch, 2 * NSTATE), f32),
            pltpu.VMEM((nch, CH), f32),
        ],
        cost_estimate=pl.CostEstimate(flops=int(3.5e10), bytes_accessed=4 * 2**20, transcendentals=0),
        name="state_backward",
    )(ends, prm, x, g, prior, *tables, coefs)

def mixing(step_log, decay_log, frequency, out_real, out_imag):
    delta = jnp.exp(step_log)[:, None]
    rate_re = -jnp.exp(decay_log)
    arg_re, arg_im = delta * rate_re, delta * frequency
    magnitude = jnp.exp(arg_re)
    p_re, p_im = magnitude * jnp.cos(arg_im), magnitude * jnp.sin(arg_im)
    inverse = 1.0 / (rate_re * rate_re + frequency * frequency)
    ratio_re = ((p_re - 1.0) * rate_re + p_im * frequency) * inverse
    ratio_im = (p_im * rate_re - (p_re - 1.0) * frequency) * inverse
    mix_re = out_real * ratio_re - out_imag * ratio_im
    mix_im = out_real * ratio_im + out_imag * ratio_re
    magnitude = jnp.exp(arg_re * CH)
    f_re, f_im = magnitude * jnp.cos(arg_im * CH), magnitude * jnp.sin(arg_im * CH)
    wide = jnp.broadcast_to(delta, arg_re.shape)
    coefs = jnp.stack([p_re, p_im, f_re, f_im, mix_re, mix_im, out_real, out_imag, ratio_re, ratio_im, rate_re, frequency, inverse, wide])
    return (arg_re, arg_im, mix_re, mix_im), coefs

def pair(left, right):
    return jnp.concatenate([left, right], axis=-1)

def mode_rows(arg_re, arg_im, mix_re, mix_im, gain, bias, skip):
    nch = arg_re.shape[0]
    scale = jnp.asarray([2.0**b for b in range(8)], f32)[None, :, None]
    magnitude = jnp.exp(arg_re[:, None] * scale)
    p_re = magnitude * jnp.cos(arg_im[:, None] * scale)
    p_im = magnitude * jnp.sin(arg_im[:, None] * scale)
    powers = jnp.stack([pair(p_re, p_re), pair(-p_im, p_im)], axis=2).reshape(nch, 16, 2 * NSTATE)
    c_re = mix_re * p_re[:, 0] - mix_im * p_im[:, 0]
    c_im = mix_re * p_im[:, 0] + mix_im * p_re[:, 0]
    flat = lambda v: jnp.broadcast_to(v[:, None], (nch, 2 * NSTATE))
    rest = jnp.stack([pair(mix_re, -mix_im), pair(c_re, -c_re), pair(-c_im, -c_im), flat(gain), flat(bias), flat(skip), flat(0 * gain), flat(0 * gain)], axis=1)
    return jnp.concatenate([powers, rest], axis=1)

def mode_grads(rows, coefs):
    p_re, p_im, f_re, f_im, mix_re, mix_im, out_real, out_imag, ratio_re, ratio_im, rate, freq, inverse, delta = coefs
    lo = [v[:, :NSTATE] for v in rows]
    hi = [v[:, NSTATE:] for v in rows]
    a_re, a_im = lo[2] - hi[2], -(hi[3] + lo[3])
    b_re, b_im = lo[4] - hi[4] + a_re, a_im - (hi[5] + lo[5])
    w_re = lo[0] + p_re * a_re + p_im * a_im
    w_im = -hi[0] + p_re * a_im - p_im * a_re
    v_re = lo[1] + p_re * b_re + p_im * b_im
    v_im = -hi[1] + p_re * b_im - p_im * b_re
    d_re, d_im = lo[8] + hi[8], hi[9] - lo[9]
    g_re = mix_re * v_re + mix_im * v_im + lo[6] + hi[6] + CH * (f_re * d_re + f_im * d_im)
    g_im = mix_re * v_im - mix_im * v_re + hi[7] - lo[7] + CH * (f_re * d_im - f_im * d_re)
    d_real, d_imag = w_re * ratio_re + w_im * ratio_im, w_im * ratio_re - w_re * ratio_im
    r_re = (w_re * out_real + w_im * out_imag) * inverse
    r_im = (w_im * out_real - w_re * out_imag) * inverse
    fall = 2.0 * (r_re * ratio_re + r_im * ratio_im)
    pole_re = r_re * rate - r_im * freq
    pole_im = r_re * freq + r_im * rate
    d_rate = r_re * (p_re - 1.0) + r_im * p_im - fall * rate
    d_freq = r_re * p_im - r_im * (p_re - 1.0) - fall * freq
    g_re = g_re + pole_re * p_re + pole_im * p_im
    g_im = g_im + pole_im * p_re - pole_re * p_im
    d_step = delta * (rate * g_re + freq * g_im)
    return d_step, (d_rate + delta * g_re) * rate, d_freq + delta * g_im, d_real, d_imag


def gelu(values):
    return 0.5 * values * (1.0 + lax.erf(values * root_half))


def gelu_slope(values):
    return (
        0.5 * (1.0 + lax.erf(values * root_half))
        + values * jnp.exp(-0.5 * values * values) * inv_root_two_pi
    )


def normalize(values):
    center = values - jnp.mean(values, axis=-1, keepdims=True)
    scale = lax.rsqrt(jnp.mean(center * center, axis=-1, keepdims=True) + norm_eps)
    return (center * scale, scale)


def norm_back(d_hat, hat, scale):
    return scale * (
        d_hat
        - jnp.mean(d_hat, axis=-1, keepdims=True)
        - hat * jnp.mean(d_hat * hat, axis=-1, keepdims=True)
    )


TILE = 1024
GATE_AT, EXPAND_AT, REDUCE_AT = 130, 644, 1670
SMALL_AT = (642, 643, 1668, 1669, 2694)
MODE_TILES = 130
BLOCK = 512


def lay(share, devices):
    base = share // TILE
    return base, base + 2, (devices - 1) * share // TILE + base + 2


def product(a, b, ca, cb):
    return lax.dot_general(a, b, (((ca,), (cb,)), ((), ())), preferred_element_type=f32)


def narrow(flat, out, first, rows, per):
    def one(i, _):
        for k in range(per):
            v = flat[pl.ds(first * 8 + i * 16 * per + k, 16, stride=per), :]
            out[pl.ds(pl.multiple_of(i * 16, 16), 16), k * CH:(k + 1) * CH] = v.astype(bf16)
        return 0

    lax.fori_loop(0, rows // 16, one, 0, unroll=max(1, 16 // per))


def small_row(flat, tile, begin, count):
    return jnp.concatenate([flat[tile * 8 + (begin + k) // CH:tile * 8 + (begin + k) // CH + 1, :] for k in range(0, count, CH)], axis=1)


def put_small(small_ref, begin, row):
    for k in range(row.shape[1] // CH):
        small_ref[begin // CH + k:begin // CH + k + 1, :] = row[:, k * CH:(k + 1) * CH]


def column_sum(v):
    return jnp.sum(v, axis=0, keepdims=True)


def mlp_body(share, devices, nseq, streams, plan, place_ref, ids, slots, *refs):
    boxes = refs[:len(streams)]
    resp_ref, x_ref, cot_ref, out_ref, dmid_ref, dresp_ref, lead_ref = refs[len(streams):len(streams) + 7]
    ways = 2 if len(plan) > 1 else 1
    outs = refs[len(streams) + 7:len(streams) + 7 + ways * len(plan)]
    small_ref, hidden_ref, active_ref, normed_ref, back_ref, dopen_ref, dlift_ref, flat, side, gate, expand, reduce, acc, dnorm, sems, out_sems = refs[len(streams) + 7 + len(outs):]
    base, box, _ = lay(share, devices)
    nch = D // nseq
    group = x_ref.shape[0]
    start_of = lambda j: (j * share) // TILE
    inside = 0
    for k, (first, last, off, count) in enumerate(streams):
        lo, hi = max(first, 1), min(last, base)

        def copy_box(i, _, k=k, first=first, last=last, lo=lo, hi=hi, off=off):
            j = ids[off + i]
            begin = (i * (last - first) - first) * 8
            for s, tile in enumerate((0, base, base + 1)):
                if first <= tile < last:
                    pltpu.make_async_copy(boxes[k].at[pl.ds(pl.multiple_of(begin + tile * 8, 8), 8), :], side.at[s, pl.ds(pl.multiple_of(j * 8, 8), 8), :], sems.at[1]).start()
            pltpu.make_async_copy(
                boxes[k].at[pl.ds(pl.multiple_of(begin + lo * 8, 8), (hi - lo) * 8), :],
                flat.at[pl.ds(pl.multiple_of((start_of(j) + lo) * 8, 8), (hi - lo) * 8), :],
                sems.at[0],
            ).start()
            return 0

        lax.fori_loop(0, count, copy_box, 0)
        inside += (hi - lo) * count
    parts = group // CH
    turned = [
        jnp.concatenate([resp_ref[pl.ds((d * parts + k) * nch, nch), :] for d in range(nseq)], axis=0).T
        for k in range(parts)
    ]
    response = jnp.concatenate(turned, axis=0)
    hidden_ref[...] = gelu(response).astype(bf16)
    pos = place_ref[DOCS] + lax.broadcasted_iota(jnp.int32, (group, D), 0)
    total = jnp.zeros((group, D), jnp.int32)
    for k in range(DOCS):
        total = total + (pos >= place_ref[k]).astype(jnp.int32)
    back = jnp.where(total < DOCS - 1, cot_ref[...].astype(f32), 0.0)
    back_ref[...] = back.astype(bf16)
    put_small(small_ref, 2 * G + FF, column_sum(back))
    small_ref[36:40, :] = jnp.zeros((4, CH), f32)
    inner = side.at[:, pl.ds(0, devices * 8), :]
    pltpu.make_async_copy(inner, inner, sems.at[1]).wait()
    side[0, devices * 8:, :] = jnp.zeros((8, CH), f32)
    flat[:8, :] = side[0, :8, :]

    def join(j, _):
        at = start_of(j)
        step = start_of(j + 1) - at
        far = jnp.broadcast_to(step, (8, CH)) > base
        here = pl.ds(pl.multiple_of(j * 8, 8), 8)
        one, two, then = side[1, here, :], side[2, here, :], side[0, pl.ds(pl.multiple_of(j * 8 + 8, 8), 8), :]
        flat[pl.ds(pl.multiple_of((at + base) * 8, 8), 8), :] = one + jnp.where(far, 0.0, then)
        flat[pl.ds(pl.multiple_of((at + step) * 8, 8), 8), :] = jnp.where(far, two, one) + then
        return 0

    lax.fori_loop(0, devices, join, 0)

    some = flat.at[pl.ds(0, inside * 8), :]
    pltpu.make_async_copy(some, some, sems.at[0]).wait()
    lead_ref[...] = flat[:MODE_TILES * 8, :]
    narrow(flat, gate, GATE_AT, D, G // CH)
    gate_bias = small_row(flat, SMALL_AT[0], 0, G)
    second_gain = small_row(flat, SMALL_AT[1], 0, D)
    second_bias = small_row(flat, SMALL_AT[1], D, D)
    hidden = hidden_ref[...]
    linear = product(hidden, gate[:, :D], 1, 0) + gate_bias[:, :D]
    gating = jax.nn.sigmoid(product(hidden, gate[:, D:], 1, 0) + gate_bias[:, D:])
    mid = x_ref[...].astype(f32) + linear * gating
    hat, scale = normalize(mid)
    normed_ref[...] = (hat * second_gain + second_bias).astype(bf16)
    narrow(flat, expand, EXPAND_AT, D, FF // CH)
    narrow(flat, reduce, REDUCE_AT, FF, D // CH)
    dnorm[...] = jnp.zeros((group, D), f32)
    acc[...] = mid + small_row(flat, SMALL_AT[4], 0, D)
    for b in range(FF // BLOCK):
        at = slice(b * BLOCK, (b + 1) * BLOCK)
        bias = small_row(flat, SMALL_AT[2] + b * BLOCK // TILE, b * BLOCK % TILE, BLOCK)
        lifted = product(normed_ref[...], expand[:, at], 1, 0) + bias
        half = 0.5 * (1.0 + lax.erf(lifted * root_half))
        active = (lifted * half).astype(bf16)
        active_ref[:, at] = active
        slope = half + lifted * jnp.exp(-0.5 * lifted * lifted) * inv_root_two_pi
        d_lifted = (product(back_ref[...], reduce[at, :], 1, 1) * slope).astype(bf16)
        dlift_ref[:, at] = d_lifted
        put_small(small_ref, 2 * G + b * BLOCK, column_sum(d_lifted.astype(f32)))
        acc[...] += product(active, reduce[at, :], 1, 0)
        dnorm[...] += product(d_lifted, expand[:, at], 1, 1)
    out_ref[...] = acc[...].astype(bf16)
    d_normed = dnorm[...]
    put_small(small_ref, G, column_sum(d_normed * hat))
    put_small(small_ref, G + D, column_sum(d_normed))
    d_mid = back_ref[...].astype(f32) + norm_back(d_normed * second_gain, hat, scale)
    dmid_ref[...] = d_mid
    d_linear = (d_mid * gating).astype(bf16)
    d_gating = (d_mid * linear * gating * (1.0 - gating)).astype(bf16)
    dopen_ref[:, :D] = d_linear
    dopen_ref[:, D:] = d_gating
    put_small(small_ref, 0, column_sum(d_linear.astype(f32)))
    put_small(small_ref, D, column_sum(d_gating.astype(f32)))
    d_hidden = product(d_linear, gate[:, :D], 1, 1) + product(d_gating, gate[:, D:], 1, 1)
    for k in range(parts):
        again = jnp.concatenate([resp_ref[pl.ds((d * parts + k) * nch, nch), :] for d in range(nseq)], axis=0)
        back_turned = d_hidden[k * CH:(k + 1) * CH].T * gelu_slope(again)
        for d in range(nseq):
            dresp_ref[pl.ds((d * parts + k) * nch, nch), :] = back_turned[d * nch:(d + 1) * nch]

    flat[:MODE_TILES * 8, :] = jnp.zeros((MODE_TILES * 8, CH), f32)
    for k, tile in enumerate(SMALL_AT):
        flat[tile * 8:(tile + 1) * 8, :] = small_ref[k * 8:(k + 1) * 8, :]
    flat[(SMALL_AT[-1] + 1) * 8:, :] = jnp.zeros((flat.shape[0] - (SMALL_AT[-1] + 1) * 8, CH), f32)
    sent = 0
    for first, left, right, per, until in (
        (GATE_AT, hidden_ref, dopen_ref, G // CH, EXPAND_AT),
        (EXPAND_AT, normed_ref, dlift_ref, FF // CH, REDUCE_AT),
        (REDUCE_AT, active_ref, back_ref, D // CH, flat.shape[0]),
    ):
        flip = left[...].T
        for k in range(left.shape[1] // CH):
            v = product(flip[k * CH:(k + 1) * CH], right[...], 1, 0)
            for c in range(per):
                flat[pl.ds(first * 8 + k * CH * per + c, CH, stride=per), :] = v[:, c * CH:(c + 1) * CH]
        ready = sum((j * share) // TILE + box <= until for j in range(devices))
        for k, (low, high) in enumerate(plan):
            rows = (high - low) * 8

            def send(j, _, k=k, low=low, rows=rows):
                slot = slots[k * devices + j]
                block = flat.at[pl.ds(pl.multiple_of((start_of(j) + low) * 8, 8), rows), :]
                for o in range(ways):
                    at = slot - o * (devices // ways)

                    @pl.when((at >= 0) & (at < devices // ways))
                    def _():
                        target = outs[k * ways + o].at[pl.ds(pl.multiple_of(at * rows, 8), rows), :]
                        pltpu.make_async_copy(block, target, out_sems.at[k * ways + o]).start()

                return 0

            lax.fori_loop(sent, ready, send, 0)
        sent = ready
    for k, out in enumerate(outs):
        pltpu.make_async_copy(out, out, out_sems.at[k]).wait()


def mlp_kernel(place, streams, ids, boxes, plan, slots, response, rows, cotangent, share, devices, nseq):
    base, box, tiles = lay(share, devices)
    group = rows.shape[0]
    vm = pl.BlockSpec(memory_space=pltpu.VMEM)
    hbm = pl.BlockSpec(memory_space=pl.ANY)
    smem = pl.BlockSpec(memory_space=pltpu.SMEM)
    shape = lambda r, c, t: jax.ShapeDtypeStruct((r, c), t)
    count = 2 if len(plan) > 1 else 1
    packed = [shape(devices // count * (high - low) * 8, CH, f32) for low, high in plan for _ in range(count)]
    return pl.pallas_call(
        partial(mlp_body, share, devices, nseq, streams, plan),
        out_shape=(
            shape(group, D, bf16),
            shape(group, D, f32),
            jax.ShapeDtypeStruct(response.shape, f32),
            shape(MODE_TILES * 8, CH, f32),
            *packed,
        ),
        in_specs=[smem] * 3 + [hbm] * len(boxes) + [vm] * 3,
        out_specs=(vm,) * 4 + (hbm,) * len(packed),
        scratch_shapes=[
            pltpu.VMEM((len(SMALL_AT) * 8, CH), f32),
            pltpu.VMEM((group, D), bf16),
            pltpu.VMEM((group, FF), bf16),
            pltpu.VMEM((group, D), bf16),
            pltpu.VMEM((group, D), bf16),
            pltpu.VMEM((group, G), bf16),
            pltpu.VMEM((group, FF), bf16),
            pltpu.VMEM((tiles * 8, CH), f32),
            pltpu.VMEM((3, devices * 8 + 8, CH), f32),
            pltpu.VMEM((D, G), bf16),
            pltpu.VMEM((D, FF), bf16),
            pltpu.VMEM((FF, D), bf16),
            pltpu.VMEM((group, D), f32),
            pltpu.VMEM((group, D), f32),
            pltpu.SemaphoreType.DMA((2,)),
            pltpu.SemaphoreType.DMA((len(packed),)),
        ],
        cost_estimate=pl.CostEstimate(flops=int(2.0e10), bytes_accessed=30 * 2**20, transcendentals=0),
        name="feed_forward",
    )(place, ids, slots, *boxes, response, rows, cotangent)


AXES = ("seq", "batch")
PAIR = [(0, 1), (1, 0)]


def hop(v, step):
    return lax.ppermute(v, "seq", [(i, i ^ step) for i in range(16)])


def swap_cores(v):
    return lax.ppermute(v, "batch", PAIR)


def direct():
    return lax.axis_size("seq") == 16 and lax.axis_size("batch") == 2


def device_index():
    return lax.axis_index("seq") * lax.axis_size("batch") + lax.axis_index("batch")


def places_of(steps, other):
    seq, batch = lax.axis_index("seq"), lax.axis_index("batch")
    return 2 * (seq ^ np.asarray(steps, np.int32)) + (batch ^ other)


def cuts_of(tiles):
    one = round(tiles * (1.0 - Z_FIRST) / 2)
    return one, 2 * one


def container(master, share, devices):
    _, tiles, _ = lay(share, devices)
    box = lax.dynamic_update_slice(jnp.zeros((tiles * TILE,), f32), master, (device_index() * share % TILE,))
    return box.reshape(tiles * 8, CH)


def gather_near(box):
    half = box.shape[0] // 16 * 8
    sets = [box] + [hop(box, step) for step in (4, 8, 12)]
    return [jnp.concatenate([v[at] for v in sets]) for at in (slice(0, half), slice(half, None))]


def gather_plane(near):
    return [jnp.concatenate([near[0], hop(near[0], 1)]), jnp.concatenate([near[1], hop(near[1], 2)])]


def gather_cores(plane, far, tiles):
    half = tiles // 2
    arrays, streams, ids = [], [], []
    for v, first, second in ((plane[0], 0, 1), (plane[1], 0, 2), (far[0], 2, 3), (far[1], 1, 3)):
        for other in range(2):
            arrays.append(swap_cores(v) if other else v)
            streams.append(((0, half) if len(arrays) % 4 in (1, 2) else (half, tiles)) + (8 * len(ids), 8))
            ids.append(places_of([4 * z + p for p in (first, second) for z in range(4)], other))
    return tuple(streams), jnp.concatenate(ids).astype(jnp.int32), arrays


def scatter_plan(share, devices):
    _, tiles, _ = lay(share, devices)
    if not direct():
        return ((0, tiles),), jnp.arange(devices, dtype=jnp.int32)
    one, two = cuts_of(tiles)
    index = np.arange(devices, dtype=np.int32)
    step, other = index // 2 ^ lax.axis_index("seq"), index % 2 ^ lax.axis_index("batch")
    slots = []
    for bits in ((1, 2, 8, 4), (2, 1, 8, 4), (8, 4, 2, 1)):
        at = 16 * other
        for k, bit in enumerate(bits[::-1]):
            at = at + jnp.where(step & bit != 0, 1 << k, 0)
        slots.append(at)
    return ((0, one), (one, two), (two, tiles)), jnp.concatenate(slots).astype(jnp.int32)


def pieces(v, count):
    return v.reshape(count, -1, CH)


def halve(two, step):
    return pieces(two[0] + hop(two[1], step), 2)


def join_cores(arrays):
    sums = []
    for own, far in zip(arrays[::2], arrays[1::2]):
        own, far = pieces(own, 2), pieces(swap_cores(far), 2)
        sums.append([own[k] + far[k] for k in range(2)])
    return sums


def join_first(sums):
    return [halve(v, step) for v, step in zip(sums, (1, 2, 8))]


def join_second(sums):
    return [halve(v, step) for v, step in zip(sums, (2, 1, 4))]


def join_last(sums):
    rows = [pieces(v.reshape(-1, CH), 4) for v in sums[:2]]
    four = [jnp.concatenate([v[k] for v in rows]) for k in range(4)]
    near = halve(sums[2], 2)
    one = four[0] + hop(four[1], 4) + hop(four[2], 8) + hop(four[3], 12)
    return jnp.concatenate([one, near[0] + hop(near[1], 1)])


MODE_ROWS = 65


def scatter_modes(master):
    other = swap_cores(master)
    even = lax.axis_index("batch") == 0
    lead = jnp.concatenate([jnp.where(even, master, other), jnp.where(even, other, master)])[:MODE_TILES * TILE]
    small = lead[:4 * D].reshape(4, 16, 32).transpose(1, 0, 2).reshape(16, 1, CH)
    rest = lead[4 * D:].reshape(4, 16, 16, CH).transpose(1, 0, 2, 3).reshape(16, 64, CH)
    blocks = jnp.concatenate([small, rest], axis=1)
    seq = lax.axis_index("seq")
    blocks = blocks.reshape(2, 2, 2, 2, MODE_ROWS, CH).transpose(3, 2, 1, 0, 4, 5)
    for step in (1, 2, 4, 8):
        come = lax.ppermute(blocks[1], "seq", [(i, i + step) for i in range(step)])
        blocks = jnp.where(seq & step == 0, blocks[0], come)
    return blocks


def read_modes(block):
    nch = D // 16
    small = block[0].reshape(4, nch)
    rest = block[1:].reshape(4, nch, NSTATE)
    return small, rest


def gather_modes(block, steps):
    for step in steps:
        pairs = [(i, i - step) for i in range(2 * step) if i >= step]
        block = jnp.concatenate([block, lax.ppermute(block, "seq", pairs)])
    return block


def mode_vector(block):
    blocks = block.reshape(2, 2, 2, 2, 3, -1, CH).transpose(4, 3, 2, 1, 0, 5, 6).reshape(3, D, CH)
    few = blocks[2, :, :4].T
    return jnp.concatenate([v.reshape(-1) for v in (few, blocks[0, :, :NSTATE], blocks[0, :, NSTATE:], blocks[1, :, :NSTATE], blocks[1, :, NSTATE:])])


def total_of(v):
    if not direct():
        return lax.psum(v, AXES)
    terms = lax.all_to_all(jnp.broadcast_to(v, (32, CH)), AXES, 0, 0)
    return jnp.sum(terms[:, 0])


def to_channels(rows):
    seq = lax.axis_size("seq")
    parts = rows.shape[0] // CH
    turned = rows.reshape(parts, CH, seq, D // seq).transpose(2, 0, 3, 1)
    return lax.all_to_all(turned, "seq", 0, 0).reshape(-1, CH)


def to_tokens(rows, group):
    seq = lax.axis_size("seq")
    turned = lax.all_to_all(rows.reshape(seq, group // CH, D // seq, CH), "seq", 0, 0)
    return turned.transpose(1, 3, 0, 2).reshape(group, D)


def per_device(inputs, cotangent, lengths, master, first_moment, second_moment):
    seq, batch = lax.axis_size("seq"), lax.axis_size("batch")
    devices = seq * batch
    share = master.shape[0]
    box = container(master, share, devices)
    if direct():
        near = gather_near(box)
    else:
        streams, ids = ((0, box.shape[0] // 8, 0, devices),), jnp.arange(devices, dtype=jnp.int32)
        boxes = [lax.all_gather(box, AXES, axis=0, tiled=True)]
    group = inputs.shape[1]
    nch, nck = D // seq, seq * group // CH
    rows = inputs[0].astype(jnp.float32)
    ends = jnp.cumsum(lengths[0]).astype(jnp.int32)
    place = jnp.concatenate([ends, lax.axis_index("seq")[None] * group]).astype(jnp.int32)
    first_hat, first_scale = normalize(rows)
    hats = to_channels(first_hat)

    plan, slots = scatter_plan(share, devices)

    def feed_forward(response):
        return mlp_kernel(place, streams, ids, boxes, plan, slots, response, inputs[0], cotangent[0], share, devices, seq)

    if direct():
        few, many = read_modes(scatter_modes(master))
    else:
        lead = jnp.concatenate([lax.dynamic_slice(boxes[0][j * box.shape[0]:(j + 1) * box.shape[0]].reshape(-1), (j * share % TILE,), (share,)) for j in range(MODE_TILES * TILE // share + 1)])
        mine = lambda v: lax.dynamic_slice_in_dim(v, lax.axis_index("seq") * nch, nch, 1)
        few = mine(lead[:4 * D].reshape(4, D))
        many = mine(lead[4 * D:MODE_TILES * TILE].reshape(4, D, NSTATE))
    if direct():
        plane = gather_plane(near)
    modes, coefs = mixing(few[2], many[0], many[1], many[2], many[3])
    prm = mode_rows(*modes, few[0], few[1], few[3])
    outs, prior, *tables = ssm_forward(ends, prm, hats, nck, nch)
    response = lax.all_to_all(outs.reshape(seq, -1, nch, CH), "seq", 0, 0).reshape(-1, CH)
    if direct():
        far = [hop(plane[0], 2), hop(plane[1], 1)]
        response, far = lax.optimization_barrier((response, far))
        streams, ids, boxes = gather_cores(plane, far, box.shape[0] // 8)
    output, d_mid, d_response, lead, *packed = feed_forward(response)
    d_outs = lax.all_to_all(d_response.reshape(seq, -1, nch, CH), "seq", 0, 0).reshape(-1, CH)
    if direct():
        packed = join_cores(packed)
        d_outs, packed = lax.optimization_barrier((d_outs, packed))
    d_signals, sums = ssm_backward(ends, prm, hats, d_outs, prior, tables, coefs, nck, nch)
    if direct():
        d_signals, sums, packed = lax.optimization_barrier((d_signals, sums, join_first(packed)))
    d_signal = to_tokens(d_signals, group)
    norm_gain = lead[:D // CH].reshape(D)
    me = device_index()
    if direct():
        own = sums.reshape(-1, CH)
        own, packed = lax.optimization_barrier((own + swap_cores(own), join_second(packed)))
        box, block, d_signal = lax.optimization_barrier((join_last(packed), gather_modes(own, (8, 4, 2)), d_signal))
    else:
        box = lax.psum_scatter(packed[0].reshape(devices, -1, CH), AXES, scatter_dimension=0)
    d_rows = d_mid + norm_back(d_signal * norm_gain, first_hat, first_scale)
    shard = lax.dynamic_slice(box.reshape(-1), (me * share % TILE,), (share,))
    mark = me * share + jnp.arange(share, dtype=jnp.int32) < MODE_TILES * TILE
    squares = jnp.sum(jnp.where(mark, 0.0, shard * shard))
    if direct():
        squares = squares + 0.5 * jnp.sum(own * own)
        lead = mode_vector(gather_modes(block, (1,)))
    else:

        def spread(v):
            whole = jnp.zeros((v.shape[0], D) + v.shape[2:], f32)
            return lax.dynamic_update_slice_in_dim(whole, v, lax.axis_index("seq") * nch, 1)

        few = sums[2, :, :4].T
        many = jnp.stack([sums[0, :, :NSTATE], sums[0, :, NSTATE:], sums[1, :, :NSTATE], sums[1, :, NSTATE:]])
        lead = lax.psum(jnp.concatenate([spread(few).reshape(-1), spread(many).reshape(-1)]), AXES)
        squares = squares + jnp.sum(lead * lead) / devices
    lead = lax.dynamic_slice(jnp.pad(lead, (0, share)), (jnp.minimum(me * share, MODE_TILES * TILE),), (share,))
    shard = jnp.where(mark, lead, shard)
    total = total_of(squares)
    grad_norm = jnp.sqrt(total)
    factor = jnp.minimum(1.0, 1.0 / (grad_norm + 1e-06))
    clipped = shard * factor
    first_new = 0.9 * first_moment + 0.1 * clipped
    second_new = 0.999 * second_moment + 0.001 * clipped * clipped
    first_hat_new = first_new / (1.0 - 0.9**10)
    second_hat_new = second_new / (1.0 - 0.999**10)
    update = -0.05 * (first_hat_new / (jnp.sqrt(second_hat_new) + 1e-08) + 0.1 * master)
    return (output[None], d_rows[None], shard, update, first_new, second_new, grad_norm)


def solution(mesh):
    placed = (
        P("batch", "seq", None),
        P("batch", "seq", None),
        P("batch", None),
        P(("seq", "batch")),
        P(("seq", "batch")),
        P(("seq", "batch")),
    )
    return jax.shard_map(
        per_device,
        mesh=mesh,
        in_specs=placed,
        out_specs=(
            P("batch", "seq", None),
            P("batch", "seq", None),
            P(("seq", "batch")),
            P(("seq", "batch")),
            P(("seq", "batch")),
            P(("seq", "batch")),
            P(),
        ),
        check_vma=False,
    )
```

```python
from functools import partial
import jax
import jax.numpy as jnp
import numpy as np
from jax import lax
from jax.experimental import pallas as pl
from jax.experimental.pallas import tpu as pltpu
from jax.sharding import PartitionSpec as P

D = 512
NSTATE = 64
CH = 128
DOCS = 4
G = 1024
FF = 2048
Z_FIRST = 0.2


norm_eps = 1e-05
root_half = 0.7071067811865476
inv_root_two_pi = 0.3989422804014327


f32 = jnp.float32
bf16 = jnp.bfloat16

def split(v):
    hi = v.astype(bf16)
    return hi, (v - hi.astype(f32)).astype(bf16)

def dot3(a, b, ca, cb):
    ah, al = a
    bh, bl = b
    lhs = jnp.concatenate([ah, ah, al], axis=ca)
    rhs = jnp.concatenate([bh, bl, bh], axis=cb)
    return lax.dot_general(lhs, rhs, (((ca,), (cb,)), ((), ())), preferred_element_type=f32)

def dot2(data, table, ct):
    return dot3(data, (table[0], table[1]), 1, ct)

def swap(v):
    return pltpu.roll(v, NSTATE, 1)

def twist(table, re, im):
    return re * table + im * swap(table)

def ladder(prm, order):
    sub = lax.broadcasted_iota(jnp.int32, (8, 2 * NSTATE), 0)
    lane = lax.broadcasted_iota(jnp.int32, (8, 2 * NSTATE), 1)
    power = sub if order == 1 else 7 - sub
    table = jnp.where(lane < NSTATE, 1.0, 0.0).astype(f32)
    for bit in range(3):
        table = jnp.where((power >> bit) & 1 == 1, twist(table, prm[2 * bit:2 * bit + 1], prm[2 * bit + 1:2 * bit + 2]), table)
    for bit in range(3, 7):
        more = twist(table, prm[2 * bit:2 * bit + 1], prm[2 * bit + 1:2 * bit + 2])
        table = jnp.concatenate([table, more] if order == 1 else [more, table], axis=0)
    return table

def toeplitz(taps):
    wide = pltpu.roll(jnp.broadcast_to(taps, (CH, CH)), 0, 1, stride=1, stride_axis=0)
    row = lax.broadcasted_iota(jnp.int32, (CH, CH), 0)
    col = lax.broadcasted_iota(jnp.int32, (CH, CH), 1)
    return jnp.where(col >= row, wide, 0.0)

def label_at(ends, pos):
    total = jnp.zeros_like(pos)
    for k in range(DOCS):
        total = total + (pos >= ends[k]).astype(jnp.int32)
    return total

def make_masks(ends_ref, masks_ref, low_ref, nck):
    ends = [ends_ref[k] for k in range(DOCS)]
    row = lax.broadcasted_iota(jnp.int32, (nck, CH), 0)
    lane = lax.broadcasted_iota(jnp.int32, (nck, CH), 1)
    base = row * CH
    label = label_at(ends, base + lane)
    prev = jnp.where(base == 0, -1, label_at(ends, base - 1))
    last = label_at(ends, base + CH - 1)
    for k in range(DOCS):
        masks_ref[k] = (label == k).astype(f32)
    masks_ref[DOCS] = (label == prev).astype(f32)
    masks_ref[DOCS + 1] = (label == last).astype(f32)
    low_ref[:DOCS + 2] = masks_ref[...].astype(bf16)
    if low_ref.shape[0] > DOCS + 2:
        label = label_at(ends, base + (CH - 1 - lane))
        for k in range(DOCS):
            low_ref[DOCS + 2 + k] = (label == k).astype(f32).astype(bf16)

def keep_of(ends_ref, c):
    first = jnp.int32(0)
    second = jnp.int32(0)
    for k in range(DOCS):
        first = first + (c * CH - 1 >= ends_ref[k]).astype(jnp.int32)
        second = second + (c * CH + CH - 1 >= ends_ref[k]).astype(jnp.int32)
    return jnp.where((c > 0) & (first == second), 1.0, 0.0).astype(f32)

def masked_rows(v, low_ref):
    return [jnp.concatenate([part * low_ref[k] for k in range(DOCS)], axis=0) for part in v]

def masked(v, low_ref, k):
    return [part * low_ref[k] for part in v]

def fold_rows(v, masks_ref, nck):
    total = v[:nck] * masks_ref[0]
    for k in range(1, DOCS):
        total = total + v[k * nck:(k + 1) * nck] * masks_ref[k]
    return total

def keep(ref, h, v):
    ref[h, 0], ref[h, 1] = split(v)

def for_channels(nch, body):
    lax.fori_loop(0, nch, lambda h, _: body(h) or 0, 0, unroll=min(nch, 16))

def fwd_body(nck, nch, apart, ends_ref, prm_ref, x_ref, y_ref, prior_ref, table_ref, down_ref, out_ref, mat_ref, masks_ref, low_ref, end_ref):
    make_masks(ends_ref, masks_ref, low_ref, nck)

    def tables(h):
        prm = prm_ref[h]
        table = ladder(prm, 1)
        keep(table_ref, h, table)
        keep(out_ref, h, twist(table, prm[17:18], prm[18:19]))

    def falling(h):
        keep(down_ref, h, ladder(prm_ref[h], -1))

    def taps(h):
        wrow = jnp.broadcast_to(prm_ref[h, 16:17, :], (16, 2 * NSTATE))
        keep(mat_ref, h, toeplitz(dot2(split(wrow), table_ref[h], 1)[0:1]))

    def local(h):
        prm = prm_ref[h, 16:24, :]
        u = x_ref[pl.ds(h, nck, stride=apart), :] * prm[3:4] + prm[4:5]
        parts = split(u)
        local = dot2(masked_rows(parts, low_ref), mat_ref[h], 0)
        y_ref[pl.ds(h, nck, stride=nch), :] = fold_rows(local, masks_ref, nck) + prm[5:6] * u
        end_ref[pl.ds(h, nck, stride=nch), :] = dot2(masked(parts, low_ref, DOCS + 1), down_ref[h], 0)

    for body in (tables, falling, taps, local):
        for_channels(nch, body)
    full_re = prm_ref[:, 14, :]
    full_im = prm_ref[:, 15, :]

    def step(c, state):
        at = pl.ds(pl.multiple_of(c * nch, 8), nch)
        prior_ref[at, :] = state
        return keep_of(ends_ref, c) * twist(state, full_re, full_im) + end_ref[at, :]

    lax.fori_loop(0, nck, step, jnp.zeros((nch, 2 * NSTATE), f32))

    def carried(h):
        prior = split(prior_ref[pl.ds(h, nck, stride=nch), :])
        y_ref[pl.ds(h, nck, stride=nch), :] += dot2(prior, out_ref[h], 1) * masks_ref[DOCS]

    for_channels(nch, carried)

def ssm_forward(ends, prm, x, nck, nch):
    vm = pl.BlockSpec(memory_space=pltpu.VMEM)
    table = jax.ShapeDtypeStruct((nch, 2, CH, 2 * NSTATE), bf16)
    return pl.pallas_call(
        partial(fwd_body, nck, nch, x.shape[0] // nck),
        out_shape=(jax.ShapeDtypeStruct((nck * nch, CH), f32), jax.ShapeDtypeStruct((nck * nch, 2 * NSTATE), f32)) + (table,) * 4,
        in_specs=[pl.BlockSpec(memory_space=pltpu.SMEM), vm, vm],
        out_specs=(vm,) * 6,
        scratch_shapes=[
            pltpu.VMEM((DOCS + 2, nck, CH), f32),
            pltpu.VMEM((DOCS + 2, nck, CH), bf16),
            pltpu.VMEM((nck * nch, 2 * NSTATE), f32),
        ],
        cost_estimate=pl.CostEstimate(flops=int(2.0e10), bytes_accessed=3 * 2**20, transcendentals=0),
        name="state_forward",
    )(ends, prm, x)

def bwd_body(nck, nch, apart, ends_ref, prm_ref, x_ref, g_ref, prior_ref, table_ref, down_ref, out_ref, mat_ref, coef_ref, dx_ref, grad_ref, rows_ref, masks_ref, low_ref, lead_ref, adj_ref, taps_ref):
    make_masks(ends_ref, masks_ref, low_ref, nck)
    at_channel = lambda h: pl.ds(h, nck, stride=nch)

    def lead(h):
        lead_ref[at_channel(h), :] = dot2(masked(split(g_ref[at_channel(h), :]), low_ref, DOCS), out_ref[h], 0)

    for_channels(nch, lead)
    full_re = prm_ref[:, 14, :]
    full_im = prm_ref[:, 15, :]
    zero = jnp.zeros((nch, 2 * NSTATE), f32)

    def step(k, carry):
        adjoint, same, cross = carry
        c = nck - 1 - k
        at = pl.ds(pl.multiple_of(c * nch, 8), nch)
        adj_ref[at, :] = adjoint
        keep = keep_of(ends_ref, c)
        prior = prior_ref[at, :]
        same = same + keep * adjoint * prior
        cross = cross + keep * adjoint * swap(prior)
        adjoint = lead_ref[at, :] + keep * (full_re * adjoint - full_im * swap(adjoint))
        return adjoint, same, cross

    _, same, cross = lax.fori_loop(0, nck, step, (zero, zero, zero))
    rows_ref[8] = same
    rows_ref[9] = cross
    row = lax.broadcasted_iota(jnp.int32, (CH, CH), 0)
    col = lax.broadcasted_iota(jnp.int32, (CH, CH), 1)
    flip = (row + col == CH - 1).astype(f32).astype(bf16)
    put = lambda k, h, v: rows_ref.__setitem__((k, pl.ds(h, 1), slice(None)), jnp.sum(v, axis=0, keepdims=True))

    def signal(h):
        prm = prm_ref[h, 16:24, :]
        x = x_ref[pl.ds(h, nck, stride=apart), :]
        g = g_ref[at_channel(h), :]
        du = fold_rows(dot2(masked_rows(split(g), low_ref), mat_ref[h], 1), masks_ref, nck)
        du = du + dot2(split(adj_ref[at_channel(h), :]), down_ref[h], 1) * masks_ref[DOCS + 1]
        du = du + prm[5:6] * g
        dx_ref[at_channel(h), :] = du
        put(10, h, g * (x * prm[3:4] + prm[4:5]))
        put(11, h, du * x)
        put(12, h, du)

    def taps(h):
        prm = prm_ref[h, 16:24, :]
        u = split(x_ref[pl.ds(h, nck, stride=apart), :] * prm[3:4] + prm[4:5])
        both = jnp.dot(jnp.concatenate(u, axis=0), flip, preferred_element_type=f32).astype(bf16)
        um = []
        for part in (both[:nck], both[nck:]):
            um.append(jnp.concatenate([part * low_ref[DOCS + 2 + k] for k in range(DOCS)], axis=0))
        square = dot3(um, masked_rows(split(g_ref[at_channel(h), :]), low_ref), 0, 0)
        square = jnp.where(row + col >= CH - 1, square, 0.0)
        square = pltpu.roll(square, 1, 1, stride=1, stride_axis=0)
        taps_ref[pl.ds(h, 1), :] = jnp.sum(square, axis=0, keepdims=True)

    def kernel(h):
        place = lax.broadcasted_iota(jnp.int32, (16, CH), 1).astype(f32)
        sub = lax.broadcasted_iota(jnp.int32, (16, CH), 0)
        both = jnp.where(sub == 0, 1.0, jnp.where(sub == 1, place, 0.0)) * taps_ref[pl.ds(h, 1), :]
        both = dot2(split(both), table_ref[h], 0)
        rows_ref[0, pl.ds(h, 1), :] = both[0:1]
        rows_ref[1, pl.ds(h, 1), :] = both[1:2]

    late = row.astype(f32)

    def carried(h):
        dgt = dot3(masked(split(g_ref[at_channel(h), :]), low_ref, DOCS), split(prior_ref[at_channel(h), :]), 0, 0)
        table = table_ref[h, 0].astype(f32) + table_ref[h, 1].astype(f32)
        same, cross = dgt * table, dgt * swap(table)
        put(2, h, same)
        put(3, h, cross)
        put(4, h, same * late)
        put(5, h, cross * late)

    def ending(h):
        prm = prm_ref[h, 16:24, :]
        u = split(x_ref[pl.ds(h, nck, stride=apart), :] * prm[3:4] + prm[4:5])
        ddown = dot3(masked(u, low_ref, DOCS + 1), split(adj_ref[at_channel(h), :]), 0, 0) * ((CH - 1) - late)
        down = down_ref[h, 0].astype(f32) + down_ref[h, 1].astype(f32)
        put(6, h, ddown * down)
        put(7, h, ddown * swap(down))

    for body in (signal, taps, kernel, carried, ending):
        for_channels(nch, body)
    rows = [rows_ref[k] for k in range(13)]
    total = lambda v: jnp.sum(v, axis=1, keepdims=True)
    d_step, d_decay, d_frequency, d_real, d_imag = mode_grads(rows, [coef_ref[k] for k in range(14)])
    grad_ref[0] = jnp.concatenate([d_decay, d_frequency], axis=1)
    grad_ref[1] = jnp.concatenate([d_real, d_imag], axis=1)
    lane = lax.broadcasted_iota(jnp.int32, (nch, CH), 1)
    few = jnp.zeros((nch, CH), f32)
    for k, v in enumerate((total(rows[11]), total(rows[12]), total(d_step), total(rows[10]))):
        few = jnp.where(lane == k, v, few)
    grad_ref[2] = few

def ssm_backward(ends, prm, x, g, prior, tables, coefs, nck, nch):
    vm = pl.BlockSpec(memory_space=pltpu.VMEM)
    return pl.pallas_call(
        partial(bwd_body, nck, nch, x.shape[0] // nck),
        out_shape=(jax.ShapeDtypeStruct((nck * nch, CH), f32), jax.ShapeDtypeStruct((3, nch, 2 * NSTATE), f32)),
        in_specs=[pl.BlockSpec(memory_space=pltpu.SMEM)] + [vm] * 9,
        out_specs=(vm, vm),
        scratch_shapes=[
            pltpu.VMEM((13, nch, 2 * NSTATE), f32),
            pltpu.VMEM((DOCS + 2, nck, CH), f32),
            pltpu.VMEM((2 * DOCS + 2, nck, CH), bf16),
            pltpu.VMEM((nck * nch, 2 * NSTATE), f32),
            pltpu.VMEM((nck * nch, 2 * NSTATE), f32),
            pltpu.VMEM((nch, CH), f32),
        ],
        cost_estimate=pl.CostEstimate(flops=int(3.5e10), bytes_accessed=4 * 2**20, transcendentals=0),
        name="state_backward",
    )(ends, prm, x, g, prior, *tables, coefs)

def mixing(step_log, decay_log, frequency, out_real, out_imag):
    delta = jnp.exp(step_log)[:, None]
    rate_re = -jnp.exp(decay_log)
    arg_re, arg_im = delta * rate_re, delta * frequency
    magnitude = jnp.exp(arg_re)
    p_re, p_im = magnitude * jnp.cos(arg_im), magnitude * jnp.sin(arg_im)
    inverse = 1.0 / (rate_re * rate_re + frequency * frequency)
    ratio_re = ((p_re - 1.0) * rate_re + p_im * frequency) * inverse
    ratio_im = (p_im * rate_re - (p_re - 1.0) * frequency) * inverse
    mix_re = out_real * ratio_re - out_imag * ratio_im
    mix_im = out_real * ratio_im + out_imag * ratio_re
    magnitude = jnp.exp(arg_re * CH)
    f_re, f_im = magnitude * jnp.cos(arg_im * CH), magnitude * jnp.sin(arg_im * CH)
    wide = jnp.broadcast_to(delta, arg_re.shape)
    coefs = jnp.stack([p_re, p_im, f_re, f_im, mix_re, mix_im, out_real, out_imag, ratio_re, ratio_im, rate_re, frequency, inverse, wide])
    return (arg_re, arg_im, mix_re, mix_im), coefs

def pair(left, right):
    return jnp.concatenate([left, right], axis=-1)

def mode_rows(arg_re, arg_im, mix_re, mix_im, gain, bias, skip):
    nch = arg_re.shape[0]
    scale = jnp.asarray([2.0**b for b in range(8)], f32)[None, :, None]
    magnitude = jnp.exp(arg_re[:, None] * scale)
    p_re = magnitude * jnp.cos(arg_im[:, None] * scale)
    p_im = magnitude * jnp.sin(arg_im[:, None] * scale)
    powers = jnp.stack([pair(p_re, p_re), pair(-p_im, p_im)], axis=2).reshape(nch, 16, 2 * NSTATE)
    c_re = mix_re * p_re[:, 0] - mix_im * p_im[:, 0]
    c_im = mix_re * p_im[:, 0] + mix_im * p_re[:, 0]
    flat = lambda v: jnp.broadcast_to(v[:, None], (nch, 2 * NSTATE))
    rest = jnp.stack([pair(mix_re, -mix_im), pair(c_re, -c_re), pair(-c_im, -c_im), flat(gain), flat(bias), flat(skip), flat(0 * gain), flat(0 * gain)], axis=1)
    return jnp.concatenate([powers, rest], axis=1)

def mode_grads(rows, coefs):
    p_re, p_im, f_re, f_im, mix_re, mix_im, out_real, out_imag, ratio_re, ratio_im, rate, freq, inverse, delta = coefs
    lo = [v[:, :NSTATE] for v in rows]
    hi = [v[:, NSTATE:] for v in rows]
    a_re, a_im = lo[2] - hi[2], -(hi[3] + lo[3])
    b_re, b_im = lo[4] - hi[4] + a_re, a_im - (hi[5] + lo[5])
    w_re = lo[0] + p_re * a_re + p_im * a_im
    w_im = -hi[0] + p_re * a_im - p_im * a_re
    v_re = lo[1] + p_re * b_re + p_im * b_im
    v_im = -hi[1] + p_re * b_im - p_im * b_re
    d_re, d_im = lo[8] + hi[8], hi[9] - lo[9]
    g_re = mix_re * v_re + mix_im * v_im + lo[6] + hi[6] + CH * (f_re * d_re + f_im * d_im)
    g_im = mix_re * v_im - mix_im * v_re + hi[7] - lo[7] + CH * (f_re * d_im - f_im * d_re)
    d_real, d_imag = w_re * ratio_re + w_im * ratio_im, w_im * ratio_re - w_re * ratio_im
    r_re = (w_re * out_real + w_im * out_imag) * inverse
    r_im = (w_im * out_real - w_re * out_imag) * inverse
    fall = 2.0 * (r_re * ratio_re + r_im * ratio_im)
    pole_re = r_re * rate - r_im * freq
    pole_im = r_re * freq + r_im * rate
    d_rate = r_re * (p_re - 1.0) + r_im * p_im - fall * rate
    d_freq = r_re * p_im - r_im * (p_re - 1.0) - fall * freq
    g_re = g_re + pole_re * p_re + pole_im * p_im
    g_im = g_im + pole_im * p_re - pole_re * p_im
    d_step = delta * (rate * g_re + freq * g_im)
    return d_step, (d_rate + delta * g_re) * rate, d_freq + delta * g_im, d_real, d_imag


def gelu(values):
    return 0.5 * values * (1.0 + lax.erf(values * root_half))


def gelu_slope(values):
    return (
        0.5 * (1.0 + lax.erf(values * root_half))
        + values * jnp.exp(-0.5 * values * values) * inv_root_two_pi
    )


def normalize(values):
    center = values - jnp.mean(values, axis=-1, keepdims=True)
    scale = lax.rsqrt(jnp.mean(center * center, axis=-1, keepdims=True) + norm_eps)
    return (center * scale, scale)


def norm_back(d_hat, hat, scale):
    return scale * (
        d_hat
        - jnp.mean(d_hat, axis=-1, keepdims=True)
        - hat * jnp.mean(d_hat * hat, axis=-1, keepdims=True)
    )


TILE = 1024
GATE_AT, EXPAND_AT, REDUCE_AT = 130, 644, 1670
SMALL_AT = (642, 643, 1668, 1669, 2694)
MODE_TILES = 130
BLOCK = 512


def lay(share, devices):
    base = share // TILE
    return base, base + 2, (devices - 1) * share // TILE + base + 2


def product(a, b, ca, cb):
    return lax.dot_general(a, b, (((ca,), (cb,)), ((), ())), preferred_element_type=f32)


def narrow(flat, out, first, rows, per):
    def one(i, _):
        for k in range(per):
            v = flat[pl.ds(first * 8 + i * 16 * per + k, 16, stride=per), :]
            out[pl.ds(pl.multiple_of(i * 16, 16), 16), k * CH:(k + 1) * CH] = v.astype(bf16)
        return 0

    lax.fori_loop(0, rows // 16, one, 0, unroll=max(1, 16 // per))


def small_row(flat, tile, begin, count):
    return jnp.concatenate([flat[tile * 8 + (begin + k) // CH:tile * 8 + (begin + k) // CH + 1, :] for k in range(0, count, CH)], axis=1)


def put_small(small_ref, begin, row):
    for k in range(row.shape[1] // CH):
        small_ref[begin // CH + k:begin // CH + k + 1, :] = row[:, k * CH:(k + 1) * CH]


def column_sum(v):
    return jnp.sum(v, axis=0, keepdims=True)


def mlp_body(share, devices, nseq, streams, plan, place_ref, ids, slots, *refs):
    boxes = refs[:len(streams)]
    resp_ref, x_ref, cot_ref, out_ref, dmid_ref, dresp_ref, lead_ref = refs[len(streams):len(streams) + 7]
    ways = 2 if len(plan) > 1 else 1
    outs = refs[len(streams) + 7:len(streams) + 7 + ways * len(plan)]
    small_ref, hidden_ref, active_ref, normed_ref, back_ref, dopen_ref, dlift_ref, flat, side, gate, expand, reduce, acc, dnorm, sems, out_sems = refs[len(streams) + 7 + len(outs):]
    base, box, _ = lay(share, devices)
    nch = D // nseq
    group = x_ref.shape[0]
    start_of = lambda j: (j * share) // TILE
    inside = 0
    for k, (first, last, off, count) in enumerate(streams):
        lo, hi = max(first, 1), min(last, base)

        def copy_box(i, _, k=k, first=first, last=last, lo=lo, hi=hi, off=off):
            j = ids[off + i]
            begin = (i * (last - first) - first) * 8
            for s, tile in enumerate((0, base, base + 1)):
                if first <= tile < last:
                    pltpu.make_async_copy(boxes[k].at[pl.ds(pl.multiple_of(begin + tile * 8, 8), 8), :], side.at[s, pl.ds(pl.multiple_of(j * 8, 8), 8), :], sems.at[1]).start()
            pltpu.make_async_copy(
                boxes[k].at[pl.ds(pl.multiple_of(begin + lo * 8, 8), (hi - lo) * 8), :],
                flat.at[pl.ds(pl.multiple_of((start_of(j) + lo) * 8, 8), (hi - lo) * 8), :],
                sems.at[0],
            ).start()
            return 0

        lax.fori_loop(0, count, copy_box, 0, unroll=8)
        inside += (hi - lo) * count
    parts = group // CH
    turned = [
        jnp.concatenate([resp_ref[pl.ds((d * parts + k) * nch, nch), :] for d in range(nseq)], axis=0).T
        for k in range(parts)
    ]
    response = jnp.concatenate(turned, axis=0)
    hidden_ref[...] = gelu(response).astype(bf16)
    pos = place_ref[DOCS] + lax.broadcasted_iota(jnp.int32, (group, D), 0)
    total = jnp.zeros((group, D), jnp.int32)
    for k in range(DOCS):
        total = total + (pos >= place_ref[k]).astype(jnp.int32)
    back = jnp.where(total < DOCS - 1, cot_ref[...].astype(f32), 0.0)
    back_ref[...] = back.astype(bf16)
    put_small(small_ref, 2 * G + FF, column_sum(back))
    small_ref[36:40, :] = jnp.zeros((4, CH), f32)
    inner = side.at[:, pl.ds(0, devices * 8), :]
    pltpu.make_async_copy(inner, inner, sems.at[1]).wait()
    side[0, devices * 8:, :] = jnp.zeros((8, CH), f32)
    flat[:8, :] = side[0, :8, :]

    def join(j, _):
        at = start_of(j)
        step = start_of(j + 1) - at
        far = jnp.broadcast_to(step, (8, CH)) > base
        here = pl.ds(pl.multiple_of(j * 8, 8), 8)
        one, two, then = side[1, here, :], side[2, here, :], side[0, pl.ds(pl.multiple_of(j * 8 + 8, 8), 8), :]
        flat[pl.ds(pl.multiple_of((at + base) * 8, 8), 8), :] = one + jnp.where(far, 0.0, then)
        flat[pl.ds(pl.multiple_of((at + step) * 8, 8), 8), :] = jnp.where(far, two, one) + then
        return 0

    lax.fori_loop(0, devices, join, 0, unroll=8)

    some = flat.at[pl.ds(0, inside * 8), :]
    pltpu.make_async_copy(some, some, sems.at[0]).wait()
    lead_ref[...] = flat[:8, :]
    narrow(flat, gate, GATE_AT, D, G // CH)
    gate_bias = small_row(flat, SMALL_AT[0], 0, G)
    second_gain = small_row(flat, SMALL_AT[1], 0, D)
    second_bias = small_row(flat, SMALL_AT[1], D, D)
    hidden = hidden_ref[...]
    linear = product(hidden, gate[:, :D], 1, 0) + gate_bias[:, :D]
    gating = jax.nn.sigmoid(product(hidden, gate[:, D:], 1, 0) + gate_bias[:, D:])
    mid = x_ref[...].astype(f32) + linear * gating
    hat, scale = normalize(mid)
    normed_ref[...] = (hat * second_gain + second_bias).astype(bf16)
    narrow(flat, expand, EXPAND_AT, D, FF // CH)
    narrow(flat, reduce, REDUCE_AT, FF, D // CH)
    dnorm[...] = jnp.zeros((group, D), f32)
    acc[...] = mid + small_row(flat, SMALL_AT[4], 0, D)
    for b in range(FF // BLOCK):
        at = slice(b * BLOCK, (b + 1) * BLOCK)
        bias = small_row(flat, SMALL_AT[2] + b * BLOCK // TILE, b * BLOCK % TILE, BLOCK)
        lifted = product(normed_ref[...], expand[:, at], 1, 0) + bias
        half = 0.5 * (1.0 + lax.erf(lifted * root_half))
        active = (lifted * half).astype(bf16)
        active_ref[:, at] = active
        slope = half + lifted * jnp.exp(-0.5 * lifted * lifted) * inv_root_two_pi
        d_lifted = (product(back_ref[...], reduce[at, :], 1, 1) * slope).astype(bf16)
        dlift_ref[:, at] = d_lifted
        put_small(small_ref, 2 * G + b * BLOCK, column_sum(d_lifted.astype(f32)))
        acc[...] += product(active, reduce[at, :], 1, 0)
        dnorm[...] += product(d_lifted, expand[:, at], 1, 1)
    out_ref[...] = acc[...].astype(bf16)
    d_normed = dnorm[...]
    put_small(small_ref, G, column_sum(d_normed * hat))
    put_small(small_ref, G + D, column_sum(d_normed))
    d_mid = back_ref[...].astype(f32) + norm_back(d_normed * second_gain, hat, scale)
    dmid_ref[...] = d_mid
    d_linear = (d_mid * gating).astype(bf16)
    d_gating = (d_mid * linear * gating * (1.0 - gating)).astype(bf16)
    dopen_ref[:, :D] = d_linear
    dopen_ref[:, D:] = d_gating
    put_small(small_ref, 0, column_sum(d_linear.astype(f32)))
    put_small(small_ref, D, column_sum(d_gating.astype(f32)))
    d_hidden = product(d_linear, gate[:, :D], 1, 1) + product(d_gating, gate[:, D:], 1, 1)
    for k in range(parts):
        again = jnp.concatenate([resp_ref[pl.ds((d * parts + k) * nch, nch), :] for d in range(nseq)], axis=0)
        back_turned = d_hidden[k * CH:(k + 1) * CH].T * gelu_slope(again)
        for d in range(nseq):
            dresp_ref[pl.ds((d * parts + k) * nch, nch), :] = back_turned[d * nch:(d + 1) * nch]

    flat[:MODE_TILES * 8, :] = jnp.zeros((MODE_TILES * 8, CH), f32)
    for k, tile in enumerate(SMALL_AT):
        flat[tile * 8:(tile + 1) * 8, :] = small_ref[k * 8:(k + 1) * 8, :]
    flat[(SMALL_AT[-1] + 1) * 8:, :] = jnp.zeros((flat.shape[0] - (SMALL_AT[-1] + 1) * 8, CH), f32)
    sent = 0
    for first, left, right, per, until in (
        (GATE_AT, hidden_ref, dopen_ref, G // CH, EXPAND_AT),
        (EXPAND_AT, normed_ref, dlift_ref, FF // CH, REDUCE_AT),
        (REDUCE_AT, active_ref, back_ref, D // CH, flat.shape[0]),
    ):
        flip = left[...].T
        for k in range(left.shape[1] // CH):
            v = product(flip[k * CH:(k + 1) * CH], right[...], 1, 0)
            for c in range(per):
                flat[pl.ds(first * 8 + k * CH * per + c, CH, stride=per), :] = v[:, c * CH:(c + 1) * CH]
        ready = sum((j * share) // TILE + box <= until for j in range(devices))
        for k, (low, high) in enumerate(plan):
            rows = (high - low) * 8

            def send(j, _, k=k, low=low, rows=rows):
                slot = slots[k * devices + j]
                block = flat.at[pl.ds(pl.multiple_of((start_of(j) + low) * 8, 8), rows), :]
                for o in range(ways):
                    at = slot - o * (devices // ways)

                    @pl.when((at >= 0) & (at < devices // ways))
                    def _():
                        target = outs[k * ways + o].at[pl.ds(pl.multiple_of(at * rows, 8), rows), :]
                        pltpu.make_async_copy(block, target, out_sems.at[k * ways + o]).start()

                return 0

            lax.fori_loop(sent, ready, send, 0)
        sent = ready
    for k, out in enumerate(outs):
        pltpu.make_async_copy(out, out, out_sems.at[k]).wait()


def mlp_kernel(place, streams, ids, boxes, plan, slots, response, rows, cotangent, share, devices, nseq):
    base, box, tiles = lay(share, devices)
    group = rows.shape[0]
    vm = pl.BlockSpec(memory_space=pltpu.VMEM)
    hbm = pl.BlockSpec(memory_space=pl.ANY)
    smem = pl.BlockSpec(memory_space=pltpu.SMEM)
    shape = lambda r, c, t: jax.ShapeDtypeStruct((r, c), t)
    count = 2 if len(plan) > 1 else 1
    packed = [shape(devices // count * (high - low) * 8, CH, f32) for low, high in plan for _ in range(count)]
    return pl.pallas_call(
        partial(mlp_body, share, devices, nseq, streams, plan),
        out_shape=(
            shape(group, D, bf16),
            shape(group, D, f32),
            jax.ShapeDtypeStruct(response.shape, f32),
            shape(8, CH, f32),
            *packed,
        ),
        in_specs=[smem] * 3 + [hbm] * len(boxes) + [vm] * 3,
        out_specs=(vm,) * 4 + (hbm,) * len(packed),
        scratch_shapes=[
            pltpu.VMEM((len(SMALL_AT) * 8, CH), f32),
            pltpu.VMEM((group, D), bf16),
            pltpu.VMEM((group, FF), bf16),
            pltpu.VMEM((group, D), bf16),
            pltpu.VMEM((group, D), bf16),
            pltpu.VMEM((group, G), bf16),
            pltpu.VMEM((group, FF), bf16),
            pltpu.VMEM((tiles * 8, CH), f32),
            pltpu.VMEM((3, devices * 8 + 8, CH), f32),
            pltpu.VMEM((D, G), bf16),
            pltpu.VMEM((D, FF), bf16),
            pltpu.VMEM((FF, D), bf16),
            pltpu.VMEM((group, D), f32),
            pltpu.VMEM((group, D), f32),
            pltpu.SemaphoreType.DMA((2,)),
            pltpu.SemaphoreType.DMA((len(packed),)),
        ],
        cost_estimate=pl.CostEstimate(flops=int(2.0e10), bytes_accessed=30 * 2**20, transcendentals=0),
        name="feed_forward",
    )(place, ids, slots, *boxes, response, rows, cotangent)


AXES = ("seq", "batch")
PAIR = [(0, 1), (1, 0)]


def hop(v, step):
    return lax.ppermute(v, "seq", [(i, i ^ step) for i in range(16)])


def swap_cores(v):
    return lax.ppermute(v, "batch", PAIR)


def direct():
    return lax.axis_size("seq") == 16 and lax.axis_size("batch") == 2


def device_index():
    return lax.axis_index("seq") * lax.axis_size("batch") + lax.axis_index("batch")


def places_of(steps, other):
    seq, batch = lax.axis_index("seq"), lax.axis_index("batch")
    return 2 * (seq ^ np.asarray(steps, np.int32)) + (batch ^ other)


def cuts_of(tiles):
    one = round(tiles * (1.0 - Z_FIRST) / 2)
    return one, 2 * one


def container(master, share, devices):
    _, tiles, _ = lay(share, devices)
    box = lax.dynamic_update_slice(jnp.zeros((tiles * TILE,), f32), master, (device_index() * share % TILE,))
    return box.reshape(tiles * 8, CH)


def gather_near(box):
    half = box.shape[0] // 16 * 8
    sets = [box] + [hop(box, step) for step in (4, 8, 12)]
    return [jnp.concatenate([v[at] for v in sets]) for at in (slice(0, half), slice(half, None))]


def gather_plane(near):
    return [jnp.concatenate([near[0], hop(near[0], 1)]), jnp.concatenate([near[1], hop(near[1], 2)])]


def gather_cores(plane, far, tiles):
    half = tiles // 2
    arrays, streams, ids = [], [], []
    for v, first, second in ((plane[0], 0, 1), (plane[1], 0, 2), (far[0], 2, 3), (far[1], 1, 3)):
        for other in range(2):
            arrays.append(swap_cores(v) if other else v)
            streams.append(((0, half) if len(arrays) % 4 in (1, 2) else (half, tiles)) + (8 * len(ids), 8))
            ids.append(places_of([4 * z + p for p in (first, second) for z in range(4)], other))
    return tuple(streams), jnp.concatenate(ids).astype(jnp.int32), arrays


def scatter_plan(share, devices):
    _, tiles, _ = lay(share, devices)
    if not direct():
        return ((0, tiles),), jnp.arange(devices, dtype=jnp.int32)
    one, two = cuts_of(tiles)
    index = np.arange(devices, dtype=np.int32)
    step, other = index // 2 ^ lax.axis_index("seq"), index % 2 ^ lax.axis_index("batch")
    slots = []
    for bits in ((1, 2, 8, 4), (2, 1, 8, 4), (8, 4, 2, 1)):
        at = 16 * other
        for k, bit in enumerate(bits[::-1]):
            at = at + jnp.where(step & bit != 0, 1 << k, 0)
        slots.append(at)
    return ((0, one), (one, two), (two, tiles)), jnp.concatenate(slots).astype(jnp.int32)


def pieces(v, count):
    return v.reshape(count, -1, CH)


def halve(two, step):
    return pieces(two[0] + hop(two[1], step), 2)


def join_cores(arrays):
    sums = []
    for own, far in zip(arrays[::2], arrays[1::2]):
        own, far = pieces(own, 2), pieces(swap_cores(far), 2)
        sums.append([own[k] + far[k] for k in range(2)])
    return sums


def join_first(sums):
    return [halve(v, step) for v, step in zip(sums, (1, 2, 8))]


def join_second(sums):
    return [halve(v, step) for v, step in zip(sums, (2, 1, 4))]


def join_last(sums):
    rows = [pieces(v.reshape(-1, CH), 4) for v in sums[:2]]
    four = [jnp.concatenate([v[k] for v in rows]) for k in range(4)]
    near = halve(sums[2], 2)
    one = four[0] + hop(four[1], 4) + hop(four[2], 8) + hop(four[3], 12)
    return jnp.concatenate([one, near[0] + hop(near[1], 1)])


MODE_ROWS = 65


def scatter_modes(master):
    other = swap_cores(master)
    even = lax.axis_index("batch") == 0
    lead = jnp.concatenate([jnp.where(even, master, other), jnp.where(even, other, master)])[:MODE_TILES * TILE]
    small = lead[:4 * D].reshape(4, 16, 32).transpose(1, 0, 2).reshape(16, 1, CH)
    rest = lead[4 * D:].reshape(4, 16, 16, CH).transpose(1, 0, 2, 3).reshape(16, 64, CH)
    blocks = jnp.concatenate([small, rest], axis=1)
    seq = lax.axis_index("seq")
    blocks = blocks.reshape(2, 2, 2, 2, MODE_ROWS, CH).transpose(3, 2, 1, 0, 4, 5)
    for step in (1, 2, 4, 8):
        come = lax.ppermute(blocks[1], "seq", [(i, i + step) for i in range(step)])
        blocks = jnp.where(seq & step == 0, blocks[0], come)
    return blocks


def read_modes(block):
    nch = D // 16
    small = block[0].reshape(4, nch)
    rest = block[1:].reshape(4, nch, NSTATE)
    return small, rest


def gather_modes(block, steps):
    for step in steps:
        pairs = [(i, i - step) for i in range(2 * step) if i >= step]
        block = jnp.concatenate([block, lax.ppermute(block, "seq", pairs)])
    return block


def mode_vector(block):
    blocks = block.reshape(2, 2, 2, 2, 3, -1, CH).transpose(4, 3, 2, 1, 0, 5, 6).reshape(3, D, CH)
    few = blocks[2, :, :4].T
    return jnp.concatenate([v.reshape(-1) for v in (few, blocks[0, :, :NSTATE], blocks[0, :, NSTATE:], blocks[1, :, :NSTATE], blocks[1, :, NSTATE:])])


def total_of(v):
    if not direct():
        return lax.psum(v, AXES)
    terms = lax.all_to_all(jnp.broadcast_to(v, (32, CH)), AXES, 0, 0)
    return jnp.sum(terms[:, 0])


def to_channels(rows):
    seq = lax.axis_size("seq")
    parts = rows.shape[0] // CH
    turned = rows.reshape(parts, CH, seq, D // seq).transpose(2, 0, 3, 1)
    return lax.all_to_all(turned, "seq", 0, 0).reshape(-1, CH)


def to_tokens(rows, group):
    seq = lax.axis_size("seq")
    turned = lax.all_to_all(rows.reshape(seq, group // CH, D // seq, CH), "seq", 0, 0)
    return turned.transpose(1, 3, 0, 2).reshape(group, D)


def per_device(inputs, cotangent, lengths, master, first_moment, second_moment):
    seq, batch = lax.axis_size("seq"), lax.axis_size("batch")
    devices = seq * batch
    share = master.shape[0]
    box = container(master, share, devices)
    if direct():
        near = gather_near(box)
    else:
        streams, ids = ((0, box.shape[0] // 8, 0, devices),), jnp.arange(devices, dtype=jnp.int32)
        boxes = [lax.all_gather(box, AXES, axis=0, tiled=True)]
    group = inputs.shape[1]
    nch, nck = D // seq, seq * group // CH
    rows = inputs[0].astype(jnp.float32)
    ends = jnp.cumsum(lengths[0]).astype(jnp.int32)
    place = jnp.concatenate([ends, lax.axis_index("seq")[None] * group]).astype(jnp.int32)
    first_hat, first_scale = normalize(rows)
    hats = to_channels(first_hat)

    plan, slots = scatter_plan(share, devices)

    def feed_forward(response):
        return mlp_kernel(place, streams, ids, boxes, plan, slots, response, inputs[0], cotangent[0], share, devices, seq)

    if direct():
        few, many = read_modes(scatter_modes(master))
    else:
        lead = jnp.concatenate([lax.dynamic_slice(boxes[0][j * box.shape[0]:(j + 1) * box.shape[0]].reshape(-1), (j * share % TILE,), (share,)) for j in range(MODE_TILES * TILE // share + 1)])
        mine = lambda v: lax.dynamic_slice_in_dim(v, lax.axis_index("seq") * nch, nch, 1)
        few = mine(lead[:4 * D].reshape(4, D))
        many = mine(lead[4 * D:MODE_TILES * TILE].reshape(4, D, NSTATE))
    if direct():
        plane = gather_plane(near)
    modes, coefs = mixing(few[2], many[0], many[1], many[2], many[3])
    prm = mode_rows(*modes, few[0], few[1], few[3])
    outs, prior, *tables = ssm_forward(ends, prm, hats, nck, nch)
    response = lax.all_to_all(outs.reshape(seq, -1, nch, CH), "seq", 0, 0).reshape(-1, CH)
    if direct():
        far = [hop(plane[0], 2), hop(plane[1], 1)]
        response, far = lax.optimization_barrier((response, far))
        streams, ids, boxes = gather_cores(plane, far, box.shape[0] // 8)
    output, d_mid, d_response, lead, *packed = feed_forward(response)
    d_outs = lax.all_to_all(d_response.reshape(seq, -1, nch, CH), "seq", 0, 0).reshape(-1, CH)
    if direct():
        packed = join_cores(packed)
        d_outs, packed = lax.optimization_barrier((d_outs, packed))
    d_signals, sums = ssm_backward(ends, prm, hats, d_outs, prior, tables, coefs, nck, nch)
    if direct():
        d_signals, sums, packed = lax.optimization_barrier((d_signals, sums, join_first(packed)))
    d_signal = to_tokens(d_signals, group)
    norm_gain = lead[:D // CH].reshape(D)
    me = device_index()
    if direct():
        own = sums.reshape(-1, CH)
        own, packed = lax.optimization_barrier((own + swap_cores(own), join_second(packed)))
        box, block, d_signal = lax.optimization_barrier((join_last(packed), gather_modes(own, (8, 4, 2)), d_signal))
    else:
        box = lax.psum_scatter(packed[0].reshape(devices, -1, CH), AXES, scatter_dimension=0)
    d_rows = d_mid + norm_back(d_signal * norm_gain, first_hat, first_scale)
    shard = lax.dynamic_slice(box.reshape(-1), (me * share % TILE,), (share,))
    mark = me * share + jnp.arange(share, dtype=jnp.int32) < MODE_TILES * TILE
    squares = jnp.sum(jnp.where(mark, 0.0, shard * shard))
    if direct():
        squares = squares + 0.5 * jnp.sum(own * own)
        lead = mode_vector(gather_modes(block, (1,)))
    else:

        def spread(v):
            whole = jnp.zeros((v.shape[0], D) + v.shape[2:], f32)
            return lax.dynamic_update_slice_in_dim(whole, v, lax.axis_index("seq") * nch, 1)

        few = sums[2, :, :4].T
        many = jnp.stack([sums[0, :, :NSTATE], sums[0, :, NSTATE:], sums[1, :, :NSTATE], sums[1, :, NSTATE:]])
        lead = lax.psum(jnp.concatenate([spread(few).reshape(-1), spread(many).reshape(-1)]), AXES)
        squares = squares + jnp.sum(lead * lead) / devices
    lead = lax.dynamic_slice(jnp.pad(lead, (0, share)), (jnp.minimum(me * share, MODE_TILES * TILE),), (share,))
    shard = jnp.where(mark, lead, shard)
    total = total_of(squares)
    grad_norm = jnp.sqrt(total)
    factor = jnp.minimum(1.0, 1.0 / (grad_norm + 1e-06))
    clipped = shard * factor
    first_new = 0.9 * first_moment + 0.1 * clipped
    second_new = 0.999 * second_moment + 0.001 * clipped * clipped
    first_hat_new = first_new / (1.0 - 0.9**10)
    second_hat_new = second_new / (1.0 - 0.999**10)
    update = -0.05 * (first_hat_new / (jnp.sqrt(second_hat_new) + 1e-08) + 0.1 * master)
    return (output[None], d_rows[None], shard, update, first_new, second_new, grad_norm)


def solution(mesh):
    placed = (
        P("batch", "seq", None),
        P("batch", "seq", None),
        P("batch", None),
        P(("seq", "batch")),
        P(("seq", "batch")),
        P(("seq", "batch")),
    )
    return jax.shard_map(
        per_device,
        mesh=mesh,
        in_specs=placed,
        out_specs=(
            P("batch", "seq", None),
            P("batch", "seq", None),
            P(("seq", "batch")),
            P(("seq", "batch")),
            P(("seq", "batch")),
            P(("seq", "batch")),
            P(),
        ),
        check_vma=False,
    )
```
